32 devices in a mesh: samp: 8 (over z, y), feat: 4 (over x, core).
Axes of the slice: x: 2, y: 2, z: 4, core: 2. Of those that a mesh axis runs over, the one named last changes fastest.
Arguments:
- layer_input: bfloat16 [512, 64, 512], P('samp', 'feat'), may hold values from -6 to 6
- segment_ids: int32 [512], replicated, may hold values from 0 to 3, as said below
- context_flags: int32 [512], replicated, may hold values from 0 to 1, as said below
- first_gain: float32 [512], replicated, may hold values from 0.1 to 1.9
- first_shift: float32 [512], replicated, may hold values from -3 to 3
- sample_weight: bfloat16 [512, 1536], replicated, may hold values from -0.25 to 0.25
- sample_bias: float32 [1024], replicated, may hold values from -3 to 3
- sample_mixer: bfloat16 [512, 512], replicated, may hold values from -1 to 1
- sample_offset: float32 [512], replicated, may hold values from -3 to 3
- second_gain: float32 [512], replicated, may hold values from 0.1 to 1.9
- second_shift: float32 [512], replicated, may hold values from -3 to 3
- feature_weight: bfloat16 [512, 1536], replicated, may hold values from -0.25 to 0.25
- feature_bias: float32 [1024], replicated, may hold values from -3 to 3
- feature_mixer: bfloat16 [512, 512], replicated, may hold values from -1.5 to 1.5
- feature_offset: float32 [512], replicated, may hold values from -3 to 3
- third_gain: float32 [512], replicated, may hold values from 0.1 to 1.9
- third_shift: float32 [512], replicated, may hold values from -3 to 3
- expand_weight: bfloat16 [512, 2048], replicated, may hold values from -0.25 to 0.25
- expand_bias: float32 [2048], replicated, may hold values from -3 to 3
- reduce_weight: bfloat16 [2048, 512], replicated, may hold values from -0.125 to 0.125
- reduce_bias: float32 [512], replicated, may hold values from -3 to 3
- cotangent: bfloat16 [512, 64, 512], P('samp', 'feat'), may hold values from -6 to 6
Outputs:
- layer_output: bfloat16 [512, 64, 512], P('samp', 'feat')
- input_grad: bfloat16 [512, 64, 512], P('samp', 'feat')
- first_gain_grad: float32 [512], P('samp')
- first_shift_grad: float32 [512], P('samp')
- sample_weight_grad: float32 [512, 1536], P('samp')
- sample_bias_grad: float32 [1024], P('samp')
- sample_mixer_grad: float32 [512, 512], P('samp')
- sample_offset_grad: float32 [512], P('samp')
- second_gain_grad: float32 [512], P('samp')
- second_shift_grad: float32 [512], P('samp')
- feature_weight_grad: float32 [512, 1536], P('samp')
- feature_bias_grad: float32 [1024], P('samp')
- feature_mixer_grad: float32 [512, 512], P('samp')
- feature_offset_grad: float32 [512], P('samp')
- third_gain_grad: float32 [512], P('samp')
- third_shift_grad: float32 [512], P('samp')
- expand_weight_grad: float32 [512, 2048], P('samp')
- expand_bias_grad: float32 [2048], P('samp')
- reduce_weight_grad: float32 [2048, 512], P('samp')
- reduce_bias_grad: float32 [512], P('samp')
The draws below stay inside these ranges and needn't reach their ends.
Inputs may be any that keep to these rules, and one draw needn't show every extreme that they name: `context_flags`: the samples of one index of samp (an aligned block of 64 samples) are all context samples or all query samples; exactly 1 block are context blocks, which ones is drawn. `segment_ids`: every task holds exactly 16 context samples.
All inputs are finite; a program needn't handle non-finite values.
Results may differ from the reference program's by a relative error of at most 0.017.
Values may be sent and summed in bfloat16 or wider, within the bound.
No kernel may reach another device: no remote copies, remote signals or barrier semaphores. Data moves between devices by JAX's collectives and lax.ppermute only.
A program may use at most 256 MiB of HBM per device.

```python
import jax
import jax.numpy as jnp
from jax import lax

D = 512
HEADS = 8
HEAD_DIM = 64
FF = 2048
FEATURES = 64
SAMPLE_DEV = 64
TASKS = 4
SAMPLES = 512
CONTEXT = 64


def task_layout(key):
    base = jax.random.fold_in(key, 11)
    blocks = SAMPLES // SAMPLE_DEV
    context_blocks = CONTEXT // SAMPLE_DEV
    order_blocks = jax.random.permutation(jax.random.fold_in(base, 1), blocks)
    block_flags = (order_blocks < context_blocks).astype(jnp.int32)
    flag_rows = jnp.repeat(block_flags, SAMPLE_DEV, total_repeat_length=SAMPLES).astype(jnp.int32)
    context_rank = jnp.clip(jnp.cumsum(flag_rows) - 1, 0, CONTEXT - 1)
    shuffled = jax.random.permutation(jax.random.fold_in(base, 2), CONTEXT)
    context_task = (shuffled % TASKS).astype(jnp.int32)
    query_task = jax.random.randint(jax.random.fold_in(base, 3), (SAMPLES,), 0, TASKS)
    task_rows = jnp.where(flag_rows == 1, context_task[context_rank], query_task)
    return (task_rows.astype(jnp.int32), flag_rows)


def draw_segment_ids(key, part):
    return task_layout(key)[0]


def draw_context_flags(key, part):
    return task_layout(key)[1]


def shard_levels(rng, shape, shards, least, top_value):
    factor_of, own = 1.0, jax.random.fold_in(rng, 6)
    for dim, parts in shards:
        steps = jnp.exp(jax.random.uniform(jax.random.fold_in(own, dim), (parts,), jnp.float32, least / len(shards), top_value / len(shards)))
        factor_of = factor_of * jnp.repeat(steps, shape[dim] // parts).reshape([-1 if axis == dim else 1 for axis in range(len(shape))])
    return factor_of


def gaussian(stream_key, shape, scale, limit, cuts=(), dtype=jnp.bfloat16):
    factor_of = shard_levels(stream_key, shape, cuts, -0.22, 0.18) if cuts else 1.0
    drawn = jax.random.normal(stream_key, shape, jnp.float32) * scale * factor_of
    return jnp.minimum(jnp.maximum(drawn, -limit), limit).astype(dtype)


def setup_inputs(seed: int = 0) -> dict:
    keys = jax.random.split(jax.random.key(seed), 23)
    return {
        "layer_input": gaussian(keys[0], (SAMPLES, FEATURES, D), 1.0, 6.0, ((0, 8), (1, 4))),
        "segment_ids": draw_segment_ids(jax.random.fold_in(keys[22], 71), 0),
        "context_flags": draw_context_flags(jax.random.fold_in(keys[22], 71), 0),
        "first_gain": jnp.clip(1.0 + 0.18 * jax.random.normal(keys[3], (D,), jnp.float32), 0.1, 1.9),
        "first_shift": gaussian(keys[4], (D,), 0.5, 3.0, (), jnp.float32),
        "sample_weight": gaussian(keys[5], (D, 3 * D), D ** -0.5, 0.25),
        "sample_bias": gaussian(keys[6], (2 * D,), 0.5, 3.0, (), jnp.float32),
        "sample_mixer": gaussian(keys[7], (D, D), (D // 16) ** -0.5, 1.0),
        "sample_offset": gaussian(keys[8], (D,), 0.5, 3.0, (), jnp.float32),
        "second_gain": jnp.clip(1.0 + 0.18 * jax.random.normal(keys[9], (D,), jnp.float32), 0.1, 1.9),
        "second_shift": gaussian(keys[10], (D,), 0.5, 3.0, (), jnp.float32),
        "feature_weight": gaussian(keys[11], (D, 3 * D), D ** -0.5, 0.25),
        "feature_bias": gaussian(keys[12], (2 * D,), 0.5, 3.0, (), jnp.float32),
        "feature_mixer": gaussian(keys[13], (D, D), (D // 32) ** -0.5, 1.5),
        "feature_offset": gaussian(keys[14], (D,), 0.5, 3.0, (), jnp.float32),
        "third_gain": jnp.clip(1.0 + 0.18 * jax.random.normal(keys[15], (D,), jnp.float32), 0.1, 1.9),
        "third_shift": gaussian(keys[16], (D,), 0.5, 3.0, (), jnp.float32),
        "expand_weight": gaussian(keys[17], (D, FF), D ** -0.5, 0.25),
        "expand_bias": gaussian(keys[18], (FF,), 0.5, 3.0, (), jnp.float32),
        "reduce_weight": gaussian(keys[19], (FF, D), FF ** -0.5, 0.125),
        "reduce_bias": gaussian(keys[20], (D,), 0.5, 3.0, (), jnp.float32),
        "cotangent": gaussian(keys[21], (SAMPLES, FEATURES, D), 1.0, 6.0, ((0, 8), (1, 4))),
    }


@jax.custom_vjp
def low(v):
    return lax.optimization_barrier(v.astype(jnp.bfloat16)).astype(jnp.float32)

@jax.custom_vjp
def low_back(v):
    return v

def low_keep(v):
    return (low(v), None)

def low_pass(kept, grad):
    return (grad,)

def back_keep(v):
    return (v, None)

def back_low(kept, grad):
    return (low(grad),)
low.defvjp(low_keep, low_pass)
low_back.defvjp(back_keep, back_low)
EPS = 1e-05
MASKED = -1000000000.0
HIGHEST_PRECISION = lax.Precision.HIGHEST

def layer_norm(values, gain_row, shift_row):
    center = lax.optimization_barrier(jnp.mean(values, axis=-1, keepdims=True))
    spread = values - center
    variance = lax.optimization_barrier(jnp.mean(spread * spread, axis=-1, keepdims=True))
    return spread * lax.rsqrt(variance + EPS) * gain_row + shift_row

def apply_weight(active, weight):
    return jnp.einsum('sfd,de->sfe', active, weight, precision=HIGHEST_PRECISION)

def project(active, weight, bias_row):
    model_width = active.shape[-1]
    joined = apply_weight(active, weight)
    queries = low(low_back(joined[..., :model_width] + bias_row[:model_width]))
    key_part = low(low_back(joined[..., model_width:2 * model_width]))
    value_part = low(low_back(joined[..., 2 * model_width:] + bias_row[model_width:]))
    return (queries, key_part, value_part)

def layer(inputs, parameters, allowed, context_index):
    first_gain, first_shift, sample_weight, sample_bias, sample_mixer, sample_offset, second_gain, second_shift, feature_weight, feature_bias, feature_mixer, feature_offset, third_gain, third_shift, expand_weight, expand_bias, reduce_weight, reduce_bias = parameters
    samples, features, model_width = inputs.shape
    blocks = samples // SAMPLE_DEV
    score_scale = HEAD_DIM ** (-0.5)

    def section_one(block):
        normed = low(layer_norm(block, first_gain, first_shift))
        return project(normed, sample_weight, sample_bias)
    queries, key_part, value_part = lax.map(jax.checkpoint(section_one), inputs.reshape(blocks, SAMPLE_DEV, features, model_width))
    head_shape = (samples, features, HEADS, HEAD_DIM)
    queries = queries.reshape(head_shape)
    context_keys = key_part.reshape(head_shape)[context_index]
    context_values = value_part.reshape(head_shape)[context_index]

    def one_feature(operands):
        feature_queries, feature_keys, feature_values = operands
        scores = low_back(jnp.einsum('ihd,jhd->hij', feature_queries, feature_keys, precision=HIGHEST_PRECISION) * score_scale)
        masked = jnp.where(allowed[None], scores, MASKED)
        weights = low(jax.nn.softmax(masked, axis=-1))
        return jnp.einsum('hij,jhd->ihd', weights, feature_values, precision=HIGHEST_PRECISION)
    attended = lax.map(jax.checkpoint(one_feature), (queries.transpose(1, 0, 2, 3), context_keys.transpose(1, 0, 2, 3), context_values.transpose(1, 0, 2, 3)))
    mixed = low(low_back(attended.transpose(1, 0, 2, 3).reshape(samples, features, model_width)))

    def section_three(operands):
        block, mixed_block = operands
        first = block + low_back(apply_weight(mixed_block, sample_mixer) + sample_offset)
        normed = low(layer_norm(first, second_gain, second_shift))
        feature_queries, feature_keys, feature_values = project(normed, feature_weight, feature_bias)
        block_shape = (SAMPLE_DEV, features, HEADS, HEAD_DIM)
        scores = low_back(jnp.einsum('sfhd,sghd->shfg', feature_queries.reshape(block_shape), feature_keys.reshape(block_shape), precision=HIGHEST_PRECISION) * score_scale)
        weights = low(jax.nn.softmax(scores, axis=-1))
        attended_block = jnp.einsum('shfg,sghd->sfhd', weights, feature_values.reshape(block_shape), precision=HIGHEST_PRECISION).reshape(SAMPLE_DEV, features, model_width)
        second = first + low_back(apply_weight(low(low_back(attended_block)), feature_mixer) + feature_offset)
        normed_three = low(layer_norm(second, third_gain, third_shift))
        expanded = low_back(apply_weight(normed_three, expand_weight) + expand_bias)
        hidden = low(low_back(jax.nn.gelu(expanded, approximate=False)))
        return second + low_back(apply_weight(hidden, reduce_weight) + reduce_bias)
    result = lax.map(jax.checkpoint(section_three), (inputs.reshape(blocks, SAMPLE_DEV, features, model_width), mixed.reshape(blocks, SAMPLE_DEV, features, model_width)))
    return result.reshape(samples, features, model_width)

def reference(layer_input, segment_ids, context_flags, first_gain, first_shift, sample_weight, sample_bias, sample_mixer, sample_offset, second_gain, second_shift, feature_weight, feature_bias, feature_mixer, feature_offset, third_gain, third_shift, expand_weight, expand_bias, reduce_weight, reduce_bias, cotangent):
    context_index = jnp.nonzero(context_flags == 1, size=CONTEXT)[0].astype(jnp.int32)
    context_tasks = segment_ids[context_index]
    allowed = segment_ids[:, None] == context_tasks[None, :]
    parameters = tuple((entry.astype(jnp.float32) for entry in (first_gain, first_shift, sample_weight, sample_bias, sample_mixer, sample_offset, second_gain, second_shift, feature_weight, feature_bias, feature_mixer, feature_offset, third_gain, third_shift, expand_weight, expand_bias, reduce_weight, reduce_bias)))

    def forward(inputs, *weights_all):
        return layer(inputs, weights_all, allowed, context_index)
    output, pullback = jax.vjp(forward, layer_input.astype(jnp.float32), *parameters)
    gradients = pullback(cotangent.astype(jnp.float32))
    return (output.astype(jnp.bfloat16), gradients[0].astype(jnp.bfloat16), gradients[1], gradients[2], gradients[3], gradients[4], gradients[5], gradients[6], gradients[7], gradients[8], gradients[9], gradients[10], gradients[11], gradients[12], gradients[13], gradients[14], gradients[15], gradients[16], gradients[17], gradients[18])
```

```python
from functools import partial

import jax
import jax.numpy as jnp
from jax import lax
from jax.experimental import pallas as pl
from jax.experimental.pallas import tpu as pltpu
from jax.sharding import PartitionSpec as P

HEADS = 8
HEAD_DIM = 64
EPS = 1e-05
MASKED = -1000000000.0
SCALE = HEAD_DIM ** (-0.5)
QUAD = 4 * HEAD_DIM
BF = jnp.bfloat16
F32 = jnp.float32
VMEM_LIMIT = 56 << 20


def mm(a, b, ca=1, cb=0):
    return lax.dot_general(a, b, (((ca,), (cb,)), ((), ())), preferred_element_type=F32)


def norm_parts(values):
    center = jnp.mean(values, axis=-1, keepdims=True)
    spread = values - center
    variance = jnp.mean(spread * spread, axis=-1, keepdims=True)
    inverse = lax.rsqrt(variance + EPS)
    return spread * inverse, inverse


def norm_back(grad, unit, inverse, gain):
    scaled = grad * gain
    first = jnp.mean(scaled, axis=-1, keepdims=True)
    second = jnp.mean(scaled * unit, axis=-1, keepdims=True)
    return (scaled - first - unit * second) * inverse


def lane_ids(rows):
    return lax.broadcasted_iota(jnp.int32, (rows, 128), 1)


def group_reduce(values, op, fill):
    rows = values.shape[0]
    low = lane_ids(rows) < HEAD_DIM
    outs = []
    for t in range(values.shape[1] // 128):
        tile = values[:, t * 128 : (t + 1) * 128]
        left = op(jnp.where(low, tile, fill), axis=1, keepdims=True)
        right = op(jnp.where(low, fill, tile), axis=1, keepdims=True)
        outs.append(jnp.where(low, left, right))
    return jnp.concatenate(outs, axis=1)


def head_masks(dtype):
    lanes = lax.broadcasted_iota(jnp.int32, (1, QUAD), 1) // HEAD_DIM
    return [jnp.where(lanes == h, 1.0, 0.0).astype(dtype) for h in range(4)]


def stack_heads(part, masks):
    return jnp.concatenate([part * m for m in masks], axis=0)


def pick_heads(stacked, masks):
    rows = stacked.shape[0] // 4
    total = stacked[:rows] * masks[0]
    for h in range(1, 4):
        total = total + stacked[h * rows : (h + 1) * rows] * masks[h]
    return total


def attend(q, k, v, masks, allow):
    outs, probs = [], []
    for quad in range(2):
        cols = slice(quad * QUAD, (quad + 1) * QUAD)
        scores = mm(q[:, cols], stack_heads(k[:, cols], masks), 1, 1)
        if allow is not None:
            scores = jnp.where(allow, scores, MASKED)
        raised = jnp.exp(scores - group_reduce(scores, jnp.max, -jnp.inf))
        prob = raised / group_reduce(raised, jnp.sum, 0.0)
        outs.append(mm(prob.astype(BF), stack_heads(v[:, cols], masks)))
        probs.append(prob)
    return jnp.concatenate(outs, axis=1), jnp.concatenate(probs, axis=1)


def attend_back(q, k, v, prob, grad, masks, masks32):
    dqs, dks, dvs = [], [], []
    for quad in range(2):
        cols = slice(quad * QUAD, (quad + 1) * QUAD)
        p, g = prob[:, cols], grad[:, cols]
        back = mm(g, stack_heads(v[:, cols], masks), 1, 1)
        inner = group_reduce(p * back, jnp.sum, 0.0)
        gs = (p * (back - inner)).astype(BF)
        dqs.append(mm(gs, stack_heads(k[:, cols], masks)) * SCALE)
        dks.append(pick_heads(mm(gs, q[:, cols], 0, 0), masks32))
        dvs.append(pick_heads(mm(p.astype(BF), g, 0, 0), masks32))
    join = lambda parts: jnp.concatenate(parts, axis=1).astype(BF)
    return join(dqs), join(dks), join(dvs)


def swap_matrix(n):
    r = lax.broadcasted_iota(jnp.int32, (n, n), 0)
    c = lax.broadcasted_iota(jnp.int32, (n, n), 1)
    return jnp.where((r // 16 == c % 16) & (r % 16 == c // 16), 1.0, 0.0).astype(BF)


def swap(matrix, values):
    return mm(matrix, values).astype(BF)


def gelu_parts(u):
    cdf = 0.5 * (1.0 + lax.erf(u * (2.0**-0.5)))
    density = jnp.exp(u * u * -0.5) * 0.3989422804014327
    return cdf, density


def col_sum(values):
    return jnp.sum(values.astype(F32), axis=0, keepdims=True)


def forward_one(
    me_ref, x_ref, c_ref, allow_ref, gain_ref, shift_ref, w_ref, b_ref,
    o_ref, q_ref, k_ref, v_ref, p_ref, o_scr,
):
    me = me_ref[0]
    gain, shift = gain_ref[...], shift_ref[...]
    matrix = swap_matrix(256)
    for d in range(4):
        unit, _ = norm_parts(x_ref[d ^ me].astype(F32))
        act = swap(matrix, (unit * gain + shift).astype(BF))
        q = (mm(act, w_ref[:, :512]) + b_ref[:, :512]).astype(BF) * SCALE
        q_ref[:, d] = q.astype(BF).reshape(16, 16, 512)
        unit, _ = norm_parts(c_ref[d].astype(F32))
        act = swap(matrix, (unit * gain + shift).astype(BF))
        kv = mm(act, w_ref[:, 512:])
        k_ref[:, d] = kv[:, :512].astype(BF).reshape(16, 16, 512)
        v_ref[:, d] = (kv[:, 512:] + b_ref[:, 512:]).astype(BF).reshape(16, 16, 512)
    masks = head_masks(BF)
    allow = allow_ref[...] > 0.5

    def body(i, carry):
        for j in range(2):
            f = i * 2 + j
            q, k, v = (r[f].reshape(64, 512) for r in (q_ref, k_ref, v_ref))
            out, prob = attend(q, k, v, masks, allow)
            o_scr[f] = out.astype(BF).reshape(4, 16, 512)
            p_ref[f] = prob
        return carry

    lax.fori_loop(0, 8, body, 0)
    for d in range(4):
        o_ref[d] = swap(matrix, o_scr[:, d].reshape(256, 512))


def middle(
    o1_ref, x_ref, cot_ref,
    wm1_ref, off1_ref, g2_ref, s2_ref, wf_ref, bf_ref, wm2_ref, off2_ref,
    g3_ref, s3_ref, we_ref, be_ref, wr_ref, br_ref,
    out_ref, gb1_ref, a2_ref, dqkv_ref, o2_ref, gb2_ref, a3_ref, gu_ref, hid_ref, gb3_ref,
    vec_ref, bias_ref,
):
    samples = 4

    def gather(ref):
        return jnp.concatenate(
            [ref[d, s * 16 : (s + 1) * 16] for s in range(samples) for d in range(4)], axis=0
        )

    def scatter(ref, values):
        for s in range(samples):
            for d in range(4):
                at = (s * 4 + d) * 16
                ref[d, s * 16 : (s + 1) * 16] = values[at : at + 16]

    masks, masks32 = head_masks(BF), head_masks(F32)
    o1, cot = gather(o1_ref), gather(cot_ref)
    gb3_ref[...] = cot
    r1 = gather(x_ref).astype(F32) + mm(o1, wm1_ref[...]) + off1_ref[...]
    unit2, inv2 = norm_parts(r1)
    act2 = (unit2 * g2_ref[...] + s2_ref[...]).astype(BF)
    a2_ref[...] = act2
    qkv = mm(act2, wf_ref[...])
    q = (qkv[:, :512] + bf_ref[:, :512]).astype(BF) * jnp.asarray(SCALE, BF)
    k = qkv[:, 512:1024].astype(BF)
    v = (qkv[:, 1024:] + bf_ref[:, 512:]).astype(BF)
    parts = []
    for s in range(samples):
        rows = slice(s * 64, (s + 1) * 64)
        parts.append(attend(q[rows], k[rows], v[rows], masks, None))
    o2 = jnp.concatenate([part[0] for part in parts], axis=0).astype(BF)
    o2_ref[...] = o2
    r2 = r1 + mm(o2, wm2_ref[...]) + off2_ref[...]
    unit3, inv3 = norm_parts(r2)
    act3 = (unit3 * g3_ref[...] + s3_ref[...]).astype(BF)
    a3_ref[...] = act3
    out = r2 + br_ref[...]
    back = None
    bias = []
    for b in range(4):
        cols = slice(b * 512, (b + 1) * 512)
        u = mm(act3, we_ref[:, cols]) + be_ref[:, cols]
        cdf, density = gelu_parts(u)
        hidden = (u * cdf).astype(BF)
        hid_ref[:, cols] = hidden
        out = out + mm(hidden, wr_ref[cols, :])
        gh = mm(cot, wr_ref[cols, :], 1, 1).astype(BF).astype(F32)
        gu = (gh * (cdf + u * density)).astype(BF)
        gu_ref[:, cols] = gu
        bias.append(col_sum(gu))
        term = mm(gu, we_ref[:, cols], 1, 1)
        back = term if back is None else back + term
    scatter(out_ref, out.astype(BF))
    vecs = [col_sum(back * unit3), col_sum(back)]
    gr2 = cot.astype(F32) + norm_back(back, unit3, inv3, g3_ref[...])
    gb2 = gr2.astype(BF)
    gb2_ref[...] = gb2
    go2 = mm(gb2, wm2_ref[...], 1, 1).astype(BF)
    grads = []
    for s in range(samples):
        rows = slice(s * 64, (s + 1) * 64)
        grads.append(
            jnp.concatenate(
                attend_back(q[rows], k[rows], v[rows], parts[s][1], go2[rows], masks, masks32),
                axis=1,
            )
        )
    dqkv = jnp.concatenate(grads, axis=0)
    dqkv_ref[...] = dqkv
    back = mm(dqkv, wf_ref[...], 1, 1)
    vecs += [col_sum(back * unit2), col_sum(back)]
    gr1 = gr2 + norm_back(back, unit2, inv2, g2_ref[...])
    scatter(gb1_ref, gr1.astype(BF))
    vecs += [col_sum(gb2), col_sum(cot), col_sum(dqkv[:, :512]), col_sum(dqkv[:, 1024:])]

    @pl.when(pl.program_id(0) == 0)
    def _():
        vec_ref[...] = jnp.zeros_like(vec_ref)
        bias_ref[...] = jnp.zeros_like(bias_ref)

    vec_ref[...] += jnp.concatenate(vecs, axis=0)
    bias_ref[...] += jnp.concatenate(bias, axis=1)


def backward_one(
    me_ref, gb1_ref, x_ref, c_ref, q_ref, k_ref, v_ref, p_ref, gain_ref, shift_ref, w_ref, wm_ref,
    base_ref, term_ref, act_ref, dq_ref, cact_ref, dkv_ref, vec_ref,
    go_scr, dq_scr, dkv_scr,
):
    me = me_ref[0]
    gain, shift = gain_ref[...], shift_ref[...]
    matrix = swap_matrix(256)
    masks, masks32 = head_masks(BF), head_masks(F32)
    for d in range(4):
        go = mm(gb1_ref[d], wm_ref[...], 1, 1).astype(BF)
        go_scr[:, d] = swap(matrix, go).reshape(16, 16, 512)

    def body(i, carry):
        for j in range(2):
            f = i * 2 + j
            q, k, v, go = (r[f].reshape(64, 512) for r in (q_ref, k_ref, v_ref, go_scr))
            dq, dk, dv = attend_back(q, k, v, p_ref[f], go, masks, masks32)
            dq_scr[f] = dq.reshape(4, 16, 512)
            dkv_scr[f] = jnp.concatenate([dk, dv], axis=1).reshape(4, 16, 1024)
        return carry

    lax.fori_loop(0, 8, body, 0)
    gain_sum = jnp.zeros((1, 512), F32)
    shift_sum, off_sum, q_sum, v_sum = gain_sum, gain_sum, gain_sum, gain_sum
    for d in range(4):
        unit, inverse = norm_parts(x_ref[d ^ me].astype(F32))
        act_ref[d] = (unit * gain + shift).astype(BF)
        dq = swap(matrix, dq_scr[:, d].reshape(256, 512))
        dq_ref[d] = dq
        back = mm(dq, w_ref[:, :512], 1, 1)
        base_ref[d] = gb1_ref[d].astype(F32) + norm_back(back, unit, inverse, gain)
        gain_sum += col_sum(back * unit)
        shift_sum += col_sum(back)
        off_sum += col_sum(gb1_ref[d])
        q_sum += col_sum(dq)
        unit, inverse = norm_parts(c_ref[d].astype(F32))
        cact_ref[d] = (unit * gain + shift).astype(BF)
        dkv = swap(matrix, dkv_scr[:, d].reshape(256, 1024))
        dkv_ref[d] = dkv
        back = mm(dkv, w_ref[:, 512:], 1, 1)
        term_ref[d] = back.astype(BF)
        gain_sum += col_sum(back * unit)
        shift_sum += col_sum(back)
        v_sum += col_sum(dkv[:, 512:])
    zero = jnp.zeros((1, 512), F32)
    vec_ref[...] = jnp.concatenate(
        [gain_sum, shift_sum, off_sum, q_sum, v_sum, zero, zero, zero], axis=0
    )


def finish(
    me_ref, base_ref, sum_ref, x_ref, gain_ref, out_ref,
):
    unit, inverse = norm_parts(x_ref[0].astype(F32))
    extra = norm_back(sum_ref[0].astype(F32), unit, inverse, gain_ref[...])
    out_ref[0] = (base_ref[0] + jnp.where(me_ref[1] == 1, extra, 0.0)).astype(BF)


def spec(shape, index=None):
    return pl.BlockSpec(shape, index if index is not None else (lambda *a: (0,) * len(shape)))


def sds(shape, dtype=BF):
    return jax.ShapeDtypeStruct(shape, dtype)


def params():
    return pltpu.CompilerParams(vmem_limit_bytes=VMEM_LIMIT)


def row(vector):
    return vector.reshape(1, -1)


def shuffle(value, axis, mask, names=None):
    size = lax.axis_size(axis)
    return lax.ppermute(value, axis, [(i, i ^ mask) for i in range(size)])


def at(stacked, index, axis=0):
    return lax.dynamic_index_in_dim(stacked, index, axis, keepdims=False)


def swap_blocks(blocks, me, axis):
    return [blocks[0]] + [shuffle(blocks[d], axis, d) for d in range(1, len(blocks))]


def reduce_rows(buffer, samp, core):
    zz, yy = samp // 2, samp % 2
    halves = buffer.reshape(8, 2, 128, 512)
    got = shuffle(at(halves, 1 - core, 1), "feat", 1)
    part = (at(halves, core, 1).astype(F32) + got.astype(F32)).astype(BF)
    part = part.reshape(4, 2, 128, 512)
    got = shuffle(at(part, 1 - yy, 1), "samp", 1)
    part = (at(part, yy, 1).astype(F32) + got.astype(F32)).astype(BF)
    total = at(part, zz).astype(F32)
    for d in range(1, 4):
        total = total + shuffle(at(part, zz ^ d), "samp", 2 * d).astype(F32)
    mine = total.astype(BF)
    total = mine.astype(F32) + shuffle(mine, "feat", 2).astype(F32)
    mine = total.astype(BF)
    other = shuffle(mine, "feat", 1)
    first = jnp.where(core == 0, mine, other)
    second = jnp.where(core == 0, other, mine)
    return jnp.concatenate([first, second], axis=0).astype(F32)


def sum_everywhere(value):
    for axis, mask in (("feat", 1), ("feat", 2), ("samp", 1), ("samp", 2), ("samp", 4)):
        value = value + shuffle(value, axis, mask)
    return value


def rows_of(grad):
    return jnp.concatenate(
        [grad[:, c : c + 512].reshape(8, 64, 512) for c in range(0, grad.shape[1], 512)], axis=1
    )


def local_small(
    layer_input, segment_ids, context_flags,
    first_gain, first_shift, sample_weight, sample_bias, sample_mixer, sample_offset,
    second_gain, second_shift, feature_weight, feature_bias, feature_mixer, feature_offset,
    third_gain, third_shift, expand_weight, expand_bias, reduce_weight, reduce_bias, cotangent,
):
    samp, feat = lax.axis_index("samp"), lax.axis_index("feat")
    core = feat % 2
    flags = context_flags.reshape(8, 64)[:, 0]
    root = jnp.argmax(flags).astype(jnp.int32)
    me = jnp.stack([feat, (root == samp).astype(jnp.int32), samp, core]).astype(jnp.int32)

    pieces = layer_input.reshape(8, 128, 512)
    sent = [at(pieces, samp)] + [shuffle(at(pieces, samp ^ d), "samp", d) for d in range(1, 8)]
    offset = samp ^ root
    piece = sent[0]
    for d in range(1, 8):
        piece = jnp.where(offset == d, sent[d], piece)
    context = jnp.concatenate(swap_blocks([piece] * 8, samp, "samp"), axis=0).reshape(4, 256, 512)
    order = (samp ^ jnp.arange(8, dtype=jnp.int32)) * 8
    order = (order[:, None] + jnp.arange(8, dtype=jnp.int32)[None, :]).reshape(64)
    context_tasks = jnp.take(jnp.take(segment_ids.reshape(8, 64), root, axis=0), order)
    blocks_of = (feat ^ jnp.arange(4, dtype=jnp.int32)) * 16
    blocks_of = (blocks_of[:, None] + jnp.arange(16, dtype=jnp.int32)[None, :]).reshape(64)
    own_tasks = jnp.take(lax.dynamic_slice_in_dim(segment_ids, samp * 64, 64), blocks_of)
    allow = (own_tasks[:, None] == context_tasks[None, :]).astype(F32)
    allow = jnp.concatenate([allow] * 4, axis=1)

    x4 = layer_input.reshape(4, 256, 512)
    cot4 = cotangent.reshape(4, 256, 512)
    x_f = jnp.stack(swap_blocks([at(x4, feat ^ d) for d in range(4)], feat, "feat"))
    cot_f = jnp.stack(swap_blocks([at(cot4, feat ^ d) for d in range(4)], feat, "feat"))

    heads = sds((16, 4, 16, 512))
    smem = pl.BlockSpec(memory_space=pltpu.SMEM)
    o1, q1, k1, v1, p1 = pl.pallas_call(
        forward_one,
        out_shape=(sds((4, 256, 512)), heads, heads, heads, sds((16, 64, 512), F32)),
        in_specs=[smem] + [pl.BlockSpec()] * 7,
        scratch_shapes=[pltpu.VMEM((16, 4, 16, 512), BF)],
        compiler_params=params(),
        name="forward_one",
    )(
        me, x4, context, allow, row(first_gain), row(first_shift), sample_weight,
        row(sample_bias),
    )
    o1_f = jnp.stack(swap_blocks([o1[d] for d in range(4)], feat, "feat"))

    weights = [
        sample_mixer, row(sample_offset), row(second_gain), row(second_shift), feature_weight,
        row(feature_bias), feature_mixer, row(feature_offset), row(third_gain), row(third_shift),
        expand_weight, row(expand_bias), reduce_weight, row(reduce_bias),
    ]
    blocked = spec((4, 64, 512), lambda i: (0, i, 0))
    wide = lambda n: spec((256, n), lambda i: (i, 0))
    out_f, gb1_f, act2, dqkv, o2, gb2, act3, gu, hidden, gb3, vec2, bias2 = pl.pallas_call(
        middle,
        grid=(4,),
        out_shape=(
            sds((4, 256, 512)), sds((4, 256, 512)), sds((1024, 512)), sds((1024, 1536)),
            sds((1024, 512)), sds((1024, 512)), sds((1024, 512)), sds((1024, 2048)),
            sds((1024, 2048)), sds((1024, 512)), sds((8, 512), F32), sds((1, 2048), F32),
        ),
        in_specs=[blocked] * 3
        + [pl.BlockSpec(w.shape, lambda i: (0, 0), pipeline_mode=pl.Buffered(1)) for w in weights],
        out_specs=[
            blocked, blocked, wide(512), wide(1536), wide(512), wide(512), wide(512), wide(2048),
            wide(2048), wide(512), spec((8, 512)), spec((1, 2048)),
        ],
        compiler_params=params(),
        name="middle",
    )(o1_f, x_f, cot_f, *weights)

    out4 = jnp.stack(swap_blocks([out_f[d] for d in range(4)], feat, "feat"))
    gb1 = jnp.stack(swap_blocks([gb1_f[d] for d in range(4)], feat, "feat"))
    order4 = feat ^ jnp.arange(4, dtype=jnp.int32)
    layer_output = jnp.take(out4, order4, axis=0).reshape(64, 16, 512)

    grad = lambda a, b: jnp.einsum("td,te->de", a, b, preferred_element_type=F32).astype(BF)
    reduce_rows_grad = reduce_rows(grad(hidden, gb3).reshape(8, 256, 512), samp, core)
    expand_rows = reduce_rows(rows_of(grad(act3, gu)), samp, core)
    feature_rows = reduce_rows(
        jnp.concatenate([rows_of(grad(act2, dqkv)), rows_of(grad(o2, gb2))], axis=1), samp, core
    )

    base, term, act1, dq1, cact, dkv, vec1 = pl.pallas_call(
        backward_one,
        out_shape=(
            sds((4, 256, 512), F32), sds((4, 256, 512)), sds((4, 256, 512)), sds((4, 256, 512)),
            sds((4, 256, 512)), sds((4, 256, 1024)), sds((8, 512), F32),
        ),
        in_specs=[smem] + [pl.BlockSpec()] * 11,
        scratch_shapes=[
            pltpu.VMEM((16, 4, 16, 512), BF),
            pltpu.VMEM((16, 4, 16, 512), BF),
            pltpu.VMEM((16, 4, 16, 1024), BF),
        ],
        compiler_params=params(),
        name="backward_one",
    )(
        me, gb1, x4, context, q1, k1, v1, p1, row(first_gain), row(first_shift), sample_weight,
        sample_mixer,
    )

    terms = term.reshape(8, 128, 512)
    total = terms[0].astype(F32)
    for d in range(1, 8):
        total = total + shuffle(terms[d], "samp", d).astype(F32)
    summed = jnp.stack(swap_blocks([total.astype(BF)] * 8, samp, "samp"))
    order8 = samp ^ jnp.arange(8, dtype=jnp.int32)
    summed = jnp.take(summed, order8, axis=0).reshape(4, 256, 512)

    flat = lambda a: a.reshape(1024, -1)
    sample_rows = reduce_rows(
        jnp.concatenate(
            [
                rows_of(grad(flat(act1), flat(dq1))),
                rows_of(grad(flat(cact), flat(dkv))),
                rows_of(grad(flat(o1), flat(gb1))),
            ],
            axis=1,
        ),
        samp,
        core,
    )
    vectors = sum_everywhere(
        jnp.concatenate([vec2.reshape(-1), bias2.reshape(-1), vec1.reshape(-1)])
    )

    input_grad = pl.pallas_call(
        finish,
        grid_spec=pltpu.PrefetchScalarGridSpec(
            num_scalar_prefetch=1,
            grid=(4,),
            in_specs=[
                spec((1, 256, 512), lambda i, m: (i ^ m[0], 0, 0)),
                spec((1, 256, 512), lambda i, m: (i, 0, 0)),
                spec((1, 256, 512), lambda i, m: (i, 0, 0)),
                spec((1, 512)),
            ],
            out_specs=spec((1, 256, 512), lambda i, m: (i, 0, 0)),
        ),
        out_shape=sds((4, 256, 512)),
        compiler_params=params(),
        name="finish",
    )(me, base, summed, x4, row(first_gain)).reshape(64, 16, 512)

    def vector(start, size):
        return lax.dynamic_slice_in_dim(vectors[start : start + size], samp * (size // 8), size // 8)

    gain3, shift3, gain2, shift2, off2, bias_r, qs2, vs2 = (vector(i * 512, 512) for i in range(8))
    expand_b = vector(4096, 2048)
    gain1, shift1, off1, qs1, vs1 = (vector(6144 + i * 512, 512) for i in range(5))

    def joined(first, second):
        both = jnp.concatenate([vectors[first : first + 512], vectors[second : second + 512]])
        return lax.dynamic_slice_in_dim(both, samp * 128, 128)

    columns = lambda rows, first, count: jnp.concatenate(
        [rows[64 * (first + i) : 64 * (first + i + 1)] for i in range(count)], axis=1
    )

    def unmix(rows):
        return rows

    return (
        layer_output, input_grad,
        gain1, shift1, columns(sample_rows, 0, 3), joined(6144 + 3 * 512, 6144 + 4 * 512),
        columns(sample_rows, 3, 1), off1,
        gain2, shift2, columns(feature_rows, 0, 3), joined(6 * 512, 7 * 512),
        columns(feature_rows, 3, 1), off2,
        gain3, shift3, columns(expand_rows, 0, 4), expand_b,
        reduce_rows_grad, bias_r,
    )


def spread_2(block, axis, owner):
    block = jnp.where(lax.axis_index(axis) == owner, block, jnp.zeros_like(block))
    return lax.psum(block, axis)


def layer_norm(values, gain_row, shift_row):
    center = jnp.mean(values, axis=-1, keepdims=True)
    spread = values - center
    variance = jnp.mean(spread * spread, axis=-1, keepdims=True)
    return spread * lax.rsqrt(variance + EPS) * gain_row + shift_row


def apply_weight(active, weight):
    return jnp.einsum("sfd,de->sfe", active, weight, preferred_element_type=jnp.float32)


def input_back(grad_out, weight):
    return jnp.einsum("sfe,de->sfd", grad_out, weight, preferred_element_type=jnp.float32)


def weight_grad(active, grad_out):
    return jnp.einsum("sfd,sfe->de", active, grad_out, preferred_element_type=jnp.float32)


def column_sum(values):
    return jnp.sum(values.astype(jnp.float32), axis=(0, 1))


def project(active, weight, bias_row):
    model_width = active.shape[-1]
    joined = apply_weight(active, weight)
    queries = (joined[..., :model_width] + bias_row[:model_width]).astype(jnp.bfloat16)
    key_part = joined[..., model_width : 2 * model_width].astype(jnp.bfloat16)
    value_part = (joined[..., 2 * model_width :] + bias_row[model_width:]).astype(jnp.bfloat16)
    return (queries, key_part, value_part)


def split_heads(values):
    return values.reshape(values.shape[0], values.shape[1], HEADS, HEAD_DIM)


def join_heads(values):
    return values.reshape(values.shape[0], values.shape[1], HEADS * HEAD_DIM)


def soft_weights(scores):
    top_score = jnp.max(scores, axis=-1, keepdims=True)
    raised = jnp.exp(scores - top_score)
    return raised / jnp.sum(raised, axis=-1, keepdims=True)


def feature_attend(queries, key_part, value_part):
    score_scale = HEAD_DIM ** (-0.5)
    scores = (
        jnp.einsum(
            "sfhd,sghd->shfg",
            split_heads(queries),
            split_heads(key_part),
            preferred_element_type=jnp.float32,
        )
        * score_scale
    )
    probability = soft_weights(scores)
    mixed = jnp.einsum(
        "shfg,sghd->sfhd",
        probability.astype(jnp.bfloat16),
        split_heads(value_part),
        preferred_element_type=jnp.float32,
    )
    return (join_heads(mixed).astype(jnp.bfloat16), probability)


def feature_grads(queries, key_part, value_part, probability, grad_mixed):
    score_scale = HEAD_DIM ** (-0.5)
    grad_heads = split_heads(grad_mixed)
    grad_weights = jnp.einsum(
        "sfhd,sghd->shfg", grad_heads, split_heads(value_part), preferred_element_type=jnp.float32
    )
    inner_sum = jnp.sum(probability * grad_weights, axis=-1, keepdims=True)
    grad_scores = (probability * (grad_weights - inner_sum)).astype(jnp.bfloat16)
    grad_queries = (
        jnp.einsum(
            "shfg,sghd->sfhd",
            grad_scores,
            split_heads(key_part),
            preferred_element_type=jnp.float32,
        )
        * score_scale
    )
    grad_keys = (
        jnp.einsum(
            "shfg,sfhd->sghd", grad_scores, split_heads(queries), preferred_element_type=jnp.float32
        )
        * score_scale
    )
    grad_values = jnp.einsum(
        "shfg,sfhd->sghd",
        probability.astype(jnp.bfloat16),
        grad_heads,
        preferred_element_type=jnp.float32,
    )
    return (join_heads(grad_queries), join_heads(grad_keys), join_heads(grad_values))


def local_large(
    layer_input,
    segment_ids,
    context_flags,
    first_gain,
    first_shift,
    sample_weight,
    sample_bias,
    sample_mixer,
    sample_offset,
    second_gain,
    second_shift,
    feature_weight,
    feature_bias,
    feature_mixer,
    feature_offset,
    third_gain,
    third_shift,
    expand_weight,
    expand_bias,
    reduce_weight,
    reduce_bias,
    cotangent,
):
    sample_rows = layer_input.shape[0]
    feature_rows = layer_input.shape[1]
    model_width = layer_input.shape[2]
    score_scale = HEAD_DIM ** (-0.5)
    shard_count = lax.axis_size("samp")
    context_shards = shard_count // 8
    total_context = context_shards * sample_rows
    residual_zero = layer_input.astype(jnp.float32)
    normed_one, norm_one_back = jax.vjp(layer_norm, residual_zero, first_gain, first_shift)
    active_one = normed_one.astype(jnp.bfloat16)
    queries_one, keys_one, values_one = project(active_one, sample_weight, sample_bias)
    my_index = lax.axis_index("samp")
    shard_flags = context_flags.reshape(shard_count, sample_rows)[:, 0]
    shard_rank = jnp.cumsum(shard_flags) - 1
    shard_ids = jnp.arange(shard_count, dtype=jnp.int32)
    slot_ids = jnp.arange(context_shards, dtype=jnp.int32)
    root_hits = (shard_rank[None, :] == slot_ids[:, None]) & (shard_flags[None, :] == 1)
    roots = jnp.sum(jnp.where(root_hits, shard_ids[None, :], 0), axis=1)
    context_tasks = jnp.take(segment_ids.reshape(shard_count, sample_rows), roots, axis=0).reshape(
        total_context
    )
    local_tasks = lax.dynamic_slice_in_dim(segment_ids, my_index * sample_rows, sample_rows)
    allowed = local_tasks[:, None] == context_tasks[None, :]
    is_context = shard_flags[my_index] == 1
    own_rank = jnp.maximum(shard_rank[my_index], 0)
    own_block = jnp.concatenate([keys_one, values_one], axis=-1)

    def fetch_rows(step, buffer):
        piece = spread_2(own_block, "samp", roots[step])
        return lax.dynamic_update_slice_in_dim(buffer, piece, step * sample_rows, 0)

    empty_rows = jnp.zeros((total_context, feature_rows, 2 * model_width), jnp.bfloat16)
    fetched = lax.fori_loop(0, context_shards, fetch_rows, empty_rows)
    context_keys = fetched[..., :model_width]
    context_values = fetched[..., model_width:]
    query_heads = split_heads(queries_one)
    key_heads = split_heads(context_keys)
    value_heads = split_heads(context_values)
    scores = (
        jnp.einsum("sfhd,cfhd->fhsc", query_heads, key_heads, preferred_element_type=jnp.float32)
        * score_scale
    )
    sample_prob = soft_weights(jnp.where(allowed[None, None], scores, MASKED))
    sample_weights = sample_prob.astype(jnp.bfloat16)
    mixed_one = join_heads(
        jnp.einsum(
            "fhsc,cfhd->sfhd", sample_weights, value_heads, preferred_element_type=jnp.float32
        )
    ).astype(jnp.bfloat16)
    residual_one = residual_zero + apply_weight(mixed_one, sample_mixer) + sample_offset
    normed_two, norm_two_back = jax.vjp(layer_norm, residual_one, second_gain, second_shift)
    active_two = normed_two.astype(jnp.bfloat16)
    queries_two, keys_two, values_two = project(active_two, feature_weight, feature_bias)
    all_keys, all_values = (
        lax.all_gather(keys_two, "feat", axis=1, tiled=True),
        lax.all_gather(values_two, "feat", axis=1, tiled=True),
    )
    mixed_two, feature_prob = feature_attend(queries_two, all_keys, all_values)
    residual_two = residual_one + apply_weight(mixed_two, feature_mixer) + feature_offset
    normed_three, norm_three_back = jax.vjp(layer_norm, residual_two, third_gain, third_shift)
    active_three = normed_three.astype(jnp.bfloat16)
    expanded = apply_weight(active_three, expand_weight) + expand_bias
    activated, gelu_back = jax.vjp(partial(jax.nn.gelu, approximate=False), expanded)
    hidden = activated.astype(jnp.bfloat16)
    layer_output = (residual_two + apply_weight(hidden, reduce_weight) + reduce_bias).astype(
        jnp.bfloat16
    )
    grad_out = cotangent.astype(jnp.float32)
    grad_branch = cotangent
    reduce_bias_grad = column_sum(grad_branch)
    reduce_weight_grad = weight_grad(hidden, grad_branch)
    grad_hidden = input_back(grad_branch, reduce_weight).astype(jnp.bfloat16)
    grad_expanded = gelu_back(grad_hidden.astype(jnp.float32))[0].astype(jnp.bfloat16)
    expand_bias_grad = column_sum(grad_expanded)
    expand_weight_grad = weight_grad(active_three, grad_expanded)
    grad_norm, third_gain_grad, third_shift_grad = norm_three_back(
        input_back(grad_expanded, expand_weight)
    )
    grad_two = grad_out + grad_norm
    grad_branch = grad_two.astype(jnp.bfloat16)
    feature_offset_grad = column_sum(grad_branch)
    feature_mixer_grad = weight_grad(mixed_two, grad_branch)
    grad_mixed = input_back(grad_branch, feature_mixer).astype(jnp.bfloat16)
    grad_queries, grad_keys, grad_values = feature_grads(
        queries_two, all_keys, all_values, feature_prob, grad_mixed
    )
    own_key_grads, own_value_grads = (
        lax.psum_scatter(grad_keys, "feat", scatter_dimension=1, tiled=True),
        lax.psum_scatter(grad_values, "feat", scatter_dimension=1, tiled=True),
    )
    grad_project = jnp.concatenate(
        [
            grad_queries.astype(jnp.bfloat16),
            own_key_grads.astype(jnp.bfloat16),
            own_value_grads.astype(jnp.bfloat16),
        ],
        axis=-1,
    )
    feature_weight_grad = weight_grad(active_two, grad_project)
    feature_bias_grad = jnp.concatenate(
        [
            column_sum(grad_project[..., :model_width]),
            column_sum(grad_project[..., 2 * model_width :]),
        ]
    )
    grad_norm, second_gain_grad, second_shift_grad = norm_two_back(
        input_back(grad_project, feature_weight)
    )
    grad_one = grad_two + grad_norm
    grad_branch = grad_one.astype(jnp.bfloat16)
    sample_offset_grad = column_sum(grad_branch)
    sample_mixer_grad = weight_grad(mixed_one, grad_branch)
    grad_heads = split_heads(input_back(grad_branch, sample_mixer).astype(jnp.bfloat16))
    grad_weights = jnp.einsum(
        "sfhd,cfhd->fhsc", grad_heads, value_heads, preferred_element_type=jnp.float32
    )
    inner_sum = jnp.sum(sample_prob * grad_weights, axis=-1, keepdims=True)
    grad_scores = (sample_prob * (grad_weights - inner_sum)).astype(jnp.bfloat16)
    grad_queries = (
        join_heads(
            jnp.einsum(
                "fhsc,cfhd->sfhd", grad_scores, key_heads, preferred_element_type=jnp.float32
            )
        )
        * score_scale
    ).astype(jnp.bfloat16)
    key_terms = (
        join_heads(
            jnp.einsum(
                "fhsc,sfhd->cfhd", grad_scores, query_heads, preferred_element_type=jnp.float32
            )
        )
        * score_scale
    )
    value_terms = join_heads(
        jnp.einsum(
            "fhsc,sfhd->cfhd", sample_weights, grad_heads, preferred_element_type=jnp.float32
        )
    )
    term_block = jnp.concatenate([key_terms, value_terms], axis=-1)
    summed_terms = lax.psum_scatter(term_block, "samp", scatter_dimension=0, tiled=True)
    summed_rows = lax.all_gather(summed_terms.astype(jnp.bfloat16), "samp", axis=0, tiled=True)
    own_grads = lax.dynamic_slice_in_dim(summed_rows, own_rank * sample_rows, sample_rows, 0)
    own_grads = jnp.where(is_context, own_grads, jnp.zeros_like(own_grads))
    grad_project = jnp.concatenate([grad_queries, own_grads], axis=-1)
    sample_weight_grad = weight_grad(active_one, grad_project)
    sample_bias_grad = jnp.concatenate(
        [column_sum(grad_queries), column_sum(own_grads[..., model_width:])]
    )
    grad_norm, first_gain_grad, first_shift_grad = norm_one_back(
        input_back(grad_project, sample_weight)
    )
    input_grad = (grad_one + grad_norm).astype(jnp.bfloat16)
    summed = lax.psum(
        (
            first_gain_grad,
            first_shift_grad,
            sample_weight_grad,
            sample_bias_grad,
            sample_mixer_grad,
            sample_offset_grad,
            second_gain_grad,
            second_shift_grad,
            feature_weight_grad,
            feature_bias_grad,
            feature_mixer_grad,
            feature_offset_grad,
            third_gain_grad,
            third_shift_grad,
            expand_weight_grad,
            expand_bias_grad,
            reduce_weight_grad,
            reduce_bias_grad,
        ),
        "feat",
    )
    shares = (
        lax.psum_scatter(summed[0], "samp", scatter_dimension=0, tiled=True),
        lax.psum_scatter(summed[1], "samp", scatter_dimension=0, tiled=True),
        lax.psum_scatter(summed[2], "samp", scatter_dimension=0, tiled=True),
        lax.psum_scatter(summed[3], "samp", scatter_dimension=0, tiled=True),
        lax.psum_scatter(summed[4], "samp", scatter_dimension=0, tiled=True),
        lax.psum_scatter(summed[5], "samp", scatter_dimension=0, tiled=True),
        lax.psum_scatter(summed[6], "samp", scatter_dimension=0, tiled=True),
        lax.psum_scatter(summed[7], "samp", scatter_dimension=0, tiled=True),
        lax.psum_scatter(summed[8], "samp", scatter_dimension=0, tiled=True),
        lax.psum_scatter(summed[9], "samp", scatter_dimension=0, tiled=True),
        lax.psum_scatter(summed[10], "samp", scatter_dimension=0, tiled=True),
        lax.psum_scatter(summed[11], "samp", scatter_dimension=0, tiled=True),
        lax.psum_scatter(summed[12], "samp", scatter_dimension=0, tiled=True),
        lax.psum_scatter(summed[13], "samp", scatter_dimension=0, tiled=True),
        lax.psum_scatter(summed[14], "samp", scatter_dimension=0, tiled=True),
        lax.psum_scatter(summed[15], "samp", scatter_dimension=0, tiled=True),
        lax.psum_scatter(summed[16], "samp", scatter_dimension=0, tiled=True),
        lax.psum_scatter(summed[17], "samp", scatter_dimension=0, tiled=True),
    )
    return (
        layer_output,
        input_grad,
        shares[0],
        shares[1],
        shares[2],
        shares[3],
        shares[4],
        shares[5],
        shares[6],
        shares[7],
        shares[8],
        shares[9],
        shares[10],
        shares[11],
        shares[12],
        shares[13],
        shares[14],
        shares[15],
        shares[16],
        shares[17],
    )


def solution(mesh):
    small = mesh.shape["samp"] == 8 and mesh.shape["feat"] == 4
    return jax.shard_map(
        local_small if small else local_large,
        mesh=mesh,
        in_specs=(
            P("samp", "feat", None),
            P(),
            P(),
            P(),
            P(),
            P(),
            P(),
            P(),
            P(),
            P(),
            P(),
            P(),
            P(),
            P(),
            P(),
            P(),
            P(),
            P(),
            P(),
            P(),
            P(),
            P("samp", "feat", None),
        ),
        out_specs=(
            P("samp", "feat", None),
            P("samp", "feat", None),
            P("samp"),
            P("samp"),
            P("samp", None),
            P("samp"),
            P("samp", None),
            P("samp"),
            P("samp"),
            P("samp"),
            P("samp", None),
            P("samp"),
            P("samp", None),
            P("samp"),
            P("samp"),
            P("samp"),
            P("samp", None),
            P("samp"),
            P("samp", None),
            P("samp"),
        ),
        check_vma=False,
    )
```

```python
from functools import partial

import jax
import jax.numpy as jnp
from jax import lax
from jax.experimental import pallas as pl
from jax.experimental.pallas import tpu as pltpu
from jax.sharding import PartitionSpec as P

HEADS = 8
HEAD_DIM = 64
EPS = 1e-05
MASKED = -1000000000.0
SCALE = HEAD_DIM ** (-0.5)
QUAD = 4 * HEAD_DIM
BF = jnp.bfloat16
F32 = jnp.float32
VMEM_LIMIT = 56 << 20


def mm(a, b, ca=1, cb=0):
    return lax.dot_general(a, b, (((ca,), (cb,)), ((), ())), preferred_element_type=F32)


def norm_parts(values):
    center = jnp.mean(values, axis=-1, keepdims=True)
    spread = values - center
    variance = jnp.mean(spread * spread, axis=-1, keepdims=True)
    inverse = lax.rsqrt(variance + EPS)
    return spread * inverse, inverse


def norm_back(grad, unit, inverse, gain):
    scaled = grad * gain
    first = jnp.mean(scaled, axis=-1, keepdims=True)
    second = jnp.mean(scaled * unit, axis=-1, keepdims=True)
    return (scaled - first - unit * second) * inverse


def lane_ids(rows):
    return lax.broadcasted_iota(jnp.int32, (rows, 128), 1)


def group_reduce(values, op, fill):
    rows = values.shape[0]
    low = lane_ids(rows) < HEAD_DIM
    outs = []
    for t in range(values.shape[1] // 128):
        tile = values[:, t * 128 : (t + 1) * 128]
        left = op(jnp.where(low, tile, fill), axis=1, keepdims=True)
        right = op(jnp.where(low, fill, tile), axis=1, keepdims=True)
        outs.append(jnp.where(low, left, right))
    return jnp.concatenate(outs, axis=1)


def head_masks(dtype):
    lanes = lax.broadcasted_iota(jnp.int32, (1, QUAD), 1) // HEAD_DIM
    return [jnp.where(lanes == h, 1.0, 0.0).astype(dtype) for h in range(4)]


def stack_heads(part, masks):
    return jnp.concatenate([part * m for m in masks], axis=0)


def pick_heads(stacked, masks):
    rows = stacked.shape[0] // 4
    total = stacked[:rows] * masks[0]
    for h in range(1, 4):
        total = total + stacked[h * rows : (h + 1) * rows] * masks[h]
    return total


def attend(q, k, v, masks, allow):
    outs, probs = [], []
    for quad in range(2):
        cols = slice(quad * QUAD, (quad + 1) * QUAD)
        scores = mm(q[:, cols], stack_heads(k[:, cols], masks), 1, 1)
        if allow is not None:
            scores = jnp.where(allow, scores, MASKED)
        raised = jnp.exp(scores - group_reduce(scores, jnp.max, -jnp.inf))
        prob = raised / group_reduce(raised, jnp.sum, 0.0)
        outs.append(mm(prob.astype(BF), stack_heads(v[:, cols], masks)))
        probs.append(prob)
    return jnp.concatenate(outs, axis=1), jnp.concatenate(probs, axis=1)


def attend_back(q, k, v, prob, grad, masks, masks32):
    dqs, dks, dvs = [], [], []
    for quad in range(2):
        cols = slice(quad * QUAD, (quad + 1) * QUAD)
        p, g = prob[:, cols], grad[:, cols]
        back = mm(g, stack_heads(v[:, cols], masks), 1, 1)
        inner = group_reduce(p * back, jnp.sum, 0.0)
        gs = (p * (back - inner)).astype(BF)
        dqs.append(mm(gs, stack_heads(k[:, cols], masks)) * SCALE)
        dks.append(pick_heads(mm(gs, q[:, cols], 0, 0), masks32))
        dvs.append(pick_heads(mm(p.astype(BF), g, 0, 0), masks32))
    join = lambda parts: jnp.concatenate(parts, axis=1).astype(BF)
    return join(dqs), join(dks), join(dvs)


def swap_matrix(n):
    r = lax.broadcasted_iota(jnp.int32, (n, n), 0)
    c = lax.broadcasted_iota(jnp.int32, (n, n), 1)
    return jnp.where((r // 16 == c % 16) & (r % 16 == c // 16), 1.0, 0.0).astype(BF)


def swap(matrix, values):
    return mm(matrix, values).astype(BF)


def gelu_parts(u):
    cdf = 0.5 * (1.0 + lax.erf(u * (2.0**-0.5)))
    density = jnp.exp(u * u * -0.5) * 0.3989422804014327
    return cdf, density


def col_sum(values):
    return jnp.sum(values.astype(F32), axis=0, keepdims=True)


THIRDS = (0, 336, 672)
THIRD = 352
HELD = (
    (0, 0, 0), (6, 4, 5), (9, 5, 8), (8, 9, 7),
    (1, 2, 3), (5, 2, 3), (6, 3, 9), (8, 9, 2),
)


def forward_one(
    me_ref, x_ref, y1, y2, y3, p1, p2, p3, m1, m2, m3,
    allow_ref, gain_ref, shift_ref, w_ref, b_ref,
    o_ref, c_ref, q_ref, k_ref, v_ref, p_ref, o_scr,
):
    me = me_ref[0]
    got = (None, y1, y2, y3, p1, p2, p3, m1, m2, m3)
    for position, held in enumerate(HELD):

        @pl.when(me_ref[2] == position)
        def _(held=held):
            for start, index in zip(THIRDS, held):
                rows = slice(start, start + THIRD)
                c_ref[rows] = x_ref[rows] if index == 0 else got[index][...]

    gain, shift = gain_ref[...], shift_ref[...]
    matrix = swap_matrix(256)
    for d in range(4):
        rows = slice(d * 256, (d + 1) * 256)
        unit, _ = norm_parts(x_ref[rows].astype(F32))
        act = swap(matrix, (unit * gain + shift).astype(BF))
        q = (mm(act, w_ref[:, :512]) + b_ref[:, :512]).astype(BF) * SCALE
        q_ref[:, d] = q.astype(BF).reshape(16, 16, 512)
        unit, _ = norm_parts(c_ref[rows].astype(F32))
        act = swap(matrix, (unit * gain + shift).astype(BF))
        kv = mm(act, w_ref[:, 512:])
        k_ref[:, d] = kv[:, :512].astype(BF).reshape(16, 16, 512)
        v_ref[:, d] = (kv[:, 512:] + b_ref[:, 512:]).astype(BF).reshape(16, 16, 512)
    masks = head_masks(BF)
    allow = allow_ref[...] > 0.5

    def body(i, carry):
        for j in range(2):
            f = i * 2 + j
            q, k, v = (r[f].reshape(64, 512) for r in (q_ref, k_ref, v_ref))
            out, prob = attend(q, k, v, masks, allow)
            o_scr[f] = out.astype(BF).reshape(4, 16, 512)
            p_ref[f] = prob
        return carry

    lax.fori_loop(0, 8, body, 0)
    for d in range(4):
        o_ref[d] = swap(matrix, o_scr[:, d ^ me].reshape(256, 512))


def middle(
    o1_ref, x_ref, cot_ref,
    wm1_ref, off1_ref, g2_ref, s2_ref, wf_ref, bf_ref, wm2_ref, off2_ref,
    g3_ref, s3_ref, we_ref, be_ref, wr_ref, br_ref,
    out_ref, gb1_ref, a2_ref, dqkv_ref, o2_ref, gb2_ref, a3_ref, gu_ref, hid_ref, gb3_ref,
    vec_ref, bias_ref,
):
    samples = 4

    def gather(ref):
        return jnp.concatenate(
            [ref[d, s * 16 : (s + 1) * 16] for s in range(samples) for d in range(4)], axis=0
        )

    def scatter(ref, values):
        for s in range(samples):
            for d in range(4):
                at = (s * 4 + d) * 16
                ref[d, s * 16 : (s + 1) * 16] = values[at : at + 16]

    masks, masks32 = head_masks(BF), head_masks(F32)
    o1, cot = gather(o1_ref), gather(cot_ref)
    gb3_ref[...] = cot
    r1 = gather(x_ref).astype(F32) + mm(o1, wm1_ref[...]) + off1_ref[...]
    unit2, inv2 = norm_parts(r1)
    act2 = (unit2 * g2_ref[...] + s2_ref[...]).astype(BF)
    a2_ref[...] = act2
    qkv = mm(act2, wf_ref[...])
    q = (qkv[:, :512] + bf_ref[:, :512]).astype(BF) * jnp.asarray(SCALE, BF)
    k = qkv[:, 512:1024].astype(BF)
    v = (qkv[:, 1024:] + bf_ref[:, 512:]).astype(BF)
    parts = []
    for s in range(samples):
        rows = slice(s * 64, (s + 1) * 64)
        parts.append(attend(q[rows], k[rows], v[rows], masks, None))
    o2 = jnp.concatenate([part[0] for part in parts], axis=0).astype(BF)
    o2_ref[...] = o2
    r2 = r1 + mm(o2, wm2_ref[...]) + off2_ref[...]
    unit3, inv3 = norm_parts(r2)
    act3 = (unit3 * g3_ref[...] + s3_ref[...]).astype(BF)
    a3_ref[...] = act3
    out = r2 + br_ref[...]
    back = None
    bias = []
    for b in range(4):
        cols = slice(b * 512, (b + 1) * 512)
        u = mm(act3, we_ref[:, cols]) + be_ref[:, cols]
        cdf, density = gelu_parts(u)
        hidden = (u * cdf).astype(BF)
        hid_ref[:, cols] = hidden
        out = out + mm(hidden, wr_ref[cols, :])
        gh = mm(cot, wr_ref[cols, :], 1, 1).astype(BF).astype(F32)
        gu = (gh * (cdf + u * density)).astype(BF)
        gu_ref[:, cols] = gu
        bias.append(col_sum(gu))
        term = mm(gu, we_ref[:, cols], 1, 1)
        back = term if back is None else back + term
    scatter(out_ref, out.astype(BF))
    vecs = [col_sum(back * unit3), col_sum(back)]
    gr2 = cot.astype(F32) + norm_back(back, unit3, inv3, g3_ref[...])
    gb2 = gr2.astype(BF)
    gb2_ref[...] = gb2
    go2 = mm(gb2, wm2_ref[...], 1, 1).astype(BF)
    grads = []
    for s in range(samples):
        rows = slice(s * 64, (s + 1) * 64)
        grads.append(
            jnp.concatenate(
                attend_back(q[rows], k[rows], v[rows], parts[s][1], go2[rows], masks, masks32),
                axis=1,
            )
        )
    dqkv = jnp.concatenate(grads, axis=0)
    dqkv_ref[...] = dqkv
    back = mm(dqkv, wf_ref[...], 1, 1)
    vecs += [col_sum(back * unit2), col_sum(back)]
    gr1 = gr2 + norm_back(back, unit2, inv2, g2_ref[...])
    scatter(gb1_ref, gr1.astype(BF))
    vecs += [col_sum(gb2), col_sum(cot), col_sum(dqkv[:, :512]), col_sum(dqkv[:, 1024:])]

    @pl.when(pl.program_id(0) == 0)
    def _():
        vec_ref[...] = jnp.zeros_like(vec_ref)
        bias_ref[...] = jnp.zeros_like(bias_ref)

    vec_ref[...] += jnp.concatenate(vecs, axis=0)
    bias_ref[...] += jnp.concatenate(bias, axis=1)


def backward_one(
    me_ref, gb1_ref, c_ref, q_ref, k_ref, v_ref, p_ref, gain_ref, shift_ref, w_ref, wm_ref,
    ta_ref, tb_ref, tc_ref, cact_ref, dkv_ref, dq_ref, vec_ref,
    go_scr, dkv_scr, t_scr,
):
    me = me_ref[0]
    gain, shift = gain_ref[...], shift_ref[...]
    matrix = swap_matrix(256)
    masks, masks32 = head_masks(BF), head_masks(F32)
    for d in range(4):
        go = mm(gb1_ref[d ^ me], wm_ref[...], 1, 1).astype(BF)
        go_scr[:, d] = swap(matrix, go).reshape(16, 16, 512)

    def body(i, carry):
        for j in range(2):
            f = i * 2 + j
            q, k, v, go = (r[f].reshape(64, 512) for r in (q_ref, k_ref, v_ref, go_scr))
            dq, dk, dv = attend_back(q, k, v, p_ref[f], go, masks, masks32)
            dq_ref[f] = dq.reshape(4, 16, 512)
            dkv_scr[f] = jnp.concatenate([dk, dv], axis=1).reshape(4, 16, 1024)
        return carry

    lax.fori_loop(0, 8, body, 0)
    gain_sum = jnp.zeros((1, 512), F32)
    shift_sum, v_sum = gain_sum, gain_sum
    for d in range(4):
        rows = slice(d * 256, (d + 1) * 256)
        unit, inverse = norm_parts(c_ref[rows].astype(F32))
        cact_ref[rows] = (unit * gain + shift).astype(BF)
        dkv = swap(matrix, dkv_scr[:, d].reshape(256, 1024))
        dkv_ref[rows] = dkv
        back = mm(dkv, w_ref[:, 512:], 1, 1)
        t_scr[rows] = back.astype(BF)
        gain_sum += col_sum(back * unit)
        shift_sum += col_sum(back)
        v_sum += col_sum(dkv[:, 512:])
    for ref, start in zip((ta_ref, tb_ref, tc_ref), THIRDS):
        ref[...] = t_scr[start : start + THIRD]
    zero = jnp.zeros((1, 512), F32)
    vec_ref[...] = jnp.concatenate([gain_sum, shift_sum, v_sum] + [zero] * 5, axis=0)


def backward_query(
    me_ref, gb1_ref, x_ref, dq_ref, vecc_ref, gain_ref, shift_ref, w_ref,
    base_ref, act_ref, dqn_ref, vec_ref,
):
    me = me_ref[0]
    gain, shift = gain_ref[...], shift_ref[...]
    matrix = swap_matrix(256)
    gain_sum, shift_sum, v_sum = vecc_ref[0:1], vecc_ref[1:2], vecc_ref[2:3]
    off_sum = jnp.zeros((1, 512), F32)
    q_sum = off_sum
    for d in range(4):
        rows = slice(d * 256, (d + 1) * 256)
        unit, inverse = norm_parts(x_ref[rows].astype(F32))
        act_ref[rows] = (unit * gain + shift).astype(BF)
        dq = swap(matrix, dq_ref[:, d].reshape(256, 512))
        dqn_ref[rows] = dq
        back = mm(dq, w_ref[:, :512], 1, 1)
        gb1 = gb1_ref[d ^ me]
        base_ref[rows] = gb1.astype(F32) + norm_back(back, unit, inverse, gain)
        gain_sum += col_sum(back * unit)
        shift_sum += col_sum(back)
        off_sum += col_sum(gb1)
        q_sum += col_sum(dq)
    zero = jnp.zeros((1, 512), F32)
    vec_ref[...] = jnp.concatenate(
        [gain_sum, shift_sum, off_sum, q_sum, v_sum, zero, zero, zero], axis=0
    )


def finish(me_ref, base_ref, a_ref, b_ref, c_ref, x_ref, gain_ref, out_ref):
    owner = me_ref[1] == 1

    @pl.when(owner)
    def _():
        for ref, start, rows in ((a_ref, 0, 336), (b_ref, 336, 336), (c_ref, 672, 352)):
            at = slice(start, start + rows)
            unit, inverse = norm_parts(x_ref[at].astype(F32))
            extra = norm_back(ref[:rows], unit, inverse, gain_ref[...])
            out_ref[at] = (base_ref[at] + extra).astype(BF)

    @pl.when(jnp.logical_not(owner))
    def _():
        out_ref[...] = base_ref[...].astype(BF)


def shard_of(me_ref, dy, d1, d3):
    return ((me_ref[6] ^ d1 ^ (3 * d3)) * 2) + (me_ref[5] ^ dy)


BITS = [(a, b, c) for a in range(2) for b in range(2) for c in range(2)]


def grads_reduce(me_ref, hid_ref, gb3_ref, keep_ref, send_ref, scr):
    core = me_ref[3]
    for i in range(8):
        scr[i * 256 : (i + 1) * 256] = mm(
            hid_ref[:, i * 256 : (i + 1) * 256], gb3_ref[...], 0, 0
        ).astype(BF)
    for i, (d1, d3, dy) in enumerate(BITS):
        start = shard_of(me_ref, dy, d1, d3) * 256
        keep_ref[i] = scr[pl.ds(pl.multiple_of(start + core * 128, 128), 128)]
        send_ref[i] = scr[pl.ds(pl.multiple_of(start + (1 - core) * 128, 128), 128)]


def grads_expand(me_ref, act_ref, gu_ref, keep_ref, send_ref, scr):
    core = me_ref[3]
    for n in range(4):
        scr[n] = mm(act_ref[...], gu_ref[:, n * 512 : (n + 1) * 512], 0, 0).astype(BF)
    for i, (dy, d1, d3) in enumerate(BITS):
        rows = pl.ds(pl.multiple_of(shard_of(me_ref, dy, d1, d3) * 64, 64), 64)
        for u in range(2):
            keep_ref[i, u] = scr[2 * core + u, rows]
            send_ref[i, u] = scr[2 * (1 - core) + u, rows]


def grads_feature(me_ref, act_ref, dqkv_ref, o_ref, gb_ref, keep_ref, send_ref, scr):
    core, xx = me_ref[3], me_ref[4]
    for n in range(3):
        scr[n] = mm(act_ref[...], dqkv_ref[:, n * 512 : (n + 1) * 512], 0, 0).astype(BF)
    scr[3] = mm(o_ref[...], gb_ref[...], 0, 0).astype(BF)
    for i, (dy, d1, d3) in enumerate(BITS):
        rows = pl.ds(pl.multiple_of(shard_of(me_ref, dy, d1, d3) * 64, 64), 64)
        for dx in range(2):
            keep_ref[dx, i] = scr[2 * core + (dx ^ xx), rows]
            send_ref[dx, i] = scr[2 * (1 - core) + (dx ^ xx), rows]


def grads_sample(
    me_ref, act_ref, dq_ref, cact_ref, dkv_ref, o_ref, gb1_ref,
    keepx_ref, sendx_ref, keepy_ref, sendy_ref, scr,
):
    core, xx = me_ref[3], me_ref[4]
    scr[0] = mm(act_ref[...], dq_ref[...], 0, 0).astype(BF)
    scr[1] = mm(cact_ref[...], dkv_ref[:, :512], 0, 0).astype(BF)
    scr[2] = mm(cact_ref[...], dkv_ref[:, 512:], 0, 0).astype(BF)
    total = jnp.zeros((512, 512), F32)
    for d in range(4):
        total += mm(o_ref[d], gb1_ref[d], 0, 0)
    scr[3] = total.astype(BF)
    for i, (dy, d1, d3) in enumerate(BITS):
        start = shard_of(me_ref, dy, d1, d3) * 64
        rows = pl.ds(pl.multiple_of(start, 64), 64)
        keepy_ref[i] = scr[2 * core + 1, rows]
        sendy_ref[i] = scr[2 * (1 - core) + 1, rows]
        for dx in range(2):
            rows = pl.ds(pl.multiple_of(start + (dx ^ xx) * 32, 32), 32)
            keepx_ref[dx, i] = scr[2 * core, rows]
            sendx_ref[dx, i] = scr[2 * (1 - core), rows]


def spec(shape, index=None):
    return pl.BlockSpec(shape, index if index is not None else (lambda *a: (0,) * len(shape)))


def sds(shape, dtype=BF):
    return jax.ShapeDtypeStruct(shape, dtype)


def params():
    return pltpu.CompilerParams(vmem_limit_bytes=VMEM_LIMIT)


def row(vector):
    return vector.reshape(1, -1)


def whole(kernel, name, outs, scratch, *inputs):
    return pl.pallas_call(
        kernel,
        out_shape=outs,
        in_specs=[pl.BlockSpec(memory_space=pltpu.SMEM)] + [pl.BlockSpec()] * (len(inputs) - 1),
        scratch_shapes=scratch,
        compiler_params=params(),
        name=name,
    )(*inputs)


def shuffle(value, axis, mask):
    size = lax.axis_size(axis)
    return lax.ppermute(value, axis, [(i, i ^ mask) for i in range(size)])


CORE, X, Y, Z, Z3 = ("feat", 1), ("feat", 2), ("samp", 1), ("samp", 2), ("samp", 6)


def turn(value, step):
    return lax.ppermute(value, "samp", [(i, (i + 2 * step) % 8) for i in range(8)])


def at(stacked, index, axis=0):
    return lax.dynamic_index_in_dim(stacked, index, axis, keepdims=False)


def swap_blocks(blocks, axis):
    return [blocks[0]] + [shuffle(blocks[d], axis, d) for d in range(1, len(blocks))]


def plus(a, b):
    return (a.astype(F32) + b.astype(F32)).astype(BF)


def halve(keep, sent, where):
    got = shuffle(sent, *where)
    return plus(keep[0], got[0]), plus(keep[1], got[1])


def join_two(mine, index, where):
    other = shuffle(mine, *where)
    return jnp.stack([jnp.where(index == 0, mine, other), jnp.where(index == 0, other, mine)])


def chain(keep, sent, dims):
    mine, out = halve(keep, sent, CORE)
    for i, where in enumerate(dims):
        if i == len(dims) - 1:
            return plus(mine, shuffle(out, *where))
        mine, out = halve(mine, out, where)


def send_context(x, position):
    dy, dz = position // 4, position % 4
    owner = position == 0
    a, b, c = (x[start : start + THIRD] for start in THIRDS)
    y1, p1, m1 = shuffle(a, *Y), turn(b, 1), turn(c, -1)
    pick = jnp.where
    y2 = shuffle(pick(owner, b, pick(dz == 1, p1, m1)), *Y)
    p2 = turn(pick(owner, c, pick(dy == 1, y1, p1)), 1)
    m2 = turn(pick(owner, a, pick(dy == 1, y1, m1)), -1)
    y3 = shuffle(pick(owner, c, p2), *Y)
    p3 = turn(pick(owner, a, p2), 1)
    m3 = turn(pick(owner, b, pick((dy == 0) & (dz == 3), m2, y2)), -1)
    return y1, y2, y3, p1, p2, p3, m1, m2, m3


def sum_context(a, b, c, position):
    pick = jnp.where

    def to(places):
        hit = position == places[0]
        for place in places[1:]:
            hit = hit | (position == place)
        return hit

    def add(value, places, got):
        return pick(to(places), plus(value, got), value)

    y = shuffle(pick(to([6]), b, c), *Y)
    m = turn(a, -1)
    p = turn(pick(to([3, 7]), b, pick(to([2]), a, c)), 1)
    a, b, c = (
        add(add(a, [0, 5], m), [3], p),
        add(add(b, [2], y), [0, 4], p),
        add(add(c, [0, 1], y), [7], p),
    )
    y = shuffle(pick(to([7]), c, b), *Y)
    m = turn(pick(to([1]), c, pick(to([5]), a, b)), -1)
    p = turn(pick(to([2]), c, a), 1)
    a, b, c = (
        add(add(a, [4], m), [0, 4], p),
        add(add(b, [0, 1], y), [1], m),
        add(add(add(c, [3], y), [0], m), [3], p),
    )
    y, m, p = shuffle(a, *Y), turn(b, -1), turn(c, 1)
    return tuple(u.astype(F32) + v.astype(F32) for u, v in ((a, y), (b, m), (c, p)))


def sum_everywhere(value):
    for where in (CORE, X, Y, Z, Z3):
        value = value + shuffle(value, *where)
    return value


def local_small(
    layer_input, segment_ids, context_flags,
    first_gain, first_shift, sample_weight, sample_bias, sample_mixer, sample_offset,
    second_gain, second_shift, feature_weight, feature_bias, feature_mixer, feature_offset,
    third_gain, third_shift, expand_weight, expand_bias, reduce_weight, reduce_bias, cotangent,
):
    samp, feat = lax.axis_index("samp"), lax.axis_index("feat")
    core, xx = feat % 2, feat // 2
    yy, zz = samp % 2, samp // 2
    flags = context_flags.reshape(8, 64)[:, 0]
    root = jnp.sum(jnp.where(flags == 1, jnp.arange(8, dtype=jnp.int32), 0))
    position = ((yy ^ (root % 2)) * 4 + (zz - root // 2 + 4) % 4).astype(jnp.int32)
    own = (position == 0).astype(jnp.int32)
    me = jnp.stack([feat, own, position, core, xx, yy, zz]).astype(jnp.int32)

    x = layer_input.reshape(1024, 512)
    pieces = send_context(x, position)
    tasks = segment_ids.reshape(8, 64)
    allow = (at(tasks, samp)[:, None] == at(tasks, root)[None, :]).astype(F32)
    allow = jnp.concatenate([allow] * 4, axis=1)

    both = jnp.stack([layer_input.reshape(4, 256, 512), cotangent.reshape(4, 256, 512)], axis=1)
    both = swap_blocks([at(both, feat ^ d) for d in range(4)], "feat")
    x_f = jnp.stack([pair[0] for pair in both])
    cot_f = jnp.stack([pair[1] for pair in both])

    heads = sds((16, 4, 16, 512))
    o1, context, q1, k1, v1, p1 = whole(
        forward_one, "forward_one",
        (sds((4, 256, 512)), sds((1024, 512)), heads, heads, heads, sds((16, 64, 512), F32)),
        [pltpu.VMEM((16, 4, 16, 512), BF)],
        me, x, *pieces, allow, row(first_gain), row(first_shift), sample_weight, row(sample_bias),
    )
    o1_f = jnp.stack(swap_blocks([o1[d] for d in range(4)], "feat"))

    weights = [
        sample_mixer, row(sample_offset), row(second_gain), row(second_shift), feature_weight,
        row(feature_bias), feature_mixer, row(feature_offset), row(third_gain), row(third_shift),
        expand_weight, row(expand_bias), reduce_weight, row(reduce_bias),
    ]
    blocked = spec((4, 64, 512), lambda i: (0, i, 0))
    wide = lambda n: spec((256, n), lambda i: (i, 0))
    out_f, gb1_f, act2, dqkv, o2, gb2, act3, gu, hidden, gb3, vec2, bias2 = pl.pallas_call(
        middle,
        grid=(4,),
        out_shape=(
            sds((4, 256, 512)), sds((4, 256, 512)), sds((1024, 512)), sds((1024, 1536)),
            sds((1024, 512)), sds((1024, 512)), sds((1024, 512)), sds((1024, 2048)),
            sds((1024, 2048)), sds((1024, 512)), sds((8, 512), F32), sds((1, 2048), F32),
        ),
        in_specs=[blocked] * 3
        + [pl.BlockSpec(w.shape, lambda i: (0, 0), pipeline_mode=pl.Buffered(1)) for w in weights],
        out_specs=[
            blocked, blocked, wide(512), wide(1536), wide(512), wide(512), wide(512), wide(2048),
            wide(2048), wide(512), spec((8, 512)), spec((1, 2048)),
        ],
        compiler_params=params(),
        name="middle",
    )(o1_f, x_f, cot_f, *weights)

    gb1 = jnp.stack(swap_blocks([gb1_f[d] for d in range(4)], "feat"))
    out4 = jnp.stack(swap_blocks([out_f[d] for d in range(4)], "feat"))
    order4 = feat ^ jnp.arange(4, dtype=jnp.int32)
    layer_output = jnp.take(out4, order4, axis=0).reshape(64, 16, 512)

    rk, rs = whole(
        grads_reduce, "grads_reduce", (sds((8, 128, 512)), sds((8, 128, 512))),
        [pltpu.VMEM((2048, 512), BF)], me, hidden, gb3,
    )
    ek, es = whole(
        grads_expand, "grads_expand", (sds((8, 2, 64, 512)), sds((8, 2, 64, 512))),
        [pltpu.VMEM((4, 512, 512), BF)], me, act3, gu,
    )
    fk, fs = whole(
        grads_feature, "grads_feature", (sds((2, 8, 64, 512)), sds((2, 8, 64, 512))),
        [pltpu.VMEM((4, 512, 512), BF)], me, act2, dqkv, o2, gb2,
    )
    three = lambda a: a.reshape((2, 2, 2) + a.shape[1:])
    four = lambda a: a.reshape((2, 2, 2, 2) + a.shape[2:])
    r_part = chain(three(rk), three(rs), (Z, Z3, Y))
    e_part = chain(three(ek), three(es), (Y, Z, Z3))
    f_part = chain(four(fk), four(fs), (X, Y, Z, Z3))

    third = sds((THIRD, 512))
    ta, tb, tc, cact, dkv, dq_heads, vec_c = whole(
        backward_one, "backward_one",
        (third, third, third, sds((1024, 512)), sds((1024, 1024)), heads, sds((8, 512), F32)),
        [
            pltpu.VMEM((16, 4, 16, 512), BF),
            pltpu.VMEM((16, 4, 16, 1024), BF),
            pltpu.VMEM((1024, 512), BF),
        ],
        me, gb1, context, q1, k1, v1, p1, row(first_gain), row(first_shift), sample_weight,
        sample_mixer,
    )
    sums = sum_context(ta, tb, tc, position)
    base, act1, dq1, vec1 = whole(
        backward_query, "backward_query",
        (sds((1024, 512), F32), sds((1024, 512)), sds((1024, 512)), sds((8, 512), F32)),
        [],
        me, gb1, x, dq_heads, vec_c, row(first_gain), row(first_shift), sample_weight,
    )
    sxk, sxs, syk, sys_ = whole(
        grads_sample, "grads_sample",
        (sds((2, 8, 32, 512)), sds((2, 8, 32, 512)), sds((8, 64, 512)), sds((8, 64, 512))),
        [pltpu.VMEM((4, 512, 512), BF)],
        me, act1, dq1, cact, dkv, o1, gb1,
    )
    sx_part = chain(four(sxk), four(sxs), (X, Y, Z, Z3))
    sy_part = chain(three(syk), three(sys_), (Y, Z, Z3))

    vectors = sum_everywhere(
        jnp.concatenate([vec2.reshape(-1), bias2.reshape(-1), vec1.reshape(-1)])
    )

    both_x = lambda part: plus(part, shuffle(part, *X))
    reduce_grad = join_two(both_x(r_part), core, CORE).reshape(256, 512).astype(F32)
    expand_blocks = join_two(both_x(e_part), core, CORE).reshape(4, 64, 512).astype(F32)
    feature_blocks = join_two(join_two(f_part, xx, X), core, CORE).reshape(4, 64, 512).astype(F32)
    sx = join_two(f_or_s(sx_part, xx), core, CORE).astype(F32)
    sy = join_two(both_x(sy_part), core, CORE).astype(F32)

    input_grad = whole(
        finish, "finish", sds((1024, 512)), [], me, base, *sums, x, row(first_gain)
    ).reshape(64, 16, 512)

    def vector(start, size):
        return lax.dynamic_slice_in_dim(vectors[start : start + size], samp * (size // 8), size // 8)

    gain3, shift3, gain2, shift2, off2, bias_r = (vector(i * 512, 512) for i in range(6))
    expand_b = vector(4096, 2048)
    gain1, shift1, off1 = (vector(6144 + i * 512, 512) for i in range(3))
    columns = lambda blocks: jnp.concatenate(blocks, axis=1)

    return (
        layer_output, input_grad,
        gain1, shift1, columns([sx[0], sy[0], sx[1]]), vector(6144 + 3 * 512, 1024), sy[1], off1,
        gain2, shift2, columns([feature_blocks[i] for i in range(3)]), vector(6 * 512, 1024),
        feature_blocks[3], off2,
        gain3, shift3, columns([expand_blocks[i] for i in range(4)]), expand_b,
        reduce_grad, bias_r,
    )


def f_or_s(half, xx):
    return join_two(half, xx, X).reshape(64, 512)


def spread_2(block, axis, owner):
    block = jnp.where(lax.axis_index(axis) == owner, block, jnp.zeros_like(block))
    return lax.psum(block, axis)


def layer_norm(values, gain_row, shift_row):
    center = jnp.mean(values, axis=-1, keepdims=True)
    spread = values - center
    variance = jnp.mean(spread * spread, axis=-1, keepdims=True)
    return spread * lax.rsqrt(variance + EPS) * gain_row + shift_row


def apply_weight(active, weight):
    return jnp.einsum("sfd,de->sfe", active, weight, preferred_element_type=jnp.float32)


def input_back(grad_out, weight):
    return jnp.einsum("sfe,de->sfd", grad_out, weight, preferred_element_type=jnp.float32)


def weight_grad(active, grad_out):
    return jnp.einsum("sfd,sfe->de", active, grad_out, preferred_element_type=jnp.float32)


def column_sum(values):
    return jnp.sum(values.astype(jnp.float32), axis=(0, 1))


def project(active, weight, bias_row):
    model_width = active.shape[-1]
    joined = apply_weight(active, weight)
    queries = (joined[..., :model_width] + bias_row[:model_width]).astype(jnp.bfloat16)
    key_part = joined[..., model_width : 2 * model_width].astype(jnp.bfloat16)
    value_part = (joined[..., 2 * model_width :] + bias_row[model_width:]).astype(jnp.bfloat16)
    return (queries, key_part, value_part)


def split_heads(values):
    return values.reshape(values.shape[0], values.shape[1], HEADS, HEAD_DIM)


def join_heads(values):
    return values.reshape(values.shape[0], values.shape[1], HEADS * HEAD_DIM)


def soft_weights(scores):
    top_score = jnp.max(scores, axis=-1, keepdims=True)
    raised = jnp.exp(scores - top_score)
    return raised / jnp.sum(raised, axis=-1, keepdims=True)


def feature_attend(queries, key_part, value_part):
    score_scale = HEAD_DIM ** (-0.5)
    scores = (
        jnp.einsum(
            "sfhd,sghd->shfg",
            split_heads(queries),
            split_heads(key_part),
            preferred_element_type=jnp.float32,
        )
        * score_scale
    )
    probability = soft_weights(scores)
    mixed = jnp.einsum(
        "shfg,sghd->sfhd",
        probability.astype(jnp.bfloat16),
        split_heads(value_part),
        preferred_element_type=jnp.float32,
    )
    return (join_heads(mixed).astype(jnp.bfloat16), probability)


def feature_grads(queries, key_part, value_part, probability, grad_mixed):
    score_scale = HEAD_DIM ** (-0.5)
    grad_heads = split_heads(grad_mixed)
    grad_weights = jnp.einsum(
        "sfhd,sghd->shfg", grad_heads, split_heads(value_part), preferred_element_type=jnp.float32
    )
    inner_sum = jnp.sum(probability * grad_weights, axis=-1, keepdims=True)
    grad_scores = (probability * (grad_weights - inner_sum)).astype(jnp.bfloat16)
    grad_queries = (
        jnp.einsum(
            "shfg,sghd->sfhd",
            grad_scores,
            split_heads(key_part),
            preferred_element_type=jnp.float32,
        )
        * score_scale
    )
    grad_keys = (
        jnp.einsum(
            "shfg,sfhd->sghd", grad_scores, split_heads(queries), preferred_element_type=jnp.float32
        )
        * score_scale
    )
    grad_values = jnp.einsum(
        "shfg,sfhd->sghd",
        probability.astype(jnp.bfloat16),
        grad_heads,
        preferred_element_type=jnp.float32,
    )
    return (join_heads(grad_queries), join_heads(grad_keys), join_heads(grad_values))


def local_large(
    layer_input,
    segment_ids,
    context_flags,
    first_gain,
    first_shift,
    sample_weight,
    sample_bias,
    sample_mixer,
    sample_offset,
    second_gain,
    second_shift,
    feature_weight,
    feature_bias,
    feature_mixer,
    feature_offset,
    third_gain,
    third_shift,
    expand_weight,
    expand_bias,
    reduce_weight,
    reduce_bias,
    cotangent,
):
    sample_rows = layer_input.shape[0]
    feature_rows = layer_input.shape[1]
    model_width = layer_input.shape[2]
    score_scale = HEAD_DIM ** (-0.5)
    shard_count = lax.axis_size("samp")
    context_shards = shard_count // 8
    total_context = context_shards * sample_rows
    residual_zero = layer_input.astype(jnp.float32)
    normed_one, norm_one_back = jax.vjp(layer_norm, residual_zero, first_gain, first_shift)
    active_one = normed_one.astype(jnp.bfloat16)
    queries_one, keys_one, values_one = project(active_one, sample_weight, sample_bias)
    my_index = lax.axis_index("samp")
    shard_flags = context_flags.reshape(shard_count, sample_rows)[:, 0]
    shard_rank = jnp.cumsum(shard_flags) - 1
    shard_ids = jnp.arange(shard_count, dtype=jnp.int32)
    slot_ids = jnp.arange(context_shards, dtype=jnp.int32)
    root_hits = (shard_rank[None, :] == slot_ids[:, None]) & (shard_flags[None, :] == 1)
    roots = jnp.sum(jnp.where(root_hits, shard_ids[None, :], 0), axis=1)
    context_tasks = jnp.take(segment_ids.reshape(shard_count, sample_rows), roots, axis=0).reshape(
        total_context
    )
    local_tasks = lax.dynamic_slice_in_dim(segment_ids, my_index * sample_rows, sample_rows)
    allowed = local_tasks[:, None] == context_tasks[None, :]
    is_context = shard_flags[my_index] == 1
    own_rank = jnp.maximum(shard_rank[my_index], 0)
    own_block = jnp.concatenate([keys_one, values_one], axis=-1)

    def fetch_rows(step, buffer):
        piece = spread_2(own_block, "samp", roots[step])
        return lax.dynamic_update_slice_in_dim(buffer, piece, step * sample_rows, 0)

    empty_rows = jnp.zeros((total_context, feature_rows, 2 * model_width), jnp.bfloat16)
    fetched = lax.fori_loop(0, context_shards, fetch_rows, empty_rows)
    context_keys = fetched[..., :model_width]
    context_values = fetched[..., model_width:]
    query_heads = split_heads(queries_one)
    key_heads = split_heads(context_keys)
    value_heads = split_heads(context_values)
    scores = (
        jnp.einsum("sfhd,cfhd->fhsc", query_heads, key_heads, preferred_element_type=jnp.float32)
        * score_scale
    )
    sample_prob = soft_weights(jnp.where(allowed[None, None], scores, MASKED))
    sample_weights = sample_prob.astype(jnp.bfloat16)
    mixed_one = join_heads(
        jnp.einsum(
            "fhsc,cfhd->sfhd", sample_weights, value_heads, preferred_element_type=jnp.float32
        )
    ).astype(jnp.bfloat16)
    residual_one = residual_zero + apply_weight(mixed_one, sample_mixer) + sample_offset
    normed_two, norm_two_back = jax.vjp(layer_norm, residual_one, second_gain, second_shift)
    active_two = normed_two.astype(jnp.bfloat16)
    queries_two, keys_two, values_two = project(active_two, feature_weight, feature_bias)
    all_keys, all_values = (
        lax.all_gather(keys_two, "feat", axis=1, tiled=True),
        lax.all_gather(values_two, "feat", axis=1, tiled=True),
    )
    mixed_two, feature_prob = feature_attend(queries_two, all_keys, all_values)
    residual_two = residual_one + apply_weight(mixed_two, feature_mixer) + feature_offset
    normed_three, norm_three_back = jax.vjp(layer_norm, residual_two, third_gain, third_shift)
    active_three = normed_three.astype(jnp.bfloat16)
    expanded = apply_weight(active_three, expand_weight) + expand_bias
    activated, gelu_back = jax.vjp(partial(jax.nn.gelu, approximate=False), expanded)
    hidden = activated.astype(jnp.bfloat16)
    layer_output = (residual_two + apply_weight(hidden, reduce_weight) + reduce_bias).astype(
        jnp.bfloat16
    )
    grad_out = cotangent.astype(jnp.float32)
    grad_branch = cotangent
    reduce_bias_grad = column_sum(grad_branch)
    reduce_weight_grad = weight_grad(hidden, grad_branch)
    grad_hidden = input_back(grad_branch, reduce_weight).astype(jnp.bfloat16)
    grad_expanded = gelu_back(grad_hidden.astype(jnp.float32))[0].astype(jnp.bfloat16)
    expand_bias_grad = column_sum(grad_expanded)
    expand_weight_grad = weight_grad(active_three, grad_expanded)
    grad_norm, third_gain_grad, third_shift_grad = norm_three_back(
        input_back(grad_expanded, expand_weight)
    )
    grad_two = grad_out + grad_norm
    grad_branch = grad_two.astype(jnp.bfloat16)
    feature_offset_grad = column_sum(grad_branch)
    feature_mixer_grad = weight_grad(mixed_two, grad_branch)
    grad_mixed = input_back(grad_branch, feature_mixer).astype(jnp.bfloat16)
    grad_queries, grad_keys, grad_values = feature_grads(
        queries_two, all_keys, all_values, feature_prob, grad_mixed
    )
    own_key_grads, own_value_grads = (
        lax.psum_scatter(grad_keys, "feat", scatter_dimension=1, tiled=True),
        lax.psum_scatter(grad_values, "feat", scatter_dimension=1, tiled=True),
    )
    grad_project = jnp.concatenate(
        [
            grad_queries.astype(jnp.bfloat16),
            own_key_grads.astype(jnp.bfloat16),
            own_value_grads.astype(jnp.bfloat16),
        ],
        axis=-1,
    )
    feature_weight_grad = weight_grad(active_two, grad_project)
    feature_bias_grad = jnp.concatenate(
        [
            column_sum(grad_project[..., :model_width]),
            column_sum(grad_project[..., 2 * model_width :]),
        ]
    )
    grad_norm, second_gain_grad, second_shift_grad = norm_two_back(
        input_back(grad_project, feature_weight)
    )
    grad_one = grad_two + grad_norm
    grad_branch = grad_one.astype(jnp.bfloat16)
    sample_offset_grad = column_sum(grad_branch)
    sample_mixer_grad = weight_grad(mixed_one, grad_branch)
    grad_heads = split_heads(input_back(grad_branch, sample_mixer).astype(jnp.bfloat16))
    grad_weights = jnp.einsum(
        "sfhd,cfhd->fhsc", grad_heads, value_heads, preferred_element_type=jnp.float32
    )
    inner_sum = jnp.sum(sample_prob * grad_weights, axis=-1, keepdims=True)
    grad_scores = (sample_prob * (grad_weights - inner_sum)).astype(jnp.bfloat16)
    grad_queries = (
        join_heads(
            jnp.einsum(
                "fhsc,cfhd->sfhd", grad_scores, key_heads, preferred_element_type=jnp.float32
            )
        )
        * score_scale
    ).astype(jnp.bfloat16)
    key_terms = (
        join_heads(
            jnp.einsum(
                "fhsc,sfhd->cfhd", grad_scores, query_heads, preferred_element_type=jnp.float32
            )
        )
        * score_scale
    )
    value_terms = join_heads(
        jnp.einsum(
            "fhsc,sfhd->cfhd", sample_weights, grad_heads, preferred_element_type=jnp.float32
        )
    )
    term_block = jnp.concatenate([key_terms, value_terms], axis=-1)
    summed_terms = lax.psum_scatter(term_block, "samp", scatter_dimension=0, tiled=True)
    summed_rows = lax.all_gather(summed_terms.astype(jnp.bfloat16), "samp", axis=0, tiled=True)
    own_grads = lax.dynamic_slice_in_dim(summed_rows, own_rank * sample_rows, sample_rows, 0)
    own_grads = jnp.where(is_context, own_grads, jnp.zeros_like(own_grads))
    grad_project = jnp.concatenate([grad_queries, own_grads], axis=-1)
    sample_weight_grad = weight_grad(active_one, grad_project)
    sample_bias_grad = jnp.concatenate(
        [column_sum(grad_queries), column_sum(own_grads[..., model_width:])]
    )
    grad_norm, first_gain_grad, first_shift_grad = norm_one_back(
        input_back(grad_project, sample_weight)
    )
    input_grad = (grad_one + grad_norm).astype(jnp.bfloat16)
    summed = lax.psum(
        (
            first_gain_grad,
            first_shift_grad,
            sample_weight_grad,
            sample_bias_grad,
            sample_mixer_grad,
            sample_offset_grad,
            second_gain_grad,
            second_shift_grad,
            feature_weight_grad,
            feature_bias_grad,
            feature_mixer_grad,
            feature_offset_grad,
            third_gain_grad,
            third_shift_grad,
            expand_weight_grad,
            expand_bias_grad,
            reduce_weight_grad,
            reduce_bias_grad,
        ),
        "feat",
    )
    shares = (
        lax.psum_scatter(summed[0], "samp", scatter_dimension=0, tiled=True),
        lax.psum_scatter(summed[1], "samp", scatter_dimension=0, tiled=True),
        lax.psum_scatter(summed[2], "samp", scatter_dimension=0, tiled=True),
        lax.psum_scatter(summed[3], "samp", scatter_dimension=0, tiled=True),
        lax.psum_scatter(summed[4], "samp", scatter_dimension=0, tiled=True),
        lax.psum_scatter(summed[5], "samp", scatter_dimension=0, tiled=True),
        lax.psum_scatter(summed[6], "samp", scatter_dimension=0, tiled=True),
        lax.psum_scatter(summed[7], "samp", scatter_dimension=0, tiled=True),
        lax.psum_scatter(summed[8], "samp", scatter_dimension=0, tiled=True),
        lax.psum_scatter(summed[9], "samp", scatter_dimension=0, tiled=True),
        lax.psum_scatter(summed[10], "samp", scatter_dimension=0, tiled=True),
        lax.psum_scatter(summed[11], "samp", scatter_dimension=0, tiled=True),
        lax.psum_scatter(summed[12], "samp", scatter_dimension=0, tiled=True),
        lax.psum_scatter(summed[13], "samp", scatter_dimension=0, tiled=True),
        lax.psum_scatter(summed[14], "samp", scatter_dimension=0, tiled=True),
        lax.psum_scatter(summed[15], "samp", scatter_dimension=0, tiled=True),
        lax.psum_scatter(summed[16], "samp", scatter_dimension=0, tiled=True),
        lax.psum_scatter(summed[17], "samp", scatter_dimension=0, tiled=True),
    )
    return (
        layer_output,
        input_grad,
        shares[0],
        shares[1],
        shares[2],
        shares[3],
        shares[4],
        shares[5],
        shares[6],
        shares[7],
        shares[8],
        shares[9],
        shares[10],
        shares[11],
        shares[12],
        shares[13],
        shares[14],
        shares[15],
        shares[16],
        shares[17],
    )


def solution(mesh):
    small = mesh.shape["samp"] == 8 and mesh.shape["feat"] == 4
    return jax.shard_map(
        local_small if small else local_large,
        mesh=mesh,
        in_specs=(
            P("samp", "feat", None),
            P(),
            P(),
            P(),
            P(),
            P(),
            P(),
            P(),
            P(),
            P(),
            P(),
            P(),
            P(),
            P(),
            P(),
            P(),
            P(),
            P(),
            P(),
            P(),
            P(),
            P("samp", "feat", None),
        ),
        out_specs=(
            P("samp", "feat", None),
            P("samp", "feat", None),
            P("samp"),
            P("samp"),
            P("samp", None),
            P("samp"),
            P("samp", None),
            P("samp"),
            P("samp"),
            P("samp"),
            P("samp", None),
            P("samp"),
            P("samp", None),
            P("samp"),
            P("samp"),
            P("samp"),
            P("samp", None),
            P("samp"),
            P("samp", None),
            P("samp"),
        ),
        check_vma=False,
    )
```

```python
from functools import partial

import jax
import jax.numpy as jnp
from jax import lax
from jax.experimental import pallas as pl
from jax.experimental.pallas import tpu as pltpu
from jax.sharding import PartitionSpec as P

HEADS = 8
HEAD_DIM = 64
EPS = 1e-05
MASKED = -1000000000.0
SCALE = HEAD_DIM ** (-0.5)
QUAD = 4 * HEAD_DIM
BF = jnp.bfloat16
F32 = jnp.float32


def mm(a, b, ca=1, cb=0):
    return lax.dot_general(a, b, (((ca,), (cb,)), ((), ())), preferred_element_type=F32)


def norm_parts(values):
    center = jnp.mean(values, axis=-1, keepdims=True)
    spread = values - center
    variance = jnp.mean(spread * spread, axis=-1, keepdims=True)
    inverse = lax.rsqrt(variance + EPS)
    return spread * inverse, inverse


def norm_back(grad, unit, inverse, gain):
    scaled = grad * gain
    first = jnp.mean(scaled, axis=-1, keepdims=True)
    second = jnp.mean(scaled * unit, axis=-1, keepdims=True)
    return (scaled - first - unit * second) * inverse


def lane_ids(rows):
    return lax.broadcasted_iota(jnp.int32, (rows, 128), 1)


def group_reduce(values, op, fill):
    rows = values.shape[0]
    low = lane_ids(rows) < HEAD_DIM
    outs = []
    for t in range(values.shape[1] // 128):
        tile = values[:, t * 128 : (t + 1) * 128]
        left = op(jnp.where(low, tile, fill), axis=1, keepdims=True)
        right = op(jnp.where(low, fill, tile), axis=1, keepdims=True)
        outs.append(jnp.where(low, left, right))
    return jnp.concatenate(outs, axis=1)


def head_masks(dtype):
    lanes = lax.broadcasted_iota(jnp.int32, (1, QUAD), 1) // HEAD_DIM
    return [jnp.where(lanes == h, 1.0, 0.0).astype(dtype) for h in range(4)]


def stack_heads(part, masks):
    return jnp.concatenate([part * m for m in masks], axis=0)


def pick_heads(stacked, masks):
    rows = stacked.shape[0] // 4
    total = stacked[:rows] * masks[0]
    for h in range(1, 4):
        total = total + stacked[h * rows : (h + 1) * rows] * masks[h]
    return total


def attend(q, k, v, masks, allow):
    outs, probs = [], []
    for quad in range(2):
        cols = slice(quad * QUAD, (quad + 1) * QUAD)
        scores = mm(q[:, cols], stack_heads(k[:, cols], masks), 1, 1)
        if allow is not None:
            scores = jnp.where(allow, scores, MASKED)
        raised = jnp.exp(scores - group_reduce(scores, jnp.max, -jnp.inf))
        prob = raised / group_reduce(raised, jnp.sum, 0.0)
        outs.append(mm(prob.astype(BF), stack_heads(v[:, cols], masks)))
        probs.append(prob)
    return jnp.concatenate(outs, axis=1), jnp.concatenate(probs, axis=1)


def attend_back(q, k, v, prob, grad, masks, masks32):
    dqs, dks, dvs = [], [], []
    for quad in range(2):
        cols = slice(quad * QUAD, (quad + 1) * QUAD)
        p, g = prob[:, cols], grad[:, cols]
        back = mm(g, stack_heads(v[:, cols], masks), 1, 1)
        inner = group_reduce(p * back, jnp.sum, 0.0)
        gs = (p * (back - inner)).astype(BF)
        dqs.append(mm(gs, stack_heads(k[:, cols], masks)) * SCALE)
        dks.append(pick_heads(mm(gs, q[:, cols], 0, 0), masks32))
        dvs.append(pick_heads(mm(p.astype(BF), g, 0, 0), masks32))
    join = lambda parts: jnp.concatenate(parts, axis=1).astype(BF)
    return join(dqs), join(dks), join(dvs)


def swap_matrix(n):
    r = lax.broadcasted_iota(jnp.int32, (n, n), 0)
    c = lax.broadcasted_iota(jnp.int32, (n, n), 1)
    return jnp.where((r // 16 == c % 16) & (r % 16 == c // 16), 1.0, 0.0).astype(BF)


def swap(matrix, values):
    return mm(matrix, values).astype(BF)


def gelu_parts(u):
    cdf = 0.5 * (1.0 + lax.erf(u * (2.0**-0.5)))
    density = jnp.exp(u * u * -0.5) * 0.3989422804014327
    return cdf, density


def col_sum(values):
    return jnp.sum(values.astype(F32), axis=0, keepdims=True)


THIRDS = (0, 336, 672)
THIRD = 352
HELD = (
    (0, 0, 0), (6, 4, 5), (9, 5, 8), (8, 9, 7),
    (1, 2, 3), (5, 2, 3), (6, 3, 9), (8, 9, 2),
)


def forward_one(
    me_ref, x_ref, y1, y2, y3, p1, p2, p3, m1, m2, m3,
    allow_ref, gain_ref, shift_ref, w_ref, b_ref,
    o0, o1, o2, o3, on_ref, c_ref, q_ref, k_ref, v_ref, p_ref, o_scr,
):
    me = me_ref[0]
    got = (None, y1, y2, y3, p1, p2, p3, m1, m2, m3)
    for position, held in enumerate(HELD):

        @pl.when(me_ref[2] == position)
        def _(held=held):
            for start, index in zip(THIRDS, held):
                rows = slice(start, start + THIRD)
                c_ref[rows] = x_ref[rows] if index == 0 else got[index][...]

    gain, shift = gain_ref[...], shift_ref[...]
    matrix = swap_matrix(256)
    for d in range(4):
        rows = slice(d * 256, (d + 1) * 256)
        unit, _ = norm_parts(x_ref[rows].astype(F32))
        act = swap(matrix, (unit * gain + shift).astype(BF))
        q = (mm(act, w_ref[:, :512]) + b_ref[:, :512]).astype(BF) * SCALE
        q_ref[:, d] = q.astype(BF).reshape(16, 16, 512)
        unit, _ = norm_parts(c_ref[rows].astype(F32))
        act = swap(matrix, (unit * gain + shift).astype(BF))
        kv = mm(act, w_ref[:, 512:])
        k_ref[:, d] = kv[:, :512].astype(BF).reshape(16, 16, 512)
        v_ref[:, d] = (kv[:, 512:] + b_ref[:, 512:]).astype(BF).reshape(16, 16, 512)
    masks = head_masks(BF)
    allow = allow_ref[...] > 0.5

    def body(i, carry):
        for j in range(2):
            f = i * 2 + j
            q, k, v = (r[f].reshape(64, 512) for r in (q_ref, k_ref, v_ref))
            out, prob = attend(q, k, v, masks, allow)
            o_scr[f] = out.astype(BF).reshape(4, 16, 512)
            p_ref[f] = prob
        return carry

    lax.fori_loop(0, 8, body, 0)
    for d, ref in enumerate((o0, o1, o2, o3)):
        value = swap(matrix, o_scr[:, d ^ me].reshape(256, 512))
        ref[...] = value
        on_ref[d ^ me] = value


def middle(
    me_ref, o0, o1, o2_, o3, x0, x1, x2, x3, c0, c1, c2, c3,
    wm1_ref, off1_ref, g2_ref, s2_ref, wf_ref, bf_ref, wm2_ref, off2_ref,
    g3_ref, s3_ref, we_ref, be_ref, wr_ref, br_ref,
    out0, out2, out13, gb10, gb11, gb12, gb13,
    a2_ref, dqkv_ref, o2_ref, gb2_ref, a3_ref, gu_ref, hid_ref, gb3_ref, vec_ref, bias_ref,
):
    samples = 4

    def gather(*refs):
        return jnp.concatenate(
            [ref[s * 16 : (s + 1) * 16] for s in range(samples) for ref in refs], axis=0
        )

    def scatter(values, *refs):
        for s in range(samples):
            for d, ref in enumerate(refs):
                at = (s * 4 + d) * 16
                ref[s * 16 : (s + 1) * 16] = values[at : at + 16]

    masks, masks32 = head_masks(BF), head_masks(F32)
    attended, cot = gather(o0, o1, o2_, o3), gather(c0, c1, c2, c3)
    gb3_ref[...] = cot
    r1 = gather(x0, x1, x2, x3).astype(F32) + mm(attended, wm1_ref[...]) + off1_ref[...]
    unit2, inv2 = norm_parts(r1)
    act2 = (unit2 * g2_ref[...] + s2_ref[...]).astype(BF)
    a2_ref[...] = act2
    qkv = mm(act2, wf_ref[...])
    q = (qkv[:, :512] + bf_ref[:, :512]).astype(BF) * jnp.asarray(SCALE, BF)
    k = qkv[:, 512:1024].astype(BF)
    v = (qkv[:, 1024:] + bf_ref[:, 512:]).astype(BF)
    parts = []
    for s in range(samples):
        rows = slice(s * 64, (s + 1) * 64)
        parts.append(attend(q[rows], k[rows], v[rows], masks, None))
    o2 = jnp.concatenate([part[0] for part in parts], axis=0).astype(BF)
    o2_ref[...] = o2
    r2 = r1 + mm(o2, wm2_ref[...]) + off2_ref[...]
    unit3, inv3 = norm_parts(r2)
    act3 = (unit3 * g3_ref[...] + s3_ref[...]).astype(BF)
    a3_ref[...] = act3
    out = r2 + br_ref[...]
    back = None
    bias = []
    for b in range(4):
        cols = slice(b * 512, (b + 1) * 512)
        u = mm(act3, we_ref[:, cols]) + be_ref[:, cols]
        cdf, density = gelu_parts(u)
        hidden = (u * cdf).astype(BF)
        hid_ref[:, cols] = hidden
        out = out + mm(hidden, wr_ref[cols, :])
        gh = mm(cot, wr_ref[cols, :], 1, 1).astype(BF).astype(F32)
        gu = (gh * (cdf + u * density)).astype(BF)
        gu_ref[:, cols] = gu
        bias.append(col_sum(gu))
        term = mm(gu, we_ref[:, cols], 1, 1)
        back = term if back is None else back + term
    scatter(out.astype(BF), out0, out13.at[0], out2, out13.at[1])
    vecs = [col_sum(back * unit3), col_sum(back)]
    gr2 = cot.astype(F32) + norm_back(back, unit3, inv3, g3_ref[...])
    gb2 = gr2.astype(BF)
    gb2_ref[...] = gb2
    go2 = mm(gb2, wm2_ref[...], 1, 1).astype(BF)
    grads = []
    for s in range(samples):
        rows = slice(s * 64, (s + 1) * 64)
        grads.append(
            jnp.concatenate(
                attend_back(q[rows], k[rows], v[rows], parts[s][1], go2[rows], masks, masks32),
                axis=1,
            )
        )
    dqkv = jnp.concatenate(grads, axis=0)
    dqkv_ref[...] = dqkv
    back = mm(dqkv, wf_ref[...], 1, 1)
    vecs += [col_sum(back * unit2), col_sum(back)]
    gr1 = gr2 + norm_back(back, unit2, inv2, g2_ref[...])
    scatter(gr1.astype(BF), gb10, gb11, gb12, gb13)
    vecs += [col_sum(gb2), col_sum(cot), col_sum(dqkv[:, :512]), col_sum(dqkv[:, 1024:])]

    @pl.when(pl.program_id(0) == 0)
    def _():
        vec_ref[...] = jnp.zeros_like(vec_ref)
        bias_ref[...] = jnp.zeros_like(bias_ref)

    vec_ref[...] += jnp.concatenate(vecs, axis=0)
    bias_ref[...] += jnp.concatenate(bias, axis=1)


def attend_half(q_ref, k_ref, v_ref, p_ref, go_ref, half, dq_ref, dkv_ref):
    masks, masks32 = head_masks(BF), head_masks(F32)

    def body(i, carry):
        for j in range(2):
            f = i * 2 + j
            q, k, v, go = (
                r.reshape(64, 512)
                for r in (q_ref[f], k_ref[f], v_ref[f], go_ref[half * 8 + f])
            )
            dq, dk, dv = attend_back(q, k, v, p_ref[f], go, masks, masks32)
            dq_ref[f] = dq.reshape(4, 16, 512)
            dkv_ref[f] = jnp.concatenate([dk, dv], axis=1).reshape(4, 16, 1024)
        return carry

    lax.fori_loop(0, 4, body, 0)


def backward_first(
    me_ref, g0, g1, g2, g3, q_ref, k_ref, v_ref, p_ref, wm_ref,
    gb1_ref, go_ref, dq_ref, dkv_ref,
):
    me = me_ref[0]
    matrix = swap_matrix(256)
    for d, ref in enumerate((g0, g1, g2, g3)):
        value = ref[...]
        gb1_ref[d ^ me] = value
        go = mm(value, wm_ref[...], 1, 1).astype(BF)
        go_ref[:, d ^ me] = swap(matrix, go).reshape(16, 16, 512)
    attend_half(q_ref, k_ref, v_ref, p_ref, go_ref, 0, dq_ref, dkv_ref)


def backward_second(
    me_ref, go_ref, q_ref, k_ref, v_ref, p_ref, dkva_ref, c_ref, gain_ref, shift_ref, w_ref,
    ta_ref, tb_ref, tc_ref, cact_ref, dkv_ref, dq_ref, vec_ref,
    dkv_scr, t_scr,
):
    attend_half(q_ref, k_ref, v_ref, p_ref, go_ref, 1, dq_ref, dkv_scr)
    gain, shift = gain_ref[...], shift_ref[...]
    matrix = swap_matrix(256)
    gain_sum = jnp.zeros((1, 512), F32)
    shift_sum, v_sum = gain_sum, gain_sum
    for d in range(4):
        rows = slice(d * 256, (d + 1) * 256)
        unit, inverse = norm_parts(c_ref[rows].astype(F32))
        cact_ref[rows] = (unit * gain + shift).astype(BF)
        heads = jnp.concatenate(
            [r[:, d].reshape(128, 1024) for r in (dkva_ref, dkv_scr)], axis=0
        )
        dkv = swap(matrix, heads)
        dkv_ref[rows] = dkv
        back = mm(dkv, w_ref[:, 512:], 1, 1)
        t_scr[rows] = back.astype(BF)
        gain_sum += col_sum(back * unit)
        shift_sum += col_sum(back)
        v_sum += col_sum(dkv[:, 512:])
    for ref, start in zip((ta_ref, tb_ref, tc_ref), THIRDS):
        ref[...] = t_scr[start : start + THIRD]
    zero = jnp.zeros((1, 512), F32)
    vec_ref[...] = jnp.concatenate([gain_sum, shift_sum, v_sum] + [zero] * 5, axis=0)


def backward_query(
    me_ref, gb1_ref, x_ref, dqa_ref, dqb_ref, vecc_ref, gain_ref, shift_ref, w_ref,
    base_ref, act_ref, dqn_ref, vec_ref,
):
    gain, shift = gain_ref[...], shift_ref[...]
    matrix = swap_matrix(256)
    gain_sum, shift_sum, v_sum = vecc_ref[0:1], vecc_ref[1:2], vecc_ref[2:3]
    off_sum = jnp.zeros((1, 512), F32)
    q_sum = off_sum
    for d in range(4):
        rows = slice(d * 256, (d + 1) * 256)
        unit, inverse = norm_parts(x_ref[rows].astype(F32))
        act_ref[rows] = (unit * gain + shift).astype(BF)
        heads = jnp.concatenate([r[:, d].reshape(128, 512) for r in (dqa_ref, dqb_ref)], axis=0)
        dq = swap(matrix, heads)
        dqn_ref[rows] = dq
        back = mm(dq, w_ref[:, :512], 1, 1)
        gb1 = gb1_ref[d]
        base_ref[rows] = gb1.astype(F32) + norm_back(back, unit, inverse, gain)
        gain_sum += col_sum(back * unit)
        shift_sum += col_sum(back)
        off_sum += col_sum(gb1)
        q_sum += col_sum(dq)
    zero = jnp.zeros((1, 512), F32)
    vec_ref[...] = jnp.concatenate(
        [gain_sum, shift_sum, off_sum, q_sum, v_sum, zero, zero, zero], axis=0
    )


def finish(
    me_ref, base_ref, a_ref, ag_ref, b_ref, bg_ref, c_ref, cg_ref, x_ref, gain_ref, out_ref
):
    owner = me_ref[1] == 1

    @pl.when(owner)
    def _():
        for ref, got, start, rows in (
            (a_ref, ag_ref, 0, 336), (b_ref, bg_ref, 336, 336), (c_ref, cg_ref, 672, 352)
        ):
            at = slice(start, start + rows)
            unit, inverse = norm_parts(x_ref[at].astype(F32))
            total = ref[:rows].astype(F32) + got[:rows].astype(F32)
            extra = norm_back(total, unit, inverse, gain_ref[...])
            out_ref[at] = (base_ref[at] + extra).astype(BF)

    @pl.when(jnp.logical_not(owner))
    def _():
        out_ref[...] = base_ref[...].astype(BF)


def place(me_ref, b0, b1, b2, b3, out_ref):
    for d, ref in enumerate((b0, b1, b2, b3)):
        out_ref[d ^ me_ref[0]] = ref[...]


def shard_of(me_ref, dy, d1, d3):
    return ((me_ref[6] ^ d1 ^ (3 * d3)) * 2) + (me_ref[5] ^ dy)


BITS = [(a, b, c) for a in range(2) for b in range(2) for c in range(2)]


def grads_reduce(me_ref, hid_ref, gb3_ref, keep_ref, send_ref, scr):
    core = me_ref[3]
    for i in range(8):
        scr[i * 256 : (i + 1) * 256] = mm(
            hid_ref[:, i * 256 : (i + 1) * 256], gb3_ref[...], 0, 0
        ).astype(BF)
    for i, (d1, d3, dy) in enumerate(BITS):
        start = shard_of(me_ref, dy, d1, d3) * 256
        keep_ref[i] = scr[pl.ds(pl.multiple_of(start + core * 128, 128), 128)]
        send_ref[i] = scr[pl.ds(pl.multiple_of(start + (1 - core) * 128, 128), 128)]


def grads_expand(me_ref, act_ref, gu_ref, keep_ref, send_ref, scr):
    core = me_ref[3]
    for n in range(4):
        scr[n] = mm(act_ref[...], gu_ref[:, n * 512 : (n + 1) * 512], 0, 0).astype(BF)
    for i, (dy, d1, d3) in enumerate(BITS):
        rows = pl.ds(pl.multiple_of(shard_of(me_ref, dy, d1, d3) * 64, 64), 64)
        for u in range(2):
            keep_ref[i, u] = scr[2 * core + u, rows]
            send_ref[i, u] = scr[2 * (1 - core) + u, rows]


def grads_feature(me_ref, act_ref, dqkv_ref, o_ref, gb_ref, keep_ref, send_ref, scr):
    core, xx = me_ref[3], me_ref[4]
    for n in range(3):
        scr[n] = mm(act_ref[...], dqkv_ref[:, n * 512 : (n + 1) * 512], 0, 0).astype(BF)
    scr[3] = mm(o_ref[...], gb_ref[...], 0, 0).astype(BF)
    for i, (dy, d1, d3) in enumerate(BITS):
        rows = pl.ds(pl.multiple_of(shard_of(me_ref, dy, d1, d3) * 64, 64), 64)
        for dx in range(2):
            keep_ref[dx, i] = scr[2 * core + (dx ^ xx), rows]
            send_ref[dx, i] = scr[2 * (1 - core) + (dx ^ xx), rows]


def grads_sample(
    me_ref, act_ref, dq_ref, cact_ref, dkv_ref, o_ref, gb1_ref,
    keepx_ref, sendx_ref, keepy_ref, sendy_ref, scr,
):
    core, xx = me_ref[3], me_ref[4]
    scr[0] = mm(act_ref[...], dq_ref[...], 0, 0).astype(BF)
    scr[1] = mm(cact_ref[...], dkv_ref[:, :512], 0, 0).astype(BF)
    scr[2] = mm(cact_ref[...], dkv_ref[:, 512:], 0, 0).astype(BF)
    total = jnp.zeros((512, 512), F32)
    for d in range(4):
        total += mm(o_ref[d], gb1_ref[d], 0, 0)
    scr[3] = total.astype(BF)
    for i, (dy, d1, d3) in enumerate(BITS):
        start = shard_of(me_ref, dy, d1, d3) * 64
        rows = pl.ds(pl.multiple_of(start, 64), 64)
        keepy_ref[i] = scr[2 * core + 1, rows]
        sendy_ref[i] = scr[2 * (1 - core) + 1, rows]
        for dx in range(2):
            rows = pl.ds(pl.multiple_of(start + (dx ^ xx) * 32, 32), 32)
            keepx_ref[dx, i] = scr[2 * core, rows]
            sendx_ref[dx, i] = scr[2 * (1 - core), rows]


def spec(shape, index=None):
    return pl.BlockSpec(shape, index if index is not None else (lambda *a: (0,) * len(shape)))


def sds(shape, dtype=BF):
    return jax.ShapeDtypeStruct(shape, dtype)


def params(limit):
    return pltpu.CompilerParams(vmem_limit_bytes=limit << 20)


def row(vector):
    return vector.reshape(1, -1)


def whole(kernel, name, limit, outs, scratch, *inputs):
    arrays, specs = [inputs[0]], [pl.BlockSpec(memory_space=pltpu.SMEM)]
    for entry in inputs[1:]:
        array, block, index = entry if isinstance(entry, tuple) else (entry, None, None)
        arrays.append(array)
        block = array.shape if block is None else block
        index = (0,) * array.ndim if index is None else index
        specs.append(pl.BlockSpec(block, lambda i, index=index: index))
    single = not isinstance(outs, tuple)
    return pl.pallas_call(
        kernel,
        grid=(1,),
        out_shape=outs,
        in_specs=specs,
        out_specs=jax.tree.map(lambda o: pl.BlockSpec(o.shape, lambda i: (0,) * len(o.shape)), outs),
        scratch_shapes=scratch,
        compiler_params=params(limit),
        name=name,
    )(*arrays)


def shuffle(value, axis, mask):
    size = lax.axis_size(axis)
    return lax.ppermute(value, axis, [(i, i ^ mask) for i in range(size)])


CORE, X, Y, Z, Z3 = ("feat", 1), ("feat", 2), ("samp", 1), ("samp", 2), ("samp", 6)


def turn(value, step):
    return lax.ppermute(value, "samp", [(i, (i + 2 * step) % 8) for i in range(8)])


def at(stacked, index, axis=0):
    return lax.dynamic_index_in_dim(stacked, index, axis, keepdims=False)


def fence(tree):
    return lax.optimization_barrier(tree)


def plus(a, b):
    return (a.astype(F32) + b.astype(F32)).astype(BF)


class Chain:
    def __init__(self, keep, sent, dims):
        self.keep, self.sent, self.dims = keep, sent, (CORE,) + dims

    def start(self):
        return shuffle(self.sent, *self.dims[0])

    def take(self, got):
        self.dims = self.dims[1:]
        if self.dims:
            self.keep, self.sent = plus(self.keep[0], got[0]), plus(self.keep[1], got[1])
        else:
            self.keep = plus(self.keep, got)


def together(chains, make=lambda: ()):
    got = [chain.start() for chain in chains]
    got, other = fence((got, make()))
    for chain, value in zip(chains, got):
        chain.take(value)
    return other


def last_round(parts):
    joined = jnp.concatenate([part.reshape(-1, 512) for part in parts], axis=0)
    return joined, [shuffle(joined, "feat", mask) for mask in (1, 2, 3)]


def pick_sum(rows, core):
    own, sibling, partner, other = (r.astype(F32) for r in rows)
    mine, theirs = own + partner, sibling + other
    return jnp.stack([jnp.where(core == 0, mine, theirs), jnp.where(core == 0, theirs, mine)])


def pick_join(rows, core, xx):
    place = core * 2 + xx
    outs = []
    for target in range(4):
        value = rows[0]
        for mask, index in ((1, 2), (2, 1), (3, 3)):
            value = jnp.where((place ^ target) == index, rows[mask], value)
        outs.append(value.astype(F32))
    return jnp.stack(outs)


def send_context(x, position):
    dy, dz = position // 4, position % 4
    owner = position == 0
    a, b, c = (x[start : start + THIRD] for start in THIRDS)
    pick = jnp.where
    y1, p1, m1 = yield shuffle(a, *Y), turn(b, 1), turn(c, -1)
    y2, p2, m2 = yield (
        shuffle(pick(owner, b, pick(dz == 1, p1, m1)), *Y),
        turn(pick(owner, c, pick(dy == 1, y1, p1)), 1),
        turn(pick(owner, a, pick(dy == 1, y1, m1)), -1),
    )
    y3, p3, m3 = yield (
        shuffle(pick(owner, c, p2), *Y),
        turn(pick(owner, a, p2), 1),
        turn(pick(owner, b, pick((dy == 0) & (dz == 3), m2, y2)), -1),
    )
    yield y1, y2, y3, p1, p2, p3, m1, m2, m3


def sum_context(a, b, c, position):
    pick = jnp.where

    def to(places):
        hit = position == places[0]
        for place in places[1:]:
            hit = hit | (position == place)
        return hit

    def add(value, *terms):
        total = value.astype(F32)
        for places, got in terms:
            total = total + pick(to(places), got.astype(F32), 0.0)
        return total.astype(BF)

    y, m, p = yield (
        shuffle(pick(to([6]), b, c), *Y),
        turn(a, -1),
        turn(pick(to([3, 7]), b, pick(to([2]), a, c)), 1),
    )
    a, b, c = (
        add(a, ([0, 5], m), ([3], p)),
        add(b, ([2], y), ([0, 4], p)),
        add(c, ([0, 1], y), ([7], p)),
    )
    y, m, p = yield (
        shuffle(pick(to([7]), c, b), *Y),
        turn(pick(to([1]), c, pick(to([5]), a, b)), -1),
        turn(pick(to([2]), c, a), 1),
    )
    a, b, c = (
        add(a, ([4], m), ([0, 4], p)),
        add(b, ([0, 1], y), ([1], m)),
        add(c, ([3], y), ([0], m), ([3], p)),
    )
    y, m, p = yield shuffle(a, *Y), turn(b, -1), turn(c, 1)
    yield tuple((u, v) for u, v in ((a, y), (b, m), (c, p)))


def local_small(
    layer_input, segment_ids, context_flags,
    first_gain, first_shift, sample_weight, sample_bias, sample_mixer, sample_offset,
    second_gain, second_shift, feature_weight, feature_bias, feature_mixer, feature_offset,
    third_gain, third_shift, expand_weight, expand_bias, reduce_weight, reduce_bias, cotangent,
):
    samp, feat = lax.axis_index("samp"), lax.axis_index("feat")
    core, xx = feat % 2, feat // 2
    yy, zz = samp % 2, samp // 2
    flags = context_flags.reshape(8, 64)[:, 0]
    root = jnp.sum(jnp.where(flags == 1, jnp.arange(8, dtype=jnp.int32), 0))
    position = ((yy ^ (root % 2)) * 4 + (zz - root // 2 + 4) % 4).astype(jnp.int32)
    own = (position == 0).astype(jnp.int32)
    me = jnp.stack([feat, own, position, core, xx, yy, zz]).astype(jnp.int32)

    x = layer_input.reshape(1024, 512)
    x4, cot4 = layer_input.reshape(4, 256, 512), cotangent.reshape(4, 256, 512)
    tasks = segment_ids.reshape(8, 64)
    allow = (at(tasks, samp)[:, None] == at(tasks, root)[None, :]).astype(F32)
    allow = jnp.concatenate([allow] * 4, axis=1)

    steps = send_context(x, position)
    block = lambda value, d: at(value, feat ^ d)
    to_core = jnp.stack([block(x4, 1), block(cot4, 1), block(x4, 3), block(cot4, 3)])
    got, from_core = fence((next(steps), shuffle(to_core, *CORE)))
    to_x = jnp.stack([block(x4, 2), from_core[2]])
    got, x_far = fence((steps.send(got), shuffle(to_x, *X)))
    to_x = jnp.stack([block(cot4, 2), from_core[3]])
    got, cot_far, allow = fence((steps.send(got), shuffle(to_x, *X), allow))
    pieces = steps.send(got)

    heads = sds((16, 4, 16, 512))
    quarter = sds((256, 512))
    *o_blocks, o1, context, q1, k1, v1, p1 = whole(
        forward_one, "forward_one", 32,
        (quarter,) * 4
        + (sds((4, 256, 512)), sds((1024, 512)), heads, heads, heads, sds((16, 64, 512), F32)),
        [pltpu.VMEM((16, 4, 16, 512), BF)],
        me, x, *pieces, allow, row(first_gain), row(first_shift), sample_weight, row(sample_bias),
    )
    o_blocks[1:] = fence([shuffle(o_blocks[d], "feat", d) for d in range(1, 4)])

    weights = [
        sample_mixer, row(sample_offset), row(second_gain), row(second_shift), feature_weight,
        row(feature_bias), feature_mixer, row(feature_offset), row(third_gain), row(third_shift),
        expand_weight, row(expand_bias), reduce_weight, row(reduce_bias),
    ]
    flat = spec((64, 512), lambda i, m: (i, 0))
    own = spec((None, 64, 512), lambda i, m: (m[0], i, 0))
    part = lambda n: spec((None, 64, 512), lambda i, m: (n, i, 0))
    wide = lambda n: spec((256, n), lambda i, m: (i, 0))
    still = lambda shape: spec(shape, lambda i, m: (0, 0))
    (
        out0, out2, out13, g0, g1, g2, g3,
        act2, dqkv, o2, gb2, act3, gu, hidden, gb3, vec2, bias2,
    ) = pl.pallas_call(
        middle,
        grid_spec=pltpu.PrefetchScalarGridSpec(
            num_scalar_prefetch=1,
            grid=(4,),
            in_specs=[flat] * 4
            + [own, part(0), part(0), part(1), own, part(1), part(0), part(1)]
            + [
                pl.BlockSpec(w.shape, lambda i, m: (0, 0), pipeline_mode=pl.Buffered(1))
                for w in weights
            ],
            out_specs=[
                flat, flat, spec((2, 64, 512), lambda i, m: (0, i, 0)), flat, flat, flat, flat,
                wide(512), wide(1536), wide(512), wide(512), wide(512), wide(2048), wide(2048),
                wide(512), still((8, 512)), still((1, 2048)),
            ],
        ),
        out_shape=(
            quarter, quarter, sds((2, 256, 512)), quarter, quarter, quarter, quarter,
            sds((1024, 512)), sds((1024, 1536)), sds((1024, 512)), sds((1024, 512)),
            sds((1024, 512)), sds((1024, 2048)), sds((1024, 2048)), sds((1024, 512)),
            sds((8, 512), F32), sds((1, 2048), F32),
        ),
        compiler_params=params(44),
        name="middle",
    )(me, *o_blocks, x4, from_core, x_far, x_far, cot4, from_core, cot_far, cot_far, *weights)

    rk, rs = whole(
        grads_reduce, "grads_reduce", 16, (sds((8, 128, 512)), sds((8, 128, 512))),
        [pltpu.VMEM((2048, 512), BF)], me, hidden, gb3,
    )
    ek, es = whole(
        grads_expand, "grads_expand", 16, (sds((8, 2, 64, 512)), sds((8, 2, 64, 512))),
        [pltpu.VMEM((4, 512, 512), BF)], me, act3, gu,
    )
    fk, fs = whole(
        grads_feature, "grads_feature", 16, (sds((2, 8, 64, 512)), sds((2, 8, 64, 512))),
        [pltpu.VMEM((4, 512, 512), BF)], me, act2, dqkv, o2, gb2,
    )
    three = lambda a: a.reshape((2, 2, 2) + a.shape[1:])
    four = lambda a: a.reshape((2, 2, 2, 2) + a.shape[2:])
    r_chain = Chain(three(rk), three(rs), (Z, Z3, Y))
    e_chain = Chain(three(ek), three(es), (Y, Z, Z3))
    f_chain = Chain(four(fk), four(fs), (X, Y, Z, Z3))
    g1, g2, g3 = together(
        [r_chain, e_chain, f_chain],
        lambda: [shuffle(g, "feat", d) for d, g in ((1, g1), (2, g2), (3, g3))],
    )

    half_of = lambda a, i: (a, (8,) + a.shape[1:], (i,) + (0,) * (a.ndim - 1))
    half_heads = sds((8, 4, 16, 512))
    gb1, go, dqa, dkva = together(
        [r_chain, e_chain, f_chain],
        lambda: whole(
            backward_first, "backward_first", 24,
            (sds((4, 256, 512)), heads, half_heads, sds((8, 4, 16, 1024))), [],
            me, g0, g1, g2, g3, *(half_of(a, 0) for a in (q1, k1, v1, p1)), sample_mixer,
        ),
    )

    third = sds((THIRD, 512))
    (ta, tb, tc, cact, dkv, dqb, vec_c), near = together(
        [r_chain, e_chain, f_chain],
        lambda: (
            whole(
                backward_second, "backward_second", 32,
                (
                    third, third, third, sds((1024, 512)), sds((1024, 1024)), half_heads,
                    sds((8, 512), F32),
                ),
                [pltpu.VMEM((8, 4, 16, 1024), BF), pltpu.VMEM((1024, 512), BF)],
                me, go, *(half_of(a, 1) for a in (q1, k1, v1, p1)), dkva, context,
                row(first_gain), row(first_shift), sample_weight,
            ),
            shuffle(out13, *CORE),
        ),
    )

    steps = sum_context(ta, tb, tc, position)

    def rest():
        base, act1, dq1, vec1 = whole(
            backward_query, "backward_query", 24,
            (sds((1024, 512), F32), sds((1024, 512)), sds((1024, 512)), sds((8, 512), F32)), [],
            me, gb1, x, dqa, dqb, vec_c, row(first_gain), row(first_shift), sample_weight,
        )
        grads = whole(
            grads_sample, "grads_sample", 16,
            (sds((2, 8, 32, 512)), sds((2, 8, 32, 512)), sds((8, 64, 512)), sds((8, 64, 512))),
            [pltpu.VMEM((4, 512, 512), BF)],
            me, act1, dq1, cact, dkv, o1, gb1,
        )
        far = shuffle(jnp.stack([out2, near[1]]), *X)
        return next(steps), base, vec1, grads, far

    got, base, vec1, (sxk, sxs, syk, sys_), far = together([r_chain, e_chain], rest)
    vectors = jnp.concatenate([vec2.reshape(-1), bias2.reshape(-1), vec1.reshape(-1)])
    vector_dims = [CORE, X, Y, Z, Z3]

    def add_vectors():
        return shuffle(vectors, *vector_dims.pop(0))

    sx_chain = Chain(four(sxk), four(sxs), (X, Y, Z, Z3))
    sy_chain = Chain(three(syk), three(sys_), (Y, Z, Z3))
    layer_output = whole(
        place, "place", 16, sds((4, 256, 512)), [], me, out0,
        (near, (None, 256, 512), (0, 0, 0)), (far, (None, 256, 512), (0, 0, 0)),
        (far, (None, 256, 512), (1, 0, 0)),
    ).reshape(64, 16, 512)
    rows_a, others = last_round([r_chain.keep, e_chain.keep])
    got, others, v, layer_output = together(
        [sx_chain, sy_chain, f_chain],
        lambda: (steps.send(got), others, add_vectors(), layer_output),
    )
    rows_a = [rows_a] + others
    vectors = vectors + v
    got, v = together(
        [sx_chain, sy_chain, f_chain], lambda: (steps.send(got), add_vectors())
    )
    vectors = vectors + v
    input_grad = whole(
        finish, "finish", 24, sds((1024, 512)), [],
        me, base, *(v for pair in steps.send(got) for v in pair), x, row(first_gain),
    ).reshape(64, 16, 512)
    v, input_grad = together([sx_chain, sy_chain], lambda: (add_vectors(), input_grad))
    vectors = vectors + v
    (v,) = together([sx_chain, sy_chain], lambda: (add_vectors(),))
    vectors = vectors + v
    (v,) = together([sx_chain], lambda: (add_vectors(),))
    vectors = vectors + v
    rows_b, others = last_round([f_chain.keep, sx_chain.keep, sy_chain.keep])
    rows_b = [rows_b] + others

    cut = lambda rows, start, count: [r[start : start + count] for r in rows]
    reduce_grad = pick_sum(cut(rows_a, 0, 128), core).reshape(256, 512)
    expand = pick_sum(cut(rows_a, 128, 128), core).reshape(4, 64, 512)
    feature = pick_join(cut(rows_b, 0, 64), core, xx)
    sx = pick_join(cut(rows_b, 64, 32), core, xx).reshape(2, 64, 512)
    sy = pick_sum(cut(rows_b, 96, 64), core)

    def vector(start, size):
        return lax.dynamic_slice_in_dim(vectors[start : start + size], samp * (size // 8), size // 8)

    gain3, shift3, gain2, shift2, off2, bias_r = (vector(i * 512, 512) for i in range(6))
    expand_b = vector(4096, 2048)
    gain1, shift1, off1 = (vector(6144 + i * 512, 512) for i in range(3))
    columns = lambda blocks: jnp.concatenate(blocks, axis=1)

    return (
        layer_output, input_grad,
        gain1, shift1, columns([sx[0], sy[0], sx[1]]), vector(6144 + 3 * 512, 1024), sy[1], off1,
        gain2, shift2, columns([feature[i] for i in range(3)]), vector(6 * 512, 1024),
        feature[3], off2,
        gain3, shift3, columns([expand[i] for i in range(4)]), expand_b,
        reduce_grad, bias_r,
    )


def spread_2(block, axis, owner):
    block = jnp.where(lax.axis_index(axis) == owner, block, jnp.zeros_like(block))
    return lax.psum(block, axis)


def layer_norm(values, gain_row, shift_row):
    center = jnp.mean(values, axis=-1, keepdims=True)
    spread = values - center
    variance = jnp.mean(spread * spread, axis=-1, keepdims=True)
    return spread * lax.rsqrt(variance + EPS) * gain_row + shift_row


def apply_weight(active, weight):
    return jnp.einsum("sfd,de->sfe", active, weight, preferred_element_type=jnp.float32)


def input_back(grad_out, weight):
    return jnp.einsum("sfe,de->sfd", grad_out, weight, preferred_element_type=jnp.float32)


def weight_grad(active, grad_out):
    return jnp.einsum("sfd,sfe->de", active, grad_out, preferred_element_type=jnp.float32)


def column_sum(values):
    return jnp.sum(values.astype(jnp.float32), axis=(0, 1))


def project(active, weight, bias_row):
    model_width = active.shape[-1]
    joined = apply_weight(active, weight)
    queries = (joined[..., :model_width] + bias_row[:model_width]).astype(jnp.bfloat16)
    key_part = joined[..., model_width : 2 * model_width].astype(jnp.bfloat16)
    value_part = (joined[..., 2 * model_width :] + bias_row[model_width:]).astype(jnp.bfloat16)
    return (queries, key_part, value_part)


def split_heads(values):
    return values.reshape(values.shape[0], values.shape[1], HEADS, HEAD_DIM)


def join_heads(values):
    return values.reshape(values.shape[0], values.shape[1], HEADS * HEAD_DIM)


def soft_weights(scores):
    top_score = jnp.max(scores, axis=-1, keepdims=True)
    raised = jnp.exp(scores - top_score)
    return raised / jnp.sum(raised, axis=-1, keepdims=True)


def feature_attend(queries, key_part, value_part):
    score_scale = HEAD_DIM ** (-0.5)
    scores = (
        jnp.einsum(
            "sfhd,sghd->shfg",
            split_heads(queries),
            split_heads(key_part),
            preferred_element_type=jnp.float32,
        )
        * score_scale
    )
    probability = soft_weights(scores)
    mixed = jnp.einsum(
        "shfg,sghd->sfhd",
        probability.astype(jnp.bfloat16),
        split_heads(value_part),
        preferred_element_type=jnp.float32,
    )
    return (join_heads(mixed).astype(jnp.bfloat16), probability)


def feature_grads(queries, key_part, value_part, probability, grad_mixed):
    score_scale = HEAD_DIM ** (-0.5)
    grad_heads = split_heads(grad_mixed)
    grad_weights = jnp.einsum(
        "sfhd,sghd->shfg", grad_heads, split_heads(value_part), preferred_element_type=jnp.float32
    )
    inner_sum = jnp.sum(probability * grad_weights, axis=-1, keepdims=True)
    grad_scores = (probability * (grad_weights - inner_sum)).astype(jnp.bfloat16)
    grad_queries = (
        jnp.einsum(
            "shfg,sghd->sfhd",
            grad_scores,
            split_heads(key_part),
            preferred_element_type=jnp.float32,
        )
        * score_scale
    )
    grad_keys = (
        jnp.einsum(
            "shfg,sfhd->sghd", grad_scores, split_heads(queries), preferred_element_type=jnp.float32
        )
        * score_scale
    )
    grad_values = jnp.einsum(
        "shfg,sfhd->sghd",
        probability.astype(jnp.bfloat16),
        grad_heads,
        preferred_element_type=jnp.float32,
    )
    return (join_heads(grad_queries), join_heads(grad_keys), join_heads(grad_values))


def local_large(
    layer_input,
    segment_ids,
    context_flags,
    first_gain,
    first_shift,
    sample_weight,
    sample_bias,
    sample_mixer,
    sample_offset,
    second_gain,
    second_shift,
    feature_weight,
    feature_bias,
    feature_mixer,
    feature_offset,
    third_gain,
    third_shift,
    expand_weight,
    expand_bias,
    reduce_weight,
    reduce_bias,
    cotangent,
):
    sample_rows = layer_input.shape[0]
    feature_rows = layer_input.shape[1]
    model_width = layer_input.shape[2]
    score_scale = HEAD_DIM ** (-0.5)
    shard_count = lax.axis_size("samp")
    context_shards = shard_count // 8
    total_context = context_shards * sample_rows
    residual_zero = layer_input.astype(jnp.float32)
    normed_one, norm_one_back = jax.vjp(layer_norm, residual_zero, first_gain, first_shift)
    active_one = normed_one.astype(jnp.bfloat16)
    queries_one, keys_one, values_one = project(active_one, sample_weight, sample_bias)
    my_index = lax.axis_index("samp")
    shard_flags = context_flags.reshape(shard_count, sample_rows)[:, 0]
    shard_rank = jnp.cumsum(shard_flags) - 1
    shard_ids = jnp.arange(shard_count, dtype=jnp.int32)
    slot_ids = jnp.arange(context_shards, dtype=jnp.int32)
    root_hits = (shard_rank[None, :] == slot_ids[:, None]) & (shard_flags[None, :] == 1)
    roots = jnp.sum(jnp.where(root_hits, shard_ids[None, :], 0), axis=1)
    context_tasks = jnp.take(segment_ids.reshape(shard_count, sample_rows), roots, axis=0).reshape(
        total_context
    )
    local_tasks = lax.dynamic_slice_in_dim(segment_ids, my_index * sample_rows, sample_rows)
    allowed = local_tasks[:, None] == context_tasks[None, :]
    is_context = shard_flags[my_index] == 1
    own_rank = jnp.maximum(shard_rank[my_index], 0)
    own_block = jnp.concatenate([keys_one, values_one], axis=-1)

    def fetch_rows(step, buffer):
        piece = spread_2(own_block, "samp", roots[step])
        return lax.dynamic_update_slice_in_dim(buffer, piece, step * sample_rows, 0)

    empty_rows = jnp.zeros((total_context, feature_rows, 2 * model_width), jnp.bfloat16)
    fetched = lax.fori_loop(0, context_shards, fetch_rows, empty_rows)
    context_keys = fetched[..., :model_width]
    context_values = fetched[..., model_width:]
    query_heads = split_heads(queries_one)
    key_heads = split_heads(context_keys)
    value_heads = split_heads(context_values)
    scores = (
        jnp.einsum("sfhd,cfhd->fhsc", query_heads, key_heads, preferred_element_type=jnp.float32)
        * score_scale
    )
    sample_prob = soft_weights(jnp.where(allowed[None, None], scores, MASKED))
    sample_weights = sample_prob.astype(jnp.bfloat16)
    mixed_one = join_heads(
        jnp.einsum(
            "fhsc,cfhd->sfhd", sample_weights, value_heads, preferred_element_type=jnp.float32
        )
    ).astype(jnp.bfloat16)
    residual_one = residual_zero + apply_weight(mixed_one, sample_mixer) + sample_offset
    normed_two, norm_two_back = jax.vjp(layer_norm, residual_one, second_gain, second_shift)
    active_two = normed_two.astype(jnp.bfloat16)
    queries_two, keys_two, values_two = project(active_two, feature_weight, feature_bias)
    all_keys, all_values = (
        lax.all_gather(keys_two, "feat", axis=1, tiled=True),
        lax.all_gather(values_two, "feat", axis=1, tiled=True),
    )
    mixed_two, feature_prob = feature_attend(queries_two, all_keys, all_values)
    residual_two = residual_one + apply_weight(mixed_two, feature_mixer) + feature_offset
    normed_three, norm_three_back = jax.vjp(layer_norm, residual_two, third_gain, third_shift)
    active_three = normed_three.astype(jnp.bfloat16)
    expanded = apply_weight(active_three, expand_weight) + expand_bias
    activated, gelu_back = jax.vjp(partial(jax.nn.gelu, approximate=False), expanded)
    hidden = activated.astype(jnp.bfloat16)
    layer_output = (residual_two + apply_weight(hidden, reduce_weight) + reduce_bias).astype(
        jnp.bfloat16
    )
    grad_out = cotangent.astype(jnp.float32)
    grad_branch = cotangent
    reduce_bias_grad = column_sum(grad_branch)
    reduce_weight_grad = weight_grad(hidden, grad_branch)
    grad_hidden = input_back(grad_branch, reduce_weight).astype(jnp.bfloat16)
    grad_expanded = gelu_back(grad_hidden.astype(jnp.float32))[0].astype(jnp.bfloat16)
    expand_bias_grad = column_sum(grad_expanded)
    expand_weight_grad = weight_grad(active_three, grad_expanded)
    grad_norm, third_gain_grad, third_shift_grad = norm_three_back(
        input_back(grad_expanded, expand_weight)
    )
    grad_two = grad_out + grad_norm
    grad_branch = grad_two.astype(jnp.bfloat16)
    feature_offset_grad = column_sum(grad_branch)
    feature_mixer_grad = weight_grad(mixed_two, grad_branch)
    grad_mixed = input_back(grad_branch, feature_mixer).astype(jnp.bfloat16)
    grad_queries, grad_keys, grad_values = feature_grads(
        queries_two, all_keys, all_values, feature_prob, grad_mixed
    )
    own_key_grads, own_value_grads = (
        lax.psum_scatter(grad_keys, "feat", scatter_dimension=1, tiled=True),
        lax.psum_scatter(grad_values, "feat", scatter_dimension=1, tiled=True),
    )
    grad_project = jnp.concatenate(
        [
            grad_queries.astype(jnp.bfloat16),
            own_key_grads.astype(jnp.bfloat16),
            own_value_grads.astype(jnp.bfloat16),
        ],
        axis=-1,
    )
    feature_weight_grad = weight_grad(active_two, grad_project)
    feature_bias_grad = jnp.concatenate(
        [
            column_sum(grad_project[..., :model_width]),
            column_sum(grad_project[..., 2 * model_width :]),
        ]
    )
    grad_norm, second_gain_grad, second_shift_grad = norm_two_back(
        input_back(grad_project, feature_weight)
    )
    grad_one = grad_two + grad_norm
    grad_branch = grad_one.astype(jnp.bfloat16)
    sample_offset_grad = column_sum(grad_branch)
    sample_mixer_grad = weight_grad(mixed_one, grad_branch)
    grad_heads = split_heads(input_back(grad_branch, sample_mixer).astype(jnp.bfloat16))
    grad_weights = jnp.einsum(
        "sfhd,cfhd->fhsc", grad_heads, value_heads, preferred_element_type=jnp.float32
    )
    inner_sum = jnp.sum(sample_prob * grad_weights, axis=-1, keepdims=True)
    grad_scores = (sample_prob * (grad_weights - inner_sum)).astype(jnp.bfloat16)
    grad_queries = (
        join_heads(
            jnp.einsum(
                "fhsc,cfhd->sfhd", grad_scores, key_heads, preferred_element_type=jnp.float32
            )
        )
        * score_scale
    ).astype(jnp.bfloat16)
    key_terms = (
        join_heads(
            jnp.einsum(
                "fhsc,sfhd->cfhd", grad_scores, query_heads, preferred_element_type=jnp.float32
            )
        )
        * score_scale
    )
    value_terms = join_heads(
        jnp.einsum(
            "fhsc,sfhd->cfhd", sample_weights, grad_heads, preferred_element_type=jnp.float32
        )
    )
    term_block = jnp.concatenate([key_terms, value_terms], axis=-1)
    summed_terms = lax.psum_scatter(term_block, "samp", scatter_dimension=0, tiled=True)
    summed_rows = lax.all_gather(summed_terms.astype(jnp.bfloat16), "samp", axis=0, tiled=True)
    own_grads = lax.dynamic_slice_in_dim(summed_rows, own_rank * sample_rows, sample_rows, 0)
    own_grads = jnp.where(is_context, own_grads, jnp.zeros_like(own_grads))
    grad_project = jnp.concatenate([grad_queries, own_grads], axis=-1)
    sample_weight_grad = weight_grad(active_one, grad_project)
    sample_bias_grad = jnp.concatenate(
        [column_sum(grad_queries), column_sum(own_grads[..., model_width:])]
    )
    grad_norm, first_gain_grad, first_shift_grad = norm_one_back(
        input_back(grad_project, sample_weight)
    )
    input_grad = (grad_one + grad_norm).astype(jnp.bfloat16)
    summed = lax.psum(
        (
            first_gain_grad,
            first_shift_grad,
            sample_weight_grad,
            sample_bias_grad,
            sample_mixer_grad,
            sample_offset_grad,
            second_gain_grad,
            second_shift_grad,
            feature_weight_grad,
            feature_bias_grad,
            feature_mixer_grad,
            feature_offset_grad,
            third_gain_grad,
            third_shift_grad,
            expand_weight_grad,
            expand_bias_grad,
            reduce_weight_grad,
            reduce_bias_grad,
        ),
        "feat",
    )
    shares = (
        lax.psum_scatter(summed[0], "samp", scatter_dimension=0, tiled=True),
        lax.psum_scatter(summed[1], "samp", scatter_dimension=0, tiled=True),
        lax.psum_scatter(summed[2], "samp", scatter_dimension=0, tiled=True),
        lax.psum_scatter(summed[3], "samp", scatter_dimension=0, tiled=True),
        lax.psum_scatter(summed[4], "samp", scatter_dimension=0, tiled=True),
        lax.psum_scatter(summed[5], "samp", scatter_dimension=0, tiled=True),
        lax.psum_scatter(summed[6], "samp", scatter_dimension=0, tiled=True),
        lax.psum_scatter(summed[7], "samp", scatter_dimension=0, tiled=True),
        lax.psum_scatter(summed[8], "samp", scatter_dimension=0, tiled=True),
        lax.psum_scatter(summed[9], "samp", scatter_dimension=0, tiled=True),
        lax.psum_scatter(summed[10], "samp", scatter_dimension=0, tiled=True),
        lax.psum_scatter(summed[11], "samp", scatter_dimension=0, tiled=True),
        lax.psum_scatter(summed[12], "samp", scatter_dimension=0, tiled=True),
        lax.psum_scatter(summed[13], "samp", scatter_dimension=0, tiled=True),
        lax.psum_scatter(summed[14], "samp", scatter_dimension=0, tiled=True),
        lax.psum_scatter(summed[15], "samp", scatter_dimension=0, tiled=True),
        lax.psum_scatter(summed[16], "samp", scatter_dimension=0, tiled=True),
        lax.psum_scatter(summed[17], "samp", scatter_dimension=0, tiled=True),
    )
    return (
        layer_output,
        input_grad,
        shares[0],
        shares[1],
        shares[2],
        shares[3],
        shares[4],
        shares[5],
        shares[6],
        shares[7],
        shares[8],
        shares[9],
        shares[10],
        shares[11],
        shares[12],
        shares[13],
        shares[14],
        shares[15],
        shares[16],
        shares[17],
    )


def solution(mesh):
    small = mesh.shape["samp"] == 8 and mesh.shape["feat"] == 4
    return jax.shard_map(
        local_small if small else local_large,
        mesh=mesh,
        in_specs=(
            P("samp", "feat", None),
            P(),
            P(),
            P(),
            P(),
            P(),
            P(),
            P(),
            P(),
            P(),
            P(),
            P(),
            P(),
            P(),
            P(),
            P(),
            P(),
            P(),
            P(),
            P(),
            P(),
            P("samp", "feat", None),
        ),
        out_specs=(
            P("samp", "feat", None),
            P("samp", "feat", None),
            P("samp"),
            P("samp"),
            P("samp", None),
            P("samp"),
            P("samp", None),
            P("samp"),
            P("samp"),
            P("samp"),
            P("samp", None),
            P("samp"),
            P("samp", None),
            P("samp"),
            P("samp"),
            P("samp"),
            P("samp", None),
            P("samp"),
            P("samp", None),
            P("samp"),
        ),
        check_vma=False,
    )
```

```python
from functools import partial

import jax
import jax.numpy as jnp
from jax import lax
from jax.experimental import pallas as pl
from jax.experimental.pallas import tpu as pltpu
from jax.sharding import PartitionSpec as P

HEADS = 8
HEAD_DIM = 64
EPS = 1e-05
MASKED = -1000000000.0
SCALE = HEAD_DIM ** (-0.5)
QUAD = 4 * HEAD_DIM
BF = jnp.bfloat16
F32 = jnp.float32


def mm(a, b, ca=1, cb=0):
    return lax.dot_general(a, b, (((ca,), (cb,)), ((), ())), preferred_element_type=F32)


def norm_parts(values):
    center = jnp.mean(values, axis=-1, keepdims=True)
    spread = values - center
    variance = jnp.mean(spread * spread, axis=-1, keepdims=True)
    inverse = lax.rsqrt(variance + EPS)
    return spread * inverse, inverse


def norm_back(grad, unit, inverse, gain):
    scaled = grad * gain
    first = jnp.mean(scaled, axis=-1, keepdims=True)
    second = jnp.mean(scaled * unit, axis=-1, keepdims=True)
    return (scaled - first - unit * second) * inverse


def lane_ids(rows):
    return lax.broadcasted_iota(jnp.int32, (rows, 128), 1)


def group_reduce(values, op, fill):
    rows = values.shape[0]
    low = lane_ids(rows) < HEAD_DIM
    outs = []
    for t in range(values.shape[1] // 128):
        tile = values[:, t * 128 : (t + 1) * 128]
        left = op(jnp.where(low, tile, fill), axis=1, keepdims=True)
        right = op(jnp.where(low, fill, tile), axis=1, keepdims=True)
        outs.append(jnp.where(low, left, right))
    return jnp.concatenate(outs, axis=1)


def head_masks(dtype):
    lanes = lax.broadcasted_iota(jnp.int32, (1, QUAD), 1) // HEAD_DIM
    return [jnp.where(lanes == h, 1.0, 0.0).astype(dtype) for h in range(4)]


def stack_heads(part, masks):
    return jnp.concatenate([part * m for m in masks], axis=0)


def pick_heads(stacked, masks):
    rows = stacked.shape[0] // 4
    total = stacked[:rows] * masks[0]
    for h in range(1, 4):
        total = total + stacked[h * rows : (h + 1) * rows] * masks[h]
    return total


def attend(q, k, v, masks, allow):
    outs, probs = [], []
    for quad in range(2):
        cols = slice(quad * QUAD, (quad + 1) * QUAD)
        scores = mm(q[:, cols], stack_heads(k[:, cols], masks), 1, 1)
        if allow is not None:
            scores = jnp.where(allow, scores, MASKED)
        raised = jnp.exp(scores - group_reduce(scores, jnp.max, -jnp.inf))
        prob = raised / group_reduce(raised, jnp.sum, 0.0)
        outs.append(mm(prob.astype(BF), stack_heads(v[:, cols], masks)))
        probs.append(prob)
    return jnp.concatenate(outs, axis=1), jnp.concatenate(probs, axis=1)


def attend_back(q, k, v, prob, grad, masks, masks32):
    dqs, dks, dvs = [], [], []
    for quad in range(2):
        cols = slice(quad * QUAD, (quad + 1) * QUAD)
        p, g = prob[:, cols], grad[:, cols]
        back = mm(g, stack_heads(v[:, cols], masks), 1, 1)
        inner = group_reduce(p * back, jnp.sum, 0.0)
        gs = (p * (back - inner)).astype(BF)
        dqs.append(mm(gs, stack_heads(k[:, cols], masks)) * SCALE)
        dks.append(pick_heads(mm(gs, q[:, cols], 0, 0), masks32))
        dvs.append(pick_heads(mm(p.astype(BF), g, 0, 0), masks32))
    join = lambda parts: jnp.concatenate(parts, axis=1).astype(BF)
    return join(dqs), join(dks), join(dvs)


def swap_matrix(n):
    r = lax.broadcasted_iota(jnp.int32, (n, n), 0)
    c = lax.broadcasted_iota(jnp.int32, (n, n), 1)
    return jnp.where((r // 16 == c % 16) & (r % 16 == c // 16), 1.0, 0.0).astype(BF)


def swap(matrix, values):
    return mm(matrix, values).astype(BF)


def gelu_parts(u):
    cdf = 0.5 * (1.0 + lax.erf(u * (2.0**-0.5)))
    density = jnp.exp(u * u * -0.5) * 0.3989422804014327
    return cdf, density


def col_sum(values):
    return jnp.sum(values.astype(F32), axis=0, keepdims=True)


def turn_in(me_ref, x_ref, out_ref):
    matrix = swap_matrix(256)
    for d in range(4):
        rows = x_ref[d * 256 : (d + 1) * 256]
        out_ref[:, d] = swap(matrix, rows).reshape(16, 16, 512)


def turn_out(me_ref, got_ref, out_ref):
    matrix = swap_matrix(256)
    for d in range(4):
        out_ref[d * 256 : (d + 1) * 256] = swap(matrix, got_ref[:, d].reshape(256, 512))


def forward_one(
    me_ref, x_ref, own_ref, context_ref, gain_ref, shift_ref, w_ref, b_ref,
    o_ref, q_ref, k_ref, v_ref, p_ref,
):
    root = me_ref[1]
    gain, shift = gain_ref[...], shift_ref[...]
    masks = head_masks(BF)
    allow = own_ref[...] == context_ref[...]
    for e in range(2):
        unit, _ = norm_parts(x_ref[:, e].reshape(512, 512).astype(F32))
        act = (unit * gain + shift).astype(BF)
        q = (mm(act, w_ref[:, :512]) + b_ref[:, :512]).astype(BF) * jnp.asarray(SCALE, BF)
        unit, _ = norm_parts(x_ref[root, e].astype(F32))
        kv = mm((unit * gain + shift).astype(BF), w_ref[:, 512:])
        k = kv[:, :512].astype(BF)
        v = (kv[:, 512:] + b_ref[:, 512:]).astype(BF)
        out, prob = attend(q, k, v, masks, allow)
        o_ref[:, :, e] = out.astype(BF).reshape(8, 4, 16, 512)
        q_ref[e], k_ref[e], v_ref[e], p_ref[e] = q, k, v, prob


def middle(
    me_ref, o1_ref, x0, x1, x2, x3, c0, c1, c2, c3,
    wm1_ref, off1_ref, g2_ref, s2_ref, wf_ref, bf_ref, wm2_ref, off2_ref,
    g3_ref, s3_ref, we_ref, be_ref, wr_ref, br_ref,
    out0, out2, out13, gb1_ref,
    a2_ref, dqkv_ref, o2_ref, gb2_ref, a3_ref, gu_ref, hid_ref, gb3_ref, vec_ref, bias_ref,
    o_scr, g_scr,
):
    samples = 4
    me, step = me_ref[0], pl.program_id(0)
    matrix = swap_matrix(256)
    now = pl.ds(pl.multiple_of(step * 64, 64), 64)

    @pl.when(step == 0)
    def _():
        for f in range(4):
            o_scr[f] = swap(matrix, o1_ref[:, f].reshape(256, 512))

    def gather(*refs):
        return jnp.concatenate(
            [ref[s * 16 : (s + 1) * 16] for s in range(samples) for ref in refs], axis=0
        )

    def scatter(values, *refs):
        for s in range(samples):
            for d, ref in enumerate(refs):
                at = (s * 4 + d) * 16
                ref[s * 16 : (s + 1) * 16] = values[at : at + 16]

    masks, masks32 = head_masks(BF), head_masks(F32)
    attended = gather(*(o_scr[d ^ me, now] for d in range(4)))
    cot = gather(c0, c1, c2, c3)
    gb3_ref[...] = cot
    r1 = gather(x0, x1, x2, x3).astype(F32) + mm(attended, wm1_ref[...]) + off1_ref[...]
    unit2, inv2 = norm_parts(r1)
    act2 = (unit2 * g2_ref[...] + s2_ref[...]).astype(BF)
    a2_ref[...] = act2
    qkv = mm(act2, wf_ref[...])
    q = (qkv[:, :512] + bf_ref[:, :512]).astype(BF) * jnp.asarray(SCALE, BF)
    k = qkv[:, 512:1024].astype(BF)
    v = (qkv[:, 1024:] + bf_ref[:, 512:]).astype(BF)
    parts = []
    for s in range(samples):
        rows = slice(s * 64, (s + 1) * 64)
        parts.append(attend(q[rows], k[rows], v[rows], masks, None))
    o2 = jnp.concatenate([part[0] for part in parts], axis=0).astype(BF)
    o2_ref[...] = o2
    r2 = r1 + mm(o2, wm2_ref[...]) + off2_ref[...]
    unit3, inv3 = norm_parts(r2)
    act3 = (unit3 * g3_ref[...] + s3_ref[...]).astype(BF)
    a3_ref[...] = act3
    out = r2 + br_ref[...]
    back = None
    bias = []
    for b in range(4):
        cols = slice(b * 512, (b + 1) * 512)
        u = mm(act3, we_ref[:, cols]) + be_ref[:, cols]
        cdf, density = gelu_parts(u)
        hidden = (u * cdf).astype(BF)
        hid_ref[:, cols] = hidden
        out = out + mm(hidden, wr_ref[cols, :])
        gh = mm(cot, wr_ref[cols, :], 1, 1).astype(BF).astype(F32)
        gu = (gh * (cdf + u * density)).astype(BF)
        gu_ref[:, cols] = gu
        bias.append(col_sum(gu))
        term = mm(gu, we_ref[:, cols], 1, 1)
        back = term if back is None else back + term
    scatter(out.astype(BF), out0, out13.at[0], out2, out13.at[1])
    vecs = [col_sum(back * unit3), col_sum(back)]
    gr2 = cot.astype(F32) + norm_back(back, unit3, inv3, g3_ref[...])
    gb2 = gr2.astype(BF)
    gb2_ref[...] = gb2
    go2 = mm(gb2, wm2_ref[...], 1, 1).astype(BF)
    grads = []
    for s in range(samples):
        rows = slice(s * 64, (s + 1) * 64)
        grads.append(
            jnp.concatenate(
                attend_back(q[rows], k[rows], v[rows], parts[s][1], go2[rows], masks, masks32),
                axis=1,
            )
        )
    dqkv = jnp.concatenate(grads, axis=0)
    dqkv_ref[...] = dqkv
    back = mm(dqkv, wf_ref[...], 1, 1)
    vecs += [col_sum(back * unit2), col_sum(back)]
    gr1 = gr2 + norm_back(back, unit2, inv2, g2_ref[...])
    scatter(gr1.astype(BF), *(g_scr.at[d ^ me, now] for d in range(4)))

    @pl.when(step == 3)
    def _():
        for f in range(4):
            gb1_ref[:, f] = swap(matrix, g_scr[f]).reshape(8, 2, 16, 512)

    vecs += [col_sum(gb2), col_sum(cot), col_sum(dqkv[:, :512]), col_sum(dqkv[:, 1024:])]

    @pl.when(step == 0)
    def _():
        vec_ref[...] = jnp.zeros_like(vec_ref)
        bias_ref[...] = jnp.zeros_like(bias_ref)

    vec_ref[...] += jnp.concatenate(vecs, axis=0)
    bias_ref[...] += jnp.concatenate(bias, axis=1)


def backward_one(
    me_ref, gb1_ref, x_ref, q_ref, k_ref, v_ref, p_ref, gain_ref, shift_ref, w_ref, wm_ref,
    grad_ref, act_ref, dq_ref, cact_ref, dkv_ref, vec_ref,
    a_scr,
):
    root = me_ref[1]
    gain, shift = gain_ref[...], shift_ref[...]
    masks, masks32 = head_masks(BF), head_masks(F32)
    zero = jnp.zeros((1, 512), F32)
    gain_sum, shift_sum, off_sum, q_sum, v_sum = (zero,) * 5
    for e in range(2):
        gb1 = gb1_ref[:, :, e].reshape(512, 512)
        go = mm(gb1, wm_ref[...], 1, 1).astype(BF)
        dq, dk, dv = attend_back(q_ref[e], k_ref[e], v_ref[e], p_ref[e], go, masks, masks32)
        dq_ref[e], dkv_ref[e, :, :512], dkv_ref[e, :, 512:] = dq, dk, dv
        a_scr[...] = mm(dq, w_ref[:, :512], 1, 1).reshape(8, 64, 512)
        a_scr[root] += mm(dkv_ref[e], w_ref[:, 512:], 1, 1)
        back = a_scr[...].reshape(512, 512)
        unit, inverse = norm_parts(x_ref[:, e].reshape(512, 512).astype(F32))
        act_ref[e] = (unit * gain + shift).astype(BF)
        grad = gb1.astype(F32) + norm_back(back, unit, inverse, gain)
        grad_ref[:, e] = grad.astype(BF).reshape(8, 64, 512)
        cact_ref[e] = act_ref[e, pl.ds(pl.multiple_of(root * 64, 64), 64)]
        gain_sum += col_sum(back * unit)
        shift_sum += col_sum(back)
        off_sum += col_sum(gb1)
        q_sum += col_sum(dq)
        v_sum += col_sum(dv)
    vec_ref[...] = jnp.concatenate(
        [gain_sum, shift_sum, off_sum, q_sum, v_sum, zero, zero, zero], axis=0
    )


def place(me_ref, b0, b1, b2, b3, out_ref):
    for d, ref in enumerate((b0, b1, b2, b3)):
        out_ref[d ^ me_ref[0]] = ref[...]


def lay_out(me_ref, read, order, *pairs):
    core, xx, yy, zz = me_ref[2], me_ref[3], me_ref[4], me_ref[5]
    for bits in range(16):
        index = tuple((bits >> i) & 1 for i in (3, 2, 1, 0))
        dx, dy, d1, d2 = (index[order.index(name)] for name in ("x", "y", "z", "w"))
        shard = (zz ^ d1 ^ (2 * d2)) * 2 + (yy ^ dy)
        for keep_ref, send_ref, start, rows in pairs:
            keep_ref[index] = read(2 * core + (dx ^ xx), shard, start, rows)
            send_ref[index] = read(2 * (1 - core) + (dx ^ xx), shard, start, rows)


def read_units(scr):
    def read(unit, shard, start, rows):
        return scr[unit, pl.ds(pl.multiple_of(shard * 64 + start, rows), rows)]

    return read


def grads_reduce(me_ref, hid_ref, gb3_ref, keep_ref, send_ref, scr):
    for i in range(8):
        cols = slice(i * 256, (i + 1) * 256)
        scr[cols] = mm(hid_ref[:, cols], gb3_ref[...], 0, 0).astype(BF)

    def read(unit, shard, start, rows):
        return scr[pl.ds(pl.multiple_of(shard * 256 + unit * 64, 64), 64)]

    lay_out(me_ref, read, "zxyw", (keep_ref, send_ref, 0, 64))


def grads_expand(me_ref, act_ref, gu_ref, keep_ref, send_ref, scr):
    for n in range(4):
        scr[n] = mm(act_ref[...], gu_ref[:, n * 512 : (n + 1) * 512], 0, 0).astype(BF)
    lay_out(me_ref, read_units(scr), "yxzw", (keep_ref, send_ref, 0, 64))


def grads_feature(me_ref, act_ref, dqkv_ref, o_ref, gb_ref, keep_ref, send_ref, scr):
    for n in range(3):
        scr[n] = mm(act_ref[...], dqkv_ref[:, n * 512 : (n + 1) * 512], 0, 0).astype(BF)
    scr[3] = mm(o_ref[...], gb_ref[...], 0, 0).astype(BF)
    lay_out(me_ref, read_units(scr), "xyzw", (keep_ref, send_ref, 0, 64))


def grads_sample(
    me_ref, act_ref, dq_ref, cact_ref, dkv_ref, o_ref, gb1_ref,
    keepa_ref, senda_ref, keepb_ref, sendb_ref, scr,
):
    scr[0] = mm(act_ref[...], dq_ref[...], 0, 0).astype(BF)
    scr[1] = mm(cact_ref[...], dkv_ref[:, :512], 0, 0).astype(BF)
    scr[2] = mm(cact_ref[...], dkv_ref[:, 512:], 0, 0).astype(BF)
    scr[3] = mm(o_ref[...], gb1_ref[...], 0, 0).astype(BF)
    lay_out(me_ref, read_units(scr), "xyzw", (keepa_ref, senda_ref, 0, 32))
    lay_out(me_ref, read_units(scr), "yxzw", (keepb_ref, sendb_ref, 32, 32))


def spec(shape, index=None):
    return pl.BlockSpec(shape, index if index is not None else (lambda *a: (0,) * len(shape)))


def sds(shape, dtype=BF):
    return jax.ShapeDtypeStruct(shape, dtype)


def params(limit):
    return pltpu.CompilerParams(vmem_limit_bytes=limit << 20)


def row(vector):
    return vector.reshape(1, -1)


def whole(kernel, name, limit, outs, scratch, *inputs):
    arrays, specs = [inputs[0]], [pl.BlockSpec(memory_space=pltpu.SMEM)]
    for entry in inputs[1:]:
        array, block, index = entry if isinstance(entry, tuple) else (entry, None, None)
        arrays.append(array)
        block = array.shape if block is None else block
        index = (0,) * array.ndim if index is None else index
        specs.append(pl.BlockSpec(block, lambda i, index=index: index))
    single = not isinstance(outs, tuple)
    return pl.pallas_call(
        kernel,
        grid=(1,),
        out_shape=outs,
        in_specs=specs,
        out_specs=jax.tree.map(lambda o: pl.BlockSpec(o.shape, lambda i: (0,) * len(o.shape)), outs),
        scratch_shapes=scratch,
        compiler_params=params(limit),
        name=name,
    )(*arrays)


def shuffle(value, axis, mask):
    size = lax.axis_size(axis)
    return lax.ppermute(value, axis, [(i, i ^ mask) for i in range(size)])


CORE, X, Y, Z, W = ("feat", 1), ("feat", 2), ("samp", 1), ("samp", 2), ("samp", 4)


def at(stacked, index, axis=0):
    return lax.dynamic_index_in_dim(stacked, index, axis, keepdims=False)


def fence(tree):
    return lax.optimization_barrier(tree)


def plus(a, b):
    return (a.astype(F32) + b.astype(F32)).astype(BF)


class Chain:
    def __init__(self, keep, sent, dims):
        self.keep, self.sent, self.dims = keep, sent, (CORE,) + dims

    def start(self):
        return shuffle(self.sent, *self.dims[0])

    def take(self, got):
        self.dims = self.dims[1:]
        if self.dims:
            self.keep, self.sent = plus(self.keep[0], got[0]), plus(self.keep[1], got[1])
        else:
            self.keep = plus(self.keep, got)


def together(chains, make=lambda: ()):
    got = [chain.start() for chain in chains]
    got, other = fence((got, make()))
    for chain, value in zip(chains, got):
        chain.take(value)
    return other


def last_round(parts):
    joined = jnp.concatenate([part.reshape(-1, 512) for part in parts], axis=0)
    return joined, [shuffle(joined, "feat", mask) for mask in (1, 2, 3)]


def pick_join(rows, core, xx):
    place = core * 2 + xx
    outs = []
    for target in range(4):
        value = rows[0]
        for mask, index in ((1, 2), (2, 1), (3, 3)):
            value = jnp.where((place ^ target) == index, rows[mask], value)
        outs.append(value.astype(F32))
    return jnp.stack(outs)


def local_small(
    layer_input, segment_ids, context_flags,
    first_gain, first_shift, sample_weight, sample_bias, sample_mixer, sample_offset,
    second_gain, second_shift, feature_weight, feature_bias, feature_mixer, feature_offset,
    third_gain, third_shift, expand_weight, expand_bias, reduce_weight, reduce_bias, cotangent,
):
    samp, feat = lax.axis_index("samp"), lax.axis_index("feat")
    core, xx = feat % 2, feat // 2
    flags = context_flags.reshape(8, 64)[:, 0]
    root = jnp.sum(jnp.where(flags == 1, jnp.arange(8, dtype=jnp.int32), 0))
    me = jnp.stack([feat, root, core, xx, samp % 2, samp // 2]).astype(jnp.int32)

    turned = whole(
        turn_in, "turn_in", 8, sds((16, 4, 16, 512)), [], me, layer_input.reshape(1024, 512)
    )
    x_t = lax.all_to_all(turned.reshape(8, 2, 64, 512), "samp", 0, 0)
    x4, cot4 = layer_input.reshape(4, 256, 512), cotangent.reshape(4, 256, 512)
    block = lambda value, d: at(value, feat ^ d)
    to_core = jnp.stack([block(x4, 1), block(cot4, 1), block(x4, 3), block(cot4, 3)])
    from_core = shuffle(to_core, *CORE)
    x_far = shuffle(jnp.stack([block(x4, 2), from_core[2]]), *X)
    cot_far = shuffle(jnp.stack([block(cot4, 2), from_core[3]]), *X)
    x_t, from_core, x_far, cot_far = fence((x_t, from_core, x_far, cot_far))

    tasks = segment_ids.reshape(8, 64)
    context_tasks = jnp.concatenate([at(tasks, root)] * 4).reshape(1, 256)
    half = sds((2, 512, 512))
    o1, q1, k1, v1, p1 = whole(
        forward_one, "forward_one", 24,
        (sds((8, 4, 2, 16, 512)), half, sds((2, 64, 512)), sds((2, 64, 512)), sds((2, 512, 512), F32)),
        [],
        me, x_t, segment_ids.reshape(512, 1), context_tasks, row(first_gain), row(first_shift),
        sample_weight, row(sample_bias),
    )
    both = ("samp", "feat")
    o1_f = lax.all_to_all(o1.reshape(32, 2, 16, 512), both, 0, 0).reshape(8, 4, 2, 16, 512)

    weights = [
        sample_mixer, row(sample_offset), row(second_gain), row(second_shift), feature_weight,
        row(feature_bias), feature_mixer, row(feature_offset), row(third_gain), row(third_shift),
        expand_weight, row(expand_bias), reduce_weight, row(reduce_bias),
    ]
    flat = spec((64, 512), lambda i, m: (i, 0))
    own = spec((None, 64, 512), lambda i, m: (m[0], i, 0))
    part = lambda n: spec((None, 64, 512), lambda i, m: (n, i, 0))
    wide = lambda n: spec((256, n), lambda i, m: (i, 0))
    still = lambda shape: spec(shape, lambda i, m: (0,) * len(shape))
    quarter = sds((256, 512))
    (
        out0, out2, out13, gb1_f,
        act2, dqkv, o2, gb2, act3, gu, hidden, gb3, vec2, bias2,
    ) = pl.pallas_call(
        middle,
        grid_spec=pltpu.PrefetchScalarGridSpec(
            num_scalar_prefetch=1,
            grid=(4,),
            in_specs=[still((8, 4, 2, 16, 512))]
            + [own, part(0), part(0), part(1), own, part(1), part(0), part(1)]
            + [
                pl.BlockSpec(w.shape, lambda i, m: (0, 0), pipeline_mode=pl.Buffered(1))
                for w in weights
            ],
            out_specs=[
                flat, flat, spec((2, 64, 512), lambda i, m: (0, i, 0)), still((8, 4, 2, 16, 512)),
                wide(512), wide(1536), wide(512), wide(512), wide(512), wide(2048), wide(2048),
                wide(512), still((8, 512)), still((1, 2048)),
            ],
            scratch_shapes=[pltpu.VMEM((4, 256, 512), BF), pltpu.VMEM((4, 256, 512), BF)],
        ),
        out_shape=(
            quarter, quarter, sds((2, 256, 512)), sds((8, 4, 2, 16, 512)),
            sds((1024, 512)), sds((1024, 1536)), sds((1024, 512)), sds((1024, 512)),
            sds((1024, 512)), sds((1024, 2048)), sds((1024, 2048)), sds((1024, 512)),
            sds((8, 512), F32), sds((1, 2048), F32),
        ),
        compiler_params=params(44),
        name="middle",
    )(me, o1_f, x4, from_core, x_far, x_far, cot4, from_core, cot_far, cot_far, *weights)

    gb1 = lax.all_to_all(gb1_f.reshape(32, 2, 16, 512), both, 0, 0).reshape(8, 4, 2, 16, 512)
    parts = sds((2, 2, 2, 2, 64, 512))
    rk, rs = whole(
        grads_reduce, "grads_reduce", 16, (parts, parts), [pltpu.VMEM((2048, 512), BF)],
        me, hidden, gb3,
    )
    units = [pltpu.VMEM((4, 512, 512), BF)]
    ek, es = whole(grads_expand, "grads_expand", 16, (parts, parts), units, me, act3, gu)
    fk, fs = whole(
        grads_feature, "grads_feature", 16, (parts, parts), units, me, act2, dqkv, o2, gb2
    )
    r_chain = Chain(rk, rs, (Z, X, Y, W))
    e_chain = Chain(ek, es, (Y, X, Z, W))
    f_chain = Chain(fk, fs, (X, Y, Z, W))
    chains = [r_chain, e_chain, f_chain]
    together(chains)
    gb1, near = together(chains, lambda: (gb1, shuffle(out13, *CORE)))

    grad_t, act1, dq1, cact, dkv, vec1 = together(
        chains,
        lambda: whole(
            backward_one, "backward_one", 32,
            (sds((8, 2, 64, 512)), half, half, sds((2, 64, 512)), sds((2, 64, 1024)), sds((8, 512), F32)),
            [pltpu.VMEM((8, 64, 512), F32)],
            me, gb1, x_t, q1, k1, v1, p1, row(first_gain), row(first_shift), sample_weight,
            sample_mixer,
        ),
    )
    got = lax.all_to_all(grad_t, "samp", 0, 0)

    small = sds((2, 2, 2, 2, 32, 512))
    flat2 = lambda a: a.reshape(-1, a.shape[-1])
    ak, as_, bk, bs = whole(
        grads_sample, "grads_sample", 16, (small,) * 4, units,
        me, flat2(act1), flat2(dq1), flat2(cact), flat2(dkv), flat2(o1), flat2(gb1),
    )
    far = shuffle(jnp.stack([out2, near[1]]), *X)
    vectors = jnp.concatenate([vec2.reshape(-1), bias2.reshape(-1), vec1.reshape(-1)])
    vector_dims = [CORE, X, Y, Z, W]

    def add_vectors():
        return shuffle(vectors, *vector_dims.pop(0))

    samples = [Chain(ak, as_, (X, Y, Z, W)), Chain(bk, bs, (Y, X, Z, W))]
    far, v = together(samples + chains, lambda: (far, add_vectors()))
    vectors = vectors + v
    layer_output = whole(
        place, "place", 16, sds((4, 256, 512)), [], me, out0,
        (near, (None, 256, 512), (0, 0, 0)), (far, (None, 256, 512), (0, 0, 0)),
        (far, (None, 256, 512), (1, 0, 0)),
    ).reshape(64, 16, 512)
    v, layer_output = together(samples + chains, lambda: (add_vectors(), layer_output))
    vectors = vectors + v
    rows_a, others = last_round([chain.keep for chain in chains])
    v, others = together(samples, lambda: (add_vectors(), others))
    rows_a = [rows_a] + others
    vectors = vectors + v
    (v,) = together(samples, lambda: (add_vectors(),))
    vectors = vectors + v
    v, got = together(samples, lambda: (add_vectors(), got))
    vectors = vectors + v
    rows_b, others = last_round([chain.keep for chain in samples])
    input_grad = whole(
        turn_out, "turn_out", 8, sds((1024, 512)), [], me, got.reshape(16, 4, 16, 512)
    ).reshape(64, 16, 512)
    others, input_grad = fence((others, input_grad))
    rows_b = [rows_b] + others

    cut = lambda rows, start, count: [r[start : start + count] for r in rows]
    reduce_grad = pick_join(cut(rows_a, 0, 64), core, xx).reshape(256, 512)
    expand = pick_join(cut(rows_a, 64, 64), core, xx)
    feature = pick_join(cut(rows_a, 128, 64), core, xx)
    sample = jnp.concatenate(
        [pick_join(cut(rows_b, start, 32), core, xx) for start in (0, 32)], axis=1
    )

    def vector(start, size):
        return lax.dynamic_slice_in_dim(vectors[start : start + size], samp * (size // 8), size // 8)

    gain3, shift3, gain2, shift2, off2, bias_r = (vector(i * 512, 512) for i in range(6))
    expand_b = vector(4096, 2048)
    gain1, shift1, off1 = (vector(6144 + i * 512, 512) for i in range(3))
    columns = lambda blocks: jnp.concatenate(blocks, axis=1)

    return (
        layer_output, input_grad,
        gain1, shift1, columns([sample[i] for i in range(3)]), vector(6144 + 3 * 512, 1024),
        sample[3], off1,
        gain2, shift2, columns([feature[i] for i in range(3)]), vector(6 * 512, 1024),
        feature[3], off2,
        gain3, shift3, columns([expand[i] for i in range(4)]), expand_b,
        reduce_grad, bias_r,
    )


def spread_2(block, axis, owner):
    block = jnp.where(lax.axis_index(axis) == owner, block, jnp.zeros_like(block))
    return lax.psum(block, axis)


def layer_norm(values, gain_row, shift_row):
    center = jnp.mean(values, axis=-1, keepdims=True)
    spread = values - center
    variance = jnp.mean(spread * spread, axis=-1, keepdims=True)
    return spread * lax.rsqrt(variance + EPS) * gain_row + shift_row


def apply_weight(active, weight):
    return jnp.einsum("sfd,de->sfe", active, weight, preferred_element_type=jnp.float32)


def input_back(grad_out, weight):
    return jnp.einsum("sfe,de->sfd", grad_out, weight, preferred_element_type=jnp.float32)


def weight_grad(active, grad_out):
    return jnp.einsum("sfd,sfe->de", active, grad_out, preferred_element_type=jnp.float32)


def column_sum(values):
    return jnp.sum(values.astype(jnp.float32), axis=(0, 1))


def project(active, weight, bias_row):
    model_width = active.shape[-1]
    joined = apply_weight(active, weight)
    queries = (joined[..., :model_width] + bias_row[:model_width]).astype(jnp.bfloat16)
    key_part = joined[..., model_width : 2 * model_width].astype(jnp.bfloat16)
    value_part = (joined[..., 2 * model_width :] + bias_row[model_width:]).astype(jnp.bfloat16)
    return (queries, key_part, value_part)


def split_heads(values):
    return values.reshape(values.shape[0], values.shape[1], HEADS, HEAD_DIM)


def join_heads(values):
    return values.reshape(values.shape[0], values.shape[1], HEADS * HEAD_DIM)


def soft_weights(scores):
    top_score = jnp.max(scores, axis=-1, keepdims=True)
    raised = jnp.exp(scores - top_score)
    return raised / jnp.sum(raised, axis=-1, keepdims=True)


def feature_attend(queries, key_part, value_part):
    score_scale = HEAD_DIM ** (-0.5)
    scores = (
        jnp.einsum(
            "sfhd,sghd->shfg",
            split_heads(queries),
            split_heads(key_part),
            preferred_element_type=jnp.float32,
        )
        * score_scale
    )
    probability = soft_weights(scores)
    mixed = jnp.einsum(
        "shfg,sghd->sfhd",
        probability.astype(jnp.bfloat16),
        split_heads(value_part),
        preferred_element_type=jnp.float32,
    )
    return (join_heads(mixed).astype(jnp.bfloat16), probability)


def feature_grads(queries, key_part, value_part, probability, grad_mixed):
    score_scale = HEAD_DIM ** (-0.5)
    grad_heads = split_heads(grad_mixed)
    grad_weights = jnp.einsum(
        "sfhd,sghd->shfg", grad_heads, split_heads(value_part), preferred_element_type=jnp.float32
    )
    inner_sum = jnp.sum(probability * grad_weights, axis=-1, keepdims=True)
    grad_scores = (probability * (grad_weights - inner_sum)).astype(jnp.bfloat16)
    grad_queries = (
        jnp.einsum(
            "shfg,sghd->sfhd",
            grad_scores,
            split_heads(key_part),
            preferred_element_type=jnp.float32,
        )
        * score_scale
    )
    grad_keys = (
        jnp.einsum(
            "shfg,sfhd->sghd", grad_scores, split_heads(queries), preferred_element_type=jnp.float32
        )
        * score_scale
    )
    grad_values = jnp.einsum(
        "shfg,sfhd->sghd",
        probability.astype(jnp.bfloat16),
        grad_heads,
        preferred_element_type=jnp.float32,
    )
    return (join_heads(grad_queries), join_heads(grad_keys), join_heads(grad_values))


def local_large(
    layer_input,
    segment_ids,
    context_flags,
    first_gain,
    first_shift,
    sample_weight,
    sample_bias,
    sample_mixer,
    sample_offset,
    second_gain,
    second_shift,
    feature_weight,
    feature_bias,
    feature_mixer,
    feature_offset,
    third_gain,
    third_shift,
    expand_weight,
    expand_bias,
    reduce_weight,
    reduce_bias,
    cotangent,
):
    sample_rows = layer_input.shape[0]
    feature_rows = layer_input.shape[1]
    model_width = layer_input.shape[2]
    score_scale = HEAD_DIM ** (-0.5)
    shard_count = lax.axis_size("samp")
    context_shards = shard_count // 8
    total_context = context_shards * sample_rows
    residual_zero = layer_input.astype(jnp.float32)
    normed_one, norm_one_back = jax.vjp(layer_norm, residual_zero, first_gain, first_shift)
    active_one = normed_one.astype(jnp.bfloat16)
    queries_one, keys_one, values_one = project(active_one, sample_weight, sample_bias)
    my_index = lax.axis_index("samp")
    shard_flags = context_flags.reshape(shard_count, sample_rows)[:, 0]
    shard_rank = jnp.cumsum(shard_flags) - 1
    shard_ids = jnp.arange(shard_count, dtype=jnp.int32)
    slot_ids = jnp.arange(context_shards, dtype=jnp.int32)
    root_hits = (shard_rank[None, :] == slot_ids[:, None]) & (shard_flags[None, :] == 1)
    roots = jnp.sum(jnp.where(root_hits, shard_ids[None, :], 0), axis=1)
    context_tasks = jnp.take(segment_ids.reshape(shard_count, sample_rows), roots, axis=0).reshape(
        total_context
    )
    local_tasks = lax.dynamic_slice_in_dim(segment_ids, my_index * sample_rows, sample_rows)
    allowed = local_tasks[:, None] == context_tasks[None, :]
    is_context = shard_flags[my_index] == 1
    own_rank = jnp.maximum(shard_rank[my_index], 0)
    own_block = jnp.concatenate([keys_one, values_one], axis=-1)

    def fetch_rows(step, buffer):
        piece = spread_2(own_block, "samp", roots[step])
        return lax.dynamic_update_slice_in_dim(buffer, piece, step * sample_rows, 0)

    empty_rows = jnp.zeros((total_context, feature_rows, 2 * model_width), jnp.bfloat16)
    fetched = lax.fori_loop(0, context_shards, fetch_rows, empty_rows)
    context_keys = fetched[..., :model_width]
    context_values = fetched[..., model_width:]
    query_heads = split_heads(queries_one)
    key_heads = split_heads(context_keys)
    value_heads = split_heads(context_values)
    scores = (
        jnp.einsum("sfhd,cfhd->fhsc", query_heads, key_heads, preferred_element_type=jnp.float32)
        * score_scale
    )
    sample_prob = soft_weights(jnp.where(allowed[None, None], scores, MASKED))
    sample_weights = sample_prob.astype(jnp.bfloat16)
    mixed_one = join_heads(
        jnp.einsum(
            "fhsc,cfhd->sfhd", sample_weights, value_heads, preferred_element_type=jnp.float32
        )
    ).astype(jnp.bfloat16)
    residual_one = residual_zero + apply_weight(mixed_one, sample_mixer) + sample_offset
    normed_two, norm_two_back = jax.vjp(layer_norm, residual_one, second_gain, second_shift)
    active_two = normed_two.astype(jnp.bfloat16)
    queries_two, keys_two, values_two = project(active_two, feature_weight, feature_bias)
    all_keys, all_values = (
        lax.all_gather(keys_two, "feat", axis=1, tiled=True),
        lax.all_gather(values_two, "feat", axis=1, tiled=True),
    )
    mixed_two, feature_prob = feature_attend(queries_two, all_keys, all_values)
    residual_two = residual_one + apply_weight(mixed_two, feature_mixer) + feature_offset
    normed_three, norm_three_back = jax.vjp(layer_norm, residual_two, third_gain, third_shift)
    active_three = normed_three.astype(jnp.bfloat16)
    expanded = apply_weight(active_three, expand_weight) + expand_bias
    activated, gelu_back = jax.vjp(partial(jax.nn.gelu, approximate=False), expanded)
    hidden = activated.astype(jnp.bfloat16)
    layer_output = (residual_two + apply_weight(hidden, reduce_weight) + reduce_bias).astype(
        jnp.bfloat16
    )
    grad_out = cotangent.astype(jnp.float32)
    grad_branch = cotangent
    reduce_bias_grad = column_sum(grad_branch)
    reduce_weight_grad = weight_grad(hidden, grad_branch)
    grad_hidden = input_back(grad_branch, reduce_weight).astype(jnp.bfloat16)
    grad_expanded = gelu_back(grad_hidden.astype(jnp.float32))[0].astype(jnp.bfloat16)
    expand_bias_grad = column_sum(grad_expanded)
    expand_weight_grad = weight_grad(active_three, grad_expanded)
    grad_norm, third_gain_grad, third_shift_grad = norm_three_back(
        input_back(grad_expanded, expand_weight)
    )
    grad_two = grad_out + grad_norm
    grad_branch = grad_two.astype(jnp.bfloat16)
    feature_offset_grad = column_sum(grad_branch)
    feature_mixer_grad = weight_grad(mixed_two, grad_branch)
    grad_mixed = input_back(grad_branch, feature_mixer).astype(jnp.bfloat16)
    grad_queries, grad_keys, grad_values = feature_grads(
        queries_two, all_keys, all_values, feature_prob, grad_mixed
    )
    own_key_grads, own_value_grads = (
        lax.psum_scatter(grad_keys, "feat", scatter_dimension=1, tiled=True),
        lax.psum_scatter(grad_values, "feat", scatter_dimension=1, tiled=True),
    )
    grad_project = jnp.concatenate(
        [
            grad_queries.astype(jnp.bfloat16),
            own_key_grads.astype(jnp.bfloat16),
            own_value_grads.astype(jnp.bfloat16),
        ],
        axis=-1,
    )
    feature_weight_grad = weight_grad(active_two, grad_project)
    feature_bias_grad = jnp.concatenate(
        [
            column_sum(grad_project[..., :model_width]),
            column_sum(grad_project[..., 2 * model_width :]),
        ]
    )
    grad_norm, second_gain_grad, second_shift_grad = norm_two_back(
        input_back(grad_project, feature_weight)
    )
    grad_one = grad_two + grad_norm
    grad_branch = grad_one.astype(jnp.bfloat16)
    sample_offset_grad = column_sum(grad_branch)
    sample_mixer_grad = weight_grad(mixed_one, grad_branch)
    grad_heads = split_heads(input_back(grad_branch, sample_mixer).astype(jnp.bfloat16))
    grad_weights = jnp.einsum(
        "sfhd,cfhd->fhsc", grad_heads, value_heads, preferred_element_type=jnp.float32
    )
    inner_sum = jnp.sum(sample_prob * grad_weights, axis=-1, keepdims=True)
    grad_scores = (sample_prob * (grad_weights - inner_sum)).astype(jnp.bfloat16)
    grad_queries = (
        join_heads(
            jnp.einsum(
                "fhsc,cfhd->sfhd", grad_scores, key_heads, preferred_element_type=jnp.float32
            )
        )
        * score_scale
    ).astype(jnp.bfloat16)
    key_terms = (
        join_heads(
            jnp.einsum(
                "fhsc,sfhd->cfhd", grad_scores, query_heads, preferred_element_type=jnp.float32
            )
        )
        * score_scale
    )
    value_terms = join_heads(
        jnp.einsum(
            "fhsc,sfhd->cfhd", sample_weights, grad_heads, preferred_element_type=jnp.float32
        )
    )
    term_block = jnp.concatenate([key_terms, value_terms], axis=-1)
    summed_terms = lax.psum_scatter(term_block, "samp", scatter_dimension=0, tiled=True)
    summed_rows = lax.all_gather(summed_terms.astype(jnp.bfloat16), "samp", axis=0, tiled=True)
    own_grads = lax.dynamic_slice_in_dim(summed_rows, own_rank * sample_rows, sample_rows, 0)
    own_grads = jnp.where(is_context, own_grads, jnp.zeros_like(own_grads))
    grad_project = jnp.concatenate([grad_queries, own_grads], axis=-1)
    sample_weight_grad = weight_grad(active_one, grad_project)
    sample_bias_grad = jnp.concatenate(
        [column_sum(grad_queries), column_sum(own_grads[..., model_width:])]
    )
    grad_norm, first_gain_grad, first_shift_grad = norm_one_back(
        input_back(grad_project, sample_weight)
    )
    input_grad = (grad_one + grad_norm).astype(jnp.bfloat16)
    summed = lax.psum(
        (
            first_gain_grad,
            first_shift_grad,
            sample_weight_grad,
            sample_bias_grad,
            sample_mixer_grad,
            sample_offset_grad,
            second_gain_grad,
            second_shift_grad,
            feature_weight_grad,
            feature_bias_grad,
            feature_mixer_grad,
            feature_offset_grad,
            third_gain_grad,
            third_shift_grad,
            expand_weight_grad,
            expand_bias_grad,
            reduce_weight_grad,
            reduce_bias_grad,
        ),
        "feat",
    )
    shares = (
        lax.psum_scatter(summed[0], "samp", scatter_dimension=0, tiled=True),
        lax.psum_scatter(summed[1], "samp", scatter_dimension=0, tiled=True),
        lax.psum_scatter(summed[2], "samp", scatter_dimension=0, tiled=True),
        lax.psum_scatter(summed[3], "samp", scatter_dimension=0, tiled=True),
        lax.psum_scatter(summed[4], "samp", scatter_dimension=0, tiled=True),
        lax.psum_scatter(summed[5], "samp", scatter_dimension=0, tiled=True),
        lax.psum_scatter(summed[6], "samp", scatter_dimension=0, tiled=True),
        lax.psum_scatter(summed[7], "samp", scatter_dimension=0, tiled=True),
        lax.psum_scatter(summed[8], "samp", scatter_dimension=0, tiled=True),
        lax.psum_scatter(summed[9], "samp", scatter_dimension=0, tiled=True),
        lax.psum_scatter(summed[10], "samp", scatter_dimension=0, tiled=True),
        lax.psum_scatter(summed[11], "samp", scatter_dimension=0, tiled=True),
        lax.psum_scatter(summed[12], "samp", scatter_dimension=0, tiled=True),
        lax.psum_scatter(summed[13], "samp", scatter_dimension=0, tiled=True),
        lax.psum_scatter(summed[14], "samp", scatter_dimension=0, tiled=True),
        lax.psum_scatter(summed[15], "samp", scatter_dimension=0, tiled=True),
        lax.psum_scatter(summed[16], "samp", scatter_dimension=0, tiled=True),
        lax.psum_scatter(summed[17], "samp", scatter_dimension=0, tiled=True),
    )
    return (
        layer_output,
        input_grad,
        shares[0],
        shares[1],
        shares[2],
        shares[3],
        shares[4],
        shares[5],
        shares[6],
        shares[7],
        shares[8],
        shares[9],
        shares[10],
        shares[11],
        shares[12],
        shares[13],
        shares[14],
        shares[15],
        shares[16],
        shares[17],
    )


def solution(mesh):
    small = mesh.shape["samp"] == 8 and mesh.shape["feat"] == 4
    return jax.shard_map(
        local_small if small else local_large,
        mesh=mesh,
        in_specs=(
            P("samp", "feat", None),
            P(),
            P(),
            P(),
            P(),
            P(),
            P(),
            P(),
            P(),
            P(),
            P(),
            P(),
            P(),
            P(),
            P(),
            P(),
            P(),
            P(),
            P(),
            P(),
            P(),
            P("samp", "feat", None),
        ),
        out_specs=(
            P("samp", "feat", None),
            P("samp", "feat", None),
            P("samp"),
            P("samp"),
            P("samp", None),
            P("samp"),
            P("samp", None),
            P("samp"),
            P("samp"),
            P("samp"),
            P("samp", None),
            P("samp"),
            P("samp", None),
            P("samp"),
            P("samp"),
            P("samp"),
            P("samp", None),
            P("samp"),
            P("samp", None),
            P("samp"),
        ),
        check_vma=False,
    )
```

```python
from functools import partial

import jax
import jax.numpy as jnp
from jax import lax
from jax.experimental import pallas as pl
from jax.experimental.pallas import tpu as pltpu
from jax.sharding import PartitionSpec as P

HEADS = 8
HEAD_DIM = 64
EPS = 1e-05
MASKED = -1000000000.0
SCALE = HEAD_DIM ** (-0.5)
QUAD = 4 * HEAD_DIM
BF = jnp.bfloat16
F32 = jnp.float32


def mm(a, b, ca=1, cb=0):
    return lax.dot_general(a, b, (((ca,), (cb,)), ((), ())), preferred_element_type=F32)


def norm_parts(values):
    center = jnp.mean(values, axis=-1, keepdims=True)
    spread = values - center
    variance = jnp.mean(spread * spread, axis=-1, keepdims=True)
    inverse = lax.rsqrt(variance + EPS)
    return spread * inverse, inverse


def norm_back(grad, unit, inverse, gain):
    scaled = grad * gain
    first = jnp.mean(scaled, axis=-1, keepdims=True)
    second = jnp.mean(scaled * unit, axis=-1, keepdims=True)
    return (scaled - first - unit * second) * inverse


def lane_ids(rows):
    return lax.broadcasted_iota(jnp.int32, (rows, 128), 1)


def group_reduce(values, op, fill):
    rows = values.shape[0]
    low = lane_ids(rows) < HEAD_DIM
    outs = []
    for t in range(values.shape[1] // 128):
        tile = values[:, t * 128 : (t + 1) * 128]
        left = op(jnp.where(low, tile, fill), axis=1, keepdims=True)
        right = op(jnp.where(low, fill, tile), axis=1, keepdims=True)
        outs.append(jnp.where(low, left, right))
    return jnp.concatenate(outs, axis=1)


def head_masks(dtype):
    lanes = lax.broadcasted_iota(jnp.int32, (1, QUAD), 1) // HEAD_DIM
    return [jnp.where(lanes == h, 1.0, 0.0).astype(dtype) for h in range(4)]


def stack_heads(part, masks):
    return jnp.concatenate([part * m for m in masks], axis=0)


def pick_heads(stacked, masks):
    rows = stacked.shape[0] // 4
    total = stacked[:rows] * masks[0]
    for h in range(1, 4):
        total = total + stacked[h * rows : (h + 1) * rows] * masks[h]
    return total


def attend(q, k, v, masks, allow):
    outs, probs = [], []
    for quad in range(2):
        cols = slice(quad * QUAD, (quad + 1) * QUAD)
        scores = mm(q[:, cols], stack_heads(k[:, cols], masks), 1, 1)
        if allow is not None:
            scores = jnp.where(allow, scores, MASKED)
        raised = jnp.exp(scores - group_reduce(scores, jnp.max, -jnp.inf))
        prob = raised / group_reduce(raised, jnp.sum, 0.0)
        outs.append(mm(prob.astype(BF), stack_heads(v[:, cols], masks)))
        probs.append(prob)
    return jnp.concatenate(outs, axis=1), jnp.concatenate(probs, axis=1)


def attend_back(q, k, v, prob, grad, masks, masks32):
    dqs, dks, dvs = [], [], []
    for quad in range(2):
        cols = slice(quad * QUAD, (quad + 1) * QUAD)
        p, g = prob[:, cols], grad[:, cols]
        back = mm(g, stack_heads(v[:, cols], masks), 1, 1)
        inner = group_reduce(p * back, jnp.sum, 0.0)
        gs = (p * (back - inner)).astype(BF)
        dqs.append(mm(gs, stack_heads(k[:, cols], masks)) * SCALE)
        dks.append(pick_heads(mm(gs, q[:, cols], 0, 0), masks32))
        dvs.append(pick_heads(mm(p.astype(BF), g, 0, 0), masks32))
    join = lambda parts: jnp.concatenate(parts, axis=1).astype(BF)
    return join(dqs), join(dks), join(dvs)


def swap_matrix(rows=16):
    n = rows * 16
    r = lax.broadcasted_iota(jnp.int32, (n, n), 0)
    c = lax.broadcasted_iota(jnp.int32, (n, n), 1)
    return jnp.where((r // rows == c % 16) & (r % rows == c // 16), 1.0, 0.0).astype(BF)


def swap(matrix, values, back=False):
    return mm(matrix, values, 0 if back else 1, 0).astype(BF)


def gelu_parts(u):
    cdf = 0.5 * (1.0 + lax.erf(u * (2.0**-0.5)))
    density = jnp.exp(u * u * -0.5) * 0.3989422804014327
    return cdf, density


def col_sum(values):
    return jnp.sum(values.astype(F32), axis=0, keepdims=True)


def turn_in(x_ref, out_ref):
    matrix = swap_matrix()
    for d in range(4):
        rows = x_ref[d * 256 : (d + 1) * 256]
        out_ref[:, d] = swap(matrix, rows).reshape(16, 16, 512)


def turn_out(got_ref, out_ref):
    matrix = swap_matrix()
    for d in range(4):
        out_ref[d * 256 : (d + 1) * 256] = swap(matrix, got_ref[:, d].reshape(256, 512))


def project_queries(x_ref, gain_ref, shift_ref, w_ref, b_ref, q_ref):
    for e in range(4):
        unit, _ = norm_parts(x_ref[:, e].reshape(256, 512).astype(F32))
        act = (unit * gain_ref[...] + shift_ref[...]).astype(BF)
        q = (mm(act, w_ref[:, :512]) + b_ref[:, :512]).astype(BF)
        q_ref[e] = q * jnp.asarray(SCALE, BF)


def forward_one(
    me_ref, q_ref, own_ref, got_ref, tasks_ref, context_ref, gain_ref, shift_ref, w_ref, b_ref,
    oa_ref, ob_ref, c_ref, k_ref, v_ref, p_ref,
):
    here = me_ref[1] == me_ref[2]
    masks = head_masks(BF)
    allow = tasks_ref[...] == context_ref[...]

    @pl.when(here)
    def _():
        c_ref[...] = own_ref[...]

    @pl.when(jnp.logical_not(here))
    def _():
        c_ref[...] = got_ref[...]

    unit, _ = norm_parts(c_ref[...].reshape(256, 512).astype(F32))
    kv = mm((unit * gain_ref[...] + shift_ref[...]).astype(BF), w_ref[:, 512:])
    k_ref[...] = kv[:, :512].astype(BF).reshape(4, 64, 512)
    v_ref[...] = (kv[:, 512:] + b_ref[:, 512:]).astype(BF).reshape(4, 64, 512)
    for e in range(4):
        out, prob = attend(q_ref[e], k_ref[e], v_ref[e], masks, allow)
        out = out.reshape(4, 4, 2, 8, 512)
        oa_ref[:, :, e] = out[:, :, 0].astype(BF)
        ob_ref[:, :, e] = out[:, :, 1].astype(BF)
        p_ref[e] = prob


def middle(me_ref, *refs):
    (
        o1_ref, x0, x1, x2, x3, c0, c1, c2, c3,
        wm1_ref, off1_ref, g2_ref, s2_ref, wf_ref, bf_ref, wm2_ref, off2_ref,
        g3_ref, s3_ref, we_ref, be_ref, wr_ref, br_ref,
    ) = refs[:23]
    (
        gb1_ref, vec_ref, bias_ref, out0, out2, out13,
        a2_ref, dqkv_ref, o2_ref, gb2_ref, a3_ref, gu_ref, hid_ref, gb3_ref,
        o_scr, g_scr,
    ) = refs[-16:]
    samples = 4
    me, step = me_ref[0], pl.program_id(0)
    matrix = swap_matrix(8)
    now = pl.ds(pl.multiple_of(step * 64, 64), 64)

    @pl.when(step == 0)
    def _():
        for f in range(4):
            o_scr[f] = swap(matrix, o1_ref[:, f].reshape(128, 512), True)

    def gather(*refs):
        return jnp.concatenate(
            [ref[s * 16 : (s + 1) * 16] for s in range(samples) for ref in refs], axis=0
        )

    def scatter(values, *refs):
        for s in range(samples):
            for d, ref in enumerate(refs):
                at = (s * 4 + d) * 16
                ref[s * 16 : (s + 1) * 16] = values[at : at + 16]

    masks, masks32 = head_masks(BF), head_masks(F32)
    attended = gather(*(o_scr[d ^ me, now] for d in range(4)))
    cot = gather(c0, c1, c2, c3)
    gb3_ref[...] = cot
    r1 = gather(x0, x1, x2, x3).astype(F32) + mm(attended, wm1_ref[...]) + off1_ref[...]
    unit2, inv2 = norm_parts(r1)
    act2 = (unit2 * g2_ref[...] + s2_ref[...]).astype(BF)
    a2_ref[...] = act2
    qkv = mm(act2, wf_ref[...])
    q = (qkv[:, :512] + bf_ref[:, :512]).astype(BF) * jnp.asarray(SCALE, BF)
    k = qkv[:, 512:1024].astype(BF)
    v = (qkv[:, 1024:] + bf_ref[:, 512:]).astype(BF)
    parts = []
    for s in range(samples):
        rows = slice(s * 64, (s + 1) * 64)
        parts.append(attend(q[rows], k[rows], v[rows], masks, None))
    o2 = jnp.concatenate([part[0] for part in parts], axis=0).astype(BF)
    o2_ref[...] = o2
    r2 = r1 + mm(o2, wm2_ref[...]) + off2_ref[...]
    unit3, inv3 = norm_parts(r2)
    act3 = (unit3 * g3_ref[...] + s3_ref[...]).astype(BF)
    a3_ref[...] = act3
    out = r2 + br_ref[...]
    back = None
    bias = []
    for b in range(4):
        cols = slice(b * 512, (b + 1) * 512)
        u = mm(act3, we_ref[:, cols]) + be_ref[:, cols]
        cdf, density = gelu_parts(u)
        hidden = (u * cdf).astype(BF)
        hid_ref[:, cols] = hidden
        out = out + mm(hidden, wr_ref[cols, :])
        gh = mm(cot, wr_ref[cols, :], 1, 1).astype(BF).astype(F32)
        gu = (gh * (cdf + u * density)).astype(BF)
        gu_ref[:, cols] = gu
        bias.append(col_sum(gu))
        term = mm(gu, we_ref[:, cols], 1, 1)
        back = term if back is None else back + term
    scatter(out.astype(BF), out0, out13.at[0], out2, out13.at[1])
    vecs = [col_sum(back * unit3), col_sum(back)]
    gr2 = cot.astype(F32) + norm_back(back, unit3, inv3, g3_ref[...])
    gb2 = gr2.astype(BF)
    gb2_ref[...] = gb2
    go2 = mm(gb2, wm2_ref[...], 1, 1).astype(BF)
    grads = []
    for s in range(samples):
        rows = slice(s * 64, (s + 1) * 64)
        grads.append(
            jnp.concatenate(
                attend_back(q[rows], k[rows], v[rows], parts[s][1], go2[rows], masks, masks32),
                axis=1,
            )
        )
    dqkv = jnp.concatenate(grads, axis=0)
    dqkv_ref[...] = dqkv
    back = mm(dqkv, wf_ref[...], 1, 1)
    vecs += [col_sum(back * unit2), col_sum(back)]
    gr1 = gr2 + norm_back(back, unit2, inv2, g2_ref[...])
    scatter(gr1.astype(BF), *(g_scr.at[d ^ me, now] for d in range(4)))

    @pl.when(step == 1)
    def _():
        for f in range(4):
            gb1_ref[:, f] = swap(matrix, g_scr[f]).reshape(4, 4, 8, 512)

    vecs += [col_sum(gb2), col_sum(cot), col_sum(dqkv[:, :512]), col_sum(dqkv[:, 1024:])]

    @pl.when(step == 0)
    def _():
        vec_ref[...] = jnp.zeros_like(vec_ref)
        bias_ref[...] = jnp.zeros_like(bias_ref)

    vec_ref[...] += jnp.concatenate(vecs, axis=0)
    bias_ref[...] += jnp.concatenate(bias, axis=1)


def backward_one(
    me_ref, ga_ref, gb_ref, x_ref, c_ref, q_ref, k_ref, v_ref, p_ref, gain_ref, shift_ref, w_ref,
    wm_ref,
    gb1_ref, dq_ref, dkv_ref, term_ref, act_ref, cact_ref, vec_ref,
    g_scr,
):
    gain, shift = gain_ref[...], shift_ref[...]
    masks, masks32 = head_masks(BF), head_masks(F32)
    zero = jnp.zeros((1, 512), F32)
    off_sum, q_sum = zero, zero
    for e in range(4):
        g_scr[:, :, 0] = ga_ref[:, :, e]
        g_scr[:, :, 1] = gb_ref[:, :, e]
        gb1 = g_scr[...].reshape(256, 512)
        gb1_ref[e] = gb1
        go = mm(gb1, wm_ref[...], 1, 1).astype(BF)
        dq, dk, dv = attend_back(q_ref[e], k_ref[e], v_ref[e], p_ref[e], go, masks, masks32)
        dq_ref[e], dkv_ref[e, :, :512], dkv_ref[e, :, 512:] = dq, dk, dv
        off_sum += col_sum(gb1)
        q_sum += col_sum(dq)
    dkv = dkv_ref[...].reshape(256, 1024)
    term = mm(dkv, w_ref[:, 512:], 1, 1)
    term_ref[...] = term.astype(BF).reshape(4, 64, 512)
    unit, _ = norm_parts(c_ref[...].reshape(256, 512).astype(F32))
    cact_ref[...] = (unit * gain + shift).astype(BF).reshape(4, 64, 512)
    gain_sum, shift_sum, v_sum = col_sum(term * unit), col_sum(term), col_sum(dkv[:, 512:])
    for e in range(4):
        unit, _ = norm_parts(x_ref[:, e].reshape(256, 512).astype(F32))
        act_ref[e] = (unit * gain + shift).astype(BF)
    vec_ref[...] = jnp.concatenate(
        [gain_sum, shift_sum, off_sum, q_sum, v_sum, zero, zero, zero], axis=0
    )


def backward_input(
    me_ref, gb1_ref, x_ref, dq_ref, term_ref, got_ref, vec1_ref, gain_ref, w_ref,
    grad_ref, vec_ref, a_scr,
):
    here, quad = me_ref[1] == me_ref[2], me_ref[3]
    gain = gain_ref[...]
    gain_sum, shift_sum = vec1_ref[0:1], vec1_ref[1:2]
    for e in range(4):
        back = mm(dq_ref[e], w_ref[:, :512], 1, 1)
        unit, inverse = norm_parts(x_ref[:, e].reshape(256, 512).astype(F32))
        gain_sum += col_sum(back * unit)
        shift_sum += col_sum(back)
        a_scr[...] = back.reshape(4, 64, 512)

        @pl.when(here)
        def _(e=e):
            a_scr[quad] += term_ref[e].astype(F32) + got_ref[e].astype(F32)

        back = a_scr[...].reshape(256, 512)
        grad = gb1_ref[e].astype(F32) + norm_back(back, unit, inverse, gain)
        grad_ref[:, e] = grad.astype(BF).reshape(4, 64, 512)
    vec_ref[...] = vec1_ref[...]
    vec_ref[0:2] = jnp.concatenate([gain_sum, shift_sum], axis=0)


def place(me_ref, b0, b1, b2, b3, out_ref):
    for d, ref in enumerate((b0, b1, b2, b3)):
        out_ref[d ^ me_ref[0]] = ref[...]


def lay_out(me_ref, read, order, *pairs):
    core, xx, yy, zz = me_ref[4], me_ref[5], me_ref[6], me_ref[7]
    for bits in range(16):
        index = tuple((bits >> i) & 1 for i in (3, 2, 1, 0))
        dx, dy, d1, d2 = (index[order.index(name)] for name in ("x", "y", "z", "w"))
        shard = (zz ^ d1 ^ (2 * d2)) * 2 + (yy ^ dy)
        for keep_ref, send_ref, start, rows in pairs:
            keep_ref[index] = read(2 * core + (dx ^ xx), shard, start, rows)
            send_ref[index] = read(2 * (1 - core) + (dx ^ xx), shard, start, rows)


def read_units(scr):
    def read(unit, shard, start, rows):
        return scr[unit, pl.ds(pl.multiple_of(shard * 64 + start, rows), rows)]

    return read


def over_tokens(*pairs):
    return sum(mm(a[...], b[...], 0, 0) for a, b in pairs).astype(BF)


def grads_reduce(me_ref, hida_ref, hidb_ref, gba_ref, gbb_ref, keep_ref, send_ref, scr):
    step = pl.program_id(0)
    start = pl.multiple_of(step * 512, 512)
    scr[pl.ds(start, 512)] = over_tokens((hida_ref, gba_ref), (hidb_ref, gbb_ref))

    def read(unit, shard, start, rows):
        return scr[pl.ds(pl.multiple_of(shard * 256 + unit * 64, 64), 64)]

    @pl.when(step == 3)
    def _():
        lay_out(me_ref, read, "zxyw", (keep_ref, send_ref, 0, 64))


def grads_expand(me_ref, acta_ref, actb_ref, gua_ref, gub_ref, keep_ref, send_ref, scr):
    step = pl.program_id(0)
    scr[step] = over_tokens((acta_ref, gua_ref), (actb_ref, gub_ref))

    @pl.when(step == 3)
    def _():
        lay_out(me_ref, read_units(scr), "yxzw", (keep_ref, send_ref, 0, 64))


def grads_feature(
    me_ref, acta_ref, actb_ref, dqa_ref, dqb_ref, oa_ref, ob_ref, gba_ref, gbb_ref,
    keep_ref, send_ref, scr,
):
    step = pl.program_id(0)

    @pl.when(step < 3)
    def _():
        scr[step] = over_tokens((acta_ref, dqa_ref), (actb_ref, dqb_ref))

    @pl.when(step == 3)
    def _():
        scr[3] = over_tokens((oa_ref, gba_ref), (ob_ref, gbb_ref))
        lay_out(me_ref, read_units(scr), "xyzw", (keep_ref, send_ref, 0, 64))


def grads_sample(
    me_ref, act_ref, dq_ref, cact_ref, dkv_ref, oa_ref, ga_ref, ob_ref, gb_ref,
    keepa_ref, senda_ref, keepb_ref, sendb_ref, scr,
):
    scr[0] = mm(act_ref[...], dq_ref[...], 0, 0).astype(BF)
    scr[1] = mm(cact_ref[...], dkv_ref[:, :512], 0, 0).astype(BF)
    scr[2] = mm(cact_ref[...], dkv_ref[:, 512:], 0, 0).astype(BF)
    total = mm(oa_ref[...], ga_ref[...], 0, 0) + mm(ob_ref[...], gb_ref[...], 0, 0)
    scr[3] = total.astype(BF)
    lay_out(me_ref, read_units(scr), "xyzw", (keepa_ref, senda_ref, 0, 32))
    lay_out(me_ref, read_units(scr), "yxzw", (keepb_ref, sendb_ref, 32, 32))


def spec(shape, index=None):
    return pl.BlockSpec(shape, index if index is not None else (lambda *a: (0,) * len(shape)))


def sds(shape, dtype=BF):
    return jax.ShapeDtypeStruct(shape, dtype)


def big(shape, dtype=BF):
    return pltpu.HBM(shape, dtype)


def outside(array):
    if array.size * array.dtype.itemsize < 1 << 18:
        return array
    return pltpu.with_memory_space_constraint(array, pltpu.HBM)


def params(limit):
    return pltpu.CompilerParams(vmem_limit_bytes=limit << 20)


def row(vector):
    return vector.reshape(1, -1)


def whole_block(out):
    shape = out.shape
    return pl.BlockSpec(shape, lambda i: (0,) * len(shape))


def whole(kernel, name, limit, outs, scratch, *inputs, steps=1):
    arrays, specs = [], []
    for entry in inputs:
        if not isinstance(entry, tuple) and entry.ndim == 1:
            arrays.append(entry)
            specs.append(pl.BlockSpec(memory_space=pltpu.SMEM))
            continue
        array, block, index = entry if isinstance(entry, tuple) else (entry, None, None)
        arrays.append(outside(array))
        block = array.shape if block is None else block
        index = (0,) * array.ndim if index is None else index
        if not callable(index):
            index = lambda i, index=index: index
        specs.append(pl.BlockSpec(block, index))
    return pl.pallas_call(
        kernel,
        grid=(steps,),
        out_shape=outs,
        in_specs=specs,
        out_specs=jax.tree.map(whole_block, outs, is_leaf=lambda o: hasattr(o, "dtype")),
        scratch_shapes=scratch,
        compiler_params=params(limit),
        name=name,
    )(*arrays)


def shuffle(value, axis, mask):
    size = lax.axis_size(axis)
    return lax.ppermute(value, axis, [(i, i ^ mask) for i in range(size)])


SAMP = ("half", "quad")
CORE, X, Y, Z, W = ("feat", 1), ("feat", 2), ("quad", 1), ("quad", 2), ("half", 1)


def at(stacked, index, axis=0):
    return lax.dynamic_index_in_dim(stacked, index, axis, keepdims=False)


def fence(tree):
    return lax.optimization_barrier(tree)


def plus(a, b):
    return (a.astype(F32) + b.astype(F32)).astype(BF)


class Chain:
    def __init__(self, keep, sent, dims):
        self.keep, self.sent, self.dims = keep, sent, (CORE,) + dims

    def start(self):
        return shuffle(self.sent, *self.dims[0])

    def take(self, got):
        self.dims = self.dims[1:]
        if self.dims:
            self.keep, self.sent = plus(self.keep[0], got[0]), plus(self.keep[1], got[1])
        else:
            self.keep = plus(self.keep, got)


def together(chains, make=lambda: ()):
    got = [chain.start() for chain in chains]
    got, other = fence((got, make()))
    for chain, value in zip(chains, got):
        chain.take(value)
    return other


def last_round(parts):
    joined = jnp.concatenate([part.reshape(-1, 512) for part in parts], axis=0)
    return joined, [shuffle(joined, "feat", mask) for mask in (1, 2, 3)]


def pick_join(rows, core, xx):
    place = core * 2 + xx
    outs = []
    for target in range(4):
        value = rows[0]
        for mask, index in ((1, 2), (2, 1), (3, 3)):
            value = jnp.where((place ^ target) == index, rows[mask], value)
        outs.append(value.astype(F32))
    return jnp.stack(outs)


def local_small(
    layer_input, segment_ids, context_flags,
    first_gain, first_shift, sample_weight, sample_bias, sample_mixer, sample_offset,
    second_gain, second_shift, feature_weight, feature_bias, feature_mixer, feature_offset,
    third_gain, third_shift, expand_weight, expand_bias, reduce_weight, reduce_bias, cotangent,
):
    half, quad, feat = (lax.axis_index(name) for name in ("half", "quad", "feat"))
    samp = half * 4 + quad
    core, xx = feat % 2, feat // 2
    flags = context_flags.reshape(8, 64)[:, 0]
    root = jnp.sum(jnp.where(flags == 1, jnp.arange(8, dtype=jnp.int32), 0))
    me = [feat, half, root // 4, root % 4, core, xx, samp % 2, samp // 2]
    me = jnp.stack(me).astype(jnp.int32)

    turned = whole(turn_in, "turn_in", 8, big((16, 4, 16, 512)), [], layer_input.reshape(1024, 512))
    turned, layer_input, cotangent = fence((turned, layer_input, cotangent))
    x_t = lax.all_to_all(turned.reshape(4, 4, 64, 512), "quad", 0, 0)
    x4, cot4 = layer_input.reshape(4, 256, 512), cotangent.reshape(4, 256, 512)
    block = lambda value, d: at(value, feat ^ d)
    to_core = jnp.stack([block(x4, 1), block(cot4, 1), block(x4, 3), block(cot4, 3)])
    from_core = shuffle(to_core, *CORE)
    x_far = shuffle(jnp.stack([block(x4, 2), from_core[2]]), *X)
    x_t, from_core, x_far = fence((x_t, from_core, x_far))
    cot_far = shuffle(jnp.stack([block(cot4, 2), from_core[3]]), *X)
    own_context = at(x_t, root % 4)
    got_context = shuffle(own_context, *W)
    queries = whole(
        project_queries, "project_queries", 16, big((4, 256, 512)), [],
        x_t, row(first_gain), row(first_shift), sample_weight, row(sample_bias),
    )
    cot_far, got_context, q1 = fence((cot_far, got_context, queries))

    tasks = segment_ids.reshape(8, 64)
    context_tasks = jnp.concatenate([at(tasks, root)] * 4).reshape(1, 256)
    sent = big((4, 4, 4, 8, 512))
    four = sds((4, 64, 512))
    oa, ob, context, k1, v1, p1 = whole(
        forward_one, "forward_one", 24, (sent, sent, four, four, four, big((4, 256, 512), F32)), [],
        me, q1, own_context, got_context, at(segment_ids.reshape(2, 256, 1), half), context_tasks,
        row(first_gain), row(first_shift), sample_weight, row(sample_bias),
    )

    def exchange(value):
        shape = value.shape
        value = value.reshape((16,) + shape[2:])
        return lax.all_to_all(value, ("quad", "feat"), 0, 0).reshape(shape)

    weights = [
        sample_mixer, row(sample_offset), row(second_gain), row(second_shift), feature_weight,
        row(feature_bias), feature_mixer, row(feature_offset), row(third_gain), row(third_shift),
        expand_weight, row(expand_bias), reduce_weight, row(reduce_bias),
    ]
    def run_middle(half, attended):
        flat = lambda n: spec((64, n), lambda i, m: (i, 0))
        own = spec((None, 64, 512), lambda i, m: (m[0], 2 * half + i, 0))
        part = lambda n: spec((None, 64, 512), lambda i, m: (n, 2 * half + i, 0))
        wide = lambda n: spec((256, n), lambda i, m: (i, 0))
        still = lambda shape: spec(shape, lambda i, m: (0,) * len(shape))
        return pl.pallas_call(
            middle,
            grid_spec=pltpu.PrefetchScalarGridSpec(
                num_scalar_prefetch=1,
                grid=(2,),
                in_specs=[still((4, 4, 4, 8, 512))]
                + [own, part(0), part(0), part(1), own, part(1), part(0), part(1)]
                + [
                    pl.BlockSpec(w.shape, lambda i, m: (0, 0), pipeline_mode=pl.Buffered(1))
                    for w in weights
                ],
                out_specs=[
                    still((4, 4, 4, 8, 512)), still((8, 512)), still((1, 2048)),
                    flat(512), flat(512), spec((2, 64, 512), lambda i, m: (0, i, 0)),
                    wide(512), wide(1536), wide(512), wide(512), wide(512), wide(2048),
                    wide(2048), wide(512),
                ],
                scratch_shapes=[pltpu.VMEM((4, 128, 512), BF), pltpu.VMEM((4, 128, 512), BF)],
            ),
            out_shape=(
                sent, sds((8, 512), F32), sds((1, 2048), F32),
                big((128, 512)), big((128, 512)), big((2, 128, 512)), big((512, 512)),
                big((512, 1536)), big((512, 512)), big((512, 512)), big((512, 512)),
                big((512, 2048)), big((512, 2048)), big((512, 512)),
            ),
            compiler_params=params(44),
            name="middle",
        )(
            me,
            *(
                outside(array)
                for array in (
                    attended, x4, from_core, x_far, x_far, cot4, from_core, cot_far, cot_far,
                    *weights,
                )
            ),
        )

    oa_f, ob = fence((exchange(oa), ob))
    ob_f = exchange(ob)
    ga, vec_a, bias_a, *first = run_middle(0, oa_f)
    ob_f, ga, first = fence((ob_f, ga, first))
    ga_t = exchange(ga)
    gb, vec_b, bias_b, *second = run_middle(1, ob_f)
    ga_t, gb, second = fence((ga_t, gb, second))
    out0, out2, out13, act2, dqkv, o2, gb2, act3, gu, hidden, gb3 = zip(first, second)
    gb_t = exchange(gb)
    vec2, bias2 = vec_a + vec_b, bias_a + bias_b
    out0, out2 = (jnp.concatenate(pair, axis=0) for pair in (out0, out2))
    out13 = jnp.concatenate(out13, axis=1)

    parts = sds((2, 2, 2, 2, 64, 512))
    moving = lambda pair: [(a, (512, 512), lambda i: (0, i)) for a in pair]
    upto = lambda pair: [(a, (512, 512), lambda i: (0, jnp.minimum(i, 2))) for a in pair]
    units = [pltpu.VMEM((4, 512, 512), BF)]
    rk, rs = whole(
        grads_reduce, "grads_reduce", 16, (parts, parts), [pltpu.VMEM((2048, 512), BF)],
        me, *moving(hidden), *gb3, steps=4,
    )
    ek, es = whole(
        grads_expand, "grads_expand", 16, (parts, parts), units, me, *act3, *moving(gu), steps=4
    )
    fk, fs = whole(
        grads_feature, "grads_feature", 20, (parts, parts), units,
        me, *act2, *upto(dqkv), *o2, *gb2, steps=4,
    )
    r_chain = Chain(rk, rs, (Z, X, Y, W))
    e_chain = Chain(ek, es, (Y, X, Z, W))
    f_chain = Chain(fk, fs, (X, Y, Z, W))
    chains = [r_chain, e_chain, f_chain]
    near = shuffle(out13, *CORE)
    got = [chain.start() for chain in chains]
    gb_t, near, got, keeps = fence((gb_t, near, got, [chain.keep for chain in chains]))
    for chain, value, keep in zip(chains, got, keeps):
        chain.keep = keep
        chain.take(value)

    full = big((4, 256, 512))
    gb1, dq1, dkv, term, act1, cact, vec1 = together(
        chains,
        lambda: whole(
            backward_one, "backward_one", 32,
            (full, full, sds((4, 64, 1024)), four, full, four, sds((8, 512), F32)),
            [pltpu.VMEM((4, 4, 2, 8, 512), BF)],
            me, ga_t, gb_t, x_t, context, q1, k1, v1, p1, row(first_gain), row(first_shift),
            sample_weight, sample_mixer,
        ),
    )
    small = sds((2, 2, 2, 2, 32, 512))
    flat2 = lambda a: a.reshape(-1, a.shape[-1])
    ak, as_, bk, bs = whole(
        grads_sample, "grads_sample", 20, (small,) * 4, units,
        me, *(flat2(a) for a in (act1, dq1, cact, dkv, oa, ga_t, ob, gb_t)),
    )
    got_term, ak, as_, bk, bs = together(
        chains, lambda: (shuffle(term, *W), ak, as_, bk, bs)
    )
    samples = [Chain(ak, as_, (X, Y)), Chain(bk, bs, (Y, X))]
    grad_t, vec1 = together(
        samples,
        lambda: whole(
            backward_input, "backward_input", 24, (big((4, 4, 64, 512)), sds((8, 512), F32)),
            [pltpu.VMEM((4, 64, 512), F32)],
            me, gb1, x_t, dq1, term, got_term, vec1, row(first_gain), sample_weight,
        ),
    )
    got = lax.all_to_all(grad_t, "quad", 0, 0)
    owned = lambda v, n: v.reshape(-1, 8, n).transpose(1, 0, 2).reshape(8, -1)
    vectors = jnp.concatenate(
        [
            owned(vec2[:6], 64), vec2[6:].reshape(8, 128), bias2.reshape(8, 256),
            owned(vec1[:3], 64), vec1[3:5].reshape(8, 128),
        ],
        axis=1,
    )
    for where in (CORE, X):
        vectors = vectors + shuffle(vectors, *where)
    far = shuffle(jnp.stack([out2.reshape(256, 512), near[1]]), *X)
    for chain in samples + chains:
        while chain.dims:
            chain.take(chain.start())
    got, far, vectors, rows, finals = fence(
        (got, far, vectors, [chain.keep for chain in samples], [chain.keep for chain in chains])
    )

    rows = jnp.concatenate(rows, axis=2)
    from_z = [
        lax.ppermute(rows[i // 2, i % 2], SAMP, [(j, j ^ (0, 4, 2, 6)[i]) for j in range(8)])
        for i in (1, 2, 3)
    ]
    rows_a, others = last_round(finals)
    layer_output = whole(
        place, "place", 16, sds((4, 256, 512)), [], me, out0,
        (near, (None, 256, 512), (0, 0, 0)), (far, (None, 256, 512), (0, 0, 0)),
        (far, (None, 256, 512), (1, 0, 0)),
    ).reshape(64, 16, 512)
    for where in (Y, Z):
        vectors = vectors + shuffle(vectors, *where)
    from_z, others, vectors, layer_output = fence((from_z, others, vectors, layer_output))
    rows_a = [rows_a] + others
    total = rows[0, 0].astype(F32)
    for value in from_z:
        total = total + value.astype(F32)
    rows_b, others = last_round([total.astype(BF)])
    input_grad = whole(
        turn_out, "turn_out", 8, sds((1024, 512)), [], got.reshape(16, 4, 16, 512)
    ).reshape(64, 16, 512)
    others, v, input_grad = fence((others, shuffle(vectors, *W), input_grad))
    rows_b = [rows_b] + others
    vectors = vectors + v

    cut = lambda rows, start, count: [r[start : start + count] for r in rows]
    reduce_grad = pick_join(cut(rows_a, 0, 64), core, xx).reshape(256, 512)
    expand = pick_join(cut(rows_a, 64, 64), core, xx)
    feature = pick_join(cut(rows_a, 128, 64), core, xx)
    sample = pick_join(rows_b, core, xx)

    mine = at(vectors, samp)
    gain3, shift3, gain2, shift2, off2, bias_r = (mine[i * 64 : (i + 1) * 64] for i in range(6))
    feature_b, expand_b = mine[384:512], mine[512:768]
    gain1, shift1, off1 = (mine[768 + i * 64 : 832 + i * 64] for i in range(3))
    sample_b = mine[960:1088]
    columns = lambda blocks: jnp.concatenate(blocks, axis=1)

    return (
        layer_output, input_grad,
        gain1, shift1, columns([sample[i] for i in range(3)]), sample_b, sample[3], off1,
        gain2, shift2, columns([feature[i] for i in range(3)]), feature_b, feature[3], off2,
        gain3, shift3, columns([expand[i] for i in range(4)]), expand_b,
        reduce_grad, bias_r,
    )


def spread_2(block, axis, owner):
    block = jnp.where(lax.axis_index(axis) == owner, block, jnp.zeros_like(block))
    return lax.psum(block, axis)


def layer_norm(values, gain_row, shift_row):
    center = jnp.mean(values, axis=-1, keepdims=True)
    spread = values - center
    variance = jnp.mean(spread * spread, axis=-1, keepdims=True)
    return spread * lax.rsqrt(variance + EPS) * gain_row + shift_row


def apply_weight(active, weight):
    return jnp.einsum("sfd,de->sfe", active, weight, preferred_element_type=jnp.float32)


def input_back(grad_out, weight):
    return jnp.einsum("sfe,de->sfd", grad_out, weight, preferred_element_type=jnp.float32)


def weight_grad(active, grad_out):
    return jnp.einsum("sfd,sfe->de", active, grad_out, preferred_element_type=jnp.float32)


def column_sum(values):
    return jnp.sum(values.astype(jnp.float32), axis=(0, 1))


def project(active, weight, bias_row):
    model_width = active.shape[-1]
    joined = apply_weight(active, weight)
    queries = (joined[..., :model_width] + bias_row[:model_width]).astype(jnp.bfloat16)
    key_part = joined[..., model_width : 2 * model_width].astype(jnp.bfloat16)
    value_part = (joined[..., 2 * model_width :] + bias_row[model_width:]).astype(jnp.bfloat16)
    return (queries, key_part, value_part)


def split_heads(values):
    return values.reshape(values.shape[0], values.shape[1], HEADS, HEAD_DIM)


def join_heads(values):
    return values.reshape(values.shape[0], values.shape[1], HEADS * HEAD_DIM)


def soft_weights(scores):
    top_score = jnp.max(scores, axis=-1, keepdims=True)
    raised = jnp.exp(scores - top_score)
    return raised / jnp.sum(raised, axis=-1, keepdims=True)


def feature_attend(queries, key_part, value_part):
    score_scale = HEAD_DIM ** (-0.5)
    scores = (
        jnp.einsum(
            "sfhd,sghd->shfg",
            split_heads(queries),
            split_heads(key_part),
            preferred_element_type=jnp.float32,
        )
        * score_scale
    )
    probability = soft_weights(scores)
    mixed = jnp.einsum(
        "shfg,sghd->sfhd",
        probability.astype(jnp.bfloat16),
        split_heads(value_part),
        preferred_element_type=jnp.float32,
    )
    return (join_heads(mixed).astype(jnp.bfloat16), probability)


def feature_grads(queries, key_part, value_part, probability, grad_mixed):
    score_scale = HEAD_DIM ** (-0.5)
    grad_heads = split_heads(grad_mixed)
    grad_weights = jnp.einsum(
        "sfhd,sghd->shfg", grad_heads, split_heads(value_part), preferred_element_type=jnp.float32
    )
    inner_sum = jnp.sum(probability * grad_weights, axis=-1, keepdims=True)
    grad_scores = (probability * (grad_weights - inner_sum)).astype(jnp.bfloat16)
    grad_queries = (
        jnp.einsum(
            "shfg,sghd->sfhd",
            grad_scores,
            split_heads(key_part),
            preferred_element_type=jnp.float32,
        )
        * score_scale
    )
    grad_keys = (
        jnp.einsum(
            "shfg,sfhd->sghd", grad_scores, split_heads(queries), preferred_element_type=jnp.float32
        )
        * score_scale
    )
    grad_values = jnp.einsum(
        "shfg,sfhd->sghd",
        probability.astype(jnp.bfloat16),
        grad_heads,
        preferred_element_type=jnp.float32,
    )
    return (join_heads(grad_queries), join_heads(grad_keys), join_heads(grad_values))


def local_large(
    layer_input,
    segment_ids,
    context_flags,
    first_gain,
    first_shift,
    sample_weight,
    sample_bias,
    sample_mixer,
    sample_offset,
    second_gain,
    second_shift,
    feature_weight,
    feature_bias,
    feature_mixer,
    feature_offset,
    third_gain,
    third_shift,
    expand_weight,
    expand_bias,
    reduce_weight,
    reduce_bias,
    cotangent,
):
    sample_rows = layer_input.shape[0]
    feature_rows = layer_input.shape[1]
    model_width = layer_input.shape[2]
    score_scale = HEAD_DIM ** (-0.5)
    shard_count = lax.axis_size("samp")
    context_shards = shard_count // 8
    total_context = context_shards * sample_rows
    residual_zero = layer_input.astype(jnp.float32)
    normed_one, norm_one_back = jax.vjp(layer_norm, residual_zero, first_gain, first_shift)
    active_one = normed_one.astype(jnp.bfloat16)
    queries_one, keys_one, values_one = project(active_one, sample_weight, sample_bias)
    my_index = lax.axis_index("samp")
    shard_flags = context_flags.reshape(shard_count, sample_rows)[:, 0]
    shard_rank = jnp.cumsum(shard_flags) - 1
    shard_ids = jnp.arange(shard_count, dtype=jnp.int32)
    slot_ids = jnp.arange(context_shards, dtype=jnp.int32)
    root_hits = (shard_rank[None, :] == slot_ids[:, None]) & (shard_flags[None, :] == 1)
    roots = jnp.sum(jnp.where(root_hits, shard_ids[None, :], 0), axis=1)
    context_tasks = jnp.take(segment_ids.reshape(shard_count, sample_rows), roots, axis=0).reshape(
        total_context
    )
    local_tasks = lax.dynamic_slice_in_dim(segment_ids, my_index * sample_rows, sample_rows)
    allowed = local_tasks[:, None] == context_tasks[None, :]
    is_context = shard_flags[my_index] == 1
    own_rank = jnp.maximum(shard_rank[my_index], 0)
    own_block = jnp.concatenate([keys_one, values_one], axis=-1)

    def fetch_rows(step, buffer):
        piece = spread_2(own_block, "samp", roots[step])
        return lax.dynamic_update_slice_in_dim(buffer, piece, step * sample_rows, 0)

    empty_rows = jnp.zeros((total_context, feature_rows, 2 * model_width), jnp.bfloat16)
    fetched = lax.fori_loop(0, context_shards, fetch_rows, empty_rows)
    context_keys = fetched[..., :model_width]
    context_values = fetched[..., model_width:]
    query_heads = split_heads(queries_one)
    key_heads = split_heads(context_keys)
    value_heads = split_heads(context_values)
    scores = (
        jnp.einsum("sfhd,cfhd->fhsc", query_heads, key_heads, preferred_element_type=jnp.float32)
        * score_scale
    )
    sample_prob = soft_weights(jnp.where(allowed[None, None], scores, MASKED))
    sample_weights = sample_prob.astype(jnp.bfloat16)
    mixed_one = join_heads(
        jnp.einsum(
            "fhsc,cfhd->sfhd", sample_weights, value_heads, preferred_element_type=jnp.float32
        )
    ).astype(jnp.bfloat16)
    residual_one = residual_zero + apply_weight(mixed_one, sample_mixer) + sample_offset
    normed_two, norm_two_back = jax.vjp(layer_norm, residual_one, second_gain, second_shift)
    active_two = normed_two.astype(jnp.bfloat16)
    queries_two, keys_two, values_two = project(active_two, feature_weight, feature_bias)
    all_keys, all_values = (
        lax.all_gather(keys_two, "feat", axis=1, tiled=True),
        lax.all_gather(values_two, "feat", axis=1, tiled=True),
    )
    mixed_two, feature_prob = feature_attend(queries_two, all_keys, all_values)
    residual_two = residual_one + apply_weight(mixed_two, feature_mixer) + feature_offset
    normed_three, norm_three_back = jax.vjp(layer_norm, residual_two, third_gain, third_shift)
    active_three = normed_three.astype(jnp.bfloat16)
    expanded = apply_weight(active_three, expand_weight) + expand_bias
    activated, gelu_back = jax.vjp(partial(jax.nn.gelu, approximate=False), expanded)
    hidden = activated.astype(jnp.bfloat16)
    layer_output = (residual_two + apply_weight(hidden, reduce_weight) + reduce_bias).astype(
        jnp.bfloat16
    )
    grad_out = cotangent.astype(jnp.float32)
    grad_branch = cotangent
    reduce_bias_grad = column_sum(grad_branch)
    reduce_weight_grad = weight_grad(hidden, grad_branch)
    grad_hidden = input_back(grad_branch, reduce_weight).astype(jnp.bfloat16)
    grad_expanded = gelu_back(grad_hidden.astype(jnp.float32))[0].astype(jnp.bfloat16)
    expand_bias_grad = column_sum(grad_expanded)
    expand_weight_grad = weight_grad(active_three, grad_expanded)
    grad_norm, third_gain_grad, third_shift_grad = norm_three_back(
        input_back(grad_expanded, expand_weight)
    )
    grad_two = grad_out + grad_norm
    grad_branch = grad_two.astype(jnp.bfloat16)
    feature_offset_grad = column_sum(grad_branch)
    feature_mixer_grad = weight_grad(mixed_two, grad_branch)
    grad_mixed = input_back(grad_branch, feature_mixer).astype(jnp.bfloat16)
    grad_queries, grad_keys, grad_values = feature_grads(
        queries_two, all_keys, all_values, feature_prob, grad_mixed
    )
    own_key_grads, own_value_grads = (
        lax.psum_scatter(grad_keys, "feat", scatter_dimension=1, tiled=True),
        lax.psum_scatter(grad_values, "feat", scatter_dimension=1, tiled=True),
    )
    grad_project = jnp.concatenate(
        [
            grad_queries.astype(jnp.bfloat16),
            own_key_grads.astype(jnp.bfloat16),
            own_value_grads.astype(jnp.bfloat16),
        ],
        axis=-1,
    )
    feature_weight_grad = weight_grad(active_two, grad_project)
    feature_bias_grad = jnp.concatenate(
        [
            column_sum(grad_project[..., :model_width]),
            column_sum(grad_project[..., 2 * model_width :]),
        ]
    )
    grad_norm, second_gain_grad, second_shift_grad = norm_two_back(
        input_back(grad_project, feature_weight)
    )
    grad_one = grad_two + grad_norm
    grad_branch = grad_one.astype(jnp.bfloat16)
    sample_offset_grad = column_sum(grad_branch)
    sample_mixer_grad = weight_grad(mixed_one, grad_branch)
    grad_heads = split_heads(input_back(grad_branch, sample_mixer).astype(jnp.bfloat16))
    grad_weights = jnp.einsum(
        "sfhd,cfhd->fhsc", grad_heads, value_heads, preferred_element_type=jnp.float32
    )
    inner_sum = jnp.sum(sample_prob * grad_weights, axis=-1, keepdims=True)
    grad_scores = (sample_prob * (grad_weights - inner_sum)).astype(jnp.bfloat16)
    grad_queries = (
        join_heads(
            jnp.einsum(
                "fhsc,cfhd->sfhd", grad_scores, key_heads, preferred_element_type=jnp.float32
            )
        )
        * score_scale
    ).astype(jnp.bfloat16)
    key_terms = (
        join_heads(
            jnp.einsum(
                "fhsc,sfhd->cfhd", grad_scores, query_heads, preferred_element_type=jnp.float32
            )
        )
        * score_scale
    )
    value_terms = join_heads(
        jnp.einsum(
            "fhsc,sfhd->cfhd", sample_weights, grad_heads, preferred_element_type=jnp.float32
        )
    )
    term_block = jnp.concatenate([key_terms, value_terms], axis=-1)
    summed_terms = lax.psum_scatter(term_block, "samp", scatter_dimension=0, tiled=True)
    summed_rows = lax.all_gather(summed_terms.astype(jnp.bfloat16), "samp", axis=0, tiled=True)
    own_grads = lax.dynamic_slice_in_dim(summed_rows, own_rank * sample_rows, sample_rows, 0)
    own_grads = jnp.where(is_context, own_grads, jnp.zeros_like(own_grads))
    grad_project = jnp.concatenate([grad_queries, own_grads], axis=-1)
    sample_weight_grad = weight_grad(active_one, grad_project)
    sample_bias_grad = jnp.concatenate(
        [column_sum(grad_queries), column_sum(own_grads[..., model_width:])]
    )
    grad_norm, first_gain_grad, first_shift_grad = norm_one_back(
        input_back(grad_project, sample_weight)
    )
    input_grad = (grad_one + grad_norm).astype(jnp.bfloat16)
    summed = lax.psum(
        (
            first_gain_grad,
            first_shift_grad,
            sample_weight_grad,
            sample_bias_grad,
            sample_mixer_grad,
            sample_offset_grad,
            second_gain_grad,
            second_shift_grad,
            feature_weight_grad,
            feature_bias_grad,
            feature_mixer_grad,
            feature_offset_grad,
            third_gain_grad,
            third_shift_grad,
            expand_weight_grad,
            expand_bias_grad,
            reduce_weight_grad,
            reduce_bias_grad,
        ),
        "feat",
    )
    shares = (
        lax.psum_scatter(summed[0], "samp", scatter_dimension=0, tiled=True),
        lax.psum_scatter(summed[1], "samp", scatter_dimension=0, tiled=True),
        lax.psum_scatter(summed[2], "samp", scatter_dimension=0, tiled=True),
        lax.psum_scatter(summed[3], "samp", scatter_dimension=0, tiled=True),
        lax.psum_scatter(summed[4], "samp", scatter_dimension=0, tiled=True),
        lax.psum_scatter(summed[5], "samp", scatter_dimension=0, tiled=True),
        lax.psum_scatter(summed[6], "samp", scatter_dimension=0, tiled=True),
        lax.psum_scatter(summed[7], "samp", scatter_dimension=0, tiled=True),
        lax.psum_scatter(summed[8], "samp", scatter_dimension=0, tiled=True),
        lax.psum_scatter(summed[9], "samp", scatter_dimension=0, tiled=True),
        lax.psum_scatter(summed[10], "samp", scatter_dimension=0, tiled=True),
        lax.psum_scatter(summed[11], "samp", scatter_dimension=0, tiled=True),
        lax.psum_scatter(summed[12], "samp", scatter_dimension=0, tiled=True),
        lax.psum_scatter(summed[13], "samp", scatter_dimension=0, tiled=True),
        lax.psum_scatter(summed[14], "samp", scatter_dimension=0, tiled=True),
        lax.psum_scatter(summed[15], "samp", scatter_dimension=0, tiled=True),
        lax.psum_scatter(summed[16], "samp", scatter_dimension=0, tiled=True),
        lax.psum_scatter(summed[17], "samp", scatter_dimension=0, tiled=True),
    )
    return (
        layer_output,
        input_grad,
        shares[0],
        shares[1],
        shares[2],
        shares[3],
        shares[4],
        shares[5],
        shares[6],
        shares[7],
        shares[8],
        shares[9],
        shares[10],
        shares[11],
        shares[12],
        shares[13],
        shares[14],
        shares[15],
        shares[16],
        shares[17],
    )


def solution(mesh):
    if mesh.shape["samp"] == 8 and mesh.shape["feat"] == 4:
        return solution_small(mesh)
    return jax.shard_map(
        local_large,
        mesh=mesh,
        in_specs=(
            P("samp", "feat", None),
            P(),
            P(),
            P(),
            P(),
            P(),
            P(),
            P(),
            P(),
            P(),
            P(),
            P(),
            P(),
            P(),
            P(),
            P(),
            P(),
            P(),
            P(),
            P(),
            P(),
            P("samp", "feat", None),
        ),
        out_specs=(
            P("samp", "feat", None),
            P("samp", "feat", None),
            P("samp"),
            P("samp"),
            P("samp", None),
            P("samp"),
            P("samp", None),
            P("samp"),
            P("samp"),
            P("samp"),
            P("samp", None),
            P("samp"),
            P("samp", None),
            P("samp"),
            P("samp"),
            P("samp"),
            P("samp", None),
            P("samp"),
            P("samp", None),
            P("samp"),
        ),
        check_vma=False,
    )


def solution_small(mesh):
    mesh = jax.sharding.Mesh(mesh.devices.reshape(2, 4, 4), ("half", "quad", "feat"))
    tokens, copied = P(SAMP, "feat", None), P()
    vector, matrix = P(SAMP), P(SAMP, None)
    return jax.shard_map(
        local_small,
        mesh=mesh,
        in_specs=(tokens,) + (copied,) * 20 + (tokens,),
        out_specs=(
            tokens, tokens, vector, vector, matrix, vector, matrix, vector,
            vector, vector, matrix, vector, matrix, vector,
            vector, vector, matrix, vector, matrix, vector,
        ),
        check_vma=False,
    )
```

```python
from functools import partial

import jax
import jax.numpy as jnp
from jax import lax
from jax.experimental import pallas as pl
from jax.experimental.pallas import tpu as pltpu
from jax.sharding import PartitionSpec as P

HEADS = 8
HEAD_DIM = 64
EPS = 1e-05
MASKED = -1000000000.0
SCALE = HEAD_DIM ** (-0.5)
QUAD = 4 * HEAD_DIM
BF = jnp.bfloat16
F32 = jnp.float32


def mm(a, b, ca=1, cb=0):
    return lax.dot_general(a, b, (((ca,), (cb,)), ((), ())), preferred_element_type=F32)


def norm_parts(values):
    center = jnp.mean(values, axis=-1, keepdims=True)
    spread = values - center
    variance = jnp.mean(spread * spread, axis=-1, keepdims=True)
    inverse = lax.rsqrt(variance + EPS)
    return spread * inverse, inverse


def norm_back(grad, unit, inverse, gain):
    scaled = grad * gain
    first = jnp.mean(scaled, axis=-1, keepdims=True)
    second = jnp.mean(scaled * unit, axis=-1, keepdims=True)
    return (scaled - first - unit * second) * inverse


def lane_ids(rows):
    return lax.broadcasted_iota(jnp.int32, (rows, 128), 1)


def group_reduce(values, op, fill):
    rows = values.shape[0]
    low = lane_ids(rows) < HEAD_DIM
    outs = []
    for t in range(values.shape[1] // 128):
        tile = values[:, t * 128 : (t + 1) * 128]
        left = op(jnp.where(low, tile, fill), axis=1, keepdims=True)
        right = op(jnp.where(low, fill, tile), axis=1, keepdims=True)
        outs.append(jnp.where(low, left, right))
    return jnp.concatenate(outs, axis=1)


def head_masks(dtype):
    lanes = lax.broadcasted_iota(jnp.int32, (1, QUAD), 1) // HEAD_DIM
    return [jnp.where(lanes == h, 1.0, 0.0).astype(dtype) for h in range(4)]


def stack_heads(part, masks):
    return jnp.concatenate([part * m for m in masks], axis=0)


def pick_heads(stacked, masks):
    rows = stacked.shape[0] // 4
    total = stacked[:rows] * masks[0]
    for h in range(1, 4):
        total = total + stacked[h * rows : (h + 1) * rows] * masks[h]
    return total


def attend(q, k, v, masks, allow):
    outs, probs = [], []
    for quad in range(2):
        cols = slice(quad * QUAD, (quad + 1) * QUAD)
        scores = mm(q[:, cols], stack_heads(k[:, cols], masks), 1, 1)
        if allow is not None:
            scores = jnp.where(allow, scores, MASKED)
        raised = jnp.exp(scores - group_reduce(scores, jnp.max, -jnp.inf))
        prob = raised / group_reduce(raised, jnp.sum, 0.0)
        outs.append(mm(prob.astype(BF), stack_heads(v[:, cols], masks)))
        probs.append(prob)
    return jnp.concatenate(outs, axis=1), jnp.concatenate(probs, axis=1)


def attend_back(q, k, v, prob, grad, masks, masks32):
    dqs, dks, dvs = [], [], []
    for quad in range(2):
        cols = slice(quad * QUAD, (quad + 1) * QUAD)
        p, g = prob[:, cols], grad[:, cols]
        back = mm(g, stack_heads(v[:, cols], masks), 1, 1)
        inner = group_reduce(p * back, jnp.sum, 0.0)
        gs = (p * (back - inner)).astype(BF)
        dqs.append(mm(gs, stack_heads(k[:, cols], masks)) * SCALE)
        dks.append(pick_heads(mm(gs, q[:, cols], 0, 0), masks32))
        dvs.append(pick_heads(mm(p.astype(BF), g, 0, 0), masks32))
    join = lambda parts: jnp.concatenate(parts, axis=1).astype(BF)
    return join(dqs), join(dks), join(dvs)


def swap_matrix(rows=16):
    n = rows * 16
    r = lax.broadcasted_iota(jnp.int32, (n, n), 0)
    c = lax.broadcasted_iota(jnp.int32, (n, n), 1)
    return jnp.where((r // rows == c % 16) & (r % rows == c // 16), 1.0, 0.0).astype(BF)


def swap(matrix, values, back=False):
    return mm(matrix, values, 0 if back else 1, 0).astype(BF)


def gelu_parts(u):
    cdf = 0.5 * (1.0 + lax.erf(u * (2.0**-0.5)))
    density = jnp.exp(u * u * -0.5) * 0.3989422804014327
    return cdf, density


def col_sum(values):
    return jnp.sum(values.astype(F32), axis=0, keepdims=True)


def turn_in(x_ref, out_ref):
    matrix = swap_matrix()
    for d in range(4):
        rows = x_ref[d * 256 : (d + 1) * 256]
        out_ref[:, d] = swap(matrix, rows).reshape(16, 16, 512)


def turn_out(got_ref, out_ref):
    matrix = swap_matrix()
    for d in range(4):
        out_ref[d * 256 : (d + 1) * 256] = swap(matrix, got_ref[:, d].reshape(256, 512))


def each_feature(body):
    lax.fori_loop(0, 4, lambda e, carry: (body(e), carry)[1], 0)


def project_queries(x_ref, gain_ref, shift_ref, w_ref, b_ref, act_ref, q_ref):
    def body(e):
        unit, _ = norm_parts(x_ref[:, e].reshape(256, 512).astype(F32))
        act = (unit * gain_ref[...] + shift_ref[...]).astype(BF)
        act_ref[e] = act
        q = (mm(act, w_ref[:, :512]) + b_ref[:, :512]).astype(BF)
        q_ref[e] = q * jnp.asarray(SCALE, BF)

    each_feature(body)


def forward_one(
    me_ref, q_ref, own_ref, got_ref, tasks_ref, context_ref, gain_ref, shift_ref, w_ref, b_ref,
    oa_ref, ob_ref, c_ref, cact_ref, k_ref, v_ref, p_ref,
):
    here = me_ref[1] == me_ref[2]
    masks = head_masks(BF)
    allow = tasks_ref[...] == context_ref[...]

    @pl.when(here)
    def _():
        c_ref[...] = own_ref[...]

    @pl.when(jnp.logical_not(here))
    def _():
        c_ref[...] = got_ref[...]

    unit, _ = norm_parts(c_ref[...].reshape(256, 512).astype(F32))
    act = (unit * gain_ref[...] + shift_ref[...]).astype(BF)
    cact_ref[...] = act.reshape(4, 64, 512)
    kv = mm(act, w_ref[:, 512:])
    k_ref[...] = kv[:, :512].astype(BF).reshape(4, 64, 512)
    v_ref[...] = (kv[:, 512:] + b_ref[:, 512:]).astype(BF).reshape(4, 64, 512)

    def body(e):
        out, prob = attend(q_ref[e], k_ref[e], v_ref[e], masks, allow)
        out = out.reshape(4, 4, 2, 8, 512)
        oa_ref[:, :, e] = out[:, :, 0].astype(BF)
        ob_ref[:, :, e] = out[:, :, 1].astype(BF)
        p_ref[e] = prob

    each_feature(body)


HALF = 512


def middle(me_ref, *refs):
    (
        o1_ref, x0, x1, x2, x3, c0, c1, c2, c3,
        off1_ref, g2_ref, s2_ref, bf_ref, off2_ref, g3_ref, s3_ref, be_ref, br_ref,
    ) = refs[:18]
    weights_hbm = refs[18:23]
    refs = refs[-42:]
    gb1_ref, vec_ref, bias_ref = refs[:3]
    outs_hbm, kept_hbm = refs[3:6], refs[6:14]
    wm1_ref, wf_ref, wm2_ref, we_ref, wr_ref = refs[14:19]
    kept = refs[19:27]
    a2_ref, dqkv_ref, o2_ref, gb2_ref, a3_ref, gu_ref, hid_ref, gb3_ref = kept
    (
        o_scr, q_scr, k_scr, v_scr, p_scr, e_scr, gs_scr, go_scr, out_scr, back_scr,
        out0, out2, out13, in_sems, out_sems,
    ) = refs[27:]
    loads = [
        pltpu.make_async_copy(source, target, in_sems.at[i])
        for i, (source, target) in enumerate(zip(weights_hbm, refs[14:19]))
    ]
    for load in loads:
        load.start()
    stores = []

    def store(source, target, i):
        stores.append(pltpu.make_async_copy(source, target, out_sems.at[i]))
        stores[-1].start()

    def keep(ref):
        i = next(j for j in range(8) if kept[j] is ref)
        store(ref, kept_hbm[i], i)

    me = me_ref[0]
    matrix = swap_matrix(8)
    masks, masks32 = head_masks(BF), head_masks(F32)
    for f in range(4):
        o_scr[f] = swap(matrix, o1_ref[:, f].reshape(128, 512), True)

    def gather(*refs):
        return jnp.concatenate(
            [ref[s * 16 : (s + 1) * 16] for s in range(8) for ref in refs], axis=0
        )

    def scatter(values, *refs):
        for s in range(8):
            for d, ref in enumerate(refs):
                at = (s * 4 + d) * 16
                ref[s * 16 : (s + 1) * 16] = values[at : at + 16]

    def each_sample(body):
        def step(i, carry):
            for j in range(SAMPLE_UNROLL):
                rows = pl.ds(pl.multiple_of((i * SAMPLE_UNROLL + j) * 64, 64), 64)
                for quad in range(2):
                    body(rows, slice(quad * QUAD, (quad + 1) * QUAD))
            return carry

        lax.fori_loop(0, 8 // SAMPLE_UNROLL, step, 0)

    attended = gather(*(o_scr.at[d ^ me] for d in range(4)))
    gb3_ref[...] = gather(c0, c1, c2, c3)
    keep(gb3_ref)
    loads[0].wait()
    r1 = gather(x0, x1, x2, x3).astype(F32) + mm(attended, wm1_ref[...]) + off1_ref[...]
    unit2, inv2 = norm_parts(r1)
    a2_ref[...] = (unit2 * g2_ref[...] + s2_ref[...]).astype(BF)
    keep(a2_ref)
    loads[1].wait()
    q = (mm(a2_ref[...], wf_ref[:, :512]) + bf_ref[:, :512]).astype(BF)
    q_scr[...] = q * jnp.asarray(SCALE, BF)
    k_scr[...] = mm(a2_ref[...], wf_ref[:, 512:1024]).astype(BF)
    v_scr[...] = (mm(a2_ref[...], wf_ref[:, 1024:]) + bf_ref[:, 512:]).astype(BF)

    def score(rows, cols):
        p_scr[rows, cols] = mm(q_scr[rows, cols], stack_heads(k_scr[rows, cols], masks), 1, 1)

    each_sample(score)
    for i in range(4):
        rows = slice(i * 128, (i + 1) * 128)
        scores = p_scr[rows]
        raised = jnp.exp(scores - group_reduce(scores, jnp.max, -jnp.inf))
        p_scr[rows] = raised / group_reduce(raised, jnp.sum, 0.0)

    def mix(rows, cols):
        o2_ref[rows, cols] = mm(
            p_scr[rows, cols].astype(BF), stack_heads(v_scr[rows, cols], masks)
        ).astype(BF)

    each_sample(mix)
    keep(o2_ref)
    loads[2].wait()
    r2 = r1 + mm(o2_ref[...], wm2_ref[...]) + off2_ref[...]
    unit3, inv3 = norm_parts(r2)
    a3_ref[...] = (unit3 * g3_ref[...] + s3_ref[...]).astype(BF)
    keep(a3_ref)
    loads[3].wait()
    loads[4].wait()
    out_scr[...] = r2 + br_ref[...]
    back_scr[...] = jnp.zeros((HALF, 512), F32)

    def expand(b, carry):
        cols = pl.ds(pl.multiple_of(b * WIDE, WIDE), WIDE)
        u = mm(a3_ref[...], we_ref[:, cols]) + be_ref[:, cols]
        cdf, density = gelu_parts(u)
        hidden = (u * cdf).astype(BF)
        hid_ref[:, cols] = hidden
        gh = mm(gb3_ref[...], wr_ref[cols, :], 1, 1).astype(BF).astype(F32)
        gu = (gh * (cdf + u * density)).astype(BF)
        gu_ref[:, cols] = gu
        bias_ref[:, cols] = col_sum(gu)
        out_scr[...] += mm(hidden, wr_ref[cols, :])
        back_scr[...] += mm(gu, we_ref[:, cols], 1, 1)
        return carry

    lax.fori_loop(0, 2048 // WIDE, expand, 0, unroll=EXPAND_UNROLL)
    keep(hid_ref)
    keep(gu_ref)
    scatter(out_scr[...].astype(BF), out0, out13.at[0], out2, out13.at[1])
    rows = pl.ds(pl.multiple_of(me_ref[8] * 128, 128), 128)
    store(out0, outs_hbm[0].at[rows], 8)
    store(out2, outs_hbm[1].at[rows], 9)
    store(out13, outs_hbm[2].at[:, rows], 10)
    back, cot = back_scr[...], gb3_ref[...]
    vecs = [col_sum(back * unit3), col_sum(back)]
    gr2 = cot.astype(F32) + norm_back(back, unit3, inv3, g3_ref[...])
    gb2_ref[...] = gr2.astype(BF)
    keep(gb2_ref)
    go_scr[...] = mm(gb2_ref[...], wm2_ref[...], 1, 1).astype(BF)

    def weigh(rows, cols):
        e_scr[rows, cols] = mm(go_scr[rows, cols], stack_heads(v_scr[rows, cols], masks), 1, 1)

    each_sample(weigh)
    for i in range(4):
        rows = slice(i * 128, (i + 1) * 128)
        prob, grad = p_scr[rows], e_scr[rows]
        inner = group_reduce(prob * grad, jnp.sum, 0.0)
        gs_scr[rows] = (prob * (grad - inner)).astype(BF)

    def spread(rows, cols):
        gs, at = gs_scr[rows, cols], cols.start
        dq = mm(gs, stack_heads(k_scr[rows, cols], masks)) * SCALE
        dqkv_ref[rows, at : at + QUAD] = dq.astype(BF)
        dk = pick_heads(mm(gs, q_scr[rows, cols], 0, 0), masks32)
        dqkv_ref[rows, 512 + at : 512 + at + QUAD] = dk.astype(BF)
        dv = pick_heads(mm(p_scr[rows, cols].astype(BF), go_scr[rows, cols], 0, 0), masks32)
        dqkv_ref[rows, 1024 + at : 1024 + at + QUAD] = dv.astype(BF)

    each_sample(spread)
    keep(dqkv_ref)
    dqkv = dqkv_ref[...]
    back = mm(dqkv, wf_ref[...], 1, 1)
    vecs += [col_sum(back * unit2), col_sum(back)]
    gr1 = gr2 + norm_back(back, unit2, inv2, g2_ref[...])
    scatter(gr1.astype(BF), *(o_scr.at[d ^ me] for d in range(4)))
    for f in range(4):
        gb1_ref[:, f] = swap(matrix, o_scr[f]).reshape(4, 4, 8, 512)
    vecs += [
        col_sum(gb2_ref[...]), col_sum(cot), col_sum(dqkv[:, :512]), col_sum(dqkv[:, 1024:])
    ]
    vec_ref[...] = jnp.concatenate(vecs, axis=0)
    for copy in stores:
        copy.wait()


SAMPLE_UNROLL = 8
EXPAND_UNROLL = False
WIDE = 512


def backward_one(
    ga_ref, gb_ref, c_ref, q_ref, k_ref, v_ref, p_ref, w_ref, wm_ref,
    gb1_ref, dq_ref, dkv_ref, term_ref, vec_ref,
    g_scr,
):
    masks, masks32 = head_masks(BF), head_masks(F32)
    vec_ref[...] = jnp.zeros((8, 512), F32)

    def body(e):
        g_scr[:, :, 0] = ga_ref[:, :, e]
        g_scr[:, :, 1] = gb_ref[:, :, e]
        gb1 = g_scr[...].reshape(256, 512)
        gb1_ref[e] = gb1
        go = mm(gb1, wm_ref[...], 1, 1).astype(BF)
        dq, dk, dv = attend_back(q_ref[e], k_ref[e], v_ref[e], p_ref[e], go, masks, masks32)
        dq_ref[e], dkv_ref[e, :, :512], dkv_ref[e, :, 512:] = dq, dk, dv
        vec_ref[2:3] += col_sum(gb1)
        vec_ref[3:4] += col_sum(dq)

    each_feature(body)
    dkv = dkv_ref[...].reshape(256, 1024)
    term = mm(dkv, w_ref[:, 512:], 1, 1)
    term_ref[...] = term.astype(BF).reshape(4, 64, 512)
    unit, _ = norm_parts(c_ref[...].reshape(256, 512).astype(F32))
    vec_ref[0:1], vec_ref[1:2] = col_sum(term * unit), col_sum(term)
    vec_ref[4:5] = col_sum(dkv[:, 512:])


def backward_input(
    me_ref, gb1_ref, x_ref, dq_ref, term_ref, got_ref, vec1_ref, gain_ref, w_ref,
    grad_ref, vec_ref, a_scr,
):
    here, quad = me_ref[1] == me_ref[2], me_ref[3]
    gain = gain_ref[...]
    vec_ref[...] = vec1_ref[...]

    def body(e):
        back = mm(dq_ref[e], w_ref[:, :512], 1, 1)
        unit, inverse = norm_parts(x_ref[:, e].reshape(256, 512).astype(F32))
        vec_ref[0:1] += col_sum(back * unit)
        vec_ref[1:2] += col_sum(back)
        a_scr[...] = back.reshape(4, 64, 512)

        @pl.when(here)
        def _():
            a_scr[quad] += term_ref[e].astype(F32) + got_ref[e].astype(F32)

        back = a_scr[...].reshape(256, 512)
        grad = gb1_ref[e].astype(F32) + norm_back(back, unit, inverse, gain)
        grad_ref[:, e] = grad.astype(BF).reshape(4, 64, 512)

    each_feature(body)


def split(got_ref, out_ref):
    rest = jnp.sum(got_ref[...], axis=0, keepdims=True)
    out_ref[...] = jnp.zeros_like(out_ref)
    for i in range(3):
        term = rest.astype(BF)
        out_ref[i : i + 1] = term
        rest = rest - term.astype(F32)


def place(me_ref, b0, b1, b2, b3, out_ref):
    for d, ref in enumerate((b0, b1, b2, b3)):
        out_ref[d ^ me_ref[0]] = ref[...]


def lay_out(me_ref, read, order, *pairs):
    core, xx, yy, zz = me_ref[4], me_ref[5], me_ref[6], me_ref[7]
    for bits in range(16):
        index = tuple((bits >> i) & 1 for i in (3, 2, 1, 0))
        dx, dy, d1, d2 = (index[order.index(name)] for name in ("x", "y", "z", "w"))
        shard = (zz ^ d1 ^ (2 * d2)) * 2 + (yy ^ dy)
        for keep_ref, send_ref, start, rows in pairs:
            keep_ref[index] = read(2 * core + (dx ^ xx), shard, start, rows)
            send_ref[index] = read(2 * (1 - core) + (dx ^ xx), shard, start, rows)


def read_units(scr):
    def read(unit, shard, start, rows):
        return scr[unit, pl.ds(pl.multiple_of(shard * 64 + start, rows), rows)]

    return read


def over_tokens(*pairs):
    return sum(mm(a[...], b[...], 0, 0) for a, b in pairs).astype(BF)


def grads_reduce(me_ref, hida_ref, hidb_ref, gba_ref, gbb_ref, keep_ref, send_ref, scr):
    step = pl.program_id(0)
    start = pl.multiple_of(step * 512, 512)
    scr[pl.ds(start, 512)] = over_tokens((hida_ref, gba_ref), (hidb_ref, gbb_ref))

    def read(unit, shard, start, rows):
        return scr[pl.ds(pl.multiple_of(shard * 256 + unit * 64, 64), 64)]

    @pl.when(step == 3)
    def _():
        lay_out(me_ref, read, "zxyw", (keep_ref, send_ref, 0, 64))


def grads_expand(me_ref, acta_ref, actb_ref, gua_ref, gub_ref, keep_ref, send_ref, scr):
    step = pl.program_id(0)
    scr[step] = over_tokens((acta_ref, gua_ref), (actb_ref, gub_ref))

    @pl.when(step == 3)
    def _():
        lay_out(me_ref, read_units(scr), "yxzw", (keep_ref, send_ref, 0, 64))


def grads_feature(
    me_ref, acta_ref, actb_ref, dqa_ref, dqb_ref, oa_ref, ob_ref, gba_ref, gbb_ref,
    keep_ref, send_ref, scr,
):
    step = pl.program_id(0)

    @pl.when(step < 3)
    def _():
        scr[step] = over_tokens((acta_ref, dqa_ref), (actb_ref, dqb_ref))

    @pl.when(step == 3)
    def _():
        scr[3] = over_tokens((oa_ref, gba_ref), (ob_ref, gbb_ref))
        lay_out(me_ref, read_units(scr), "xyzw", (keep_ref, send_ref, 0, 64))


def grads_sample(
    me_ref, act_ref, dq_ref, cact_ref, dkv_ref, oa_ref, ga_ref, ob_ref, gb_ref,
    keepa_ref, senda_ref, keepb_ref, sendb_ref, scr,
):
    scr[0] = mm(act_ref[...], dq_ref[...], 0, 0).astype(BF)
    scr[1] = mm(cact_ref[...], dkv_ref[:, :512], 0, 0).astype(BF)
    scr[2] = mm(cact_ref[...], dkv_ref[:, 512:], 0, 0).astype(BF)
    total = mm(oa_ref[...], ga_ref[...], 0, 0) + mm(ob_ref[...], gb_ref[...], 0, 0)
    scr[3] = total.astype(BF)
    lay_out(me_ref, read_units(scr), "xyzw", (keepa_ref, senda_ref, 0, 32))
    lay_out(me_ref, read_units(scr), "xyzw", (keepb_ref, sendb_ref, 32, 32))


def spec(shape, index=None):
    return pl.BlockSpec(shape, index if index is not None else (lambda *a: (0,) * len(shape)))


def sds(shape, dtype=BF):
    return jax.ShapeDtypeStruct(shape, dtype)


def big(shape, dtype=BF):
    return pltpu.HBM(shape, dtype)


def outside(array):
    if array.size * array.dtype.itemsize < 1 << 18:
        return array
    return pltpu.with_memory_space_constraint(array, pltpu.HBM)


def params(limit):
    return pltpu.CompilerParams(vmem_limit_bytes=limit << 20)


def row(vector):
    return vector.reshape(1, -1)


def cost(microseconds):
    return pl.CostEstimate(
        flops=int(microseconds * 1.1e9), transcendentals=0, bytes_accessed=int(microseconds * 2e6)
    )


def whole_block(out):
    shape = out.shape
    return pl.BlockSpec(shape, lambda i: (0,) * len(shape))


def whole(kernel, name, limit, outs, scratch, *inputs, steps=1, time=3):
    arrays, specs = [], []
    for entry in inputs:
        if not isinstance(entry, tuple) and entry.ndim == 1:
            arrays.append(entry)
            specs.append(pl.BlockSpec(memory_space=pltpu.SMEM))
            continue
        array, block, index = entry if isinstance(entry, tuple) else (entry, None, None)
        arrays.append(outside(array))
        block = array.shape if block is None else block
        index = (0,) * array.ndim if index is None else index
        if not callable(index):
            index = lambda i, index=index: index
        specs.append(pl.BlockSpec(block, index))
    return pl.pallas_call(
        kernel,
        grid=(steps,),
        out_shape=outs,
        in_specs=specs,
        out_specs=jax.tree.map(whole_block, outs, is_leaf=lambda o: hasattr(o, "dtype")),
        scratch_shapes=scratch,
        compiler_params=params(limit),
        cost_estimate=cost(time),
        name=name,
    )(*arrays)


def shuffle(value, axis, mask):
    size = lax.axis_size(axis)
    return lax.ppermute(value, axis, [(i, i ^ mask) for i in range(size)])


SAMP = ("half", "quad")
CORE, X, Y, Z, W = ("feat", 1), ("feat", 2), ("quad", 1), ("quad", 2), ("half", 1)


def at(stacked, index, axis=0):
    return lax.dynamic_index_in_dim(stacked, index, axis, keepdims=False)


def fence(tree):
    return lax.optimization_barrier(tree)


def plus(a, b):
    return (a.astype(F32) + b.astype(F32)).astype(BF)


class Chain:
    def __init__(self, keep, sent, dims):
        self.keep, self.sent, self.dims = keep, sent, (CORE,) + dims

    def start(self):
        return shuffle(self.sent, *self.dims[0])

    def take(self, got):
        self.dims = self.dims[1:]
        if self.dims:
            self.keep, self.sent = plus(self.keep[0], got[0]), plus(self.keep[1], got[1])
        else:
            self.keep = plus(self.keep, got)


def together(chains, make=lambda: ()):
    got = [chain.start() for chain in chains]
    got, other = fence((got, make()))
    for chain, value in zip(chains, got):
        chain.take(value)
    return other


def local_small(
    layer_input, segment_ids, context_flags,
    first_gain, first_shift, sample_weight, sample_bias, sample_mixer, sample_offset,
    second_gain, second_shift, feature_weight, feature_bias, feature_mixer, feature_offset,
    third_gain, third_shift, expand_weight, expand_bias, reduce_weight, reduce_bias, cotangent,
):
    half, quad, feat = (lax.axis_index(name) for name in ("half", "quad", "feat"))
    samp = half * 4 + quad
    core, xx = feat % 2, feat // 2
    flags = context_flags.reshape(8, 64)[:, 0]
    root = jnp.sum(jnp.where(flags == 1, jnp.arange(8, dtype=jnp.int32), 0))
    me = [feat, half, root // 4, root % 4, core, xx, samp % 2, samp // 2]
    me = jnp.stack(me).astype(jnp.int32)

    turned = whole(turn_in, "turn_in", 8, big((16, 4, 16, 512)), [], layer_input.reshape(1024, 512))
    turned, layer_input, cotangent = fence((turned, layer_input, cotangent))
    x_t = lax.all_to_all(turned.reshape(4, 4, 64, 512), "quad", 0, 0)
    x4, cot4 = layer_input.reshape(4, 256, 512), cotangent.reshape(4, 256, 512)
    block = lambda value, d: at(value, feat ^ d)
    to_core = jnp.stack([block(x4, 1), block(cot4, 1), block(x4, 3), block(cot4, 3)])
    from_core = shuffle(to_core, *CORE)
    x_far = shuffle(jnp.stack([block(x4, 2), from_core[2]]), *X)
    x_t, from_core, x_far = fence((x_t, from_core, x_far))
    cot_far = shuffle(jnp.stack([block(cot4, 2), from_core[3]]), *X)
    own_context = at(x_t, root % 4)
    got_context = shuffle(own_context, *W)
    act1, queries = whole(
        project_queries, "project_queries", 16, (big((4, 256, 512)), big((4, 256, 512))), [],
        x_t, row(first_gain), row(first_shift), sample_weight, row(sample_bias),
    )
    cot_far, got_context, q1 = fence((cot_far, got_context, queries))

    tasks = segment_ids.reshape(8, 64)
    context_tasks = jnp.concatenate([at(tasks, root)] * 4).reshape(1, 256)
    sent = big((4, 4, 4, 8, 512))
    four = sds((4, 64, 512))
    oa, ob, context, cact, k1, v1, p1 = whole(
        forward_one, "forward_one", 24,
        (sent, sent, four, four, four, four, big((4, 256, 512), F32)), [],
        me, q1, own_context, got_context, at(segment_ids.reshape(2, 256, 1), half), context_tasks,
        row(first_gain), row(first_shift), sample_weight, row(sample_bias), time=7,
    )

    def exchange(value):
        shape = value.shape
        value = value.reshape((16,) + shape[2:])
        return lax.all_to_all(value, ("quad", "feat"), 0, 0).reshape(shape)

    rows_in = [
        row(v)
        for v in (
            sample_offset, second_gain, second_shift, feature_bias, feature_offset, third_gain,
            third_shift, expand_bias, reduce_bias,
        )
    ]
    weights = [sample_mixer, feature_weight, feature_mixer, expand_weight, reduce_weight]

    def run_middle(half, attended, earlier):
        own = spec((None, 128, 512), lambda i, m: (m[0], m[8], 0))
        part = lambda n: spec((None, 128, 512), lambda i, m: (n, m[8], 0))
        outs = (sent, sds((8, 512), F32), sds((1, 2048), F32))
        blocks = ((256, 512), (256, 512), (2, 256, 512))
        kept = tuple((HALF, n) for n in (512, 1536, 512, 512, 512, 2048, 2048, 512))
        still = lambda shape: spec(shape, lambda i, m: (0,) * len(shape))
        far = pl.BlockSpec(memory_space=pl.ANY)
        vmem = lambda shape, dtype=BF: pltpu.VMEM(shape, dtype)
        rows, rows32 = vmem((HALF, 512)), vmem((HALF, 512), F32)
        return pl.pallas_call(
            middle,
            grid_spec=pltpu.PrefetchScalarGridSpec(
                num_scalar_prefetch=1,
                grid=(1,),
                in_specs=[still((4, 4, 4, 8, 512))]
                + [own, part(0), part(0), part(1), own, part(1), part(0), part(1)]
                + [still(r.shape) for r in rows_in]
                + [far] * (5 + len(earlier)),
                out_specs=[still(o.shape) for o in outs] + [far] * 11,
                scratch_shapes=[vmem(w.shape) for w in weights]
                + [vmem(shape) for shape in kept]
                + [
                    vmem((4, 128, 512)), rows, rows, rows, rows32, rows32, rows, rows, rows32,
                    rows32, vmem((128, 512)), vmem((128, 512)), vmem((2, 128, 512)),
                    pltpu.SemaphoreType.DMA((5,)), pltpu.SemaphoreType.DMA((11,)),
                ],
            ),
            out_shape=outs + tuple(big(shape) for shape in blocks + kept),
            input_output_aliases={24 + i: 3 + i for i in range(len(earlier))},
            compiler_params=params(44),
            cost_estimate=cost(30),
            name="middle",
        )(
            jnp.concatenate([me, jnp.full((1,), half, jnp.int32)]),
            *(
                outside(array)
                for array in (
                    attended, x4, from_core, x_far, x_far, cot4, from_core, cot_far, cot_far,
                    *rows_in, *weights, *earlier,
                )
            ),
        )

    oa_f, ob = fence((exchange(oa), ob))
    ob_f = exchange(ob)
    ga, vec_a, bias_a, *first = run_middle(0, oa_f, [])
    ob_f, ga, first = fence((ob_f, ga, first))
    ga_t = exchange(ga)
    gb, vec_b, bias_b, *second = run_middle(1, ob_f, first[:3])
    ga_t, gb, second = fence((ga_t, gb, second))
    out0, out2, out13 = second[:3]
    act2, dqkv, o2, gb2, act3, gu, hidden, gb3 = zip(first[3:], second[3:])
    gb_t = exchange(gb)
    vec2, bias2 = vec_a + vec_b, bias_a + bias_b

    parts = sds((2, 2, 2, 2, 64, 512))
    moving = lambda pair: [(a, (512, 512), lambda i: (0, i)) for a in pair]
    upto = lambda pair: [(a, (512, 512), lambda i: (0, jnp.minimum(i, 2))) for a in pair]
    units = [pltpu.VMEM((4, 512, 512), BF)]
    r_chain = Chain(
        *whole(
            grads_reduce, "grads_reduce", 16, (parts, parts), [pltpu.VMEM((2048, 512), BF)],
            me, *moving(hidden), *gb3, steps=4, time=6,
        ),
        (Z, X, Y, W),
    )
    e_chain = Chain(
        *whole(
            grads_expand, "grads_expand", 16, (parts, parts), units,
            me, *act3, *moving(gu), steps=4, time=6,
        ),
        (Y, X, Z, W),
    )
    f_chain = Chain(
        *whole(
            grads_feature, "grads_feature", 20, (parts, parts), units,
            me, *act2, *upto(dqkv), *o2, *gb2, steps=4, time=6,
        ),
        (X, Y, Z, W),
    )
    chains = [r_chain, e_chain, f_chain]
    near = shuffle(out13, *CORE)
    gb_t, near, kept = fence((gb_t, near, [(chain.keep, chain.sent) for chain in chains]))
    for chain, pair in zip(chains, kept):
        chain.keep, chain.sent = pair

    full = big((4, 256, 512))
    gb1, dq1, dkv, term, vec1 = together(
        chains,
        lambda: whole(
            backward_one, "backward_one", 32,
            (full, full, sds((4, 64, 1024)), four, sds((8, 512), F32)),
            [pltpu.VMEM((4, 4, 2, 8, 512), BF)],
            ga_t, gb_t, context, q1, k1, v1, p1, sample_weight, sample_mixer, time=10,
        ),
    )

    small = sds((2, 2, 2, 2, 32, 512))
    flat2 = lambda a: a.reshape(-1, a.shape[-1])
    grads = whole(
        grads_sample, "grads_sample", 20, (small,) * 4, units,
        me, *(flat2(a) for a in (act1, dq1, cact, dkv, oa, ga_t, ob, gb_t)),
    )
    got_term, (ak, as_, bk, bs) = together(chains, lambda: (shuffle(term, *W), grads))
    late = [Chain(ak, as_, (X, Y)), Chain(bk, bs, (X, Y))]
    grad_t, vec1 = together(
        late + chains,
        lambda: whole(
            backward_input, "backward_input", 24, (big((4, 4, 64, 512)), sds((8, 512), F32)),
            [pltpu.VMEM((4, 64, 512), F32)],
            me, gb1, x_t, dq1, term, got_term, vec1, row(first_gain), sample_weight,
        ),
    )

    owned = lambda v, n: v.reshape(-1, 8, n).transpose(1, 0, 2).reshape(8, -1)
    vectors = jnp.concatenate(
        [
            owned(vec2[:6], 64), vec2[6:].reshape(8, 128), bias2.reshape(8, 256),
            owned(vec1[:3], 64), vec1[3:5].reshape(8, 128),
        ],
        axis=1,
    )
    got, far, vectors = together(
        late + chains,
        lambda: (
            lax.all_to_all(grad_t, "quad", 0, 0),
            shuffle(jnp.stack([out2, near[1]]), *X),
            vectors,
        ),
    )
    vectors = lax.all_to_all(vectors, SAMP, 0, 0)
    input_grad = whole(
        turn_out, "turn_out", 8, sds((1024, 512)), [], got.reshape(16, 4, 16, 512)
    ).reshape(64, 16, 512)
    layer_output = whole(
        place, "place", 16, sds((4, 256, 512)), [], me, out0,
        (near, (None, 256, 512), (0, 0, 0)), (far, (None, 256, 512), (0, 0, 0)),
        (far, (None, 256, 512), (1, 0, 0)),
    ).reshape(64, 16, 512)
    vectors, input_grad, layer_output = together(
        late + chains, lambda: (vectors, input_grad, layer_output)
    )

    rows = jnp.concatenate([chain.keep for chain in late], axis=2)
    around_z = lambda value, mask: lax.ppermute(value, SAMP, [(j, j ^ mask) for j in range(8)])
    from_z = [around_z(rows[i // 2, i % 2], (0, 4, 2, 6)[i]) for i in (1, 2, 3)]
    vectors = whole(split, "split", 8, sds((24, 1088)), [], vectors)
    early = lax.all_gather(jnp.concatenate([chain.keep for chain in chains]), "feat")
    from_z, early, vectors = fence((from_z, early, vectors))
    total = rows[0, 0].astype(F32)
    for value in from_z:
        total = total + value.astype(F32)
    vectors = jnp.pad(vectors[:3].reshape(-1), (0, 8 * 512 - 3 * 1088)).reshape(8, 512)
    last = lax.all_gather(jnp.concatenate([total.astype(BF), vectors]), "feat")
    mine = last[:, 64:].reshape(4, -1).astype(F32)
    mine = sum(mine[:, i * 1088 : (i + 1) * 1088] for i in range(3))
    mine = (mine[0] + mine[1]) + (mine[2] + mine[3])

    units_of = lambda rows: [rows[i].astype(F32) for i in (0, 2, 1, 3)]
    reduce_grad = jnp.concatenate(units_of(early[:, :64]))
    expand, feature = units_of(early[:, 64:128]), units_of(early[:, 128:])
    sample = units_of(last[:, :64])

    gain3, shift3, gain2, shift2, off2, bias_r = (mine[i * 64 : (i + 1) * 64] for i in range(6))
    feature_b, expand_b = mine[384:512], mine[512:768]
    gain1, shift1, off1 = (mine[768 + i * 64 : 832 + i * 64] for i in range(3))
    sample_b = mine[960:1088]
    columns = lambda blocks: jnp.concatenate(blocks, axis=1)

    return (
        layer_output, input_grad,
        gain1, shift1, columns(sample[:3]), sample_b, sample[3], off1,
        gain2, shift2, columns(feature[:3]), feature_b, feature[3], off2,
        gain3, shift3, columns(expand), expand_b,
        reduce_grad, bias_r,
    )


def spread_2(block, axis, owner):
    block = jnp.where(lax.axis_index(axis) == owner, block, jnp.zeros_like(block))
    return lax.psum(block, axis)


def layer_norm(values, gain_row, shift_row):
    center = jnp.mean(values, axis=-1, keepdims=True)
    spread = values - center
    variance = jnp.mean(spread * spread, axis=-1, keepdims=True)
    return spread * lax.rsqrt(variance + EPS) * gain_row + shift_row


def apply_weight(active, weight):
    return jnp.einsum("sfd,de->sfe", active, weight, preferred_element_type=jnp.float32)


def input_back(grad_out, weight):
    return jnp.einsum("sfe,de->sfd", grad_out, weight, preferred_element_type=jnp.float32)


def weight_grad(active, grad_out):
    return jnp.einsum("sfd,sfe->de", active, grad_out, preferred_element_type=jnp.float32)


def column_sum(values):
    return jnp.sum(values.astype(jnp.float32), axis=(0, 1))


def project(active, weight, bias_row):
    model_width = active.shape[-1]
    joined = apply_weight(active, weight)
    queries = (joined[..., :model_width] + bias_row[:model_width]).astype(jnp.bfloat16)
    key_part = joined[..., model_width : 2 * model_width].astype(jnp.bfloat16)
    value_part = (joined[..., 2 * model_width :] + bias_row[model_width:]).astype(jnp.bfloat16)
    return (queries, key_part, value_part)


def split_heads(values):
    return values.reshape(values.shape[0], values.shape[1], HEADS, HEAD_DIM)


def join_heads(values):
    return values.reshape(values.shape[0], values.shape[1], HEADS * HEAD_DIM)


def soft_weights(scores):
    top_score = jnp.max(scores, axis=-1, keepdims=True)
    raised = jnp.exp(scores - top_score)
    return raised / jnp.sum(raised, axis=-1, keepdims=True)


def feature_attend(queries, key_part, value_part):
    score_scale = HEAD_DIM ** (-0.5)
    scores = (
        jnp.einsum(
            "sfhd,sghd->shfg",
            split_heads(queries),
            split_heads(key_part),
            preferred_element_type=jnp.float32,
        )
        * score_scale
    )
    probability = soft_weights(scores)
    mixed = jnp.einsum(
        "shfg,sghd->sfhd",
        probability.astype(jnp.bfloat16),
        split_heads(value_part),
        preferred_element_type=jnp.float32,
    )
    return (join_heads(mixed).astype(jnp.bfloat16), probability)


def feature_grads(queries, key_part, value_part, probability, grad_mixed):
    score_scale = HEAD_DIM ** (-0.5)
    grad_heads = split_heads(grad_mixed)
    grad_weights = jnp.einsum(
        "sfhd,sghd->shfg", grad_heads, split_heads(value_part), preferred_element_type=jnp.float32
    )
    inner_sum = jnp.sum(probability * grad_weights, axis=-1, keepdims=True)
    grad_scores = (probability * (grad_weights - inner_sum)).astype(jnp.bfloat16)
    grad_queries = (
        jnp.einsum(
            "shfg,sghd->sfhd",
            grad_scores,
            split_heads(key_part),
            preferred_element_type=jnp.float32,
        )
        * score_scale
    )
    grad_keys = (
        jnp.einsum(
            "shfg,sfhd->sghd", grad_scores, split_heads(queries), preferred_element_type=jnp.float32
        )
        * score_scale
    )
    grad_values = jnp.einsum(
        "shfg,sfhd->sghd",
        probability.astype(jnp.bfloat16),
        grad_heads,
        preferred_element_type=jnp.float32,
    )
    return (join_heads(grad_queries), join_heads(grad_keys), join_heads(grad_values))


def local_large(
    layer_input,
    segment_ids,
    context_flags,
    first_gain,
    first_shift,
    sample_weight,
    sample_bias,
    sample_mixer,
    sample_offset,
    second_gain,
    second_shift,
    feature_weight,
    feature_bias,
    feature_mixer,
    feature_offset,
    third_gain,
    third_shift,
    expand_weight,
    expand_bias,
    reduce_weight,
    reduce_bias,
    cotangent,
):
    sample_rows = layer_input.shape[0]
    feature_rows = layer_input.shape[1]
    model_width = layer_input.shape[2]
    score_scale = HEAD_DIM ** (-0.5)
    shard_count = lax.axis_size("samp")
    context_shards = shard_count // 8
    total_context = context_shards * sample_rows
    residual_zero = layer_input.astype(jnp.float32)
    normed_one, norm_one_back = jax.vjp(layer_norm, residual_zero, first_gain, first_shift)
    active_one = normed_one.astype(jnp.bfloat16)
    queries_one, keys_one, values_one = project(active_one, sample_weight, sample_bias)
    my_index = lax.axis_index("samp")
    shard_flags = context_flags.reshape(shard_count, sample_rows)[:, 0]
    shard_rank = jnp.cumsum(shard_flags) - 1
    shard_ids = jnp.arange(shard_count, dtype=jnp.int32)
    slot_ids = jnp.arange(context_shards, dtype=jnp.int32)
    root_hits = (shard_rank[None, :] == slot_ids[:, None]) & (shard_flags[None, :] == 1)
    roots = jnp.sum(jnp.where(root_hits, shard_ids[None, :], 0), axis=1)
    context_tasks = jnp.take(segment_ids.reshape(shard_count, sample_rows), roots, axis=0).reshape(
        total_context
    )
    local_tasks = lax.dynamic_slice_in_dim(segment_ids, my_index * sample_rows, sample_rows)
    allowed = local_tasks[:, None] == context_tasks[None, :]
    is_context = shard_flags[my_index] == 1
    own_rank = jnp.maximum(shard_rank[my_index], 0)
    own_block = jnp.concatenate([keys_one, values_one], axis=-1)

    def fetch_rows(step, buffer):
        piece = spread_2(own_block, "samp", roots[step])
        return lax.dynamic_update_slice_in_dim(buffer, piece, step * sample_rows, 0)

    empty_rows = jnp.zeros((total_context, feature_rows, 2 * model_width), jnp.bfloat16)
    fetched = lax.fori_loop(0, context_shards, fetch_rows, empty_rows)
    context_keys = fetched[..., :model_width]
    context_values = fetched[..., model_width:]
    query_heads = split_heads(queries_one)
    key_heads = split_heads(context_keys)
    value_heads = split_heads(context_values)
    scores = (
        jnp.einsum("sfhd,cfhd->fhsc", query_heads, key_heads, preferred_element_type=jnp.float32)
        * score_scale
    )
    sample_prob = soft_weights(jnp.where(allowed[None, None], scores, MASKED))
    sample_weights = sample_prob.astype(jnp.bfloat16)
    mixed_one = join_heads(
        jnp.einsum(
            "fhsc,cfhd->sfhd", sample_weights, value_heads, preferred_element_type=jnp.float32
        )
    ).astype(jnp.bfloat16)
    residual_one = residual_zero + apply_weight(mixed_one, sample_mixer) + sample_offset
    normed_two, norm_two_back = jax.vjp(layer_norm, residual_one, second_gain, second_shift)
    active_two = normed_two.astype(jnp.bfloat16)
    queries_two, keys_two, values_two = project(active_two, feature_weight, feature_bias)
    all_keys, all_values = (
        lax.all_gather(keys_two, "feat", axis=1, tiled=True),
        lax.all_gather(values_two, "feat", axis=1, tiled=True),
    )
    mixed_two, feature_prob = feature_attend(queries_two, all_keys, all_values)
    residual_two = residual_one + apply_weight(mixed_two, feature_mixer) + feature_offset
    normed_three, norm_three_back = jax.vjp(layer_norm, residual_two, third_gain, third_shift)
    active_three = normed_three.astype(jnp.bfloat16)
    expanded = apply_weight(active_three, expand_weight) + expand_bias
    activated, gelu_back = jax.vjp(partial(jax.nn.gelu, approximate=False), expanded)
    hidden = activated.astype(jnp.bfloat16)
    layer_output = (residual_two + apply_weight(hidden, reduce_weight) + reduce_bias).astype(
        jnp.bfloat16
    )
    grad_out = cotangent.astype(jnp.float32)
    grad_branch = cotangent
    reduce_bias_grad = column_sum(grad_branch)
    reduce_weight_grad = weight_grad(hidden, grad_branch)
    grad_hidden = input_back(grad_branch, reduce_weight).astype(jnp.bfloat16)
    grad_expanded = gelu_back(grad_hidden.astype(jnp.float32))[0].astype(jnp.bfloat16)
    expand_bias_grad = column_sum(grad_expanded)
    expand_weight_grad = weight_grad(active_three, grad_expanded)
    grad_norm, third_gain_grad, third_shift_grad = norm_three_back(
        input_back(grad_expanded, expand_weight)
    )
    grad_two = grad_out + grad_norm
    grad_branch = grad_two.astype(jnp.bfloat16)
    feature_offset_grad = column_sum(grad_branch)
    feature_mixer_grad = weight_grad(mixed_two, grad_branch)
    grad_mixed = input_back(grad_branch, feature_mixer).astype(jnp.bfloat16)
    grad_queries, grad_keys, grad_values = feature_grads(
        queries_two, all_keys, all_values, feature_prob, grad_mixed
    )
    own_key_grads, own_value_grads = (
        lax.psum_scatter(grad_keys, "feat", scatter_dimension=1, tiled=True),
        lax.psum_scatter(grad_values, "feat", scatter_dimension=1, tiled=True),
    )
    grad_project = jnp.concatenate(
        [
            grad_queries.astype(jnp.bfloat16),
            own_key_grads.astype(jnp.bfloat16),
            own_value_grads.astype(jnp.bfloat16),
        ],
        axis=-1,
    )
    feature_weight_grad = weight_grad(active_two, grad_project)
    feature_bias_grad = jnp.concatenate(
        [
            column_sum(grad_project[..., :model_width]),
            column_sum(grad_project[..., 2 * model_width :]),
        ]
    )
    grad_norm, second_gain_grad, second_shift_grad = norm_two_back(
        input_back(grad_project, feature_weight)
    )
    grad_one = grad_two + grad_norm
    grad_branch = grad_one.astype(jnp.bfloat16)
    sample_offset_grad = column_sum(grad_branch)
    sample_mixer_grad = weight_grad(mixed_one, grad_branch)
    grad_heads = split_heads(input_back(grad_branch, sample_mixer).astype(jnp.bfloat16))
    grad_weights = jnp.einsum(
        "sfhd,cfhd->fhsc", grad_heads, value_heads, preferred_element_type=jnp.float32
    )
    inner_sum = jnp.sum(sample_prob * grad_weights, axis=-1, keepdims=True)
    grad_scores = (sample_prob * (grad_weights - inner_sum)).astype(jnp.bfloat16)
    grad_queries = (
        join_heads(
            jnp.einsum(
                "fhsc,cfhd->sfhd", grad_scores, key_heads, preferred_element_type=jnp.float32
            )
        )
        * score_scale
    ).astype(jnp.bfloat16)
    key_terms = (
        join_heads(
            jnp.einsum(
                "fhsc,sfhd->cfhd", grad_scores, query_heads, preferred_element_type=jnp.float32
            )
        )
        * score_scale
    )
    value_terms = join_heads(
        jnp.einsum(
            "fhsc,sfhd->cfhd", sample_weights, grad_heads, preferred_element_type=jnp.float32
        )
    )
    term_block = jnp.concatenate([key_terms, value_terms], axis=-1)
    summed_terms = lax.psum_scatter(term_block, "samp", scatter_dimension=0, tiled=True)
    summed_rows = lax.all_gather(summed_terms.astype(jnp.bfloat16), "samp", axis=0, tiled=True)
    own_grads = lax.dynamic_slice_in_dim(summed_rows, own_rank * sample_rows, sample_rows, 0)
    own_grads = jnp.where(is_context, own_grads, jnp.zeros_like(own_grads))
    grad_project = jnp.concatenate([grad_queries, own_grads], axis=-1)
    sample_weight_grad = weight_grad(active_one, grad_project)
    sample_bias_grad = jnp.concatenate(
        [column_sum(grad_queries), column_sum(own_grads[..., model_width:])]
    )
    grad_norm, first_gain_grad, first_shift_grad = norm_one_back(
        input_back(grad_project, sample_weight)
    )
    input_grad = (grad_one + grad_norm).astype(jnp.bfloat16)
    summed = lax.psum(
        (
            first_gain_grad,
            first_shift_grad,
            sample_weight_grad,
            sample_bias_grad,
            sample_mixer_grad,
            sample_offset_grad,
            second_gain_grad,
            second_shift_grad,
            feature_weight_grad,
            feature_bias_grad,
            feature_mixer_grad,
            feature_offset_grad,
            third_gain_grad,
            third_shift_grad,
            expand_weight_grad,
            expand_bias_grad,
            reduce_weight_grad,
            reduce_bias_grad,
        ),
        "feat",
    )
    shares = (
        lax.psum_scatter(summed[0], "samp", scatter_dimension=0, tiled=True),
        lax.psum_scatter(summed[1], "samp", scatter_dimension=0, tiled=True),
        lax.psum_scatter(summed[2], "samp", scatter_dimension=0, tiled=True),
        lax.psum_scatter(summed[3], "samp", scatter_dimension=0, tiled=True),
        lax.psum_scatter(summed[4], "samp", scatter_dimension=0, tiled=True),
        lax.psum_scatter(summed[5], "samp", scatter_dimension=0, tiled=True),
        lax.psum_scatter(summed[6], "samp", scatter_dimension=0, tiled=True),
        lax.psum_scatter(summed[7], "samp", scatter_dimension=0, tiled=True),
        lax.psum_scatter(summed[8], "samp", scatter_dimension=0, tiled=True),
        lax.psum_scatter(summed[9], "samp", scatter_dimension=0, tiled=True),
        lax.psum_scatter(summed[10], "samp", scatter_dimension=0, tiled=True),
        lax.psum_scatter(summed[11], "samp", scatter_dimension=0, tiled=True),
        lax.psum_scatter(summed[12], "samp", scatter_dimension=0, tiled=True),
        lax.psum_scatter(summed[13], "samp", scatter_dimension=0, tiled=True),
        lax.psum_scatter(summed[14], "samp", scatter_dimension=0, tiled=True),
        lax.psum_scatter(summed[15], "samp", scatter_dimension=0, tiled=True),
        lax.psum_scatter(summed[16], "samp", scatter_dimension=0, tiled=True),
        lax.psum_scatter(summed[17], "samp", scatter_dimension=0, tiled=True),
    )
    return (
        layer_output,
        input_grad,
        shares[0],
        shares[1],
        shares[2],
        shares[3],
        shares[4],
        shares[5],
        shares[6],
        shares[7],
        shares[8],
        shares[9],
        shares[10],
        shares[11],
        shares[12],
        shares[13],
        shares[14],
        shares[15],
        shares[16],
        shares[17],
    )


def solution(mesh):
    if mesh.shape["samp"] == 8 and mesh.shape["feat"] == 4:
        return solution_small(mesh)
    return jax.shard_map(
        local_large,
        mesh=mesh,
        in_specs=(
            P("samp", "feat", None),
            P(),
            P(),
            P(),
            P(),
            P(),
            P(),
            P(),
            P(),
            P(),
            P(),
            P(),
            P(),
            P(),
            P(),
            P(),
            P(),
            P(),
            P(),
            P(),
            P(),
            P("samp", "feat", None),
        ),
        out_specs=(
            P("samp", "feat", None),
            P("samp", "feat", None),
            P("samp"),
            P("samp"),
            P("samp", None),
            P("samp"),
            P("samp", None),
            P("samp"),
            P("samp"),
            P("samp"),
            P("samp", None),
            P("samp"),
            P("samp", None),
            P("samp"),
            P("samp"),
            P("samp"),
            P("samp", None),
            P("samp"),
            P("samp", None),
            P("samp"),
        ),
        check_vma=False,
    )


def solution_small(mesh):
    mesh = jax.sharding.Mesh(mesh.devices.reshape(2, 4, 4), ("half", "quad", "feat"))
    tokens, copied = P(SAMP, "feat", None), P()
    vector, matrix = P(SAMP), P(SAMP, None)
    return jax.shard_map(
        local_small,
        mesh=mesh,
        in_specs=(tokens,) + (copied,) * 20 + (tokens,),
        out_specs=(
            tokens, tokens, vector, vector, matrix, vector, matrix, vector,
            vector, vector, matrix, vector, matrix, vector,
            vector, vector, matrix, vector, matrix, vector,
        ),
        check_vma=False,
    )
```

```python
from functools import partial

import jax
import jax.numpy as jnp
from jax import lax
from jax.experimental import pallas as pl
from jax.experimental.pallas import tpu as pltpu
from jax.sharding import PartitionSpec as P

HEADS = 8
HEAD_DIM = 64
EPS = 1e-05
MASKED = -1000000000.0
SCALE = HEAD_DIM ** (-0.5)
QUAD = 4 * HEAD_DIM
BF = jnp.bfloat16
F32 = jnp.float32


def mm(a, b, ca=1, cb=0):
    return lax.dot_general(a, b, (((ca,), (cb,)), ((), ())), preferred_element_type=F32)


def norm_parts(values):
    center = jnp.mean(values, axis=-1, keepdims=True)
    spread = values - center
    variance = jnp.mean(spread * spread, axis=-1, keepdims=True)
    inverse = lax.rsqrt(variance + EPS)
    return spread * inverse, inverse


def norm_back(grad, unit, inverse, gain):
    scaled = grad * gain
    first = jnp.mean(scaled, axis=-1, keepdims=True)
    second = jnp.mean(scaled * unit, axis=-1, keepdims=True)
    return (scaled - first - unit * second) * inverse


def lane_ids(rows):
    return lax.broadcasted_iota(jnp.int32, (rows, 128), 1)


def group_reduce(values, op, fill):
    rows = values.shape[0]
    low = lane_ids(rows) < HEAD_DIM
    outs = []
    for t in range(values.shape[1] // 128):
        tile = values[:, t * 128 : (t + 1) * 128]
        left = op(jnp.where(low, tile, fill), axis=1, keepdims=True)
        right = op(jnp.where(low, fill, tile), axis=1, keepdims=True)
        outs.append(jnp.where(low, left, right))
    return jnp.concatenate(outs, axis=1)


def head_masks(dtype):
    lanes = lax.broadcasted_iota(jnp.int32, (1, QUAD), 1) // HEAD_DIM
    return [jnp.where(lanes == h, 1.0, 0.0).astype(dtype) for h in range(4)]


def stack_heads(part, masks):
    return jnp.concatenate([part * m for m in masks], axis=0)


def pick_heads(stacked, masks):
    rows = stacked.shape[0] // 4
    total = stacked[:rows] * masks[0]
    for h in range(1, 4):
        total = total + stacked[h * rows : (h + 1) * rows] * masks[h]
    return total


def attend(q, k, v, masks, allow):
    outs, probs = [], []
    for quad in range(2):
        cols = slice(quad * QUAD, (quad + 1) * QUAD)
        scores = mm(q[:, cols], stack_heads(k[:, cols], masks), 1, 1)
        if allow is not None:
            scores = jnp.where(allow, scores, MASKED)
        raised = jnp.exp(scores - group_reduce(scores, jnp.max, -jnp.inf))
        prob = raised / group_reduce(raised, jnp.sum, 0.0)
        outs.append(mm(prob.astype(BF), stack_heads(v[:, cols], masks)))
        probs.append(prob)
    return jnp.concatenate(outs, axis=1), jnp.concatenate(probs, axis=1)


def attend_back(q, k, v, prob, grad, masks, masks32):
    dqs, dks, dvs = [], [], []
    for quad in range(2):
        cols = slice(quad * QUAD, (quad + 1) * QUAD)
        p, g = prob[:, cols], grad[:, cols]
        back = mm(g, stack_heads(v[:, cols], masks), 1, 1)
        inner = group_reduce(p * back, jnp.sum, 0.0)
        gs = (p * (back - inner)).astype(BF)
        dqs.append(mm(gs, stack_heads(k[:, cols], masks)) * SCALE)
        dks.append(pick_heads(mm(gs, q[:, cols], 0, 0), masks32))
        dvs.append(pick_heads(mm(p.astype(BF), g, 0, 0), masks32))
    join = lambda parts: jnp.concatenate(parts, axis=1).astype(BF)
    return join(dqs), join(dks), join(dvs)


def swap_matrix(rows=16):
    n = rows * 16
    r = lax.broadcasted_iota(jnp.int32, (n, n), 0)
    c = lax.broadcasted_iota(jnp.int32, (n, n), 1)
    return jnp.where((r // rows == c % 16) & (r % rows == c // 16), 1.0, 0.0).astype(BF)


def swap(matrix, values, back=False):
    return mm(matrix, values, 0 if back else 1, 0).astype(BF)


def gelu_parts(u):
    cdf = 0.5 * (1.0 + lax.erf(u * (2.0**-0.5)))
    density = jnp.exp(u * u * -0.5) * 0.3989422804014327
    return cdf, density


def col_sum(values):
    return jnp.sum(values.astype(F32), axis=0, keepdims=True)


def turn_in(x_ref, out_ref):
    matrix = swap_matrix()
    for d in range(4):
        rows = x_ref[d * 256 : (d + 1) * 256]
        out_ref[:, d] = swap(matrix, rows).reshape(16, 16, 512)


def turn_out(got_ref, out_ref):
    matrix = swap_matrix()
    for d in range(4):
        out_ref[d * 256 : (d + 1) * 256] = swap(matrix, got_ref[:, d].reshape(256, 512))


def each_feature(body):
    lax.fori_loop(0, 4, lambda e, carry: (body(e), carry)[1], 0)


def project_queries(x_ref, gain_ref, shift_ref, w_ref, b_ref, act_ref, q_ref):
    def body(e):
        unit, _ = norm_parts(x_ref[:, e].reshape(256, 512).astype(F32))
        act = (unit * gain_ref[...] + shift_ref[...]).astype(BF)
        act_ref[e] = act
        q = (mm(act, w_ref[:, :512]) + b_ref[:, :512]).astype(BF)
        q_ref[e] = q * jnp.asarray(SCALE, BF)

    each_feature(body)


def forward_one(
    me_ref, q_ref, own_ref, got_ref, tasks_ref, context_ref, gain_ref, shift_ref, w_ref, b_ref,
    oa_ref, ob_ref, c_ref, cact_ref, k_ref, v_ref, p_ref,
):
    here = me_ref[1] == me_ref[2]
    masks = head_masks(BF)
    allow = tasks_ref[...] == context_ref[...]

    @pl.when(here)
    def _():
        c_ref[...] = own_ref[...]

    @pl.when(jnp.logical_not(here))
    def _():
        c_ref[...] = got_ref[...]

    unit, _ = norm_parts(c_ref[...].reshape(256, 512).astype(F32))
    act = (unit * gain_ref[...] + shift_ref[...]).astype(BF)
    cact_ref[...] = act.reshape(4, 64, 512)
    kv = mm(act, w_ref[:, 512:])
    k_ref[...] = kv[:, :512].astype(BF).reshape(4, 64, 512)
    v_ref[...] = (kv[:, 512:] + b_ref[:, 512:]).astype(BF).reshape(4, 64, 512)

    def body(e):
        out, prob = attend(q_ref[e], k_ref[e], v_ref[e], masks, allow)
        out = out.reshape(4, 4, 2, 8, 512)
        oa_ref[:, :, e] = out[:, :, 0].astype(BF)
        ob_ref[:, :, e] = out[:, :, 1].astype(BF)
        p_ref[e] = prob

    each_feature(body)


HALF = 512


def middle(me_ref, *refs):
    (
        o1_ref, x0, x1, x2, x3, c0, c1, c2, c3,
        off1_ref, g2_ref, s2_ref, bf_ref, off2_ref, g3_ref, s3_ref, be_ref, br_ref,
    ) = refs[:18]
    weights_hbm = refs[18:23]
    refs = refs[-44:]
    gb1_ref, vec_ref, bias_ref = refs[:3]
    outs_hbm, kept_hbm = refs[3:7], refs[7:15]
    wm1_ref, wf_ref, wm2_ref, we_ref, wr_ref = refs[15:20]
    kept = refs[20:28]
    a2_ref, dqkv_ref, o2_ref, gb2_ref, a3_ref, gu_ref, hid_ref, gb3_ref = kept
    (
        o_scr, q_scr, k_scr, v_scr, p_scr, e_scr, gs_scr, go_scr, out_scr, back_scr,
        out0, out1, out2, out3, in_sems, out_sems,
    ) = refs[28:]
    loads = [
        pltpu.make_async_copy(source, target, in_sems.at[i])
        for i, (source, target) in enumerate(zip(weights_hbm, refs[15:20]))
    ]
    for load in loads:
        load.start()
    stores = []

    def store(source, target, i):
        stores.append(pltpu.make_async_copy(source, target, out_sems.at[i]))
        stores[-1].start()

    def keep(ref):
        i = next(j for j in range(8) if kept[j] is ref)
        store(ref, kept_hbm[i], i)

    me = me_ref[0]
    matrix = swap_matrix(8)
    masks, masks32 = head_masks(BF), head_masks(F32)
    for f in range(4):
        o_scr[f] = swap(matrix, o1_ref[:, f].reshape(128, 512), True)

    def gather(*refs):
        return jnp.concatenate(
            [ref[s * 16 : (s + 1) * 16] for s in range(8) for ref in refs], axis=0
        )

    def scatter(values, *refs):
        for s in range(8):
            for d, ref in enumerate(refs):
                at = (s * 4 + d) * 16
                ref[s * 16 : (s + 1) * 16] = values[at : at + 16]

    def each_sample(body):
        def step(i, carry):
            for j in range(SAMPLE_UNROLL):
                rows = pl.ds(pl.multiple_of((i * SAMPLE_UNROLL + j) * 64, 64), 64)
                for quad in range(2):
                    body(rows, slice(quad * QUAD, (quad + 1) * QUAD))
            return carry

        lax.fori_loop(0, 8 // SAMPLE_UNROLL, step, 0)

    attended = gather(*(o_scr.at[d ^ me] for d in range(4)))
    gb3_ref[...] = gather(c0, c1, c2, c3)
    keep(gb3_ref)
    loads[0].wait()
    r1 = gather(x0, x1, x2, x3).astype(F32) + mm(attended, wm1_ref[...]) + off1_ref[...]
    unit2, inv2 = norm_parts(r1)
    a2_ref[...] = (unit2 * g2_ref[...] + s2_ref[...]).astype(BF)
    keep(a2_ref)
    loads[1].wait()
    q = (mm(a2_ref[...], wf_ref[:, :512]) + bf_ref[:, :512]).astype(BF)
    q_scr[...] = q * jnp.asarray(SCALE, BF)
    k_scr[...] = mm(a2_ref[...], wf_ref[:, 512:1024]).astype(BF)
    v_scr[...] = (mm(a2_ref[...], wf_ref[:, 1024:]) + bf_ref[:, 512:]).astype(BF)

    def score(rows, cols):
        p_scr[rows, cols] = mm(q_scr[rows, cols], stack_heads(k_scr[rows, cols], masks), 1, 1)

    each_sample(score)
    for i in range(4):
        rows = slice(i * 128, (i + 1) * 128)
        scores = p_scr[rows]
        raised = jnp.exp(scores - group_reduce(scores, jnp.max, -jnp.inf))
        p_scr[rows] = raised / group_reduce(raised, jnp.sum, 0.0)

    def mix(rows, cols):
        o2_ref[rows, cols] = mm(
            p_scr[rows, cols].astype(BF), stack_heads(v_scr[rows, cols], masks)
        ).astype(BF)

    each_sample(mix)
    keep(o2_ref)
    loads[2].wait()
    r2 = r1 + mm(o2_ref[...], wm2_ref[...]) + off2_ref[...]
    unit3, inv3 = norm_parts(r2)
    a3_ref[...] = (unit3 * g3_ref[...] + s3_ref[...]).astype(BF)
    keep(a3_ref)
    loads[3].wait()
    loads[4].wait()
    out_scr[...] = r2 + br_ref[...]
    back_scr[...] = jnp.zeros((HALF, 512), F32)

    def expand(b, carry):
        cols = pl.ds(pl.multiple_of(b * WIDE, WIDE), WIDE)
        u = mm(a3_ref[...], we_ref[:, cols]) + be_ref[:, cols]
        cdf, density = gelu_parts(u)
        hidden = (u * cdf).astype(BF)
        hid_ref[:, cols] = hidden
        gh = mm(gb3_ref[...], wr_ref[cols, :], 1, 1).astype(BF).astype(F32)
        gu = (gh * (cdf + u * density)).astype(BF)
        gu_ref[:, cols] = gu
        bias_ref[:, cols] = col_sum(gu)
        out_scr[...] += mm(hidden, wr_ref[cols, :])
        back_scr[...] += mm(gu, we_ref[:, cols], 1, 1)
        return carry

    lax.fori_loop(0, 2048 // WIDE, expand, 0, unroll=EXPAND_UNROLL)
    keep(hid_ref)
    keep(gu_ref)
    scatter(out_scr[...].astype(BF), out0, out1, out2, out3)
    rows = pl.ds(pl.multiple_of(me_ref[8] * 128, 128), 128)
    for i, ref in enumerate((out0, out1, out2, out3)):
        store(ref, outs_hbm[i].at[rows], 8 + i)
    back, cot = back_scr[...], gb3_ref[...]
    vecs = [col_sum(back * unit3), col_sum(back)]
    gr2 = cot.astype(F32) + norm_back(back, unit3, inv3, g3_ref[...])
    gb2_ref[...] = gr2.astype(BF)
    keep(gb2_ref)
    go_scr[...] = mm(gb2_ref[...], wm2_ref[...], 1, 1).astype(BF)

    def weigh(rows, cols):
        e_scr[rows, cols] = mm(go_scr[rows, cols], stack_heads(v_scr[rows, cols], masks), 1, 1)

    each_sample(weigh)
    for i in range(4):
        rows = slice(i * 128, (i + 1) * 128)
        prob, grad = p_scr[rows], e_scr[rows]
        inner = group_reduce(prob * grad, jnp.sum, 0.0)
        gs_scr[rows] = (prob * (grad - inner)).astype(BF)

    def spread(rows, cols):
        gs, at = gs_scr[rows, cols], cols.start
        dq = mm(gs, stack_heads(k_scr[rows, cols], masks)) * SCALE
        dqkv_ref[rows, at : at + QUAD] = dq.astype(BF)
        dk = pick_heads(mm(gs, q_scr[rows, cols], 0, 0), masks32)
        dqkv_ref[rows, 512 + at : 512 + at + QUAD] = dk.astype(BF)
        dv = pick_heads(mm(p_scr[rows, cols].astype(BF), go_scr[rows, cols], 0, 0), masks32)
        dqkv_ref[rows, 1024 + at : 1024 + at + QUAD] = dv.astype(BF)

    each_sample(spread)
    keep(dqkv_ref)
    dqkv = dqkv_ref[...]
    back = mm(dqkv, wf_ref[...], 1, 1)
    vecs += [col_sum(back * unit2), col_sum(back)]
    gr1 = gr2 + norm_back(back, unit2, inv2, g2_ref[...])
    scatter(gr1.astype(BF), *(o_scr.at[d ^ me] for d in range(4)))
    for f in range(4):
        gb1_ref[:, f] = swap(matrix, o_scr[f]).reshape(4, 4, 8, 512)
    vecs += [
        col_sum(gb2_ref[...]), col_sum(cot), col_sum(dqkv[:, :512]), col_sum(dqkv[:, 1024:])
    ]
    vec_ref[...] = jnp.concatenate(vecs, axis=0)
    for copy in stores:
        copy.wait()


SAMPLE_UNROLL = 8
EXPAND_UNROLL = False
WIDE = 512


def backward_one(
    ga_ref, gb_ref, x_ref, c_ref, q_ref, k_ref, v_ref, p_ref, w_ref, wm_ref,
    gb1_ref, a_ref, dq_ref, dkv_ref, term_ref, vec_ref,
    g_scr,
):
    masks, masks32 = head_masks(BF), head_masks(F32)
    vec_ref[...] = jnp.zeros((8, 512), F32)

    def body(e):
        g_scr[:, :, 0] = ga_ref[:, :, e]
        g_scr[:, :, 1] = gb_ref[:, :, e]
        gb1 = g_scr[...].reshape(256, 512)
        gb1_ref[e] = gb1
        go = mm(gb1, wm_ref[...], 1, 1).astype(BF)
        dq, dk, dv = attend_back(q_ref[e], k_ref[e], v_ref[e], p_ref[e], go, masks, masks32)
        dq_ref[e], dkv_ref[e, :, :512], dkv_ref[e, :, 512:] = dq, dk, dv
        back = mm(dq, w_ref[:, :512], 1, 1)
        a_ref[e] = back
        unit, _ = norm_parts(x_ref[:, e].reshape(256, 512).astype(F32))
        vec_ref[0:1] += col_sum(back * unit)
        vec_ref[1:2] += col_sum(back)
        vec_ref[2:3] += col_sum(gb1)
        vec_ref[3:4] += col_sum(dq)

    each_feature(body)
    dkv = dkv_ref[...].reshape(256, 1024)
    term = mm(dkv, w_ref[:, 512:], 1, 1)
    term_ref[...] = term.astype(BF).reshape(4, 64, 512)
    unit, _ = norm_parts(c_ref[...].reshape(256, 512).astype(F32))
    vec_ref[0:1] += col_sum(term * unit)
    vec_ref[1:2] += col_sum(term)
    vec_ref[4:5] = col_sum(dkv[:, 512:])


def backward_input(me_ref, gb1_ref, x_ref, a_ref, term_ref, got_ref, gain_ref, grad_ref, a_scr):
    here, quad = me_ref[1] == me_ref[2], me_ref[3]

    def body(e):
        unit, inverse = norm_parts(x_ref[:, e].reshape(256, 512).astype(F32))
        a_scr[...] = a_ref[e].reshape(4, 64, 512)

        @pl.when(here)
        def _():
            a_scr[quad] += term_ref[e].astype(F32) + got_ref[e].astype(F32)

        back = a_scr[...].reshape(256, 512)
        grad = gb1_ref[e].astype(F32) + norm_back(back, unit, inverse, gain_ref[...])
        grad_ref[:, e] = grad.astype(BF).reshape(4, 64, 512)

    each_feature(body)


def split(got_ref, out_ref):
    rest = jnp.sum(got_ref[...], axis=0, keepdims=True)
    out_ref[...] = jnp.zeros_like(out_ref)
    for i in range(3):
        term = rest.astype(BF)
        out_ref[i : i + 1] = term
        rest = rest - term.astype(F32)


def place(me_ref, b0, b1, b2, b3, out_ref):
    for d, ref in enumerate((b0, b1, b2, b3)):
        out_ref[d ^ me_ref[0]] = ref[...]


def lay_out(me_ref, read, order, *pairs):
    core, xx, yy, zz = me_ref[4], me_ref[5], me_ref[6], me_ref[7]
    for bits in range(16):
        index = tuple((bits >> i) & 1 for i in (3, 2, 1, 0))
        dx, dy, d1, d2 = (index[order.index(name)] for name in ("x", "y", "z", "w"))
        shard = (zz ^ d1 ^ (2 * d2)) * 2 + (yy ^ dy)
        for keep_ref, send_ref, start, rows in pairs:
            keep_ref[index] = read(2 * core + (dx ^ xx), shard, start, rows)
            send_ref[index] = read(2 * (1 - core) + (dx ^ xx), shard, start, rows)


def read_units(scr):
    def read(unit, shard, start, rows):
        return scr[unit, pl.ds(pl.multiple_of(shard * 64 + start, rows), rows)]

    return read


def grads_middle(me_ref, *refs):
    sources, targets, held, staged = refs[:16], refs[16:22], refs[22:30], refs[30:36]
    scr, in_sems, out_sems = refs[36:]
    loads = []
    for i in range(16):
        rows = pl.ds((i % 2) * 512, 512)
        loads.append(
            pltpu.make_async_copy(sources[i], held[i // 2].at[rows], in_sems.at[i])
        )
        loads[-1].start()
    stores = []

    def wait(*places):
        for place in places:
            loads[2 * place].wait()
            loads[2 * place + 1].wait()

    def put(part, order):
        lay_out(me_ref, read_units(scr), order, (staged[2 * part], staged[2 * part + 1], 0, 64))
        for i in (2 * part, 2 * part + 1):
            stores.append(pltpu.make_async_copy(staged[i], targets[i], out_sems.at[i]))
            stores[-1].start()

    gb3, hid, act3, gu, act2, dqkv, o2, gb2 = held
    wait(0, 1)

    def loop(count, body):
        lax.fori_loop(0, count, lambda n, carry: (body(n), carry)[1], 0)

    block = lambda n: pl.ds(pl.multiple_of(n * 512, 512), 512)

    def from_hidden(n):
        piece = mm(hid[:, block(n)], gb3[...], 0, 0).astype(BF).reshape(2, 4, 64, 512)
        for i in range(2):
            rows = pl.ds(pl.multiple_of((2 * n + i) * 64, 64), 64)
            for unit in range(4):
                scr[unit, rows] = piece[i, unit]

    loop(4, from_hidden)
    put(0, "zxyw")
    wait(2, 3)

    def from_expand(n):
        scr[n] = mm(act3[...], gu[:, block(n)], 0, 0).astype(BF)

    loop(4, from_expand)
    put(1, "yxzw")
    wait(4, 5, 6, 7)

    def from_feature(n):
        scr[n] = mm(act2[...], dqkv[:, block(n)], 0, 0).astype(BF)

    loop(3, from_feature)
    scr[3] = mm(o2[...], gb2[...], 0, 0).astype(BF)
    put(2, "xyzw")
    for store in stores:
        store.wait()


def grads_sample(
    me_ref, act_ref, dq_ref, cact_ref, dkv_ref, oa_ref, ga_ref, ob_ref, gb_ref,
    keep_ref, send_ref, scr,
):
    scr[0] = mm(act_ref[...], dq_ref[...], 0, 0).astype(BF)
    scr[1] = mm(cact_ref[...], dkv_ref[:, :512], 0, 0).astype(BF)
    scr[2] = mm(cact_ref[...], dkv_ref[:, 512:], 0, 0).astype(BF)
    total = mm(oa_ref[...], ga_ref[...], 0, 0) + mm(ob_ref[...], gb_ref[...], 0, 0)
    scr[3] = total.astype(BF)
    lay_out(me_ref, read_units(scr), "xyzw", (keep_ref, send_ref, 0, 64))


def spec(shape, index=None):
    return pl.BlockSpec(shape, index if index is not None else (lambda *a: (0,) * len(shape)))


def sds(shape, dtype=BF):
    return jax.ShapeDtypeStruct(shape, dtype)


def big(shape, dtype=BF):
    return pltpu.HBM(shape, dtype)


def outside(array):
    if array.size * array.dtype.itemsize < 1 << 18:
        return array
    return pltpu.with_memory_space_constraint(array, pltpu.HBM)


def params(limit):
    return pltpu.CompilerParams(vmem_limit_bytes=limit << 20)


def row(vector):
    return vector.reshape(1, -1)


def cost(microseconds):
    return pl.CostEstimate(
        flops=int(microseconds * 1.1e9), transcendentals=0, bytes_accessed=int(microseconds * 2e6)
    )


def whole_block(out):
    shape = out.shape
    return pl.BlockSpec(shape, lambda i: (0,) * len(shape))


def whole(kernel, name, limit, outs, scratch, *inputs, steps=1, time=3):
    arrays, specs = [], []
    for entry in inputs:
        if not isinstance(entry, tuple) and entry.ndim == 1:
            arrays.append(entry)
            specs.append(pl.BlockSpec(memory_space=pltpu.SMEM))
            continue
        array, block, index = entry if isinstance(entry, tuple) else (entry, None, None)
        arrays.append(outside(array))
        block = array.shape if block is None else block
        index = (0,) * array.ndim if index is None else index
        if not callable(index):
            index = lambda i, index=index: index
        specs.append(pl.BlockSpec(block, index))
    return pl.pallas_call(
        kernel,
        grid=(steps,),
        out_shape=outs,
        in_specs=specs,
        out_specs=jax.tree.map(whole_block, outs, is_leaf=lambda o: hasattr(o, "dtype")),
        scratch_shapes=scratch,
        compiler_params=params(limit),
        cost_estimate=cost(time),
        name=name,
    )(*arrays)


def shuffle(value, axis, mask):
    size = lax.axis_size(axis)
    return lax.ppermute(value, axis, [(i, i ^ mask) for i in range(size)])


SAMP = ("half", "quad")
CORE, X, Y, Z, W = ("feat", 1), ("feat", 2), ("quad", 1), ("quad", 2), ("half", 1)


def at(stacked, index, axis=0):
    return lax.dynamic_index_in_dim(stacked, index, axis, keepdims=False)


def fence(tree):
    return lax.optimization_barrier(tree)


def plus(a, b):
    return (a.astype(F32) + b.astype(F32)).astype(BF)


class Chain:
    def __init__(self, keep, sent, dims):
        self.keep, self.sent, self.dims = keep, sent, (CORE,) + dims

    def start(self):
        return shuffle(self.sent, *self.dims[0])

    def take(self, got):
        self.dims = self.dims[1:]
        if self.dims:
            self.keep, self.sent = plus(self.keep[0], got[0]), plus(self.keep[1], got[1])
        else:
            self.keep = plus(self.keep, got)


def together(chains, make=lambda: ()):
    got = [chain.start() for chain in chains]
    got, other = fence((got, make()))
    for chain, value in zip(chains, got):
        chain.take(value)
    return other


def local_small(
    layer_input, segment_ids, context_flags,
    first_gain, first_shift, sample_weight, sample_bias, sample_mixer, sample_offset,
    second_gain, second_shift, feature_weight, feature_bias, feature_mixer, feature_offset,
    third_gain, third_shift, expand_weight, expand_bias, reduce_weight, reduce_bias, cotangent,
):
    half, quad, feat = (lax.axis_index(name) for name in ("half", "quad", "feat"))
    samp = half * 4 + quad
    core, xx = feat % 2, feat // 2
    flags = context_flags.reshape(8, 64)[:, 0]
    root = jnp.sum(jnp.where(flags == 1, jnp.arange(8, dtype=jnp.int32), 0))
    me = [feat, half, root // 4, root % 4, core, xx, samp % 2, samp // 2]
    me = jnp.stack(me).astype(jnp.int32)

    turned = whole(turn_in, "turn_in", 8, big((16, 4, 16, 512)), [], layer_input.reshape(1024, 512))
    turned, layer_input, cotangent = fence((turned, layer_input, cotangent))
    x_t = lax.all_to_all(turned.reshape(4, 4, 64, 512), "quad", 0, 0)
    x4, cot4 = layer_input.reshape(4, 256, 512), cotangent.reshape(4, 256, 512)
    block = lambda value, d: at(value, feat ^ d)
    to_core = jnp.stack([block(x4, 1), block(cot4, 1), block(x4, 3), block(cot4, 3)])
    from_core = shuffle(to_core, *CORE)
    x_far = shuffle(jnp.stack([block(x4, 2), from_core[2]]), *X)
    x_t, from_core, x_far = fence((x_t, from_core, x_far))
    cot_far = shuffle(jnp.stack([block(cot4, 2), from_core[3]]), *X)
    own_context = at(x_t, root % 4)
    got_context = shuffle(own_context, *W)
    act1, queries = whole(
        project_queries, "project_queries", 16, (big((4, 256, 512)), big((4, 256, 512))), [],
        x_t, row(first_gain), row(first_shift), sample_weight, row(sample_bias),
    )
    cot_far, got_context, q1 = fence((cot_far, got_context, queries))

    tasks = segment_ids.reshape(8, 64)
    context_tasks = jnp.concatenate([at(tasks, root)] * 4).reshape(1, 256)
    sent = big((4, 4, 4, 8, 512))
    four = big((4, 64, 512))
    oa, ob, context, cact, k1, v1, p1 = whole(
        forward_one, "forward_one", 24,
        (sent, sent, four, four, four, four, big((4, 256, 512), F32)), [],
        me, q1, own_context, got_context, at(segment_ids.reshape(2, 256, 1), half), context_tasks,
        row(first_gain), row(first_shift), sample_weight, row(sample_bias), time=7,
    )

    def exchange(value):
        shape = value.shape
        value = value.reshape((16,) + shape[2:])
        return lax.all_to_all(value, ("quad", "feat"), 0, 0).reshape(shape)

    rows_in = [
        row(v)
        for v in (
            sample_offset, second_gain, second_shift, feature_bias, feature_offset, third_gain,
            third_shift, expand_bias, reduce_bias,
        )
    ]
    weights = [sample_mixer, feature_weight, feature_mixer, expand_weight, reduce_weight]

    def run_middle(half, attended, earlier):
        own = spec((None, 128, 512), lambda i, m: (m[0], m[8], 0))
        part = lambda n: spec((None, 128, 512), lambda i, m: (n, m[8], 0))
        outs = (sent, sds((8, 512), F32), sds((1, 2048), F32))
        blocks = ((256, 512),) * 4
        kept = tuple((HALF, n) for n in (512, 1536, 512, 512, 512, 2048, 2048, 512))
        still = lambda shape: spec(shape, lambda i, m: (0,) * len(shape))
        far = pl.BlockSpec(memory_space=pl.ANY)
        vmem = lambda shape, dtype=BF: pltpu.VMEM(shape, dtype)
        rows, rows32 = vmem((HALF, 512)), vmem((HALF, 512), F32)
        return pl.pallas_call(
            middle,
            grid_spec=pltpu.PrefetchScalarGridSpec(
                num_scalar_prefetch=1,
                grid=(1,),
                in_specs=[still((4, 4, 4, 8, 512))]
                + [own, part(0), part(0), part(1), own, part(1), part(0), part(1)]
                + [still(r.shape) for r in rows_in]
                + [far] * (5 + len(earlier)),
                out_specs=[still(o.shape) for o in outs] + [far] * 12,
                scratch_shapes=[vmem(w.shape) for w in weights]
                + [vmem(shape) for shape in kept]
                + [
                    vmem((4, 128, 512)), rows, rows, rows, rows32, rows32, rows, rows, rows32,
                    rows32, *(vmem((128, 512)) for _ in range(4)),
                    pltpu.SemaphoreType.DMA((5,)), pltpu.SemaphoreType.DMA((12,)),
                ],
            ),
            out_shape=outs + tuple(big(shape) for shape in blocks + kept),
            input_output_aliases={24 + i: 3 + i for i in range(len(earlier))},
            compiler_params=params(44),
            cost_estimate=cost(30),
            name="middle",
        )(
            jnp.concatenate([me, jnp.full((1,), half, jnp.int32)]),
            *(
                outside(array)
                for array in (
                    attended, x4, from_core, x_far, x_far, cot4, from_core, cot_far, cot_far,
                    *rows_in, *weights, *earlier,
                )
            ),
        )

    oa_f, ob = fence((exchange(oa), ob))
    ob_f = exchange(ob)
    ga, vec_a, bias_a, *first = run_middle(0, oa_f, [])
    ob_f, ga, first = fence((ob_f, ga, first))
    ga_t = exchange(ga)
    gb, vec_b, bias_b, *second = run_middle(1, ob_f, first[:4])
    ga_t, gb, second = fence((ga_t, gb, second))
    out0, out1, out2, out3 = second[:4]
    act2, dqkv, o2, gb2, act3, gu, hidden, gb3 = zip(first[4:], second[4:])
    gb_t = exchange(gb)
    vec2, bias2 = vec_a + vec_b, bias_a + bias_b

    parts = sds((2, 2, 2, 2, 64, 512))
    units = [pltpu.VMEM((4, 512, 512), BF)]
    far = pl.BlockSpec(memory_space=pl.ANY)
    sources = [*gb3, *hidden, *act3, *gu, *act2, *dqkv, *o2, *gb2]
    widths = (512, 2048, 512, 2048, 512, 1536, 512, 512)
    rk, rs, ek, es, fk, fs = pl.pallas_call(
        grads_middle,
        grid=(1,),
        out_shape=(parts,) * 6,
        in_specs=[pl.BlockSpec(memory_space=pltpu.SMEM)] + [far] * 16,
        out_specs=[far] * 6,
        scratch_shapes=[pltpu.VMEM((1024, n), BF) for n in widths]
        + [pltpu.VMEM(parts.shape, BF)] * 6
        + units
        + [pltpu.SemaphoreType.DMA((16,)), pltpu.SemaphoreType.DMA((6,))],
        compiler_params=params(32),
        cost_estimate=cost(9),
        name="grads_middle",
    )(me, *(outside(a) for a in sources))
    r_chain = Chain(rk, rs, (Z, X, Y, W))
    e_chain = Chain(ek, es, (Y, X))
    f_chain = Chain(fk, fs, (X, Y))
    chains = [r_chain, e_chain, f_chain]
    for chain in chains:
        chain.take(chain.start())

    full = big((4, 256, 512))
    gb1, back, dq1, dkv, term, vec1 = together(
        chains,
        lambda: whole(
            backward_one, "backward_one", 28,
            (
                full, big((4, 256, 512), F32), full, sds((4, 64, 1024)), four, sds((8, 512), F32),
            ),
            [pltpu.VMEM((4, 4, 2, 8, 512), BF)],
            ga_t, gb_t, x_t, context, q1, k1, v1, p1, sample_weight, sample_mixer, time=10,
        ),
    )

    owned = lambda v, n: v.reshape(-1, 8, n).transpose(1, 0, 2).reshape(8, -1)
    vectors = jnp.concatenate(
        [
            owned(vec2[:6], 64), vec2[6:].reshape(8, 128), bias2.reshape(8, 256),
            owned(vec1[:3], 64), vec1[3:5].reshape(8, 128),
        ],
        axis=1,
    )
    flat2 = lambda a: a.reshape(-1, a.shape[-1])
    grads = whole(
        grads_sample, "grads_sample", 20, (parts, parts), units,
        me, *(flat2(a) for a in (act1, dq1, cact, dkv, oa, ga_t, ob, gb_t)),
    )
    got_term, grads = together(chains, lambda: (shuffle(term, *W), grads))
    both = [jnp.concatenate([e_chain.keep[i], f_chain.keep[i]], axis=-2) for i in range(2)]
    both_chain = Chain(both[0], both[1], (W,))
    both_chain.dims = (Z, W)
    s_chain = Chain(*grads, (X, Y))
    grad_t = together(
        [s_chain, r_chain, both_chain],
        lambda: whole(
            backward_input, "backward_input", 24, big((4, 4, 64, 512)),
            [pltpu.VMEM((4, 64, 512), F32)],
            me, gb1, x_t, back, term, got_term, row(first_gain),
        ),
    )
    got, vectors = together(
        [s_chain, r_chain, both_chain],
        lambda: (lax.all_to_all(grad_t, "quad", 0, 0), vectors),
    )
    input_grad = whole(
        turn_out, "turn_out", 8, sds((1024, 512)), [], got.reshape(16, 4, 16, 512)
    ).reshape(64, 16, 512)
    early = lax.all_gather(jnp.concatenate([both_chain.keep, r_chain.keep]), "feat")
    input_grad, vectors, early = together(
        [s_chain], lambda: (input_grad, lax.all_to_all(vectors, SAMP, 0, 0), early)
    )
    vectors = whole(split, "split", 8, sds((24, 1088)), [], vectors)

    rows = s_chain.keep
    around_z = lambda value, mask: lax.ppermute(value, SAMP, [(j, j ^ mask) for j in range(8)])
    from_z = [around_z(rows[i // 2, i % 2], (0, 4, 2, 6)[i]) for i in (1, 2, 3)]
    outs = [shuffle(out, "feat", d + 1) for d, out in enumerate((out1, out2, out3))]
    from_z, vectors, outs = fence((from_z, vectors, outs))
    layer_output = whole(
        place, "place", 16, sds((4, 256, 512)), [], me, out0, *outs
    ).reshape(64, 16, 512)
    total = rows[0, 0].astype(F32)
    for value in from_z:
        total = total + value.astype(F32)
    vectors = jnp.pad(vectors[:3].reshape(-1), (0, 8 * 512 - 3 * 1088)).reshape(8, 512)
    last = lax.all_gather(jnp.concatenate([total.astype(BF), vectors]), "feat")
    mine = last[:, 64:].reshape(4, -1).astype(F32)
    mine = sum(mine[:, i * 1088 : (i + 1) * 1088] for i in range(3))
    mine = (mine[0] + mine[1]) + (mine[2] + mine[3])

    units_of = lambda rows: [rows[i].astype(F32) for i in (0, 2, 1, 3)]
    expand, feature = units_of(early[:, :64]), units_of(early[:, 64:128])
    reduce_grad = jnp.concatenate(units_of(early[:, 128:]))
    sample = units_of(last[:, :64])

    gain3, shift3, gain2, shift2, off2, bias_r = (mine[i * 64 : (i + 1) * 64] for i in range(6))
    feature_b, expand_b = mine[384:512], mine[512:768]
    gain1, shift1, off1 = (mine[768 + i * 64 : 832 + i * 64] for i in range(3))
    sample_b = mine[960:1088]
    columns = lambda blocks: jnp.concatenate(blocks, axis=1)

    return (
        layer_output, input_grad,
        gain1, shift1, columns(sample[:3]), sample_b, sample[3], off1,
        gain2, shift2, columns(feature[:3]), feature_b, feature[3], off2,
        gain3, shift3, columns(expand), expand_b,
        reduce_grad, bias_r,
    )


def spread_2(block, axis, owner):
    block = jnp.where(lax.axis_index(axis) == owner, block, jnp.zeros_like(block))
    return lax.psum(block, axis)


def layer_norm(values, gain_row, shift_row):
    center = jnp.mean(values, axis=-1, keepdims=True)
    spread = values - center
    variance = jnp.mean(spread * spread, axis=-1, keepdims=True)
    return spread * lax.rsqrt(variance + EPS) * gain_row + shift_row


def apply_weight(active, weight):
    return jnp.einsum("sfd,de->sfe", active, weight, preferred_element_type=jnp.float32)


def input_back(grad_out, weight):
    return jnp.einsum("sfe,de->sfd", grad_out, weight, preferred_element_type=jnp.float32)


def weight_grad(active, grad_out):
    return jnp.einsum("sfd,sfe->de", active, grad_out, preferred_element_type=jnp.float32)


def column_sum(values):
    return jnp.sum(values.astype(jnp.float32), axis=(0, 1))


def project(active, weight, bias_row):
    model_width = active.shape[-1]
    joined = apply_weight(active, weight)
    queries = (joined[..., :model_width] + bias_row[:model_width]).astype(jnp.bfloat16)
    key_part = joined[..., model_width : 2 * model_width].astype(jnp.bfloat16)
    value_part = (joined[..., 2 * model_width :] + bias_row[model_width:]).astype(jnp.bfloat16)
    return (queries, key_part, value_part)


def split_heads(values):
    return values.reshape(values.shape[0], values.shape[1], HEADS, HEAD_DIM)


def join_heads(values):
    return values.reshape(values.shape[0], values.shape[1], HEADS * HEAD_DIM)


def soft_weights(scores):
    top_score = jnp.max(scores, axis=-1, keepdims=True)
    raised = jnp.exp(scores - top_score)
    return raised / jnp.sum(raised, axis=-1, keepdims=True)


def feature_attend(queries, key_part, value_part):
    score_scale = HEAD_DIM ** (-0.5)
    scores = (
        jnp.einsum(
            "sfhd,sghd->shfg",
            split_heads(queries),
            split_heads(key_part),
            preferred_element_type=jnp.float32,
        )
        * score_scale
    )
    probability = soft_weights(scores)
    mixed = jnp.einsum(
        "shfg,sghd->sfhd",
        probability.astype(jnp.bfloat16),
        split_heads(value_part),
        preferred_element_type=jnp.float32,
    )
    return (join_heads(mixed).astype(jnp.bfloat16), probability)


def feature_grads(queries, key_part, value_part, probability, grad_mixed):
    score_scale = HEAD_DIM ** (-0.5)
    grad_heads = split_heads(grad_mixed)
    grad_weights = jnp.einsum(
        "sfhd,sghd->shfg", grad_heads, split_heads(value_part), preferred_element_type=jnp.float32
    )
    inner_sum = jnp.sum(probability * grad_weights, axis=-1, keepdims=True)
    grad_scores = (probability * (grad_weights - inner_sum)).astype(jnp.bfloat16)
    grad_queries = (
        jnp.einsum(
            "shfg,sghd->sfhd",
            grad_scores,
            split_heads(key_part),
            preferred_element_type=jnp.float32,
        )
        * score_scale
    )
    grad_keys = (
        jnp.einsum(
            "shfg,sfhd->sghd", grad_scores, split_heads(queries), preferred_element_type=jnp.float32
        )
        * score_scale
    )
    grad_values = jnp.einsum(
        "shfg,sfhd->sghd",
        probability.astype(jnp.bfloat16),
        grad_heads,
        preferred_element_type=jnp.float32,
    )
    return (join_heads(grad_queries), join_heads(grad_keys), join_heads(grad_values))


def local_large(
    layer_input,
    segment_ids,
    context_flags,
    first_gain,
    first_shift,
    sample_weight,
    sample_bias,
    sample_mixer,
    sample_offset,
    second_gain,
    second_shift,
    feature_weight,
    feature_bias,
    feature_mixer,
    feature_offset,
    third_gain,
    third_shift,
    expand_weight,
    expand_bias,
    reduce_weight,
    reduce_bias,
    cotangent,
):
    sample_rows = layer_input.shape[0]
    feature_rows = layer_input.shape[1]
    model_width = layer_input.shape[2]
    score_scale = HEAD_DIM ** (-0.5)
    shard_count = lax.axis_size("samp")
    context_shards = shard_count // 8
    total_context = context_shards * sample_rows
    residual_zero = layer_input.astype(jnp.float32)
    normed_one, norm_one_back = jax.vjp(layer_norm, residual_zero, first_gain, first_shift)
    active_one = normed_one.astype(jnp.bfloat16)
    queries_one, keys_one, values_one = project(active_one, sample_weight, sample_bias)
    my_index = lax.axis_index("samp")
    shard_flags = context_flags.reshape(shard_count, sample_rows)[:, 0]
    shard_rank = jnp.cumsum(shard_flags) - 1
    shard_ids = jnp.arange(shard_count, dtype=jnp.int32)
    slot_ids = jnp.arange(context_shards, dtype=jnp.int32)
    root_hits = (shard_rank[None, :] == slot_ids[:, None]) & (shard_flags[None, :] == 1)
    roots = jnp.sum(jnp.where(root_hits, shard_ids[None, :], 0), axis=1)
    context_tasks = jnp.take(segment_ids.reshape(shard_count, sample_rows), roots, axis=0).reshape(
        total_context
    )
    local_tasks = lax.dynamic_slice_in_dim(segment_ids, my_index * sample_rows, sample_rows)
    allowed = local_tasks[:, None] == context_tasks[None, :]
    is_context = shard_flags[my_index] == 1
    own_rank = jnp.maximum(shard_rank[my_index], 0)
    own_block = jnp.concatenate([keys_one, values_one], axis=-1)

    def fetch_rows(step, buffer):
        piece = spread_2(own_block, "samp", roots[step])
        return lax.dynamic_update_slice_in_dim(buffer, piece, step * sample_rows, 0)

    empty_rows = jnp.zeros((total_context, feature_rows, 2 * model_width), jnp.bfloat16)
    fetched = lax.fori_loop(0, context_shards, fetch_rows, empty_rows)
    context_keys = fetched[..., :model_width]
    context_values = fetched[..., model_width:]
    query_heads = split_heads(queries_one)
    key_heads = split_heads(context_keys)
    value_heads = split_heads(context_values)
    scores = (
        jnp.einsum("sfhd,cfhd->fhsc", query_heads, key_heads, preferred_element_type=jnp.float32)
        * score_scale
    )
    sample_prob = soft_weights(jnp.where(allowed[None, None], scores, MASKED))
    sample_weights = sample_prob.astype(jnp.bfloat16)
    mixed_one = join_heads(
        jnp.einsum(
            "fhsc,cfhd->sfhd", sample_weights, value_heads, preferred_element_type=jnp.float32
        )
    ).astype(jnp.bfloat16)
    residual_one = residual_zero + apply_weight(mixed_one, sample_mixer) + sample_offset
    normed_two, norm_two_back = jax.vjp(layer_norm, residual_one, second_gain, second_shift)
    active_two = normed_two.astype(jnp.bfloat16)
    queries_two, keys_two, values_two = project(active_two, feature_weight, feature_bias)
    all_keys, all_values = (
        lax.all_gather(keys_two, "feat", axis=1, tiled=True),
        lax.all_gather(values_two, "feat", axis=1, tiled=True),
    )
    mixed_two, feature_prob = feature_attend(queries_two, all_keys, all_values)
    residual_two = residual_one + apply_weight(mixed_two, feature_mixer) + feature_offset
    normed_three, norm_three_back = jax.vjp(layer_norm, residual_two, third_gain, third_shift)
    active_three = normed_three.astype(jnp.bfloat16)
    expanded = apply_weight(active_three, expand_weight) + expand_bias
    activated, gelu_back = jax.vjp(partial(jax.nn.gelu, approximate=False), expanded)
    hidden = activated.astype(jnp.bfloat16)
    layer_output = (residual_two + apply_weight(hidden, reduce_weight) + reduce_bias).astype(
        jnp.bfloat16
    )
    grad_out = cotangent.astype(jnp.float32)
    grad_branch = cotangent
    reduce_bias_grad = column_sum(grad_branch)
    reduce_weight_grad = weight_grad(hidden, grad_branch)
    grad_hidden = input_back(grad_branch, reduce_weight).astype(jnp.bfloat16)
    grad_expanded = gelu_back(grad_hidden.astype(jnp.float32))[0].astype(jnp.bfloat16)
    expand_bias_grad = column_sum(grad_expanded)
    expand_weight_grad = weight_grad(active_three, grad_expanded)
    grad_norm, third_gain_grad, third_shift_grad = norm_three_back(
        input_back(grad_expanded, expand_weight)
    )
    grad_two = grad_out + grad_norm
    grad_branch = grad_two.astype(jnp.bfloat16)
    feature_offset_grad = column_sum(grad_branch)
    feature_mixer_grad = weight_grad(mixed_two, grad_branch)
    grad_mixed = input_back(grad_branch, feature_mixer).astype(jnp.bfloat16)
    grad_queries, grad_keys, grad_values = feature_grads(
        queries_two, all_keys, all_values, feature_prob, grad_mixed
    )
    own_key_grads, own_value_grads = (
        lax.psum_scatter(grad_keys, "feat", scatter_dimension=1, tiled=True),
        lax.psum_scatter(grad_values, "feat", scatter_dimension=1, tiled=True),
    )
    grad_project = jnp.concatenate(
        [
            grad_queries.astype(jnp.bfloat16),
            own_key_grads.astype(jnp.bfloat16),
            own_value_grads.astype(jnp.bfloat16),
        ],
        axis=-1,
    )
    feature_weight_grad = weight_grad(active_two, grad_project)
    feature_bias_grad = jnp.concatenate(
        [
            column_sum(grad_project[..., :model_width]),
            column_sum(grad_project[..., 2 * model_width :]),
        ]
    )
    grad_norm, second_gain_grad, second_shift_grad = norm_two_back(
        input_back(grad_project, feature_weight)
    )
    grad_one = grad_two + grad_norm
    grad_branch = grad_one.astype(jnp.bfloat16)
    sample_offset_grad = column_sum(grad_branch)
    sample_mixer_grad = weight_grad(mixed_one, grad_branch)
    grad_heads = split_heads(input_back(grad_branch, sample_mixer).astype(jnp.bfloat16))
    grad_weights = jnp.einsum(
        "sfhd,cfhd->fhsc", grad_heads, value_heads, preferred_element_type=jnp.float32
    )
    inner_sum = jnp.sum(sample_prob * grad_weights, axis=-1, keepdims=True)
    grad_scores = (sample_prob * (grad_weights - inner_sum)).astype(jnp.bfloat16)
    grad_queries = (
        join_heads(
            jnp.einsum(
                "fhsc,cfhd->sfhd", grad_scores, key_heads, preferred_element_type=jnp.float32
            )
        )
        * score_scale
    ).astype(jnp.bfloat16)
    key_terms = (
        join_heads(
            jnp.einsum(
                "fhsc,sfhd->cfhd", grad_scores, query_heads, preferred_element_type=jnp.float32
            )
        )
        * score_scale
    )
    value_terms = join_heads(
        jnp.einsum(
            "fhsc,sfhd->cfhd", sample_weights, grad_heads, preferred_element_type=jnp.float32
        )
    )
    term_block = jnp.concatenate([key_terms, value_terms], axis=-1)
    summed_terms = lax.psum_scatter(term_block, "samp", scatter_dimension=0, tiled=True)
    summed_rows = lax.all_gather(summed_terms.astype(jnp.bfloat16), "samp", axis=0, tiled=True)
    own_grads = lax.dynamic_slice_in_dim(summed_rows, own_rank * sample_rows, sample_rows, 0)
    own_grads = jnp.where(is_context, own_grads, jnp.zeros_like(own_grads))
    grad_project = jnp.concatenate([grad_queries, own_grads], axis=-1)
    sample_weight_grad = weight_grad(active_one, grad_project)
    sample_bias_grad = jnp.concatenate(
        [column_sum(grad_queries), column_sum(own_grads[..., model_width:])]
    )
    grad_norm, first_gain_grad, first_shift_grad = norm_one_back(
        input_back(grad_project, sample_weight)
    )
    input_grad = (grad_one + grad_norm).astype(jnp.bfloat16)
    summed = lax.psum(
        (
            first_gain_grad,
            first_shift_grad,
            sample_weight_grad,
            sample_bias_grad,
            sample_mixer_grad,
            sample_offset_grad,
            second_gain_grad,
            second_shift_grad,
            feature_weight_grad,
            feature_bias_grad,
            feature_mixer_grad,
            feature_offset_grad,
            third_gain_grad,
            third_shift_grad,
            expand_weight_grad,
            expand_bias_grad,
            reduce_weight_grad,
            reduce_bias_grad,
        ),
        "feat",
    )
    shares = (
        lax.psum_scatter(summed[0], "samp", scatter_dimension=0, tiled=True),
        lax.psum_scatter(summed[1], "samp", scatter_dimension=0, tiled=True),
        lax.psum_scatter(summed[2], "samp", scatter_dimension=0, tiled=True),
        lax.psum_scatter(summed[3], "samp", scatter_dimension=0, tiled=True),
        lax.psum_scatter(summed[4], "samp", scatter_dimension=0, tiled=True),
        lax.psum_scatter(summed[5], "samp", scatter_dimension=0, tiled=True),
        lax.psum_scatter(summed[6], "samp", scatter_dimension=0, tiled=True),
        lax.psum_scatter(summed[7], "samp", scatter_dimension=0, tiled=True),
        lax.psum_scatter(summed[8], "samp", scatter_dimension=0, tiled=True),
        lax.psum_scatter(summed[9], "samp", scatter_dimension=0, tiled=True),
        lax.psum_scatter(summed[10], "samp", scatter_dimension=0, tiled=True),
        lax.psum_scatter(summed[11], "samp", scatter_dimension=0, tiled=True),
        lax.psum_scatter(summed[12], "samp", scatter_dimension=0, tiled=True),
        lax.psum_scatter(summed[13], "samp", scatter_dimension=0, tiled=True),
        lax.psum_scatter(summed[14], "samp", scatter_dimension=0, tiled=True),
        lax.psum_scatter(summed[15], "samp", scatter_dimension=0, tiled=True),
        lax.psum_scatter(summed[16], "samp", scatter_dimension=0, tiled=True),
        lax.psum_scatter(summed[17], "samp", scatter_dimension=0, tiled=True),
    )
    return (
        layer_output,
        input_grad,
        shares[0],
        shares[1],
        shares[2],
        shares[3],
        shares[4],
        shares[5],
        shares[6],
        shares[7],
        shares[8],
        shares[9],
        shares[10],
        shares[11],
        shares[12],
        shares[13],
        shares[14],
        shares[15],
        shares[16],
        shares[17],
    )


def solution(mesh):
    if mesh.shape["samp"] == 8 and mesh.shape["feat"] == 4:
        return solution_small(mesh)
    return jax.shard_map(
        local_large,
        mesh=mesh,
        in_specs=(
            P("samp", "feat", None),
            P(),
            P(),
            P(),
            P(),
            P(),
            P(),
            P(),
            P(),
            P(),
            P(),
            P(),
            P(),
            P(),
            P(),
            P(),
            P(),
            P(),
            P(),
            P(),
            P(),
            P("samp", "feat", None),
        ),
        out_specs=(
            P("samp", "feat", None),
            P("samp", "feat", None),
            P("samp"),
            P("samp"),
            P("samp", None),
            P("samp"),
            P("samp", None),
            P("samp"),
            P("samp"),
            P("samp"),
            P("samp", None),
            P("samp"),
            P("samp", None),
            P("samp"),
            P("samp"),
            P("samp"),
            P("samp", None),
            P("samp"),
            P("samp", None),
            P("samp"),
        ),
        check_vma=False,
    )


def solution_small(mesh):
    mesh = jax.sharding.Mesh(mesh.devices.reshape(2, 4, 4), ("half", "quad", "feat"))
    tokens, copied = P(SAMP, "feat", None), P()
    vector, matrix = P(SAMP), P(SAMP, None)
    return jax.shard_map(
        local_small,
        mesh=mesh,
        in_specs=(tokens,) + (copied,) * 20 + (tokens,),
        out_specs=(
            tokens, tokens, vector, vector, matrix, vector, matrix, vector,
            vector, vector, matrix, vector, matrix, vector,
            vector, vector, matrix, vector, matrix, vector,
        ),
        check_vma=False,
    )
```

```python
from functools import partial

import jax
import jax.numpy as jnp
from jax import lax
from jax.experimental import pallas as pl
from jax.experimental.pallas import tpu as pltpu
from jax.sharding import PartitionSpec as P

HEADS = 8
HEAD_DIM = 64
EPS = 1e-05
MASKED = -1000000000.0
SCALE = HEAD_DIM ** (-0.5)
QUAD = 4 * HEAD_DIM
BF = jnp.bfloat16
F32 = jnp.float32


def mm(a, b, ca=1, cb=0):
    return lax.dot_general(a, b, (((ca,), (cb,)), ((), ())), preferred_element_type=F32)


def norm_parts(values):
    center = jnp.mean(values, axis=-1, keepdims=True)
    spread = values - center
    variance = jnp.mean(spread * spread, axis=-1, keepdims=True)
    inverse = lax.rsqrt(variance + EPS)
    return spread * inverse, inverse


def norm_back(grad, unit, inverse, gain):
    scaled = grad * gain
    first = jnp.mean(scaled, axis=-1, keepdims=True)
    second = jnp.mean(scaled * unit, axis=-1, keepdims=True)
    return (scaled - first - unit * second) * inverse


def lane_ids(rows):
    return lax.broadcasted_iota(jnp.int32, (rows, 128), 1)


def group_reduce(values, op, fill):
    rows = values.shape[0]
    low = lane_ids(rows) < HEAD_DIM
    outs = []
    for t in range(values.shape[1] // 128):
        tile = values[:, t * 128 : (t + 1) * 128]
        left = op(jnp.where(low, tile, fill), axis=1, keepdims=True)
        right = op(jnp.where(low, fill, tile), axis=1, keepdims=True)
        outs.append(jnp.where(low, left, right))
    return jnp.concatenate(outs, axis=1)


def head_masks(dtype):
    lanes = lax.broadcasted_iota(jnp.int32, (1, QUAD), 1) // HEAD_DIM
    return [jnp.where(lanes == h, 1.0, 0.0).astype(dtype) for h in range(4)]


def stack_heads(part, masks):
    return jnp.concatenate([part * m for m in masks], axis=0)


def pick_heads(stacked, masks):
    rows = stacked.shape[0] // 4
    total = stacked[:rows] * masks[0]
    for h in range(1, 4):
        total = total + stacked[h * rows : (h + 1) * rows] * masks[h]
    return total


def attend(q, k, v, masks, allow):
    outs, probs = [], []
    for quad in range(2):
        cols = slice(quad * QUAD, (quad + 1) * QUAD)
        scores = mm(q[:, cols], stack_heads(k[:, cols], masks), 1, 1)
        if allow is not None:
            scores = jnp.where(allow, scores, MASKED)
        raised = jnp.exp(scores - group_reduce(scores, jnp.max, -jnp.inf))
        prob = raised / group_reduce(raised, jnp.sum, 0.0)
        outs.append(mm(prob.astype(BF), stack_heads(v[:, cols], masks)))
        probs.append(prob)
    return jnp.concatenate(outs, axis=1), jnp.concatenate(probs, axis=1)


def attend_back(q, k, v, prob, grad, masks, masks32):
    dqs, dks, dvs = [], [], []
    for quad in range(2):
        cols = slice(quad * QUAD, (quad + 1) * QUAD)
        p, g = prob[:, cols], grad[:, cols]
        back = mm(g, stack_heads(v[:, cols], masks), 1, 1)
        inner = group_reduce(p * back, jnp.sum, 0.0)
        gs = (p * (back - inner)).astype(BF)
        dqs.append(mm(gs, stack_heads(k[:, cols], masks)) * SCALE)
        dks.append(pick_heads(mm(gs, q[:, cols], 0, 0), masks32))
        dvs.append(pick_heads(mm(p.astype(BF), g, 0, 0), masks32))
    join = lambda parts: jnp.concatenate(parts, axis=1).astype(BF)
    return join(dqs), join(dks), join(dvs)


def swap_matrix(rows=16):
    n = rows * 16
    r = lax.broadcasted_iota(jnp.int32, (n, n), 0)
    c = lax.broadcasted_iota(jnp.int32, (n, n), 1)
    return jnp.where((r // rows == c % 16) & (r % rows == c // 16), 1.0, 0.0).astype(BF)


def swap(matrix, values, back=False):
    return mm(matrix, values, 0 if back else 1, 0).astype(BF)


def gelu_parts(u):
    cdf = 0.5 * (1.0 + lax.erf(u * (2.0**-0.5)))
    density = jnp.exp(u * u * -0.5) * 0.3989422804014327
    return cdf, density


def col_sum(values):
    return jnp.sum(values.astype(F32), axis=0, keepdims=True)


def turn_in(x_ref, out_ref):
    matrix = swap_matrix()
    for d in range(4):
        rows = x_ref[d * 256 : (d + 1) * 256]
        out_ref[:, d] = swap(matrix, rows).reshape(16, 16, 512)


def turn_out(got_ref, out_ref):
    matrix = swap_matrix()
    for d in range(4):
        out_ref[d * 256 : (d + 1) * 256] = swap(matrix, got_ref[:, d].reshape(256, 512))


def project_queries(x_ref, gain_ref, shift_ref, w_ref, b_ref, act_ref, q_ref):
    unit, _ = norm_parts(x_ref[:, 0].reshape(256, 512).astype(F32))
    act = (unit * gain_ref[...] + shift_ref[...]).astype(BF)
    act_ref[0] = act
    q = (mm(act, w_ref[:, :512]) + b_ref[:, :512]).astype(BF)
    q_ref[0] = q * jnp.asarray(SCALE, BF)


def forward_one(
    me_ref, q_ref, own_ref, got_ref, x_ref, tasks_ref, context_ref, gain_ref, shift_ref, w_ref,
    b_ref, wm_ref, off_ref,
    r_ref, o_ref, c_ref, cact_ref, k_ref, v_ref, p_ref,
):
    here = me_ref[1] == me_ref[2]
    masks = head_masks(BF)
    allow = tasks_ref[...] == context_ref[...]

    @pl.when(here)
    def _():
        c_ref[...] = own_ref[...]

    @pl.when(jnp.logical_not(here))
    def _():
        c_ref[...] = got_ref[...]

    unit, _ = norm_parts(c_ref[0].astype(F32))
    act = (unit * gain_ref[...] + shift_ref[...]).astype(BF)
    cact_ref[0] = act
    kv = mm(act, w_ref[:, 512:])
    k = kv[:, :512].astype(BF)
    v = (kv[:, 512:] + b_ref[:, 512:]).astype(BF)
    k_ref[0], v_ref[0] = k, v
    out, prob = attend(q_ref[0], k, v, masks, allow)
    o_ref[0] = out.astype(BF)
    p_ref[0] = prob
    r1 = x_ref[:, 0].reshape(256, 512).astype(F32) + mm(o_ref[0], wm_ref[...]) + off_ref[...]
    r_ref[:, :, 0] = r1.astype(BF).reshape(4, 4, 16, 512)


HALF = 512


def middle(me_ref, *refs):
    (
        r1_ref, c0, c1, c2, c3, g2_ref, s2_ref, bf_ref, off2_ref, g3_ref, s3_ref, be_ref, br_ref,
    ) = refs[:13]
    weights_hbm = refs[13:17]
    gb1_ref, vec_ref, bias_ref, out0, out1, out2, out3 = refs[17:24]
    targets = refs[24:28]
    wf_ref, wm2_ref, we_ref, wr_ref = refs[28:32]
    kept = refs[32:40]
    (
        r_scr, g_scr, q_scr, k_scr, v_scr, p_scr, e_scr, gs_scr, go_scr, out_scr, back_scr,
        part_p, part_q, turn, in_sems, out_sems,
    ) = refs[40:]
    me, step = me_ref[0], pl.program_id(0)
    tokens = pl.ds(pl.multiple_of(step * HALF, HALF), HALF)
    a2_ref, dqkv_ref, o2_ref, gb2_ref, a3_ref, gu_ref, hid_ref, gb3_ref = (
        ref.at[tokens] for ref in kept
    )
    loads = [
        pltpu.make_async_copy(source, target, in_sems.at[i])
        for i, (source, target) in enumerate(zip(weights_hbm, refs[28:32]))
    ]

    def first(make):
        pl.when(step == 0)(make)

    matrix = swap_matrix()
    masks, masks32 = head_masks(BF), head_masks(F32)

    @first
    def _():
        loads[0].start()
        loads[1].start()
        for f in range(4):
            r_scr[f] = swap(matrix, r1_ref[:, f].reshape(256, 512))

    now = pl.ds(pl.multiple_of(step * 128, 128), 128)

    def gather(*refs):
        return jnp.concatenate(
            [ref[s * 16 : (s + 1) * 16] for s in range(8) for ref in refs], axis=0
        )

    def scatter(values, *refs):
        for s in range(8):
            for d, ref in enumerate(refs):
                at = (s * 4 + d) * 16
                ref[s * 16 : (s + 1) * 16] = values[at : at + 16]

    def each_sample(body):
        def step(i, carry):
            for j in range(SAMPLE_UNROLL):
                rows = pl.ds(pl.multiple_of((i * SAMPLE_UNROLL + j) * 64, 64), 64)
                for quad in range(2):
                    body(rows, slice(quad * QUAD, (quad + 1) * QUAD))
            return carry

        lax.fori_loop(0, 8 // SAMPLE_UNROLL, step, 0)

    gb3_ref[...] = gather(c0, c1, c2, c3)
    r1 = gather(*(r_scr.at[d ^ me, now] for d in range(4))).astype(F32)
    unit2, inv2 = norm_parts(r1)
    a2_ref[...] = (unit2 * g2_ref[...] + s2_ref[...]).astype(BF)

    @first
    def _():
        loads[0].wait()
        loads[2].start()
        loads[3].start()

    q = (mm(a2_ref[...], wf_ref[:, :512]) + bf_ref[:, :512]).astype(BF)
    q_scr[...] = q * jnp.asarray(SCALE, BF)
    k_scr[...] = mm(a2_ref[...], wf_ref[:, 512:1024]).astype(BF)
    v_scr[...] = (mm(a2_ref[...], wf_ref[:, 1024:]) + bf_ref[:, 512:]).astype(BF)

    def score(rows, cols):
        p_scr[rows, cols] = mm(q_scr[rows, cols], stack_heads(k_scr[rows, cols], masks), 1, 1)

    each_sample(score)
    for i in range(4):
        rows = slice(i * 128, (i + 1) * 128)
        scores = p_scr[rows]
        raised = jnp.exp(scores - group_reduce(scores, jnp.max, -jnp.inf))
        p_scr[rows] = raised / group_reduce(raised, jnp.sum, 0.0)

    def mix(rows, cols):
        o2_ref[rows, cols] = mm(
            p_scr[rows, cols].astype(BF), stack_heads(v_scr[rows, cols], masks)
        ).astype(BF)

    each_sample(mix)
    first(loads[1].wait)
    r2 = r1 + mm(o2_ref[...], wm2_ref[...]) + off2_ref[...]
    unit3, inv3 = norm_parts(r2)
    a3_ref[...] = (unit3 * g3_ref[...] + s3_ref[...]).astype(BF)
    first(loads[2].wait)
    first(loads[3].wait)

    @first
    def _():
        vec_ref[...] = jnp.zeros((8, 512), F32)
        bias_ref[...] = jnp.zeros((1, 2048), F32)

    out_scr[...] = r2 + br_ref[...]
    back_scr[...] = jnp.zeros((HALF, 512), F32)

    def expand(b, carry):
        cols = pl.ds(pl.multiple_of(b * WIDE, WIDE), WIDE)
        u = mm(a3_ref[...], we_ref[:, cols]) + be_ref[:, cols]
        cdf, density = gelu_parts(u)
        hidden = (u * cdf).astype(BF)
        hid_ref[:, cols] = hidden
        gh = mm(gb3_ref[...], wr_ref[cols, :], 1, 1).astype(BF).astype(F32)
        gu = (gh * (cdf + u * density)).astype(BF)
        gu_ref[:, cols] = gu
        bias_ref[:, cols] += col_sum(gu)
        out_scr[...] += mm(hidden, wr_ref[cols, :])
        back_scr[...] += mm(gu, we_ref[:, cols], 1, 1)
        return carry

    lax.fori_loop(0, 2048 // WIDE, expand, 0, unroll=EXPAND_UNROLL)
    scatter(out_scr[...].astype(BF), out0, out1, out2, out3)
    back, cot = back_scr[...], gb3_ref[...]
    vecs = [col_sum(back * unit3), col_sum(back)]
    gr2 = cot.astype(F32) + norm_back(back, unit3, inv3, g3_ref[...])
    gb2_ref[...] = gr2.astype(BF)
    go_scr[...] = mm(gb2_ref[...], wm2_ref[...], 1, 1).astype(BF)

    def weigh(rows, cols):
        e_scr[rows, cols] = mm(go_scr[rows, cols], stack_heads(v_scr[rows, cols], masks), 1, 1)

    each_sample(weigh)
    for i in range(4):
        rows = slice(i * 128, (i + 1) * 128)
        prob, grad = p_scr[rows], e_scr[rows]
        inner = group_reduce(prob * grad, jnp.sum, 0.0)
        gs_scr[rows] = (prob * (grad - inner)).astype(BF)

    def spread(rows, cols):
        gs, at = gs_scr[rows, cols], cols.start
        dq = mm(gs, stack_heads(k_scr[rows, cols], masks)) * SCALE
        dqkv_ref[rows, at : at + QUAD] = dq.astype(BF)
        dk = pick_heads(mm(gs, q_scr[rows, cols], 0, 0), masks32)
        dqkv_ref[rows, 512 + at : 512 + at + QUAD] = dk.astype(BF)
        dv = pick_heads(mm(p_scr[rows, cols].astype(BF), go_scr[rows, cols], 0, 0), masks32)
        dqkv_ref[rows, 1024 + at : 1024 + at + QUAD] = dv.astype(BF)

    each_sample(spread)
    dqkv = dqkv_ref[...]
    back = mm(dqkv, wf_ref[...], 1, 1)
    vecs += [col_sum(back * unit2), col_sum(back)]
    gr1 = gr2 + norm_back(back, unit2, inv2, g2_ref[...])
    scatter(gr1.astype(BF), *(g_scr.at[d ^ me, now] for d in range(4)))
    vecs += [
        col_sum(gb2_ref[...]), col_sum(cot), col_sum(dqkv[:, :512]), col_sum(dqkv[:, 1024:])
    ]
    vec_ref[...] += jnp.concatenate(vecs, axis=0)

    @pl.when(step == 1)
    def _():
        for f in range(4):
            gb1_ref[:, f] = swap(matrix, g_scr[f]).reshape(4, 4, 16, 512)
        grads_middle(me_ref, kept, (part_p, part_q), turn, targets, out_sems)


SAMPLE_UNROLL = 8
EXPAND_UNROLL = True
WIDE = 512


def backward_one(
    me_ref, g_ref, o_ref, act_ref, cact_ref, x_ref, c_ref, q_ref, k_ref, v_ref,
    p_ref, w_ref, wm_ref,
    gb1_ref, a_ref, term_ref, vec_ref, keep_ref, send_ref,
    dq_scr, dkv_scr, g_scr,
):
    masks, masks32 = head_masks(BF), head_masks(F32)

    @pl.when(pl.program_id(0) == 0)
    def _():
        vec_ref[...] = jnp.zeros((8, 512), F32)

    gb1 = g_ref[:, :, 0].reshape(256, 512)
    gb1_ref[0] = gb1
    go = mm(gb1, wm_ref[...], 1, 1).astype(BF)
    dq, dk, dv = attend_back(q_ref[0], k_ref[0], v_ref[0], p_ref[0], go, masks, masks32)
    dkv = jnp.concatenate([dk, dv], axis=1)
    step = pl.program_id(0)
    rows = pl.ds(pl.multiple_of(step * 256, 256), 256)
    dq_scr[rows], g_scr[rows] = dq, gb1
    dkv_scr[pl.ds(pl.multiple_of(step * 64, 64), 64)] = dkv

    @pl.when(step == 3)
    def _():
        whole_rows = lambda ref: ref[...].reshape(-1, 512)
        act_c = whole_rows(cact_ref)
        terms = (
            (whole_rows(act_ref), dq_scr[...]), (act_c, dkv_scr[:, :512]),
            (act_c, dkv_scr[:, 512:]), (whole_rows(o_ref), g_scr[...]),
        )
        for unit, (left, right) in enumerate(terms):
            place_sample(me_ref, mm(left, right, 0, 0).astype(BF), unit, keep_ref, send_ref)

    back = mm(dq, w_ref[:, :512], 1, 1)
    a_ref[0] = back
    term = mm(dkv, w_ref[:, 512:], 1, 1)
    term_ref[0] = term.astype(BF)
    unit, _ = norm_parts(x_ref[:, 0].reshape(256, 512).astype(F32))
    unit_c, _ = norm_parts(c_ref[0].astype(F32))
    zero = jnp.zeros((3, 512), F32)
    vec_ref[...] += jnp.concatenate(
        [
            col_sum(back * unit) + col_sum(term * unit_c), col_sum(back) + col_sum(term),
            col_sum(gb1), col_sum(dq), col_sum(dv), zero,
        ],
        axis=0,
    )


def backward_input(me_ref, gb1_ref, x_ref, a_ref, term_ref, got_ref, gain_ref, grad_ref, a_scr):
    here, quad = me_ref[1] == me_ref[2], me_ref[3]
    unit, inverse = norm_parts(x_ref[:, 0].reshape(256, 512).astype(F32))
    a_scr[...] = a_ref[0].reshape(4, 64, 512)

    @pl.when(here)
    def _():
        a_scr[quad] += term_ref[0].astype(F32) + got_ref[0].astype(F32)

    back = a_scr[...].reshape(256, 512)
    grad = gb1_ref[0].astype(F32) + norm_back(back, unit, inverse, gain_ref[...])
    grad_ref[:, 0] = grad.astype(BF).reshape(4, 64, 512)


def split(got_ref, out_ref):
    rest = got_ref[...]
    out_ref[...] = jnp.zeros_like(out_ref)
    for i in range(3):
        term = rest.astype(BF)
        out_ref[i : i + 1] = term
        rest = rest - term.astype(F32)


def place(me_ref, b0, b1, b2, b3, out_ref):
    for d, ref in enumerate((b0, b1, b2, b3)):
        out_ref[d ^ me_ref[0]] = ref[...]


def piece_index(me_ref, unit, shard, order):
    core, xx, yy, zz = me_ref[4], me_ref[5], me_ref[6], me_ref[7]
    other_z = (shard >> 1) ^ zz
    bit = {
        "x": (unit & 1) ^ xx, "y": (shard & 1) ^ yy, "z": other_z & 1, "w": other_z >> 1,
    }
    index = sum(bit[name] * weight for name, weight in zip(order, (8, 4, 2, 1)))
    return (unit >> 1) ^ core, index


def grads_middle(me_ref, kept, staged, turn, targets, out_sems):
    act2, dqkv, o2, gb2, act3, gu, hid, gb3 = kept
    stores = []

    def put(part):
        for i in range(2):
            source = staged[part].at[pl.ds(16 * i, 16)]
            place = 2 * part + i
            stores.append(pltpu.make_async_copy(source, targets[place], out_sems.at[place]))
            stores[-1].start()

    def loop(count, body):
        lax.fori_loop(0, count, lambda n, carry: (body(n), carry)[1], 0)

    block = lambda n: pl.ds(pl.multiple_of(n * 512, 512), 512)

    def place_piece(part, value, unit, shard, rows):
        send, index = piece_index(me_ref, unit, shard, ("xyzw", "yxzw")[part])
        staged[part][send * 16 + index, rows] = value

    def place_unit(part, value, unit):
        for shard in range(8):
            place_piece(part, value[shard * 64 : (shard + 1) * 64], unit, shard, slice(0, 64))

    def from_hidden(n):
        piece = mm(hid[:, block(n)], gb3[...], 0, 0).astype(BF)
        for i in range(8):
            for part in range(2):
                at = i * 64 + part * 32
                rows = piece[at : at + 32]
                place_piece(part, rows, i % 4, 2 * n + i // 4, slice(64, 96))

    loop(4, from_hidden)
    turn[...] = act3[...].T

    def from_expand(n):
        place_unit(1, mm(turn[...], gu[:, block(n)]).astype(BF), n)

    loop(4, from_expand)
    put(1)
    turn[...] = act2[...].T

    def from_feature(n):
        place_unit(0, mm(turn[...], dqkv[:, block(n)]).astype(BF), n)

    loop(3, from_feature)
    place_unit(0, mm(o2[...], gb2[...], 0, 0).astype(BF), 3)
    put(0)
    for store in stores:
        store.wait()


def place_sample(me_ref, value, unit, keep_ref, send_ref):
    for which, order in enumerate(("xyzw", "yxzw")):
        for shard in range(8):
            at = shard * 64 + which * 32
            send, index = piece_index(me_ref, unit, shard, order)

            @pl.when(send == 0)
            def _(at=at, index=index):
                keep_ref[which, index] = value[at : at + 32]

            @pl.when(send == 1)
            def _(at=at, index=index):
                send_ref[which, index] = value[at : at + 32]


def spec(shape, index=None):
    return pl.BlockSpec(shape, index if index is not None else (lambda *a: (0,) * len(shape)))


def sds(shape, dtype=BF):
    return jax.ShapeDtypeStruct(shape, dtype)


def big(shape, dtype=BF):
    return pltpu.HBM(shape, dtype)


def outside(array):
    if array.size * array.dtype.itemsize < 1 << 18:
        return array
    return pltpu.with_memory_space_constraint(array, pltpu.HBM)


def params(limit):
    return pltpu.CompilerParams(vmem_limit_bytes=limit << 20)


def row(vector):
    return vector.reshape(1, -1)


def cost(microseconds):
    return pl.CostEstimate(
        flops=int(microseconds * 1.1e9), transcendentals=0, bytes_accessed=int(microseconds * 2e6)
    )


def whole_block(out):
    shape = out.shape
    return pl.BlockSpec(shape, lambda i: (0,) * len(shape))


def moving_block(shape, axis):
    block = tuple(1 if i == axis else n for i, n in enumerate(shape))
    return pl.BlockSpec(block, lambda i: tuple(i if j == axis else 0 for j in range(len(shape))))


def by_feature(kernel, name, limit, outs, scratch, *inputs, time=3):
    arrays, specs = [], []
    for entry in inputs:
        array, axis = entry if isinstance(entry, tuple) else (entry, None)
        if array.ndim == 1:
            arrays.append(array)
            specs.append(pl.BlockSpec(memory_space=pltpu.SMEM))
            continue
        arrays.append(outside(array))
        specs.append(whole_block(array) if axis is None else moving_block(array.shape, axis))
    return pl.pallas_call(
        kernel,
        grid=(4,),
        out_shape=tuple(out for out, _ in outs),
        in_specs=specs,
        out_specs=[
            whole_block(out) if axis is None else moving_block(out.shape, axis)
            for out, axis in outs
        ],
        scratch_shapes=scratch,
        compiler_params=params(limit),
        cost_estimate=cost(time),
        name=name,
    )(*arrays)


def whole(kernel, name, limit, outs, scratch, *inputs, steps=1, time=3):
    arrays, specs = [], []
    for entry in inputs:
        if not isinstance(entry, tuple) and entry.ndim == 1:
            arrays.append(entry)
            specs.append(pl.BlockSpec(memory_space=pltpu.SMEM))
            continue
        array, block, index = entry if isinstance(entry, tuple) else (entry, None, None)
        arrays.append(outside(array))
        block = array.shape if block is None else block
        index = (0,) * array.ndim if index is None else index
        if not callable(index):
            index = lambda i, index=index: index
        specs.append(pl.BlockSpec(block, index))
    return pl.pallas_call(
        kernel,
        grid=(steps,),
        out_shape=outs,
        in_specs=specs,
        out_specs=jax.tree.map(whole_block, outs, is_leaf=lambda o: hasattr(o, "dtype")),
        scratch_shapes=scratch,
        compiler_params=params(limit),
        cost_estimate=cost(time),
        name=name,
    )(*arrays)


def shuffle(value, axis, mask):
    size = lax.axis_size(axis)
    return lax.ppermute(value, axis, [(i, i ^ mask) for i in range(size)])


SAMP = ("half", "quad")
CORE, X, Y, Z, W = ("feat", 1), ("feat", 2), ("quad", 1), ("quad", 2), ("half", 1)


def at(stacked, index, axis=0):
    return lax.dynamic_index_in_dim(stacked, index, axis, keepdims=False)


def fence(tree):
    return lax.optimization_barrier(tree)


def plus(a, b):
    return (a.astype(F32) + b.astype(F32)).astype(BF)


class Chain:
    def __init__(self, keep, sent, dims):
        self.keep, self.sent, self.dims = keep, sent, (CORE,) + dims

    def start(self):
        return shuffle(self.sent, *self.dims[0])

    def take(self, got):
        self.dims = self.dims[1:]
        if self.dims:
            self.keep, self.sent = plus(self.keep[0], got[0]), plus(self.keep[1], got[1])
        else:
            self.keep = plus(self.keep, got)


def together(chains, make=lambda: ()):
    got = [chain.start() for chain in chains]
    got, other = fence((got, make()))
    for chain, value in zip(chains, got):
        chain.take(value)
    return other


def local_small(
    layer_input, segment_ids, context_flags,
    first_gain, first_shift, sample_weight, sample_bias, sample_mixer, sample_offset,
    second_gain, second_shift, feature_weight, feature_bias, feature_mixer, feature_offset,
    third_gain, third_shift, expand_weight, expand_bias, reduce_weight, reduce_bias, cotangent,
):
    half, quad, feat = (lax.axis_index(name) for name in ("half", "quad", "feat"))
    samp = half * 4 + quad
    core, xx = feat % 2, feat // 2
    flags = context_flags.reshape(8, 64)[:, 0]
    root = jnp.sum(jnp.where(flags == 1, jnp.arange(8, dtype=jnp.int32), 0))
    me = [feat, half, root // 4, root % 4, core, xx, samp % 2, samp // 2]
    me = jnp.stack(me).astype(jnp.int32)

    turned = whole(turn_in, "turn_in", 8, big((16, 4, 16, 512)), [], layer_input.reshape(1024, 512))
    turned, cotangent = fence((turned, cotangent))
    x_t = lax.all_to_all(turned.reshape(4, 4, 64, 512), "quad", 0, 0)
    cot4 = cotangent.reshape(4, 256, 512)
    block = lambda value, d: at(value, feat ^ d)
    from_core = shuffle(jnp.stack([block(cot4, 1), block(cot4, 3)]), *CORE)
    cot_far = shuffle(jnp.stack([block(cot4, 2), from_core[1]]), *X)
    x_t, from_core, cot_far = fence((x_t, from_core, cot_far))
    own_context = at(x_t, root % 4)
    got_context = shuffle(own_context, *W)
    full = big((4, 256, 512))
    act1, queries = by_feature(
        project_queries, "project_queries", 12, ((full, 0), (full, 0)), [],
        (x_t, 1), row(first_gain), row(first_shift), sample_weight, row(sample_bias),
    )
    got_context, q1 = fence((got_context, queries))

    tasks = segment_ids.reshape(8, 64)
    context_tasks = jnp.concatenate([at(tasks, root)] * 4).reshape(1, 256)
    sent = big((4, 4, 4, 16, 512))
    four = big((4, 64, 512))
    r1, o1, context, cact, k1, v1, p1 = by_feature(
        forward_one, "forward_one", 20,
        (
            (sent, 2), (full, 0), (four, 0), (four, 0), (four, 0), (four, 0),
            (big((4, 256, 512), F32), 0),
        ),
        [],
        me, (q1, 0), (own_context, 0), (got_context, 0), (x_t, 1),
        at(segment_ids.reshape(2, 256, 1), half), context_tasks,
        row(first_gain), row(first_shift), sample_weight, row(sample_bias), sample_mixer,
        row(sample_offset), time=7,
    )

    def exchange(value):
        shape = value.shape
        value = value.reshape((16,) + shape[2:])
        return lax.all_to_all(value, ("quad", "feat"), 0, 0).reshape(shape)

    rows_in = [
        row(v)
        for v in (
            second_gain, second_shift, feature_bias, feature_offset, third_gain,
            third_shift, expand_bias, reduce_bias,
        )
    ]
    weights = [feature_weight, feature_mixer, expand_weight, reduce_weight]

    own = spec((None, 128, 512), lambda i, m: (m[0], i, 0))
    part = lambda n: spec((None, 128, 512), lambda i, m: (n, i, 0))
    still = lambda shape: spec(shape, lambda i, m: (0,) * len(shape))
    block = spec((128, 512), lambda i, m: (i, 0))
    far = pl.BlockSpec(memory_space=pl.ANY)
    vmem = lambda shape, dtype=BF: pltpu.VMEM(shape, dtype)
    rows, rows32 = vmem((HALF, 512)), vmem((HALF, 512), F32)
    outs = (sent, sds((8, 512), F32), sds((1, 2048), F32))
    gb1_f, vec2, bias2, out0, out1, out2, out3, *grads = pl.pallas_call(
        middle,
        grid_spec=pltpu.PrefetchScalarGridSpec(
            num_scalar_prefetch=1,
            grid=(2,),
            in_specs=[
                pl.BlockSpec(sent.shape, lambda i, m: (0,) * 5, pipeline_mode=pl.Buffered(1)),
                own, part(0), part(0), part(1),
            ]
            + [still(r.shape) for r in rows_in]
            + [far] * 4,
            out_specs=[still(o.shape) for o in outs] + [block] * 4 + [far] * 4,
            scratch_shapes=[vmem(w.shape) for w in weights]
            + [vmem((1024, n)) for n in (512, 1536, 512, 512, 512, 2048, 2048, 512)]
            + [
                vmem((4, 256, 512)), vmem((4, 256, 512)), rows, rows, rows, rows32, rows32, rows,
                rows, rows32, rows32, vmem((32, 96, 512)), vmem((32, 96, 512)), vmem((512, 1024)),
                pltpu.SemaphoreType.DMA((4,)), pltpu.SemaphoreType.DMA((4,)),
            ],
        ),
        out_shape=outs + (big((256, 512)),) * 4 + (sds((16, 96, 512)),) * 4,
        compiler_params=params(58),
        cost_estimate=cost(45),
        name="middle",
    )(
        me,
        *(
            outside(array)
            for array in (exchange(r1), cot4, from_core, cot_far, cot_far, *rows_in, *weights)
        ),
    )

    gb_t = exchange(gb1_f)
    outs = [shuffle(out, "feat", d + 1) for d, out in enumerate((out1, out2, out3))]
    pk, ps, qk, qs = (g.reshape(2, 2, 2, 2, 96, 512) for g in grads)
    p_chain, q_chain = Chain(pk, ps, (X, Y)), Chain(qk, qs, (Y, X))
    chains = [p_chain, q_chain]
    for chain in chains:
        chain.take(chain.start())

    half_rows = sds((2, 16, 32, 512))
    for chain in chains:
        chain.take(chain.start())
    gb1, back, term, vec1, keep_ab, send_ab = (
        lambda: by_feature(
            backward_one, "backward_one", 32,
            (
                (full, 0), (big((4, 256, 512), F32), 0), (four, 0), (sds((8, 512), F32), None),
                (half_rows, None), (half_rows, None),
            ),
            [pltpu.VMEM((1024, 512), BF), pltpu.VMEM((256, 1024), BF), pltpu.VMEM((1024, 512), BF)],
            me, (gb_t, 2), o1, act1, cact, (x_t, 1),
            (context, 0), (q1, 0), (k1, 0), (v1, 0), (p1, 0), sample_weight, sample_mixer,
            time=12,
        )
    )()

    owned = lambda v, n: v.reshape(-1, 8, n).transpose(1, 0, 2).reshape(8, -1)
    vectors = jnp.concatenate(
        [
            owned(vec2[:6], 64), vec2[6:].reshape(8, 128), bias2.reshape(8, 256),
            owned(vec1[:3], 64), vec1[3:5].reshape(8, 128),
        ],
        axis=1,
    )
    got_term = shuffle(term, *W)
    got_term, got_ab = together(chains, lambda: (got_term, shuffle(send_ab, *CORE)))
    bits = lambda a: a.reshape(2, 2, 2, 2, 2, 32, 512)
    keep_ab, got_ab = bits(keep_ab), bits(got_ab)
    late = []
    for which, dims in enumerate(((X, Y), (Y, X))):
        pair = [plus(keep_ab[which, i], got_ab[which, i]) for i in range(2)]
        late.append(Chain(*pair, ()))
        late[-1].dims = dims
    both = [jnp.concatenate([chain.keep[i] for chain in chains], axis=-2) for i in range(2)]
    both_chain = Chain(*both, ())
    both_chain.dims = (Z, W)
    vectors = vectors.reshape(2, 2, 2, 1088)
    (grad_t,), v = together(
        late + [both_chain],
        lambda: (
            by_feature(
                backward_input, "backward_input", 16, ((big((4, 4, 64, 512)), 1),),
                [pltpu.VMEM((4, 64, 512), F32)],
                me, (gb1, 0), (x_t, 1), (back, 0), (term, 0), (got_term, 0), row(first_gain),
            ),
            shuffle(at(vectors, 1 - samp % 2, 2), *Y),
        ),
    )
    vectors = at(vectors, samp % 2, 2) + v
    low = samp // 2 % 2
    layer_output = whole(
        place, "place", 16, sds((4, 256, 512)), [], me, out0, *outs
    ).reshape(64, 16, 512)
    got, v, layer_output = together(
        late + [both_chain],
        lambda: (
            lax.all_to_all(grad_t, "quad", 0, 0),
            shuffle(at(vectors, 1 - low, 1), *Z),
            layer_output,
        ),
    )
    vectors = at(vectors, low, 1) + v
    input_grad = whole(
        turn_out, "turn_out", 8, sds((1024, 512)), [], got.reshape(16, 4, 16, 512)
    ).reshape(64, 16, 512)

    rows = jnp.concatenate([chain.keep for chain in late], axis=2)
    around_z = lambda value, mask: lax.ppermute(value, SAMP, [(j, j ^ mask) for j in range(8)])
    from_z = [around_z(rows[i // 2, i % 2], (0, 4, 2, 6)[i]) for i in (1, 2, 3)]
    early = lax.all_gather(both_chain.keep, "feat")
    v = shuffle(at(vectors, 1 - half), *W)
    early, from_z, v, input_grad = fence((early, from_z, v, input_grad))
    vectors = (at(vectors, half) + v).reshape(1, 1088)
    vectors = whole(split, "split", 8, sds((24, 1088)), [], vectors)
    total = rows[0, 0].astype(F32)
    for value in from_z:
        total = total + value.astype(F32)
    vectors = jnp.pad(vectors[:3].reshape(-1), (0, 8 * 512 - 3 * 1088)).reshape(8, 512)
    last = lax.all_gather(jnp.concatenate([total.astype(BF), vectors]), "feat")
    mine = last[:, 64:].reshape(4, -1).astype(F32)
    mine = sum(mine[:, i * 1088 : (i + 1) * 1088] for i in range(3))
    mine = (mine[0] + mine[1]) + (mine[2] + mine[3])

    units_of = lambda rows: [rows[i].astype(F32) for i in (0, 2, 1, 3)]
    feature, expand = units_of(early[:, :64]), units_of(early[:, 96:160])
    reduce_grad = jnp.concatenate(
        units_of(jnp.concatenate([early[:, 64:96], early[:, 160:]], axis=1))
    )
    sample = units_of(last[:, :64])

    gain3, shift3, gain2, shift2, off2, bias_r = (mine[i * 64 : (i + 1) * 64] for i in range(6))
    feature_b, expand_b = mine[384:512], mine[512:768]
    gain1, shift1, off1 = (mine[768 + i * 64 : 832 + i * 64] for i in range(3))
    sample_b = mine[960:1088]
    columns = lambda blocks: jnp.concatenate(blocks, axis=1)

    return (
        layer_output, input_grad,
        gain1, shift1, columns(sample[:3]), sample_b, sample[3], off1,
        gain2, shift2, columns(feature[:3]), feature_b, feature[3], off2,
        gain3, shift3, columns(expand), expand_b,
        reduce_grad, bias_r,
    )


def spread_2(block, axis, owner):
    block = jnp.where(lax.axis_index(axis) == owner, block, jnp.zeros_like(block))
    return lax.psum(block, axis)


def layer_norm(values, gain_row, shift_row):
    center = jnp.mean(values, axis=-1, keepdims=True)
    spread = values - center
    variance = jnp.mean(spread * spread, axis=-1, keepdims=True)
    return spread * lax.rsqrt(variance + EPS) * gain_row + shift_row


def apply_weight(active, weight):
    return jnp.einsum("sfd,de->sfe", active, weight, preferred_element_type=jnp.float32)


def input_back(grad_out, weight):
    return jnp.einsum("sfe,de->sfd", grad_out, weight, preferred_element_type=jnp.float32)


def weight_grad(active, grad_out):
    return jnp.einsum("sfd,sfe->de", active, grad_out, preferred_element_type=jnp.float32)


def column_sum(values):
    return jnp.sum(values.astype(jnp.float32), axis=(0, 1))


def project(active, weight, bias_row):
    model_width = active.shape[-1]
    joined = apply_weight(active, weight)
    queries = (joined[..., :model_width] + bias_row[:model_width]).astype(jnp.bfloat16)
    key_part = joined[..., model_width : 2 * model_width].astype(jnp.bfloat16)
    value_part = (joined[..., 2 * model_width :] + bias_row[model_width:]).astype(jnp.bfloat16)
    return (queries, key_part, value_part)


def split_heads(values):
    return values.reshape(values.shape[0], values.shape[1], HEADS, HEAD_DIM)


def join_heads(values):
    return values.reshape(values.shape[0], values.shape[1], HEADS * HEAD_DIM)


def soft_weights(scores):
    top_score = jnp.max(scores, axis=-1, keepdims=True)
    raised = jnp.exp(scores - top_score)
    return raised / jnp.sum(raised, axis=-1, keepdims=True)


def feature_attend(queries, key_part, value_part):
    score_scale = HEAD_DIM ** (-0.5)
    scores = (
        jnp.einsum(
            "sfhd,sghd->shfg",
            split_heads(queries),
            split_heads(key_part),
            preferred_element_type=jnp.float32,
        )
        * score_scale
    )
    probability = soft_weights(scores)
    mixed = jnp.einsum(
        "shfg,sghd->sfhd",
        probability.astype(jnp.bfloat16),
        split_heads(value_part),
        preferred_element_type=jnp.float32,
    )
    return (join_heads(mixed).astype(jnp.bfloat16), probability)


def feature_grads(queries, key_part, value_part, probability, grad_mixed):
    score_scale = HEAD_DIM ** (-0.5)
    grad_heads = split_heads(grad_mixed)
    grad_weights = jnp.einsum(
        "sfhd,sghd->shfg", grad_heads, split_heads(value_part), preferred_element_type=jnp.float32
    )
    inner_sum = jnp.sum(probability * grad_weights, axis=-1, keepdims=True)
    grad_scores = (probability * (grad_weights - inner_sum)).astype(jnp.bfloat16)
    grad_queries = (
        jnp.einsum(
            "shfg,sghd->sfhd",
            grad_scores,
            split_heads(key_part),
            preferred_element_type=jnp.float32,
        )
        * score_scale
    )
    grad_keys = (
        jnp.einsum(
            "shfg,sfhd->sghd", grad_scores, split_heads(queries), preferred_element_type=jnp.float32
        )
        * score_scale
    )
    grad_values = jnp.einsum(
        "shfg,sfhd->sghd",
        probability.astype(jnp.bfloat16),
        grad_heads,
        preferred_element_type=jnp.float32,
    )
    return (join_heads(grad_queries), join_heads(grad_keys), join_heads(grad_values))


def local_large(
    layer_input,
    segment_ids,
    context_flags,
    first_gain,
    first_shift,
    sample_weight,
    sample_bias,
    sample_mixer,
    sample_offset,
    second_gain,
    second_shift,
    feature_weight,
    feature_bias,
    feature_mixer,
    feature_offset,
    third_gain,
    third_shift,
    expand_weight,
    expand_bias,
    reduce_weight,
    reduce_bias,
    cotangent,
):
    sample_rows = layer_input.shape[0]
    feature_rows = layer_input.shape[1]
    model_width = layer_input.shape[2]
    score_scale = HEAD_DIM ** (-0.5)
    shard_count = lax.axis_size("samp")
    context_shards = shard_count // 8
    total_context = context_shards * sample_rows
    residual_zero = layer_input.astype(jnp.float32)
    normed_one, norm_one_back = jax.vjp(layer_norm, residual_zero, first_gain, first_shift)
    active_one = normed_one.astype(jnp.bfloat16)
    queries_one, keys_one, values_one = project(active_one, sample_weight, sample_bias)
    my_index = lax.axis_index("samp")
    shard_flags = context_flags.reshape(shard_count, sample_rows)[:, 0]
    shard_rank = jnp.cumsum(shard_flags) - 1
    shard_ids = jnp.arange(shard_count, dtype=jnp.int32)
    slot_ids = jnp.arange(context_shards, dtype=jnp.int32)
    root_hits = (shard_rank[None, :] == slot_ids[:, None]) & (shard_flags[None, :] == 1)
    roots = jnp.sum(jnp.where(root_hits, shard_ids[None, :], 0), axis=1)
    context_tasks = jnp.take(segment_ids.reshape(shard_count, sample_rows), roots, axis=0).reshape(
        total_context
    )
    local_tasks = lax.dynamic_slice_in_dim(segment_ids, my_index * sample_rows, sample_rows)
    allowed = local_tasks[:, None] == context_tasks[None, :]
    is_context = shard_flags[my_index] == 1
    own_rank = jnp.maximum(shard_rank[my_index], 0)
    own_block = jnp.concatenate([keys_one, values_one], axis=-1)

    def fetch_rows(step, buffer):
        piece = spread_2(own_block, "samp", roots[step])
        return lax.dynamic_update_slice_in_dim(buffer, piece, step * sample_rows, 0)

    empty_rows = jnp.zeros((total_context, feature_rows, 2 * model_width), jnp.bfloat16)
    fetched = lax.fori_loop(0, context_shards, fetch_rows, empty_rows)
    context_keys = fetched[..., :model_width]
    context_values = fetched[..., model_width:]
    query_heads = split_heads(queries_one)
    key_heads = split_heads(context_keys)
    value_heads = split_heads(context_values)
    scores = (
        jnp.einsum("sfhd,cfhd->fhsc", query_heads, key_heads, preferred_element_type=jnp.float32)
        * score_scale
    )
    sample_prob = soft_weights(jnp.where(allowed[None, None], scores, MASKED))
    sample_weights = sample_prob.astype(jnp.bfloat16)
    mixed_one = join_heads(
        jnp.einsum(
            "fhsc,cfhd->sfhd", sample_weights, value_heads, preferred_element_type=jnp.float32
        )
    ).astype(jnp.bfloat16)
    residual_one = residual_zero + apply_weight(mixed_one, sample_mixer) + sample_offset
    normed_two, norm_two_back = jax.vjp(layer_norm, residual_one, second_gain, second_shift)
    active_two = normed_two.astype(jnp.bfloat16)
    queries_two, keys_two, values_two = project(active_two, feature_weight, feature_bias)
    all_keys, all_values = (
        lax.all_gather(keys_two, "feat", axis=1, tiled=True),
        lax.all_gather(values_two, "feat", axis=1, tiled=True),
    )
    mixed_two, feature_prob = feature_attend(queries_two, all_keys, all_values)
    residual_two = residual_one + apply_weight(mixed_two, feature_mixer) + feature_offset
    normed_three, norm_three_back = jax.vjp(layer_norm, residual_two, third_gain, third_shift)
    active_three = normed_three.astype(jnp.bfloat16)
    expanded = apply_weight(active_three, expand_weight) + expand_bias
    activated, gelu_back = jax.vjp(partial(jax.nn.gelu, approximate=False), expanded)
    hidden = activated.astype(jnp.bfloat16)
    layer_output = (residual_two + apply_weight(hidden, reduce_weight) + reduce_bias).astype(
        jnp.bfloat16
    )
    grad_out = cotangent.astype(jnp.float32)
    grad_branch = cotangent
    reduce_bias_grad = column_sum(grad_branch)
    reduce_weight_grad = weight_grad(hidden, grad_branch)
    grad_hidden = input_back(grad_branch, reduce_weight).astype(jnp.bfloat16)
    grad_expanded = gelu_back(grad_hidden.astype(jnp.float32))[0].astype(jnp.bfloat16)
    expand_bias_grad = column_sum(grad_expanded)
    expand_weight_grad = weight_grad(active_three, grad_expanded)
    grad_norm, third_gain_grad, third_shift_grad = norm_three_back(
        input_back(grad_expanded, expand_weight)
    )
    grad_two = grad_out + grad_norm
    grad_branch = grad_two.astype(jnp.bfloat16)
    feature_offset_grad = column_sum(grad_branch)
    feature_mixer_grad = weight_grad(mixed_two, grad_branch)
    grad_mixed = input_back(grad_branch, feature_mixer).astype(jnp.bfloat16)
    grad_queries, grad_keys, grad_values = feature_grads(
        queries_two, all_keys, all_values, feature_prob, grad_mixed
    )
    own_key_grads, own_value_grads = (
        lax.psum_scatter(grad_keys, "feat", scatter_dimension=1, tiled=True),
        lax.psum_scatter(grad_values, "feat", scatter_dimension=1, tiled=True),
    )
    grad_project = jnp.concatenate(
        [
            grad_queries.astype(jnp.bfloat16),
            own_key_grads.astype(jnp.bfloat16),
            own_value_grads.astype(jnp.bfloat16),
        ],
        axis=-1,
    )
    feature_weight_grad = weight_grad(active_two, grad_project)
    feature_bias_grad = jnp.concatenate(
        [
            column_sum(grad_project[..., :model_width]),
            column_sum(grad_project[..., 2 * model_width :]),
        ]
    )
    grad_norm, second_gain_grad, second_shift_grad = norm_two_back(
        input_back(grad_project, feature_weight)
    )
    grad_one = grad_two + grad_norm
    grad_branch = grad_one.astype(jnp.bfloat16)
    sample_offset_grad = column_sum(grad_branch)
    sample_mixer_grad = weight_grad(mixed_one, grad_branch)
    grad_heads = split_heads(input_back(grad_branch, sample_mixer).astype(jnp.bfloat16))
    grad_weights = jnp.einsum(
        "sfhd,cfhd->fhsc", grad_heads, value_heads, preferred_element_type=jnp.float32
    )
    inner_sum = jnp.sum(sample_prob * grad_weights, axis=-1, keepdims=True)
    grad_scores = (sample_prob * (grad_weights - inner_sum)).astype(jnp.bfloat16)
    grad_queries = (
        join_heads(
            jnp.einsum(
                "fhsc,cfhd->sfhd", grad_scores, key_heads, preferred_element_type=jnp.float32
            )
        )
        * score_scale
    ).astype(jnp.bfloat16)
    key_terms = (
        join_heads(
            jnp.einsum(
                "fhsc,sfhd->cfhd", grad_scores, query_heads, preferred_element_type=jnp.float32
            )
        )
        * score_scale
    )
    value_terms = join_heads(
        jnp.einsum(
            "fhsc,sfhd->cfhd", sample_weights, grad_heads, preferred_element_type=jnp.float32
        )
    )
    term_block = jnp.concatenate([key_terms, value_terms], axis=-1)
    summed_terms = lax.psum_scatter(term_block, "samp", scatter_dimension=0, tiled=True)
    summed_rows = lax.all_gather(summed_terms.astype(jnp.bfloat16), "samp", axis=0, tiled=True)
    own_grads = lax.dynamic_slice_in_dim(summed_rows, own_rank * sample_rows, sample_rows, 0)
    own_grads = jnp.where(is_context, own_grads, jnp.zeros_like(own_grads))
    grad_project = jnp.concatenate([grad_queries, own_grads], axis=-1)
    sample_weight_grad = weight_grad(active_one, grad_project)
    sample_bias_grad = jnp.concatenate(
        [column_sum(grad_queries), column_sum(own_grads[..., model_width:])]
    )
    grad_norm, first_gain_grad, first_shift_grad = norm_one_back(
        input_back(grad_project, sample_weight)
    )
    input_grad = (grad_one + grad_norm).astype(jnp.bfloat16)
    summed = lax.psum(
        (
            first_gain_grad,
            first_shift_grad,
            sample_weight_grad,
            sample_bias_grad,
            sample_mixer_grad,
            sample_offset_grad,
            second_gain_grad,
            second_shift_grad,
            feature_weight_grad,
            feature_bias_grad,
            feature_mixer_grad,
            feature_offset_grad,
            third_gain_grad,
            third_shift_grad,
            expand_weight_grad,
            expand_bias_grad,
            reduce_weight_grad,
            reduce_bias_grad,
        ),
        "feat",
    )
    shares = (
        lax.psum_scatter(summed[0], "samp", scatter_dimension=0, tiled=True),
        lax.psum_scatter(summed[1], "samp", scatter_dimension=0, tiled=True),
        lax.psum_scatter(summed[2], "samp", scatter_dimension=0, tiled=True),
        lax.psum_scatter(summed[3], "samp", scatter_dimension=0, tiled=True),
        lax.psum_scatter(summed[4], "samp", scatter_dimension=0, tiled=True),
        lax.psum_scatter(summed[5], "samp", scatter_dimension=0, tiled=True),
        lax.psum_scatter(summed[6], "samp", scatter_dimension=0, tiled=True),
        lax.psum_scatter(summed[7], "samp", scatter_dimension=0, tiled=True),
        lax.psum_scatter(summed[8], "samp", scatter_dimension=0, tiled=True),
        lax.psum_scatter(summed[9], "samp", scatter_dimension=0, tiled=True),
        lax.psum_scatter(summed[10], "samp", scatter_dimension=0, tiled=True),
        lax.psum_scatter(summed[11], "samp", scatter_dimension=0, tiled=True),
        lax.psum_scatter(summed[12], "samp", scatter_dimension=0, tiled=True),
        lax.psum_scatter(summed[13], "samp", scatter_dimension=0, tiled=True),
        lax.psum_scatter(summed[14], "samp", scatter_dimension=0, tiled=True),
        lax.psum_scatter(summed[15], "samp", scatter_dimension=0, tiled=True),
        lax.psum_scatter(summed[16], "samp", scatter_dimension=0, tiled=True),
        lax.psum_scatter(summed[17], "samp", scatter_dimension=0, tiled=True),
    )
    return (
        layer_output,
        input_grad,
        shares[0],
        shares[1],
        shares[2],
        shares[3],
        shares[4],
        shares[5],
        shares[6],
        shares[7],
        shares[8],
        shares[9],
        shares[10],
        shares[11],
        shares[12],
        shares[13],
        shares[14],
        shares[15],
        shares[16],
        shares[17],
    )


def solution(mesh):
    if mesh.shape["samp"] == 8 and mesh.shape["feat"] == 4:
        return solution_small(mesh)
    return jax.shard_map(
        local_large,
        mesh=mesh,
        in_specs=(
            P("samp", "feat", None),
            P(),
            P(),
            P(),
            P(),
            P(),
            P(),
            P(),
            P(),
            P(),
            P(),
            P(),
            P(),
            P(),
            P(),
            P(),
            P(),
            P(),
            P(),
            P(),
            P(),
            P("samp", "feat", None),
        ),
        out_specs=(
            P("samp", "feat", None),
            P("samp", "feat", None),
            P("samp"),
            P("samp"),
            P("samp", None),
            P("samp"),
            P("samp", None),
            P("samp"),
            P("samp"),
            P("samp"),
            P("samp", None),
            P("samp"),
            P("samp", None),
            P("samp"),
            P("samp"),
            P("samp"),
            P("samp", None),
            P("samp"),
            P("samp", None),
            P("samp"),
        ),
        check_vma=False,
    )


def solution_small(mesh):
    mesh = jax.sharding.Mesh(mesh.devices.reshape(2, 4, 4), ("half", "quad", "feat"))
    tokens, copied = P(SAMP, "feat", None), P()
    vector, matrix = P(SAMP), P(SAMP, None)
    return jax.shard_map(
        local_small,
        mesh=mesh,
        in_specs=(tokens,) + (copied,) * 20 + (tokens,),
        out_specs=(
            tokens, tokens, vector, vector, matrix, vector, matrix, vector,
            vector, vector, matrix, vector, matrix, vector,
            vector, vector, matrix, vector, matrix, vector,
        ),
        check_vma=False,
    )
```

```python
from functools import partial

import jax
import jax.numpy as jnp
from jax import lax
from jax.experimental import pallas as pl
from jax.experimental.pallas import tpu as pltpu
from jax.sharding import PartitionSpec as P

HEADS = 8
HEAD_DIM = 64
EPS = 1e-05
MASKED = -1000000000.0
SCALE = HEAD_DIM ** (-0.5)
QUAD = 4 * HEAD_DIM
BF = jnp.bfloat16
F32 = jnp.float32


def mm(a, b, ca=1, cb=0):
    return lax.dot_general(a, b, (((ca,), (cb,)), ((), ())), preferred_element_type=F32)


def norm_parts(values):
    center = jnp.mean(values, axis=-1, keepdims=True)
    spread = values - center
    variance = jnp.mean(spread * spread, axis=-1, keepdims=True)
    inverse = lax.rsqrt(variance + EPS)
    return spread * inverse, inverse


def norm_back(grad, unit, inverse, gain):
    scaled = grad * gain
    first = jnp.mean(scaled, axis=-1, keepdims=True)
    second = jnp.mean(scaled * unit, axis=-1, keepdims=True)
    return (scaled - first - unit * second) * inverse


def lane_ids(rows):
    return lax.broadcasted_iota(jnp.int32, (rows, 128), 1)


def group_reduce(values, op, fill):
    rows = values.shape[0]
    low = lane_ids(rows) < HEAD_DIM
    outs = []
    for t in range(values.shape[1] // 128):
        tile = values[:, t * 128 : (t + 1) * 128]
        left = op(jnp.where(low, tile, fill), axis=1, keepdims=True)
        right = op(jnp.where(low, fill, tile), axis=1, keepdims=True)
        outs.append(jnp.where(low, left, right))
    return jnp.concatenate(outs, axis=1)


def head_masks(dtype):
    lanes = lax.broadcasted_iota(jnp.int32, (1, QUAD), 1) // HEAD_DIM
    return [jnp.where(lanes == h, 1.0, 0.0).astype(dtype) for h in range(4)]


def stack_heads(part, masks):
    return jnp.concatenate([part * m for m in masks], axis=0)


def pick_heads(stacked, masks):
    rows = stacked.shape[0] // 4
    total = stacked[:rows] * masks[0]
    for h in range(1, 4):
        total = total + stacked[h * rows : (h + 1) * rows] * masks[h]
    return total


def attend(q, k, v, masks, allow):
    outs, probs = [], []
    for quad in range(2):
        cols = slice(quad * QUAD, (quad + 1) * QUAD)
        scores = mm(q[:, cols], stack_heads(k[:, cols], masks), 1, 1)
        if allow is not None:
            scores = jnp.where(allow, scores, MASKED)
        raised = jnp.exp(scores - group_reduce(scores, jnp.max, -jnp.inf))
        prob = raised / group_reduce(raised, jnp.sum, 0.0)
        outs.append(mm(prob.astype(BF), stack_heads(v[:, cols], masks)))
        probs.append(prob)
    return jnp.concatenate(outs, axis=1), jnp.concatenate(probs, axis=1)


def attend_back(q, k, v, prob, grad, masks, masks32):
    dqs, dks, dvs = [], [], []
    for quad in range(2):
        cols = slice(quad * QUAD, (quad + 1) * QUAD)
        p, g = prob[:, cols], grad[:, cols]
        back = mm(g, stack_heads(v[:, cols], masks), 1, 1)
        inner = group_reduce(p * back, jnp.sum, 0.0)
        gs = (p * (back - inner)).astype(BF)
        dqs.append(mm(gs, stack_heads(k[:, cols], masks)) * SCALE)
        dks.append(pick_heads(mm(gs, q[:, cols], 0, 0), masks32))
        dvs.append(pick_heads(mm(p.astype(BF), g, 0, 0), masks32))
    join = lambda parts: jnp.concatenate(parts, axis=1).astype(BF)
    return join(dqs), join(dks), join(dvs)


def swap_matrix(rows=16):
    n = rows * 16
    r = lax.broadcasted_iota(jnp.int32, (n, n), 0)
    c = lax.broadcasted_iota(jnp.int32, (n, n), 1)
    return jnp.where((r // rows == c % 16) & (r % rows == c // 16), 1.0, 0.0).astype(BF)


def swap(matrix, values, back=False):
    return mm(matrix, values, 0 if back else 1, 0).astype(BF)


def gelu_parts(u):
    cdf = 0.5 * (1.0 + lax.erf(u * (2.0**-0.5)))
    density = jnp.exp(u * u * -0.5) * 0.3989422804014327
    return cdf, density


def col_sum(values):
    return jnp.sum(values.astype(F32), axis=0, keepdims=True)


def turn_in(x_ref, out_ref):
    matrix = swap_matrix()
    for d in range(4):
        rows = x_ref[d * 256 : (d + 1) * 256]
        out_ref[:, d] = swap(matrix, rows).reshape(16, 16, 512)


def turn_out(got_ref, out_ref):
    matrix = swap_matrix()
    for d in range(4):
        out_ref[d * 256 : (d + 1) * 256] = swap(matrix, got_ref[:, d].reshape(256, 512))


def project_queries(x_ref, gain_ref, shift_ref, w_ref, b_ref, act_ref, q_ref):
    unit, _ = norm_parts(x_ref[:, 0].reshape(256, 512).astype(F32))
    act = (unit * gain_ref[...] + shift_ref[...]).astype(BF)
    act_ref[0] = act
    q = (mm(act, w_ref[:, :512]) + b_ref[:, :512]).astype(BF)
    q_ref[0] = q * jnp.asarray(SCALE, BF)


def forward_one(
    me_ref, q_ref, own_ref, got_ref, x_ref, tasks_ref, context_ref, gain_ref, shift_ref, w_ref,
    b_ref, wm_ref, off_ref,
    r_ref, o_ref, c_ref, cact_ref, k_ref, v_ref, p_ref,
):
    here = me_ref[1] == me_ref[2]
    masks = head_masks(BF)
    allow = tasks_ref[...] == context_ref[...]

    @pl.when(here)
    def _():
        c_ref[...] = own_ref[...]

    @pl.when(jnp.logical_not(here))
    def _():
        c_ref[...] = got_ref[...]

    for e in range(c_ref.shape[0]):
        unit, _ = norm_parts(c_ref[e].astype(F32))
        act = (unit * gain_ref[...] + shift_ref[...]).astype(BF)
        cact_ref[e] = act
        kv = mm(act, w_ref[:, 512:])
        k_ref[e] = kv[:, :512].astype(BF)
        v_ref[e] = (kv[:, 512:] + b_ref[:, 512:]).astype(BF)
    for e in range(c_ref.shape[0]):
        out, prob = attend(q_ref[e], k_ref[e], v_ref[e], masks, allow)
        o_ref[e] = out.astype(BF)
        p_ref[e] = prob
    for e in range(c_ref.shape[0]):
        r1 = x_ref[:, e].reshape(256, 512).astype(F32) + mm(o_ref[e], wm_ref[...]) + off_ref[...]
        r_ref[:, :, e] = r1.astype(BF).reshape(4, 4, 16, 512)


HALF = 512


def middle(me_ref, *refs):
    (
        r1_ref, c0, c1, c2, c3, g2_ref, s2_ref, bf_ref, off2_ref, g3_ref, s3_ref, be_ref, br_ref,
    ) = refs[:13]
    weights_hbm = refs[13:17]
    gb1_ref, vec_ref, bias_ref, out0, out1, out2, out3 = refs[17:24]
    targets = refs[24:28]
    wf_ref, wm2_ref, we_ref, wr_ref = refs[28:32]
    kept = refs[32:40]
    (
        r_scr, g_scr, q_scr, k_scr, v_scr, p_scr, e_scr, gs_scr, go_scr, out_scr, back_scr,
        part_p, part_q, turn, in_sems, out_sems,
    ) = refs[40:]
    me, step = me_ref[0], pl.program_id(0)
    tokens = pl.ds(pl.multiple_of(step * HALF, HALF), HALF)
    a2_ref, dqkv_ref, o2_ref, gb2_ref, a3_ref, gu_ref, hid_ref, gb3_ref = (
        ref.at[tokens] for ref in kept
    )
    loads = [
        pltpu.make_async_copy(source, target, in_sems.at[i])
        for i, (source, target) in enumerate(zip(weights_hbm, refs[28:32]))
    ]

    def first(make):
        pl.when(step == 0)(make)

    matrix = swap_matrix()
    masks, masks32 = head_masks(BF), head_masks(F32)

    @first
    def _():
        loads[0].start()
        loads[1].start()
        for f in range(4):
            r_scr[f] = swap(matrix, r1_ref[:, f].reshape(256, 512))

    now = pl.ds(pl.multiple_of(step * 128, 128), 128)

    def gather(*refs):
        return jnp.concatenate(
            [ref[s * 16 : (s + 1) * 16] for s in range(8) for ref in refs], axis=0
        )

    def scatter(values, *refs):
        for s in range(8):
            for d, ref in enumerate(refs):
                at = (s * 4 + d) * 16
                ref[s * 16 : (s + 1) * 16] = values[at : at + 16]

    def each_sample(body):
        def step(i, carry):
            for j in range(SAMPLE_UNROLL):
                rows = pl.ds(pl.multiple_of((i * SAMPLE_UNROLL + j) * 64, 64), 64)
                for quad in range(2):
                    body(rows, slice(quad * QUAD, (quad + 1) * QUAD))
            return carry

        lax.fori_loop(0, 8 // SAMPLE_UNROLL, step, 0)

    gb3_ref[...] = gather(c0, c1, c2, c3)
    r1 = gather(*(r_scr.at[d ^ me, now] for d in range(4))).astype(F32)
    unit2, inv2 = norm_parts(r1)
    a2_ref[...] = (unit2 * g2_ref[...] + s2_ref[...]).astype(BF)

    @first
    def _():
        loads[0].wait()
        loads[2].start()
        loads[3].start()

    q = (mm(a2_ref[...], wf_ref[:, :512]) + bf_ref[:, :512]).astype(BF)
    q_scr[...] = q * jnp.asarray(SCALE, BF)
    k_scr[...] = mm(a2_ref[...], wf_ref[:, 512:1024]).astype(BF)
    v_scr[...] = (mm(a2_ref[...], wf_ref[:, 1024:]) + bf_ref[:, 512:]).astype(BF)

    def score(rows, cols):
        p_scr[rows, cols] = mm(q_scr[rows, cols], stack_heads(k_scr[rows, cols], masks), 1, 1)

    each_sample(score)
    for i in range(4):
        rows = slice(i * 128, (i + 1) * 128)
        scores = p_scr[rows]
        raised = jnp.exp(scores - group_reduce(scores, jnp.max, -jnp.inf))
        p_scr[rows] = raised / group_reduce(raised, jnp.sum, 0.0)

    def mix(rows, cols):
        o2_ref[rows, cols] = mm(
            p_scr[rows, cols].astype(BF), stack_heads(v_scr[rows, cols], masks)
        ).astype(BF)

    each_sample(mix)
    first(loads[1].wait)
    r2 = r1 + mm(o2_ref[...], wm2_ref[...]) + off2_ref[...]
    unit3, inv3 = norm_parts(r2)
    a3_ref[...] = (unit3 * g3_ref[...] + s3_ref[...]).astype(BF)
    first(loads[2].wait)
    first(loads[3].wait)

    @first
    def _():
        vec_ref[...] = jnp.zeros((8, 512), F32)
        bias_ref[...] = jnp.zeros((1, 2048), F32)

    out_scr[...] = r2 + br_ref[...]
    back_scr[...] = jnp.zeros((HALF, 512), F32)

    def expand(b, carry):
        cols = pl.ds(pl.multiple_of(b * WIDE, WIDE), WIDE)
        u = mm(a3_ref[...], we_ref[:, cols]) + be_ref[:, cols]
        cdf, density = gelu_parts(u)
        hidden = (u * cdf).astype(BF)
        hid_ref[:, cols] = hidden
        gh = mm(gb3_ref[...], wr_ref[cols, :], 1, 1).astype(BF).astype(F32)
        gu = (gh * (cdf + u * density)).astype(BF)
        gu_ref[:, cols] = gu
        bias_ref[:, cols] += col_sum(gu)
        out_scr[...] += mm(hidden, wr_ref[cols, :])
        back_scr[...] += mm(gu, we_ref[:, cols], 1, 1)
        return carry

    lax.fori_loop(0, 2048 // WIDE, expand, 0, unroll=EXPAND_UNROLL)
    scatter(out_scr[...].astype(BF), out0, out1, out2, out3)
    back, cot = back_scr[...], gb3_ref[...]
    vecs = [col_sum(back * unit3), col_sum(back)]
    gr2 = cot.astype(F32) + norm_back(back, unit3, inv3, g3_ref[...])
    gb2_ref[...] = gr2.astype(BF)
    go_scr[...] = mm(gb2_ref[...], wm2_ref[...], 1, 1).astype(BF)

    def weigh(rows, cols):
        e_scr[rows, cols] = mm(go_scr[rows, cols], stack_heads(v_scr[rows, cols], masks), 1, 1)

    each_sample(weigh)
    for i in range(4):
        rows = slice(i * 128, (i + 1) * 128)
        prob, grad = p_scr[rows], e_scr[rows]
        inner = group_reduce(prob * grad, jnp.sum, 0.0)
        gs_scr[rows] = (prob * (grad - inner)).astype(BF)

    def spread(rows, cols):
        gs, at = gs_scr[rows, cols], cols.start
        dq = mm(gs, stack_heads(k_scr[rows, cols], masks)) * SCALE
        dqkv_ref[rows, at : at + QUAD] = dq.astype(BF)
        dk = pick_heads(mm(gs, q_scr[rows, cols], 0, 0), masks32)
        dqkv_ref[rows, 512 + at : 512 + at + QUAD] = dk.astype(BF)
        dv = pick_heads(mm(p_scr[rows, cols].astype(BF), go_scr[rows, cols], 0, 0), masks32)
        dqkv_ref[rows, 1024 + at : 1024 + at + QUAD] = dv.astype(BF)

    each_sample(spread)
    dqkv = dqkv_ref[...]
    back = mm(dqkv, wf_ref[...], 1, 1)
    vecs += [col_sum(back * unit2), col_sum(back)]
    gr1 = gr2 + norm_back(back, unit2, inv2, g2_ref[...])
    scatter(gr1.astype(BF), *(g_scr.at[d ^ me, now] for d in range(4)))
    vecs += [
        col_sum(gb2_ref[...]), col_sum(cot), col_sum(dqkv[:, :512]), col_sum(dqkv[:, 1024:])
    ]
    vec_ref[...] += jnp.concatenate(vecs, axis=0)

    @pl.when(step == 1)
    def _():
        for f in range(4):
            gb1_ref[:, f] = swap(matrix, g_scr[f]).reshape(4, 4, 16, 512)
        grads_middle(me_ref, kept, (part_p, part_q), turn, targets, out_sems)


SAMPLE_UNROLL = 8
EXPAND_UNROLL = True
WIDE = 512


def backward_one(
    me_ref, g_ref, o_ref, act_ref, cact_ref, x_ref, c_ref, q_ref, k_ref, v_ref,
    p_ref, w_ref, wm_ref,
    gb1_ref, a_ref, term_ref, vec_ref, keep_ref, send_ref,
    dq_scr, dkv_scr, g_scr,
):
    masks, masks32 = head_masks(BF), head_masks(F32)

    @pl.when(pl.program_id(0) == 0)
    def _():
        vec_ref[...] = jnp.zeros((8, 512), F32)

    step, per = pl.program_id(0), q_ref.shape[0]
    for e in range(per):
        gb1 = g_ref[:, :, e].reshape(256, 512)
        gb1_ref[e] = gb1
        go = mm(gb1, wm_ref[...], 1, 1).astype(BF)
        dq, dk, dv = attend_back(q_ref[e], k_ref[e], v_ref[e], p_ref[e], go, masks, masks32)
        dkv = jnp.concatenate([dk, dv], axis=1)
        at = step * per + e
        rows = pl.ds(pl.multiple_of(at * 256, 256), 256)
        dq_scr[rows], g_scr[rows] = dq, gb1
        dkv_scr[pl.ds(pl.multiple_of(at * 64, 64), 64)] = dkv
        back = mm(dq, w_ref[:, :512], 1, 1)
        a_ref[e] = back
        term = mm(dkv, w_ref[:, 512:], 1, 1)
        term_ref[e] = term.astype(BF)
        unit, _ = norm_parts(x_ref[:, e].reshape(256, 512).astype(F32))
        unit_c, _ = norm_parts(c_ref[e].astype(F32))
        zero = jnp.zeros((3, 512), F32)
        vec_ref[...] += jnp.concatenate(
            [
                col_sum(back * unit) + col_sum(term * unit_c), col_sum(back) + col_sum(term),
                col_sum(gb1), col_sum(dq), col_sum(dv), zero,
            ],
            axis=0,
        )

    @pl.when(step == pl.num_programs(0) - 1)
    def _():
        whole_rows = lambda ref: ref[...].reshape(-1, 512)
        act_c = whole_rows(cact_ref)
        terms = (
            (whole_rows(act_ref), dq_scr[...]), (act_c, dkv_scr[:, :512]),
            (act_c, dkv_scr[:, 512:]), (whole_rows(o_ref), g_scr[...]),
        )
        for unit, (left, right) in enumerate(terms):
            place_sample(me_ref, mm(left, right, 0, 0).astype(BF), unit, keep_ref, send_ref)


def backward_input(me_ref, gb1_ref, x_ref, a_ref, term_ref, got_ref, gain_ref, grad_ref, a_scr):
    here, quad = me_ref[1] == me_ref[2], me_ref[3]
    unit, inverse = norm_parts(x_ref[:, 0].reshape(256, 512).astype(F32))
    a_scr[...] = a_ref[0].reshape(4, 64, 512)

    @pl.when(here)
    def _():
        a_scr[quad] += term_ref[0].astype(F32) + got_ref[0].astype(F32)

    back = a_scr[...].reshape(256, 512)
    grad = gb1_ref[0].astype(F32) + norm_back(back, unit, inverse, gain_ref[...])
    grad_ref[:, 0] = grad.astype(BF).reshape(4, 64, 512)


def split(got_ref, out_ref):
    rest = got_ref[...]
    out_ref[...] = jnp.zeros_like(out_ref)
    for i in range(3):
        term = rest.astype(BF)
        out_ref[i : i + 1] = term
        rest = rest - term.astype(F32)


def place(me_ref, b0, b1, b2, b3, out_ref):
    for d, ref in enumerate((b0, b1, b2, b3)):
        out_ref[d ^ me_ref[0]] = ref[...]


def piece_index(me_ref, unit, shard, order):
    core, xx, yy, zz = me_ref[4], me_ref[5], me_ref[6], me_ref[7]
    other_z = (shard >> 1) ^ zz
    bit = {
        "x": (unit & 1) ^ xx, "y": (shard & 1) ^ yy, "z": other_z & 1, "w": other_z >> 1,
    }
    index = sum(bit[name] * weight for name, weight in zip(order, (8, 4, 2, 1)))
    return (unit >> 1) ^ core, index


def grads_middle(me_ref, kept, staged, turn, targets, out_sems):
    act2, dqkv, o2, gb2, act3, gu, hid, gb3 = kept
    stores = []

    def put(part):
        for i in range(2):
            source = staged[part].at[pl.ds(16 * i, 16)]
            place = 2 * part + i
            stores.append(pltpu.make_async_copy(source, targets[place], out_sems.at[place]))
            stores[-1].start()

    def loop(count, body):
        lax.fori_loop(0, count, lambda n, carry: (body(n), carry)[1], 0)

    block = lambda n: pl.ds(pl.multiple_of(n * 512, 512), 512)

    def place_piece(part, value, unit, shard, rows):
        send, index = piece_index(me_ref, unit, shard, ("xyzw", "yxzw")[part])
        staged[part][send * 16 + index, rows] = value

    def place_unit(part, value, unit):
        for shard in range(8):
            place_piece(part, value[shard * 64 : (shard + 1) * 64], unit, shard, slice(0, 64))

    def from_hidden(n):
        piece = mm(hid[:, block(n)], gb3[...], 0, 0).astype(BF)
        for i in range(8):
            for part in range(2):
                at = i * 64 + part * 32
                rows = piece[at : at + 32]
                place_piece(part, rows, i % 4, 2 * n + i // 4, slice(64, 96))

    loop(4, from_hidden)
    turn[...] = act3[...].T

    def from_expand(n):
        place_unit(1, mm(turn[...], gu[:, block(n)]).astype(BF), n)

    loop(4, from_expand)
    put(1)
    turn[...] = act2[...].T

    def from_feature(n):
        place_unit(0, mm(turn[...], dqkv[:, block(n)]).astype(BF), n)

    loop(3, from_feature)
    place_unit(0, mm(o2[...], gb2[...], 0, 0).astype(BF), 3)
    put(0)
    for store in stores:
        store.wait()


def place_sample(me_ref, value, unit, keep_ref, send_ref):
    for which, order in enumerate(("xyzw", "yxzw")):
        for shard in range(8):
            at = shard * 64 + which * 32
            send, index = piece_index(me_ref, unit, shard, order)

            @pl.when(send == 0)
            def _(at=at, index=index):
                keep_ref[which, index] = value[at : at + 32]

            @pl.when(send == 1)
            def _(at=at, index=index):
                send_ref[which, index] = value[at : at + 32]


def spec(shape, index=None):
    return pl.BlockSpec(shape, index if index is not None else (lambda *a: (0,) * len(shape)))


def sds(shape, dtype=BF):
    return jax.ShapeDtypeStruct(shape, dtype)


def big(shape, dtype=BF):
    return pltpu.HBM(shape, dtype)


def outside(array):
    if array.size * array.dtype.itemsize < 1 << 18:
        return array
    return pltpu.with_memory_space_constraint(array, pltpu.HBM)


def params(limit):
    return pltpu.CompilerParams(vmem_limit_bytes=limit << 20)


def row(vector):
    return vector.reshape(1, -1)


def cost(microseconds):
    return pl.CostEstimate(
        flops=int(microseconds * 1.1e9), transcendentals=0, bytes_accessed=int(microseconds * 2e6)
    )


def whole_block(out):
    shape = out.shape
    return pl.BlockSpec(shape, lambda i: (0,) * len(shape))


def moving_block(shape, axis, per):
    block = tuple(per if i == axis else n for i, n in enumerate(shape))
    return pl.BlockSpec(block, lambda i: tuple(i if j == axis else 0 for j in range(len(shape))))


def by_feature(kernel, name, limit, outs, scratch, *inputs, time=3, per=1):
    arrays, specs = [], []
    for entry in inputs:
        array, axis = entry if isinstance(entry, tuple) else (entry, None)
        if array.ndim == 1:
            arrays.append(array)
            specs.append(pl.BlockSpec(memory_space=pltpu.SMEM))
            continue
        arrays.append(outside(array))
        specs.append(
            whole_block(array) if axis is None else moving_block(array.shape, axis, per)
        )
    return pl.pallas_call(
        kernel,
        grid=(4 // per,),
        out_shape=tuple(out for out, _ in outs),
        in_specs=specs,
        out_specs=[
            whole_block(out) if axis is None else moving_block(out.shape, axis, per)
            for out, axis in outs
        ],
        scratch_shapes=scratch,
        compiler_params=params(limit),
        cost_estimate=cost(time),
        name=name,
    )(*arrays)


def whole(kernel, name, limit, outs, scratch, *inputs, steps=1, time=3):
    arrays, specs = [], []
    for entry in inputs:
        if not isinstance(entry, tuple) and entry.ndim == 1:
            arrays.append(entry)
            specs.append(pl.BlockSpec(memory_space=pltpu.SMEM))
            continue
        array, block, index = entry if isinstance(entry, tuple) else (entry, None, None)
        arrays.append(outside(array))
        block = array.shape if block is None else block
        index = (0,) * array.ndim if index is None else index
        if not callable(index):
            index = lambda i, index=index: index
        specs.append(pl.BlockSpec(block, index))
    return pl.pallas_call(
        kernel,
        grid=(steps,),
        out_shape=outs,
        in_specs=specs,
        out_specs=jax.tree.map(whole_block, outs, is_leaf=lambda o: hasattr(o, "dtype")),
        scratch_shapes=scratch,
        compiler_params=params(limit),
        cost_estimate=cost(time),
        name=name,
    )(*arrays)


def shuffle(value, axis, mask):
    size = lax.axis_size(axis)
    return lax.ppermute(value, axis, [(i, i ^ mask) for i in range(size)])


SAMP = ("half", "quad")
CORE, X, Y, Z, W = ("feat", 1), ("feat", 2), ("quad", 1), ("quad", 2), ("half", 1)


def at(stacked, index, axis=0):
    return lax.dynamic_index_in_dim(stacked, index, axis, keepdims=False)


def fence(tree):
    return lax.optimization_barrier(tree)


def plus(a, b):
    return (a.astype(F32) + b.astype(F32)).astype(BF)


class Chain:
    def __init__(self, keep, sent, dims):
        self.keep, self.sent, self.dims = keep, sent, (CORE,) + dims

    def start(self):
        return shuffle(self.sent, *self.dims[0])

    def take(self, got):
        self.dims = self.dims[1:]
        if self.dims:
            self.keep, self.sent = plus(self.keep[0], got[0]), plus(self.keep[1], got[1])
        else:
            self.keep = plus(self.keep, got)


def together(chains, make=lambda: ()):
    got = [chain.start() for chain in chains]
    got, other = fence((got, make()))
    for chain, value in zip(chains, got):
        chain.take(value)
    return other


def local_small(
    layer_input, segment_ids, context_flags,
    first_gain, first_shift, sample_weight, sample_bias, sample_mixer, sample_offset,
    second_gain, second_shift, feature_weight, feature_bias, feature_mixer, feature_offset,
    third_gain, third_shift, expand_weight, expand_bias, reduce_weight, reduce_bias, cotangent,
):
    half, quad, feat = (lax.axis_index(name) for name in ("half", "quad", "feat"))
    samp = half * 4 + quad
    core, xx = feat % 2, feat // 2
    flags = context_flags.reshape(8, 64)[:, 0]
    root = jnp.sum(jnp.where(flags == 1, jnp.arange(8, dtype=jnp.int32), 0))
    me = [feat, half, root // 4, root % 4, core, xx, samp % 2, samp // 2]
    me = jnp.stack(me).astype(jnp.int32)

    turned = whole(turn_in, "turn_in", 8, big((16, 4, 16, 512)), [], layer_input.reshape(1024, 512))
    turned, cotangent = fence((turned, cotangent))
    x_t = lax.all_to_all(turned.reshape(4, 4, 64, 512), "quad", 0, 0)
    cot4 = cotangent.reshape(4, 256, 512)
    block = lambda value, d: at(value, feat ^ d)
    from_core = shuffle(jnp.stack([block(cot4, 1), block(cot4, 3)]), *CORE)
    cot_far = shuffle(jnp.stack([block(cot4, 2), from_core[1]]), *X)
    x_t, from_core, cot_far = fence((x_t, from_core, cot_far))
    own_context = at(x_t, root % 4)
    got_context = shuffle(own_context, *W)
    full = big((4, 256, 512))
    act1, queries = by_feature(
        project_queries, "project_queries", 12, ((full, 0), (full, 0)), [],
        (x_t, 1), row(first_gain), row(first_shift), sample_weight, row(sample_bias),
    )
    got_context, q1 = fence((got_context, queries))

    tasks = segment_ids.reshape(8, 64)
    context_tasks = jnp.concatenate([at(tasks, root)] * 4).reshape(1, 256)
    sent = big((4, 4, 4, 16, 512))
    four = big((4, 64, 512))
    r1, o1, context, cact, k1, v1, p1 = by_feature(
        forward_one, "forward_one", 20,
        (
            (sent, 2), (full, 0), (four, 0), (four, 0), (four, 0), (four, 0),
            (big((4, 256, 512), F32), 0),
        ),
        [],
        me, (q1, 0), (own_context, 0), (got_context, 0), (x_t, 1),
        at(segment_ids.reshape(2, 256, 1), half), context_tasks,
        row(first_gain), row(first_shift), sample_weight, row(sample_bias), sample_mixer,
        row(sample_offset), time=7, per=2,
    )

    def exchange(value):
        shape = value.shape
        value = value.reshape((16,) + shape[2:])
        return lax.all_to_all(value, ("quad", "feat"), 0, 0).reshape(shape)

    rows_in = [
        row(v)
        for v in (
            second_gain, second_shift, feature_bias, feature_offset, third_gain,
            third_shift, expand_bias, reduce_bias,
        )
    ]
    weights = [feature_weight, feature_mixer, expand_weight, reduce_weight]

    own = spec((None, 128, 512), lambda i, m: (m[0], i, 0))
    part = lambda n: spec((None, 128, 512), lambda i, m: (n, i, 0))
    still = lambda shape: spec(shape, lambda i, m: (0,) * len(shape))
    block = spec((128, 512), lambda i, m: (i, 0))
    far = pl.BlockSpec(memory_space=pl.ANY)
    vmem = lambda shape, dtype=BF: pltpu.VMEM(shape, dtype)
    rows, rows32 = vmem((HALF, 512)), vmem((HALF, 512), F32)
    outs = (sent, sds((8, 512), F32), sds((1, 2048), F32))
    gb1_f, vec2, bias2, out0, out1, out2, out3, *grads = pl.pallas_call(
        middle,
        grid_spec=pltpu.PrefetchScalarGridSpec(
            num_scalar_prefetch=1,
            grid=(2,),
            in_specs=[
                pl.BlockSpec(sent.shape, lambda i, m: (0,) * 5, pipeline_mode=pl.Buffered(1)),
                own, part(0), part(0), part(1),
            ]
            + [still(r.shape) for r in rows_in]
            + [far] * 4,
            out_specs=[still(o.shape) for o in outs] + [block] * 4 + [far] * 4,
            scratch_shapes=[vmem(w.shape) for w in weights]
            + [vmem((1024, n)) for n in (512, 1536, 512, 512, 512, 2048, 2048, 512)]
            + [
                vmem((4, 256, 512)), vmem((4, 256, 512)), rows, rows, rows, rows32, rows32, rows,
                rows, rows32, rows32, vmem((32, 96, 512)), vmem((32, 96, 512)), vmem((512, 1024)),
                pltpu.SemaphoreType.DMA((4,)), pltpu.SemaphoreType.DMA((4,)),
            ],
        ),
        out_shape=outs + (big((256, 512)),) * 4 + (sds((16, 96, 512)),) * 4,
        compiler_params=params(58),
        cost_estimate=cost(45),
        name="middle",
    )(
        me,
        *(
            outside(array)
            for array in (exchange(r1), cot4, from_core, cot_far, cot_far, *rows_in, *weights)
        ),
    )

    gb_t = exchange(gb1_f)
    outs = [shuffle(out, "feat", d + 1) for d, out in enumerate((out1, out2, out3))]
    pk, ps, qk, qs = (g.reshape(2, 2, 2, 2, 96, 512) for g in grads)
    p_chain, q_chain = Chain(pk, ps, (X, Y)), Chain(qk, qs, (Y, X))
    chains = [p_chain, q_chain]
    for chain in chains:
        chain.take(chain.start())

    half_rows = sds((2, 16, 32, 512))
    for chain in chains:
        chain.take(chain.start())
    gb1, back, term, vec1, keep_ab, send_ab = (
        lambda: by_feature(
            backward_one, "backward_one", 32,
            (
                (full, 0), (big((4, 256, 512), F32), 0), (four, 0), (sds((8, 512), F32), None),
                (half_rows, None), (half_rows, None),
            ),
            [pltpu.VMEM((1024, 512), BF), pltpu.VMEM((256, 1024), BF), pltpu.VMEM((1024, 512), BF)],
            me, (gb_t, 2), o1, act1, cact, (x_t, 1),
            (context, 0), (q1, 0), (k1, 0), (v1, 0), (p1, 0), sample_weight, sample_mixer,
            time=12, per=2,
        )
    )()

    gb1, back, term, vec1, keep_ab, send_ab, outs = fence(
        (gb1, back, term, vec1, keep_ab, send_ab, outs)
    )

    owned = lambda v, n: v.reshape(-1, 8, n).transpose(1, 0, 2).reshape(8, -1)
    vectors = jnp.concatenate(
        [
            owned(vec2[:6], 64), vec2[6:].reshape(8, 128), bias2.reshape(8, 256),
            owned(vec1[:3], 64), vec1[3:5].reshape(8, 128),
        ],
        axis=1,
    )
    got_term = shuffle(term, *W)
    vectors = vectors.reshape(2, 2, 2, 1088)
    got_term, got_ab, v = together(
        chains,
        lambda: (
            got_term, shuffle(send_ab, *CORE), shuffle(at(vectors, 1 - samp % 2, 2), *Y)
        ),
    )
    vectors = at(vectors, samp % 2, 2) + v
    bits = lambda a: a.reshape(2, 2, 2, 2, 2, 32, 512)
    keep_ab, got_ab = bits(keep_ab), bits(got_ab)
    late = []
    for which, dims in enumerate(((X, Y), (Y, X))):
        pair = [plus(keep_ab[which, i], got_ab[which, i]) for i in range(2)]
        late.append(Chain(*pair, ()))
        late[-1].dims = dims
    around_z = lambda value, mask: lax.ppermute(value, SAMP, [(j, j ^ mask) for j in range(8)])

    def to_owner(rows):
        return [around_z(rows[i // 2, i % 2], (0, 4, 2, 6)[i]) for i in (1, 2, 3)]

    def add_up(rows, got):
        total = rows[0, 0].astype(F32)
        for value in got:
            total = total + value.astype(F32)
        return total.astype(BF)

    both = [jnp.concatenate([chain.keep[i] for chain in chains], axis=-2) for i in range(2)]
    both_chain = Chain(*both, ())
    both_chain.dims = (Z, W)
    (grad_t,) = together(
        late + [both_chain],
        lambda: (
            by_feature(
                backward_input, "backward_input", 16, ((big((4, 4, 64, 512)), 1),),
                [pltpu.VMEM((4, 64, 512), F32)],
                me, (gb1, 0), (x_t, 1), (back, 0), (term, 0), (got_term, 0), row(first_gain),
            )
        ),
    )
    both_chain.take(both_chain.start())
    low = samp // 2 % 2
    layer_output = whole(
        place, "place", 16, sds((4, 256, 512)), [], me, out0, *outs
    ).reshape(64, 16, 512)
    early = lax.all_gather(both_chain.keep, "feat")
    got, v, layer_output, early = together(
        late,
        lambda: (
            lax.all_to_all(grad_t, "quad", 0, 0),
            shuffle(at(vectors, 1 - low, 1), *Z),
            layer_output,
            early,
        ),
    )
    vectors = at(vectors, low, 1) + v
    input_grad = whole(
        turn_out, "turn_out", 8, sds((1024, 512)), [], got.reshape(16, 4, 16, 512)
    ).reshape(64, 16, 512)

    rows = jnp.concatenate([chain.keep for chain in late], axis=2)
    from_z, v, input_grad = fence(
        (to_owner(rows), shuffle(at(vectors, 1 - half), *W), input_grad)
    )
    vectors = (at(vectors, half) + v).reshape(1, 1088)
    vectors = whole(split, "split", 8, sds((24, 1088)), [], vectors)
    vectors = jnp.pad(vectors[:3].reshape(-1), (0, 8 * 512 - 3 * 1088)).reshape(8, 512)
    total = add_up(rows, from_z)
    last = lax.all_gather(jnp.concatenate([total, vectors]), "feat")
    mine = last[:, 64:].reshape(4, -1).astype(F32)
    mine = sum(mine[:, i * 1088 : (i + 1) * 1088] for i in range(3))
    mine = (mine[0] + mine[1]) + (mine[2] + mine[3])

    units_of = lambda rows: [rows[i].astype(F32) for i in (0, 2, 1, 3)]
    feature, expand = units_of(early[:, :64]), units_of(early[:, 96:160])
    reduce_grad = jnp.concatenate(
        units_of(jnp.concatenate([early[:, 64:96], early[:, 160:]], axis=1))
    )
    sample = units_of(last[:, :64])

    gain3, shift3, gain2, shift2, off2, bias_r = (mine[i * 64 : (i + 1) * 64] for i in range(6))
    feature_b, expand_b = mine[384:512], mine[512:768]
    gain1, shift1, off1 = (mine[768 + i * 64 : 832 + i * 64] for i in range(3))
    sample_b = mine[960:1088]
    columns = lambda blocks: jnp.concatenate(blocks, axis=1)

    return (
        layer_output, input_grad,
        gain1, shift1, columns(sample[:3]), sample_b, sample[3], off1,
        gain2, shift2, columns(feature[:3]), feature_b, feature[3], off2,
        gain3, shift3, columns(expand), expand_b,
        reduce_grad, bias_r,
    )


def spread_2(block, axis, owner):
    block = jnp.where(lax.axis_index(axis) == owner, block, jnp.zeros_like(block))
    return lax.psum(block, axis)


def layer_norm(values, gain_row, shift_row):
    center = jnp.mean(values, axis=-1, keepdims=True)
    spread = values - center
    variance = jnp.mean(spread * spread, axis=-1, keepdims=True)
    return spread * lax.rsqrt(variance + EPS) * gain_row + shift_row


def apply_weight(active, weight):
    return jnp.einsum("sfd,de->sfe", active, weight, preferred_element_type=jnp.float32)


def input_back(grad_out, weight):
    return jnp.einsum("sfe,de->sfd", grad_out, weight, preferred_element_type=jnp.float32)


def weight_grad(active, grad_out):
    return jnp.einsum("sfd,sfe->de", active, grad_out, preferred_element_type=jnp.float32)


def column_sum(values):
    return jnp.sum(values.astype(jnp.float32), axis=(0, 1))


def project(active, weight, bias_row):
    model_width = active.shape[-1]
    joined = apply_weight(active, weight)
    queries = (joined[..., :model_width] + bias_row[:model_width]).astype(jnp.bfloat16)
    key_part = joined[..., model_width : 2 * model_width].astype(jnp.bfloat16)
    value_part = (joined[..., 2 * model_width :] + bias_row[model_width:]).astype(jnp.bfloat16)
    return (queries, key_part, value_part)


def split_heads(values):
    return values.reshape(values.shape[0], values.shape[1], HEADS, HEAD_DIM)


def join_heads(values):
    return values.reshape(values.shape[0], values.shape[1], HEADS * HEAD_DIM)


def soft_weights(scores):
    top_score = jnp.max(scores, axis=-1, keepdims=True)
    raised = jnp.exp(scores - top_score)
    return raised / jnp.sum(raised, axis=-1, keepdims=True)


def feature_attend(queries, key_part, value_part):
    score_scale = HEAD_DIM ** (-0.5)
    scores = (
        jnp.einsum(
            "sfhd,sghd->shfg",
            split_heads(queries),
            split_heads(key_part),
            preferred_element_type=jnp.float32,
        )
        * score_scale
    )
    probability = soft_weights(scores)
    mixed = jnp.einsum(
        "shfg,sghd->sfhd",
        probability.astype(jnp.bfloat16),
        split_heads(value_part),
        preferred_element_type=jnp.float32,
    )
    return (join_heads(mixed).astype(jnp.bfloat16), probability)


def feature_grads(queries, key_part, value_part, probability, grad_mixed):
    score_scale = HEAD_DIM ** (-0.5)
    grad_heads = split_heads(grad_mixed)
    grad_weights = jnp.einsum(
        "sfhd,sghd->shfg", grad_heads, split_heads(value_part), preferred_element_type=jnp.float32
    )
    inner_sum = jnp.sum(probability * grad_weights, axis=-1, keepdims=True)
    grad_scores = (probability * (grad_weights - inner_sum)).astype(jnp.bfloat16)
    grad_queries = (
        jnp.einsum(
            "shfg,sghd->sfhd",
            grad_scores,
            split_heads(key_part),
            preferred_element_type=jnp.float32,
        )
        * score_scale
    )
    grad_keys = (
        jnp.einsum(
            "shfg,sfhd->sghd", grad_scores, split_heads(queries), preferred_element_type=jnp.float32
        )
        * score_scale
    )
    grad_values = jnp.einsum(
        "shfg,sfhd->sghd",
        probability.astype(jnp.bfloat16),
        grad_heads,
        preferred_element_type=jnp.float32,
    )
    return (join_heads(grad_queries), join_heads(grad_keys), join_heads(grad_values))


def local_large(
    layer_input,
    segment_ids,
    context_flags,
    first_gain,
    first_shift,
    sample_weight,
    sample_bias,
    sample_mixer,
    sample_offset,
    second_gain,
    second_shift,
    feature_weight,
    feature_bias,
    feature_mixer,
    feature_offset,
    third_gain,
    third_shift,
    expand_weight,
    expand_bias,
    reduce_weight,
    reduce_bias,
    cotangent,
):
    sample_rows = layer_input.shape[0]
    feature_rows = layer_input.shape[1]
    model_width = layer_input.shape[2]
    score_scale = HEAD_DIM ** (-0.5)
    shard_count = lax.axis_size("samp")
    context_shards = shard_count // 8
    total_context = context_shards * sample_rows
    residual_zero = layer_input.astype(jnp.float32)
    normed_one, norm_one_back = jax.vjp(layer_norm, residual_zero, first_gain, first_shift)
    active_one = normed_one.astype(jnp.bfloat16)
    queries_one, keys_one, values_one = project(active_one, sample_weight, sample_bias)
    my_index = lax.axis_index("samp")
    shard_flags = context_flags.reshape(shard_count, sample_rows)[:, 0]
    shard_rank = jnp.cumsum(shard_flags) - 1
    shard_ids = jnp.arange(shard_count, dtype=jnp.int32)
    slot_ids = jnp.arange(context_shards, dtype=jnp.int32)
    root_hits = (shard_rank[None, :] == slot_ids[:, None]) & (shard_flags[None, :] == 1)
    roots = jnp.sum(jnp.where(root_hits, shard_ids[None, :], 0), axis=1)
    context_tasks = jnp.take(segment_ids.reshape(shard_count, sample_rows), roots, axis=0).reshape(
        total_context
    )
    local_tasks = lax.dynamic_slice_in_dim(segment_ids, my_index * sample_rows, sample_rows)
    allowed = local_tasks[:, None] == context_tasks[None, :]
    is_context = shard_flags[my_index] == 1
    own_rank = jnp.maximum(shard_rank[my_index], 0)
    own_block = jnp.concatenate([keys_one, values_one], axis=-1)

    def fetch_rows(step, buffer):
        piece = spread_2(own_block, "samp", roots[step])
        return lax.dynamic_update_slice_in_dim(buffer, piece, step * sample_rows, 0)

    empty_rows = jnp.zeros((total_context, feature_rows, 2 * model_width), jnp.bfloat16)
    fetched = lax.fori_loop(0, context_shards, fetch_rows, empty_rows)
    context_keys = fetched[..., :model_width]
    context_values = fetched[..., model_width:]
    query_heads = split_heads(queries_one)
    key_heads = split_heads(context_keys)
    value_heads = split_heads(context_values)
    scores = (
        jnp.einsum("sfhd,cfhd->fhsc", query_heads, key_heads, preferred_element_type=jnp.float32)
        * score_scale
    )
    sample_prob = soft_weights(jnp.where(allowed[None, None], scores, MASKED))
    sample_weights = sample_prob.astype(jnp.bfloat16)
    mixed_one = join_heads(
        jnp.einsum(
            "fhsc,cfhd->sfhd", sample_weights, value_heads, preferred_element_type=jnp.float32
        )
    ).astype(jnp.bfloat16)
    residual_one = residual_zero + apply_weight(mixed_one, sample_mixer) + sample_offset
    normed_two, norm_two_back = jax.vjp(layer_norm, residual_one, second_gain, second_shift)
    active_two = normed_two.astype(jnp.bfloat16)
    queries_two, keys_two, values_two = project(active_two, feature_weight, feature_bias)
    all_keys, all_values = (
        lax.all_gather(keys_two, "feat", axis=1, tiled=True),
        lax.all_gather(values_two, "feat", axis=1, tiled=True),
    )
    mixed_two, feature_prob = feature_attend(queries_two, all_keys, all_values)
    residual_two = residual_one + apply_weight(mixed_two, feature_mixer) + feature_offset
    normed_three, norm_three_back = jax.vjp(layer_norm, residual_two, third_gain, third_shift)
    active_three = normed_three.astype(jnp.bfloat16)
    expanded = apply_weight(active_three, expand_weight) + expand_bias
    activated, gelu_back = jax.vjp(partial(jax.nn.gelu, approximate=False), expanded)
    hidden = activated.astype(jnp.bfloat16)
    layer_output = (residual_two + apply_weight(hidden, reduce_weight) + reduce_bias).astype(
        jnp.bfloat16
    )
    grad_out = cotangent.astype(jnp.float32)
    grad_branch = cotangent
    reduce_bias_grad = column_sum(grad_branch)
    reduce_weight_grad = weight_grad(hidden, grad_branch)
    grad_hidden = input_back(grad_branch, reduce_weight).astype(jnp.bfloat16)
    grad_expanded = gelu_back(grad_hidden.astype(jnp.float32))[0].astype(jnp.bfloat16)
    expand_bias_grad = column_sum(grad_expanded)
    expand_weight_grad = weight_grad(active_three, grad_expanded)
    grad_norm, third_gain_grad, third_shift_grad = norm_three_back(
        input_back(grad_expanded, expand_weight)
    )
    grad_two = grad_out + grad_norm
    grad_branch = grad_two.astype(jnp.bfloat16)
    feature_offset_grad = column_sum(grad_branch)
    feature_mixer_grad = weight_grad(mixed_two, grad_branch)
    grad_mixed = input_back(grad_branch, feature_mixer).astype(jnp.bfloat16)
    grad_queries, grad_keys, grad_values = feature_grads(
        queries_two, all_keys, all_values, feature_prob, grad_mixed
    )
    own_key_grads, own_value_grads = (
        lax.psum_scatter(grad_keys, "feat", scatter_dimension=1, tiled=True),
        lax.psum_scatter(grad_values, "feat", scatter_dimension=1, tiled=True),
    )
    grad_project = jnp.concatenate(
        [
            grad_queries.astype(jnp.bfloat16),
            own_key_grads.astype(jnp.bfloat16),
            own_value_grads.astype(jnp.bfloat16),
        ],
        axis=-1,
    )
    feature_weight_grad = weight_grad(active_two, grad_project)
    feature_bias_grad = jnp.concatenate(
        [
            column_sum(grad_project[..., :model_width]),
            column_sum(grad_project[..., 2 * model_width :]),
        ]
    )
    grad_norm, second_gain_grad, second_shift_grad = norm_two_back(
        input_back(grad_project, feature_weight)
    )
    grad_one = grad_two + grad_norm
    grad_branch = grad_one.astype(jnp.bfloat16)
    sample_offset_grad = column_sum(grad_branch)
    sample_mixer_grad = weight_grad(mixed_one, grad_branch)
    grad_heads = split_heads(input_back(grad_branch, sample_mixer).astype(jnp.bfloat16))
    grad_weights = jnp.einsum(
        "sfhd,cfhd->fhsc", grad_heads, value_heads, preferred_element_type=jnp.float32
    )
    inner_sum = jnp.sum(sample_prob * grad_weights, axis=-1, keepdims=True)
    grad_scores = (sample_prob * (grad_weights - inner_sum)).astype(jnp.bfloat16)
    grad_queries = (
        join_heads(
            jnp.einsum(
                "fhsc,cfhd->sfhd", grad_scores, key_heads, preferred_element_type=jnp.float32
            )
        )
        * score_scale
    ).astype(jnp.bfloat16)
    key_terms = (
        join_heads(
            jnp.einsum(
                "fhsc,sfhd->cfhd", grad_scores, query_heads, preferred_element_type=jnp.float32
            )
        )
        * score_scale
    )
    value_terms = join_heads(
        jnp.einsum(
            "fhsc,sfhd->cfhd", sample_weights, grad_heads, preferred_element_type=jnp.float32
        )
    )
    term_block = jnp.concatenate([key_terms, value_terms], axis=-1)
    summed_terms = lax.psum_scatter(term_block, "samp", scatter_dimension=0, tiled=True)
    summed_rows = lax.all_gather(summed_terms.astype(jnp.bfloat16), "samp", axis=0, tiled=True)
    own_grads = lax.dynamic_slice_in_dim(summed_rows, own_rank * sample_rows, sample_rows, 0)
    own_grads = jnp.where(is_context, own_grads, jnp.zeros_like(own_grads))
    grad_project = jnp.concatenate([grad_queries, own_grads], axis=-1)
    sample_weight_grad = weight_grad(active_one, grad_project)
    sample_bias_grad = jnp.concatenate(
        [column_sum(grad_queries), column_sum(own_grads[..., model_width:])]
    )
    grad_norm, first_gain_grad, first_shift_grad = norm_one_back(
        input_back(grad_project, sample_weight)
    )
    input_grad = (grad_one + grad_norm).astype(jnp.bfloat16)
    summed = lax.psum(
        (
            first_gain_grad,
            first_shift_grad,
            sample_weight_grad,
            sample_bias_grad,
            sample_mixer_grad,
            sample_offset_grad,
            second_gain_grad,
            second_shift_grad,
            feature_weight_grad,
            feature_bias_grad,
            feature_mixer_grad,
            feature_offset_grad,
            third_gain_grad,
            third_shift_grad,
            expand_weight_grad,
            expand_bias_grad,
            reduce_weight_grad,
            reduce_bias_grad,
        ),
        "feat",
    )
    shares = (
        lax.psum_scatter(summed[0], "samp", scatter_dimension=0, tiled=True),
        lax.psum_scatter(summed[1], "samp", scatter_dimension=0, tiled=True),
        lax.psum_scatter(summed[2], "samp", scatter_dimension=0, tiled=True),
        lax.psum_scatter(summed[3], "samp", scatter_dimension=0, tiled=True),
        lax.psum_scatter(summed[4], "samp", scatter_dimension=0, tiled=True),
        lax.psum_scatter(summed[5], "samp", scatter_dimension=0, tiled=True),
        lax.psum_scatter(summed[6], "samp", scatter_dimension=0, tiled=True),
        lax.psum_scatter(summed[7], "samp", scatter_dimension=0, tiled=True),
        lax.psum_scatter(summed[8], "samp", scatter_dimension=0, tiled=True),
        lax.psum_scatter(summed[9], "samp", scatter_dimension=0, tiled=True),
        lax.psum_scatter(summed[10], "samp", scatter_dimension=0, tiled=True),
        lax.psum_scatter(summed[11], "samp", scatter_dimension=0, tiled=True),
        lax.psum_scatter(summed[12], "samp", scatter_dimension=0, tiled=True),
        lax.psum_scatter(summed[13], "samp", scatter_dimension=0, tiled=True),
        lax.psum_scatter(summed[14], "samp", scatter_dimension=0, tiled=True),
        lax.psum_scatter(summed[15], "samp", scatter_dimension=0, tiled=True),
        lax.psum_scatter(summed[16], "samp", scatter_dimension=0, tiled=True),
        lax.psum_scatter(summed[17], "samp", scatter_dimension=0, tiled=True),
    )
    return (
        layer_output,
        input_grad,
        shares[0],
        shares[1],
        shares[2],
        shares[3],
        shares[4],
        shares[5],
        shares[6],
        shares[7],
        shares[8],
        shares[9],
        shares[10],
        shares[11],
        shares[12],
        shares[13],
        shares[14],
        shares[15],
        shares[16],
        shares[17],
    )


def solution(mesh):
    if mesh.shape["samp"] == 8 and mesh.shape["feat"] == 4:
        return solution_small(mesh)
    return jax.shard_map(
        local_large,
        mesh=mesh,
        in_specs=(
            P("samp", "feat", None),
            P(),
            P(),
            P(),
            P(),
            P(),
            P(),
            P(),
            P(),
            P(),
            P(),
            P(),
            P(),
            P(),
            P(),
            P(),
            P(),
            P(),
            P(),
            P(),
            P(),
            P("samp", "feat", None),
        ),
        out_specs=(
            P("samp", "feat", None),
            P("samp", "feat", None),
            P("samp"),
            P("samp"),
            P("samp", None),
            P("samp"),
            P("samp", None),
            P("samp"),
            P("samp"),
            P("samp"),
            P("samp", None),
            P("samp"),
            P("samp", None),
            P("samp"),
            P("samp"),
            P("samp"),
            P("samp", None),
            P("samp"),
            P("samp", None),
            P("samp"),
        ),
        check_vma=False,
    )


def solution_small(mesh):
    mesh = jax.sharding.Mesh(mesh.devices.reshape(2, 4, 4), ("half", "quad", "feat"))
    tokens, copied = P(SAMP, "feat", None), P()
    vector, matrix = P(SAMP), P(SAMP, None)
    return jax.shard_map(
        local_small,
        mesh=mesh,
        in_specs=(tokens,) + (copied,) * 20 + (tokens,),
        out_specs=(
            tokens, tokens, vector, vector, matrix, vector, matrix, vector,
            vector, vector, matrix, vector, matrix, vector,
            vector, vector, matrix, vector, matrix, vector,
        ),
        check_vma=False,
    )
```

```python
from functools import partial

import jax
import jax.numpy as jnp
from jax import lax
from jax.experimental import pallas as pl
from jax.experimental.pallas import tpu as pltpu
from jax.sharding import PartitionSpec as P

HEADS = 8
HEAD_DIM = 64
EPS = 1e-05
MASKED = -1000000000.0
SCALE = HEAD_DIM ** (-0.5)
QUAD = 4 * HEAD_DIM
BF = jnp.bfloat16
F32 = jnp.float32


def mm(a, b, ca=1, cb=0):
    return lax.dot_general(a, b, (((ca,), (cb,)), ((), ())), preferred_element_type=F32)


def norm_parts(values):
    center = jnp.mean(values, axis=-1, keepdims=True)
    spread = values - center
    variance = jnp.mean(spread * spread, axis=-1, keepdims=True)
    inverse = lax.rsqrt(variance + EPS)
    return spread * inverse, inverse


def norm_back(grad, unit, inverse, gain):
    scaled = grad * gain
    first = jnp.mean(scaled, axis=-1, keepdims=True)
    second = jnp.mean(scaled * unit, axis=-1, keepdims=True)
    return (scaled - first - unit * second) * inverse


def lane_ids(rows):
    return lax.broadcasted_iota(jnp.int32, (rows, 128), 1)


def group_reduce(values, op, fill):
    rows = values.shape[0]
    low = lane_ids(rows) < HEAD_DIM
    outs = []
    for t in range(values.shape[1] // 128):
        tile = values[:, t * 128 : (t + 1) * 128]
        left = op(jnp.where(low, tile, fill), axis=1, keepdims=True)
        right = op(jnp.where(low, fill, tile), axis=1, keepdims=True)
        outs.append(jnp.where(low, left, right))
    return jnp.concatenate(outs, axis=1)


def head_masks(dtype):
    lanes = lax.broadcasted_iota(jnp.int32, (1, QUAD), 1) // HEAD_DIM
    return [jnp.where(lanes == h, 1.0, 0.0).astype(dtype) for h in range(4)]


def stack_heads(part, masks):
    return jnp.concatenate([part * m for m in masks], axis=0)


def pick_heads(stacked, masks):
    rows = stacked.shape[0] // 4
    total = stacked[:rows] * masks[0]
    for h in range(1, 4):
        total = total + stacked[h * rows : (h + 1) * rows] * masks[h]
    return total


def attend(q, k, v, masks, allow):
    outs, probs = [], []
    for quad in range(2):
        cols = slice(quad * QUAD, (quad + 1) * QUAD)
        scores = mm(q[:, cols], stack_heads(k[:, cols], masks), 1, 1)
        if allow is not None:
            scores = jnp.where(allow, scores, MASKED)
        raised = jnp.exp(scores - group_reduce(scores, jnp.max, -jnp.inf))
        prob = raised / group_reduce(raised, jnp.sum, 0.0)
        outs.append(mm(prob.astype(BF), stack_heads(v[:, cols], masks)))
        probs.append(prob)
    return jnp.concatenate(outs, axis=1), jnp.concatenate(probs, axis=1)


def attend_back(q, k, v, prob, grad, masks, masks32):
    dqs, dks, dvs = [], [], []
    for quad in range(2):
        cols = slice(quad * QUAD, (quad + 1) * QUAD)
        p, g = prob[:, cols], grad[:, cols]
        back = mm(g, stack_heads(v[:, cols], masks), 1, 1)
        inner = group_reduce(p * back, jnp.sum, 0.0)
        gs = (p * (back - inner)).astype(BF)
        dqs.append(mm(gs, stack_heads(k[:, cols], masks)) * SCALE)
        dks.append(pick_heads(mm(gs, q[:, cols], 0, 0), masks32))
        dvs.append(pick_heads(mm(p.astype(BF), g, 0, 0), masks32))
    join = lambda parts: jnp.concatenate(parts, axis=1).astype(BF)
    return join(dqs), join(dks), join(dvs)


def swap_matrix(rows=16):
    n = rows * 16
    r = lax.broadcasted_iota(jnp.int32, (n, n), 0)
    c = lax.broadcasted_iota(jnp.int32, (n, n), 1)
    return jnp.where((r // rows == c % 16) & (r % rows == c // 16), 1.0, 0.0).astype(BF)


def swap(matrix, values, back=False):
    return mm(matrix, values, 0 if back else 1, 0).astype(BF)


def gelu_parts(u):
    cdf = 0.5 * (1.0 + lax.erf(u * (2.0**-0.5)))
    density = jnp.exp(u * u * -0.5) * 0.3989422804014327
    return cdf, density


def col_sum(values):
    return jnp.sum(values.astype(F32), axis=0, keepdims=True)


def turn_in(x_ref, out_ref):
    matrix = swap_matrix()
    for d in range(4):
        rows = x_ref[d * 256 : (d + 1) * 256]
        out_ref[:, d] = swap(matrix, rows).reshape(16, 16, 512)


def turn_out(got_ref, out_ref):
    matrix = swap_matrix()
    for d in range(4):
        out_ref[d * 256 : (d + 1) * 256] = swap(matrix, got_ref[:, d].reshape(256, 512))


def project_queries(x_ref, gain_ref, shift_ref, w_ref, b_ref, act_ref, q_ref):
    unit, _ = norm_parts(x_ref[:, 0].reshape(256, 512).astype(F32))
    act = (unit * gain_ref[...] + shift_ref[...]).astype(BF)
    act_ref[0] = act
    q = (mm(act, w_ref[:, :512]) + b_ref[:, :512]).astype(BF)
    q_ref[0] = q * jnp.asarray(SCALE, BF)


def forward_one(
    me_ref, q_ref, own_ref, got_ref, x_ref, tasks_ref, context_ref, gain_ref, shift_ref, w_ref,
    b_ref, wm_ref, off_ref,
    r_ref, o_ref, c_ref, cact_ref, k_ref, v_ref, p_ref,
):
    here = me_ref[1] == me_ref[2]
    masks = head_masks(BF)
    allow = tasks_ref[...] == context_ref[...]

    @pl.when(here)
    def _():
        c_ref[...] = own_ref[...]

    @pl.when(jnp.logical_not(here))
    def _():
        c_ref[...] = got_ref[...]

    for e in range(c_ref.shape[0]):
        unit, _ = norm_parts(c_ref[e].astype(F32))
        act = (unit * gain_ref[...] + shift_ref[...]).astype(BF)
        cact_ref[e] = act
        kv = mm(act, w_ref[:, 512:])
        k_ref[e] = kv[:, :512].astype(BF)
        v_ref[e] = (kv[:, 512:] + b_ref[:, 512:]).astype(BF)
    for e in range(c_ref.shape[0]):
        out, prob = attend(q_ref[e], k_ref[e], v_ref[e], masks, allow)
        o_ref[e] = out.astype(BF)
        p_ref[e] = prob
    for e in range(c_ref.shape[0]):
        r1 = x_ref[:, e].reshape(256, 512).astype(F32) + mm(o_ref[e], wm_ref[...]) + off_ref[...]
        r_ref[:, :, e] = r1.astype(BF).reshape(4, 4, 16, 512)


HALF = 512


def middle(me_ref, *refs):
    (
        r1_ref, c0, c1, c2, c3, g2_ref, s2_ref, bf_ref, off2_ref, g3_ref, s3_ref, be_ref, br_ref,
    ) = refs[:13]
    weights_hbm = refs[13:17]
    gb1_ref, vec_ref, bias_ref, out0, out1, out2, out3 = refs[17:24]
    targets = refs[24:28]
    wf_ref, wm2_ref, we_ref, wr_ref = refs[28:32]
    kept = refs[32:40]
    (
        r_scr, g_scr, q_scr, k_scr, v_scr, p_scr, e_scr, gs_scr, go_scr, out_scr, back_scr,
        part_p, part_q, turn, in_sems, out_sems,
    ) = refs[40:]
    me, step = me_ref[0], pl.program_id(0)
    tokens = pl.ds(pl.multiple_of(step * HALF, HALF), HALF)
    a2_ref, dqkv_ref, o2_ref, gb2_ref, a3_ref, gu_ref, hid_ref, gb3_ref = (
        ref.at[tokens] for ref in kept
    )
    loads = [
        pltpu.make_async_copy(source, target, in_sems.at[i])
        for i, (source, target) in enumerate(zip(weights_hbm, refs[28:32]))
    ]

    def first(make):
        pl.when(step == 0)(make)

    matrix = swap_matrix()
    masks, masks32 = head_masks(BF), head_masks(F32)

    @first
    def _():
        loads[0].start()
        loads[1].start()
        for f in range(4):
            r_scr[f] = swap(matrix, r1_ref[:, f].reshape(256, 512))

    now = pl.ds(pl.multiple_of(step * 128, 128), 128)

    def gather(*refs):
        return jnp.concatenate(
            [ref[s * 16 : (s + 1) * 16] for s in range(8) for ref in refs], axis=0
        )

    def scatter(values, *refs):
        for s in range(8):
            for d, ref in enumerate(refs):
                at = (s * 4 + d) * 16
                ref[s * 16 : (s + 1) * 16] = values[at : at + 16]

    def each_sample(body):
        def step(i, carry):
            for j in range(SAMPLE_UNROLL):
                rows = pl.ds(pl.multiple_of((i * SAMPLE_UNROLL + j) * 64, 64), 64)
                for quad in range(2):
                    body(rows, slice(quad * QUAD, (quad + 1) * QUAD))
            return carry

        lax.fori_loop(0, 8 // SAMPLE_UNROLL, step, 0)

    gb3_ref[...] = gather(c0, c1, c2, c3)
    r1 = gather(*(r_scr.at[d ^ me, now] for d in range(4))).astype(F32)
    unit2, inv2 = norm_parts(r1)
    a2_ref[...] = (unit2 * g2_ref[...] + s2_ref[...]).astype(BF)

    @first
    def _():
        loads[0].wait()
        loads[2].start()
        loads[3].start()

    q = (mm(a2_ref[...], wf_ref[:, :512]) + bf_ref[:, :512]).astype(BF)
    q_scr[...] = q * jnp.asarray(SCALE, BF)
    k_scr[...] = mm(a2_ref[...], wf_ref[:, 512:1024]).astype(BF)
    v_scr[...] = (mm(a2_ref[...], wf_ref[:, 1024:]) + bf_ref[:, 512:]).astype(BF)

    def score(rows, cols):
        p_scr[rows, cols] = mm(q_scr[rows, cols], stack_heads(k_scr[rows, cols], masks), 1, 1)

    each_sample(score)
    for i in range(4):
        rows = slice(i * 128, (i + 1) * 128)
        scores = p_scr[rows]
        raised = jnp.exp(scores - group_reduce(scores, jnp.max, -jnp.inf))
        p_scr[rows] = raised / group_reduce(raised, jnp.sum, 0.0)

    def mix(rows, cols):
        o2_ref[rows, cols] = mm(
            p_scr[rows, cols].astype(BF), stack_heads(v_scr[rows, cols], masks)
        ).astype(BF)

    each_sample(mix)
    first(loads[1].wait)
    r2 = r1 + mm(o2_ref[...], wm2_ref[...]) + off2_ref[...]
    unit3, inv3 = norm_parts(r2)
    a3_ref[...] = (unit3 * g3_ref[...] + s3_ref[...]).astype(BF)
    first(loads[2].wait)
    first(loads[3].wait)

    @first
    def _():
        vec_ref[...] = jnp.zeros((8, 512), F32)
        bias_ref[...] = jnp.zeros((1, 2048), F32)

    out_scr[...] = r2 + br_ref[...]
    back_scr[...] = jnp.zeros((HALF, 512), F32)

    def expand(b, carry):
        cols = pl.ds(pl.multiple_of(b * WIDE, WIDE), WIDE)
        u = mm(a3_ref[...], we_ref[:, cols]) + be_ref[:, cols]
        cdf, density = gelu_parts(u)
        hidden = (u * cdf).astype(BF)
        hid_ref[:, cols] = hidden
        gh = mm(gb3_ref[...], wr_ref[cols, :], 1, 1).astype(BF).astype(F32)
        gu = (gh * (cdf + u * density)).astype(BF)
        gu_ref[:, cols] = gu
        bias_ref[:, cols] += col_sum(gu)
        out_scr[...] += mm(hidden, wr_ref[cols, :])
        back_scr[...] += mm(gu, we_ref[:, cols], 1, 1)
        return carry

    lax.fori_loop(0, 2048 // WIDE, expand, 0, unroll=EXPAND_UNROLL)
    scatter(out_scr[...].astype(BF), out0, out1, out2, out3)
    back, cot = back_scr[...], gb3_ref[...]
    vecs = [col_sum(back * unit3), col_sum(back)]
    gr2 = cot.astype(F32) + norm_back(back, unit3, inv3, g3_ref[...])
    gb2_ref[...] = gr2.astype(BF)
    go_scr[...] = mm(gb2_ref[...], wm2_ref[...], 1, 1).astype(BF)

    def weigh(rows, cols):
        e_scr[rows, cols] = mm(go_scr[rows, cols], stack_heads(v_scr[rows, cols], masks), 1, 1)

    each_sample(weigh)
    for i in range(4):
        rows = slice(i * 128, (i + 1) * 128)
        prob, grad = p_scr[rows], e_scr[rows]
        inner = group_reduce(prob * grad, jnp.sum, 0.0)
        gs_scr[rows] = (prob * (grad - inner)).astype(BF)

    def spread(rows, cols):
        gs, at = gs_scr[rows, cols], cols.start
        dq = mm(gs, stack_heads(k_scr[rows, cols], masks)) * SCALE
        dqkv_ref[rows, at : at + QUAD] = dq.astype(BF)
        dk = pick_heads(mm(gs, q_scr[rows, cols], 0, 0), masks32)
        dqkv_ref[rows, 512 + at : 512 + at + QUAD] = dk.astype(BF)
        dv = pick_heads(mm(p_scr[rows, cols].astype(BF), go_scr[rows, cols], 0, 0), masks32)
        dqkv_ref[rows, 1024 + at : 1024 + at + QUAD] = dv.astype(BF)

    each_sample(spread)
    dqkv = dqkv_ref[...]
    back = mm(dqkv, wf_ref[...], 1, 1)
    vecs += [col_sum(back * unit2), col_sum(back)]
    gr1 = gr2 + norm_back(back, unit2, inv2, g2_ref[...])
    scatter(gr1.astype(BF), *(g_scr.at[d ^ me, now] for d in range(4)))
    vecs += [
        col_sum(gb2_ref[...]), col_sum(cot), col_sum(dqkv[:, :512]), col_sum(dqkv[:, 1024:])
    ]
    vec_ref[...] += jnp.concatenate(vecs, axis=0)

    @pl.when(step == 1)
    def _():
        for f in range(4):
            gb1_ref[:, f] = swap(matrix, g_scr[f]).reshape(4, 4, 16, 512)
        grads_middle(me_ref, kept, (part_p, part_q), turn, targets, out_sems)


SAMPLE_UNROLL = 8
EXPAND_UNROLL = True
WIDE = 512


def backward_one(
    me_ref, g_ref, o_ref, act_ref, cact_ref, x_ref, c_ref, q_ref, k_ref, v_ref,
    p_ref, w_ref, wm_ref,
    gb1_ref, a_ref, term_ref, vec_ref, keep_ref, send_ref,
    dq_scr, dkv_scr, g_scr,
):
    masks, masks32 = head_masks(BF), head_masks(F32)

    @pl.when(pl.program_id(0) == 0)
    def _():
        vec_ref[...] = jnp.zeros((8, 512), F32)

    step, per = pl.program_id(0), q_ref.shape[0]
    for e in range(per):
        gb1 = g_ref[:, :, e].reshape(256, 512)
        gb1_ref[e] = gb1
        go = mm(gb1, wm_ref[...], 1, 1).astype(BF)
        dq, dk, dv = attend_back(q_ref[e], k_ref[e], v_ref[e], p_ref[e], go, masks, masks32)
        dkv = jnp.concatenate([dk, dv], axis=1)
        at = step * per + e
        rows = pl.ds(pl.multiple_of(at * 256, 256), 256)
        dq_scr[rows], g_scr[rows] = dq, gb1
        dkv_scr[pl.ds(pl.multiple_of(at * 64, 64), 64)] = dkv
        back = mm(dq, w_ref[:, :512], 1, 1)
        a_ref[e] = back
        term = mm(dkv, w_ref[:, 512:], 1, 1)
        term_ref[e] = term.astype(BF)
        unit, _ = norm_parts(x_ref[:, e].reshape(256, 512).astype(F32))
        unit_c, _ = norm_parts(c_ref[e].astype(F32))
        zero = jnp.zeros((3, 512), F32)
        vec_ref[...] += jnp.concatenate(
            [
                col_sum(back * unit) + col_sum(term * unit_c), col_sum(back) + col_sum(term),
                col_sum(gb1), col_sum(dq), col_sum(dv), zero,
            ],
            axis=0,
        )

    @pl.when(step == pl.num_programs(0) - 1)
    def _():
        whole_rows = lambda ref: ref[...].reshape(-1, 512)
        act_c = whole_rows(cact_ref)
        terms = (
            (whole_rows(act_ref), dq_scr[...]), (act_c, dkv_scr[:, :512]),
            (act_c, dkv_scr[:, 512:]), (whole_rows(o_ref), g_scr[...]),
        )
        for unit, (left, right) in enumerate(terms):
            place_sample(me_ref, mm(left, right, 0, 0).astype(BF), unit, keep_ref, send_ref)


def backward_input(me_ref, gb1_ref, x_ref, a_ref, term_ref, got_ref, gain_ref, grad_ref, a_scr):
    here, quad = me_ref[1] == me_ref[2], me_ref[3]
    unit, inverse = norm_parts(x_ref[:, 0].reshape(256, 512).astype(F32))
    a_scr[...] = a_ref[0].reshape(4, 64, 512)

    @pl.when(here)
    def _():
        a_scr[quad] += term_ref[0].astype(F32) + got_ref[0].astype(F32)

    back = a_scr[...].reshape(256, 512)
    grad = gb1_ref[0].astype(F32) + norm_back(back, unit, inverse, gain_ref[...])
    grad_ref[:, 0] = grad.astype(BF).reshape(4, 64, 512)


VECTORS = (64,) * 6 + (128, 256, 128) + (64,) * 3


def finale(early_ref, last_ref, fw_ref, fm_ref, ew_ref, rw_ref, sw_ref, sm_ref, *vector_refs):
    for unit, feat in enumerate((0, 2, 1, 3)):
        cols = slice(unit * 512, (unit + 1) * 512)
        feature, sample = early_ref[feat, 0:64].astype(F32), last_ref[feat, 0:64].astype(F32)
        if unit < 3:
            fw_ref[:, cols], sw_ref[:, cols] = feature, sample
        else:
            fm_ref[...], sm_ref[...] = feature, sample
        ew_ref[:, cols] = early_ref[feat, 96:160].astype(F32)
        rw_ref[unit * 64 : unit * 64 + 32] = early_ref[feat, 64:96].astype(F32)
        rw_ref[unit * 64 + 32 : unit * 64 + 64] = early_ref[feat, 160:192].astype(F32)
    planes = last_ref[:, 64:88].astype(F32)
    total = (planes[0] + planes[1]) + (planes[2] + planes[3])
    total = total[0:8] + total[8:16] + total[16:24]
    start = 0
    for size, ref in zip(VECTORS, vector_refs):
        row, at = start // 512, start % 512
        ref[...] = total[row : row + 1, at : at + size]
        start += size


def split(got_ref, out_ref):
    rest = got_ref[...]
    for i in range(3):
        term = rest.astype(BF)
        out_ref[i * 8 : (i + 1) * 8] = term
        rest = rest - term.astype(F32)


def place(me_ref, b0, b1, b2, b3, out_ref):
    for d, ref in enumerate((b0, b1, b2, b3)):
        out_ref[d ^ me_ref[0]] = ref[...]


def piece_index(me_ref, unit, shard, order):
    core, xx, yy, zz = me_ref[4], me_ref[5], me_ref[6], me_ref[7]
    other_z = (shard >> 1) ^ zz
    bit = {
        "x": (unit & 1) ^ xx, "y": (shard & 1) ^ yy, "z": other_z & 1, "w": other_z >> 1,
    }
    index = sum(bit[name] * weight for name, weight in zip(order, (8, 4, 2, 1)))
    return (unit >> 1) ^ core, index


def grads_middle(me_ref, kept, staged, turn, targets, out_sems):
    act2, dqkv, o2, gb2, act3, gu, hid, gb3 = kept
    stores = []

    def put(part):
        for i in range(2):
            source = staged[part].at[pl.ds(16 * i, 16)]
            place = 2 * part + i
            stores.append(pltpu.make_async_copy(source, targets[place], out_sems.at[place]))
            stores[-1].start()

    def loop(count, body):
        lax.fori_loop(0, count, lambda n, carry: (body(n), carry)[1], 0)

    block = lambda n: pl.ds(pl.multiple_of(n * 512, 512), 512)

    def place_piece(part, value, unit, shard, rows):
        send, index = piece_index(me_ref, unit, shard, ("xyzw", "yxzw")[part])
        staged[part][send * 16 + index, rows] = value

    def place_unit(part, value, unit):
        for shard in range(8):
            place_piece(part, value[shard * 64 : (shard + 1) * 64], unit, shard, slice(0, 64))

    def from_hidden(n):
        piece = mm(hid[:, block(n)], gb3[...], 0, 0).astype(BF)
        for i in range(8):
            for part in range(2):
                at = i * 64 + part * 32
                rows = piece[at : at + 32]
                place_piece(part, rows, i % 4, 2 * n + i // 4, slice(64, 96))

    loop(4, from_hidden)
    turn[...] = act3[...].T

    def from_expand(n):
        place_unit(1, mm(turn[...], gu[:, block(n)]).astype(BF), n)

    loop(4, from_expand)
    put(1)
    turn[...] = act2[...].T

    def from_feature(n):
        place_unit(0, mm(turn[...], dqkv[:, block(n)]).astype(BF), n)

    loop(3, from_feature)
    place_unit(0, mm(o2[...], gb2[...], 0, 0).astype(BF), 3)
    put(0)
    for store in stores:
        store.wait()


def place_sample(me_ref, value, unit, keep_ref, send_ref):
    for which, order in enumerate(("xyzw", "yxzw")):
        for shard in range(8):
            at = shard * 64 + which * 32
            send, index = piece_index(me_ref, unit, shard, order)

            @pl.when(send == 0)
            def _(at=at, index=index):
                keep_ref[which, index] = value[at : at + 32]

            @pl.when(send == 1)
            def _(at=at, index=index):
                send_ref[which, index] = value[at : at + 32]


def spec(shape, index=None):
    return pl.BlockSpec(shape, index if index is not None else (lambda *a: (0,) * len(shape)))


def sds(shape, dtype=BF):
    return jax.ShapeDtypeStruct(shape, dtype)


def big(shape, dtype=BF):
    return pltpu.HBM(shape, dtype)


def outside(array):
    if array.size * array.dtype.itemsize < 1 << 18:
        return array
    return pltpu.with_memory_space_constraint(array, pltpu.HBM)


def params(limit):
    return pltpu.CompilerParams(vmem_limit_bytes=limit << 20)


def row(vector):
    return vector.reshape(1, -1)


def cost(microseconds):
    return pl.CostEstimate(
        flops=int(microseconds * 1.1e9), transcendentals=0, bytes_accessed=int(microseconds * 2e6)
    )


def whole_block(out):
    shape = out.shape
    return pl.BlockSpec(shape, lambda i: (0,) * len(shape))


def moving_block(shape, axis, per):
    block = tuple(per if i == axis else n for i, n in enumerate(shape))
    return pl.BlockSpec(block, lambda i: tuple(i if j == axis else 0 for j in range(len(shape))))


def by_feature(kernel, name, limit, outs, scratch, *inputs, time=3, per=1):
    arrays, specs = [], []
    for entry in inputs:
        array, axis = entry if isinstance(entry, tuple) else (entry, None)
        if array.ndim == 1:
            arrays.append(array)
            specs.append(pl.BlockSpec(memory_space=pltpu.SMEM))
            continue
        arrays.append(outside(array))
        specs.append(
            whole_block(array) if axis is None else moving_block(array.shape, axis, per)
        )
    return pl.pallas_call(
        kernel,
        grid=(4 // per,),
        out_shape=tuple(out for out, _ in outs),
        in_specs=specs,
        out_specs=[
            whole_block(out) if axis is None else moving_block(out.shape, axis, per)
            for out, axis in outs
        ],
        scratch_shapes=scratch,
        compiler_params=params(limit),
        cost_estimate=cost(time),
        name=name,
    )(*arrays)


def whole(kernel, name, limit, outs, scratch, *inputs, steps=1, time=3):
    arrays, specs = [], []
    for entry in inputs:
        if not isinstance(entry, tuple) and entry.ndim == 1:
            arrays.append(entry)
            specs.append(pl.BlockSpec(memory_space=pltpu.SMEM))
            continue
        array, block, index = entry if isinstance(entry, tuple) else (entry, None, None)
        arrays.append(outside(array))
        block = array.shape if block is None else block
        index = (0,) * array.ndim if index is None else index
        if not callable(index):
            index = lambda i, index=index: index
        specs.append(pl.BlockSpec(block, index))
    return pl.pallas_call(
        kernel,
        grid=(steps,),
        out_shape=outs,
        in_specs=specs,
        out_specs=jax.tree.map(whole_block, outs, is_leaf=lambda o: hasattr(o, "dtype")),
        scratch_shapes=scratch,
        compiler_params=params(limit),
        cost_estimate=cost(time),
        name=name,
    )(*arrays)


def shuffle(value, axis, mask):
    size = lax.axis_size(axis)
    return lax.ppermute(value, axis, [(i, i ^ mask) for i in range(size)])


SAMP = ("half", "quad")
CORE, X, Y, Z, W = ("feat", 1), ("feat", 2), ("quad", 1), ("quad", 2), ("half", 1)


def at(stacked, index, axis=0):
    return lax.dynamic_index_in_dim(stacked, index, axis, keepdims=False)


def fence(tree):
    return lax.optimization_barrier(tree)


def plus(a, b):
    return (a.astype(F32) + b.astype(F32)).astype(BF)


class Chain:
    def __init__(self, keep, sent, dims):
        self.keep, self.sent, self.dims = keep, sent, (CORE,) + dims

    def start(self):
        return shuffle(self.sent, *self.dims[0])

    def take(self, got):
        self.dims = self.dims[1:]
        if self.dims:
            self.keep, self.sent = plus(self.keep[0], got[0]), plus(self.keep[1], got[1])
        else:
            self.keep = plus(self.keep, got)


def together(chains, make=lambda: ()):
    got = [chain.start() for chain in chains]
    got, other = fence((got, make()))
    for chain, value in zip(chains, got):
        chain.take(value)
    return other


def local_small(
    layer_input, segment_ids, context_flags,
    first_gain, first_shift, sample_weight, sample_bias, sample_mixer, sample_offset,
    second_gain, second_shift, feature_weight, feature_bias, feature_mixer, feature_offset,
    third_gain, third_shift, expand_weight, expand_bias, reduce_weight, reduce_bias, cotangent,
):
    half, quad, feat = (lax.axis_index(name) for name in ("half", "quad", "feat"))
    samp = half * 4 + quad
    core, xx = feat % 2, feat // 2
    flags = context_flags.reshape(8, 64)[:, 0]
    root = jnp.sum(jnp.where(flags == 1, jnp.arange(8, dtype=jnp.int32), 0))
    me = [feat, half, root // 4, root % 4, core, xx, samp % 2, samp // 2]
    me = jnp.stack(me).astype(jnp.int32)

    turned = whole(turn_in, "turn_in", 8, big((16, 4, 16, 512)), [], layer_input.reshape(1024, 512))
    turned, cotangent = fence((turned, cotangent))
    x_t = lax.all_to_all(turned.reshape(4, 4, 64, 512), "quad", 0, 0)
    cot4 = cotangent.reshape(4, 256, 512)
    block = lambda value, d: at(value, feat ^ d)
    from_core = shuffle(jnp.stack([block(cot4, 1), block(cot4, 3)]), *CORE)
    cot_far = shuffle(jnp.stack([block(cot4, 2), from_core[1]]), *X)
    x_t, from_core, cot_far = fence((x_t, from_core, cot_far))
    own_context = at(x_t, root % 4)
    got_context = shuffle(own_context, *W)
    full = big((4, 256, 512))
    act1, queries = by_feature(
        project_queries, "project_queries", 12, ((full, 0), (full, 0)), [],
        (x_t, 1), row(first_gain), row(first_shift), sample_weight, row(sample_bias),
    )
    got_context, q1 = fence((got_context, queries))

    tasks = segment_ids.reshape(8, 64)
    context_tasks = jnp.concatenate([at(tasks, root)] * 4).reshape(1, 256)
    sent = big((4, 4, 4, 16, 512))
    four = big((4, 64, 512))
    r1, o1, context, cact, k1, v1, p1 = by_feature(
        forward_one, "forward_one", 20,
        (
            (sent, 2), (full, 0), (four, 0), (four, 0), (four, 0), (four, 0),
            (big((4, 256, 512), F32), 0),
        ),
        [],
        me, (q1, 0), (own_context, 0), (got_context, 0), (x_t, 1),
        at(segment_ids.reshape(2, 256, 1), half), context_tasks,
        row(first_gain), row(first_shift), sample_weight, row(sample_bias), sample_mixer,
        row(sample_offset), time=7, per=4,
    )

    def exchange(value):
        shape = value.shape
        value = value.reshape((16,) + shape[2:])
        return lax.all_to_all(value, ("quad", "feat"), 0, 0).reshape(shape)

    rows_in = [
        row(v)
        for v in (
            second_gain, second_shift, feature_bias, feature_offset, third_gain,
            third_shift, expand_bias, reduce_bias,
        )
    ]
    weights = [feature_weight, feature_mixer, expand_weight, reduce_weight]

    own = spec((None, 128, 512), lambda i, m: (m[0], i, 0))
    part = lambda n: spec((None, 128, 512), lambda i, m: (n, i, 0))
    still = lambda shape: spec(shape, lambda i, m: (0,) * len(shape))
    block = spec((128, 512), lambda i, m: (i, 0))
    far = pl.BlockSpec(memory_space=pl.ANY)
    vmem = lambda shape, dtype=BF: pltpu.VMEM(shape, dtype)
    rows, rows32 = vmem((HALF, 512)), vmem((HALF, 512), F32)
    outs = (sent, sds((8, 512), F32), sds((1, 2048), F32))
    gb1_f, vec2, bias2, out0, out1, out2, out3, *grads = pl.pallas_call(
        middle,
        grid_spec=pltpu.PrefetchScalarGridSpec(
            num_scalar_prefetch=1,
            grid=(2,),
            in_specs=[
                pl.BlockSpec(sent.shape, lambda i, m: (0,) * 5, pipeline_mode=pl.Buffered(1)),
                own, part(0), part(0), part(1),
            ]
            + [still(r.shape) for r in rows_in]
            + [far] * 4,
            out_specs=[still(o.shape) for o in outs] + [block] * 4 + [far] * 4,
            scratch_shapes=[vmem(w.shape) for w in weights]
            + [vmem((1024, n)) for n in (512, 1536, 512, 512, 512, 2048, 2048, 512)]
            + [
                vmem((4, 256, 512)), vmem((4, 256, 512)), rows, rows, rows, rows32, rows32, rows,
                rows, rows32, rows32, vmem((32, 96, 512)), vmem((32, 96, 512)), vmem((512, 1024)),
                pltpu.SemaphoreType.DMA((4,)), pltpu.SemaphoreType.DMA((4,)),
            ],
        ),
        out_shape=outs + (big((256, 512)),) * 4 + (sds((16, 96, 512)),) * 4,
        compiler_params=params(58),
        cost_estimate=cost(45),
        name="middle",
    )(
        me,
        *(
            outside(array)
            for array in (exchange(r1), cot4, from_core, cot_far, cot_far, *rows_in, *weights)
        ),
    )

    gb_t = exchange(gb1_f)
    outs = [shuffle(out, "feat", d + 1) for d, out in enumerate((out1, out2, out3))]
    pk, ps, qk, qs = (g.reshape(2, 2, 2, 2, 96, 512) for g in grads)
    p_chain, q_chain = Chain(pk, ps, (X, Y)), Chain(qk, qs, (Y, X))
    chains = [p_chain, q_chain]
    for chain in chains:
        chain.take(chain.start())

    half_rows = sds((2, 16, 32, 512))
    for chain in chains:
        chain.take(chain.start())
    gb1, back, term, vec1, keep_ab, send_ab = (
        lambda: by_feature(
            backward_one, "backward_one", 32,
            (
                (full, 0), (big((4, 256, 512), F32), 0), (four, 0), (sds((8, 512), F32), None),
                (half_rows, None), (half_rows, None),
            ),
            [pltpu.VMEM((1024, 512), BF), pltpu.VMEM((256, 1024), BF), pltpu.VMEM((1024, 512), BF)],
            me, (gb_t, 2), o1, act1, cact, (x_t, 1),
            (context, 0), (q1, 0), (k1, 0), (v1, 0), (p1, 0), sample_weight, sample_mixer,
            time=12, per=2,
        )
    )()

    gb1, back, term, vec1, keep_ab, send_ab, outs = fence(
        (gb1, back, term, vec1, keep_ab, send_ab, outs)
    )

    owned = lambda v, n: v.reshape(-1, 8, n).transpose(1, 0, 2).reshape(8, -1)
    vectors = jnp.concatenate(
        [
            owned(vec2[:6], 64), vec2[6:].reshape(8, 128), bias2.reshape(8, 256),
            vec1[3:5].reshape(8, 128), owned(vec1[:3], 64),
        ],
        axis=1,
    )
    got_term = shuffle(term, *W)
    vectors = vectors.reshape(2, 2, 2, 1088)
    got_term, got_ab, v = together(
        chains,
        lambda: (
            got_term, shuffle(send_ab, *CORE), shuffle(at(vectors, 1 - samp % 2, 2), *Y)
        ),
    )
    vectors = at(vectors, samp % 2, 2) + v
    bits = lambda a: a.reshape(2, 2, 2, 2, 2, 32, 512)
    keep_ab, got_ab = bits(keep_ab), bits(got_ab)
    late = []
    for which, dims in enumerate(((X, Y), (Y, X))):
        pair = [plus(keep_ab[which, i], got_ab[which, i]) for i in range(2)]
        late.append(Chain(*pair, ()))
        late[-1].dims = dims
    around_z = lambda value, mask: lax.ppermute(value, SAMP, [(j, j ^ mask) for j in range(8)])

    def to_owner(rows):
        return [around_z(rows[i // 2, i % 2], (0, 4, 2, 6)[i]) for i in (1, 2, 3)]

    def add_up(rows, got):
        total = rows[0, 0].astype(F32)
        for value in got:
            total = total + value.astype(F32)
        return total.astype(BF)

    both = [jnp.concatenate([chain.keep[i] for chain in chains], axis=-2) for i in range(2)]
    both_chain = Chain(*both, ())
    both_chain.dims = (Z, W)
    (grad_t,) = together(
        late + [both_chain],
        lambda: (
            by_feature(
                backward_input, "backward_input", 16, ((big((4, 4, 64, 512)), 1),),
                [pltpu.VMEM((4, 64, 512), F32)],
                me, (gb1, 0), (x_t, 1), (back, 0), (term, 0), (got_term, 0), row(first_gain),
            )
        ),
    )
    both_chain.take(both_chain.start())
    low = samp // 2 % 2
    layer_output = whole(
        place, "place", 16, sds((4, 256, 512)), [], me, out0, *outs
    ).reshape(64, 16, 512)
    early = lax.all_gather(both_chain.keep, "feat")
    got, v, layer_output, early = together(
        late,
        lambda: (
            lax.all_to_all(grad_t, "quad", 0, 0),
            shuffle(at(vectors, 1 - low, 1), *Z),
            layer_output,
            early,
        ),
    )
    vectors = at(vectors, low, 1) + v
    input_grad = whole(
        turn_out, "turn_out", 8, sds((1024, 512)), [], got.reshape(16, 4, 16, 512)
    ).reshape(64, 16, 512)

    rows = jnp.concatenate([chain.keep for chain in late], axis=2)
    from_z, v, input_grad = fence(
        (to_owner(rows), shuffle(at(vectors, 1 - half), *W), input_grad)
    )
    vectors = jnp.pad((at(vectors, half) + v).reshape(-1), (0, 8 * 512 - 1088)).reshape(8, 512)
    vectors = whole(split, "split", 8, sds((24, 512)), [], vectors)
    total = add_up(rows, from_z)
    last = lax.all_gather(jnp.concatenate([total, vectors]), "feat")
    matrices = ((64, 1536), (64, 512), (64, 2048), (256, 512), (64, 1536), (64, 512))
    feature_w, feature_m, expand_w, reduce_w, sample_w, sample_m, *mine = whole(
        finale, "finale", 12,
        tuple(sds(shape, F32) for shape in matrices + tuple((1, n) for n in VECTORS)), [],
        early, last,
    )
    mine = [v.reshape(-1) for v in mine]
    gain3, shift3, gain2, shift2, off2, bias_r, feature_b, expand_b = mine[:8]
    sample_b, gain1, shift1, off1 = mine[8:]
    return (
        layer_output, input_grad,
        gain1, shift1, sample_w, sample_b, sample_m, off1,
        gain2, shift2, feature_w, feature_b, feature_m, off2,
        gain3, shift3, expand_w, expand_b, reduce_w, bias_r,
    )


def spread_2(block, axis, owner):
    block = jnp.where(lax.axis_index(axis) == owner, block, jnp.zeros_like(block))
    return lax.psum(block, axis)


def layer_norm(values, gain_row, shift_row):
    center = jnp.mean(values, axis=-1, keepdims=True)
    spread = values - center
    variance = jnp.mean(spread * spread, axis=-1, keepdims=True)
    return spread * lax.rsqrt(variance + EPS) * gain_row + shift_row


def apply_weight(active, weight):
    return jnp.einsum("sfd,de->sfe", active, weight, preferred_element_type=jnp.float32)


def input_back(grad_out, weight):
    return jnp.einsum("sfe,de->sfd", grad_out, weight, preferred_element_type=jnp.float32)


def weight_grad(active, grad_out):
    return jnp.einsum("sfd,sfe->de", active, grad_out, preferred_element_type=jnp.float32)


def column_sum(values):
    return jnp.sum(values.astype(jnp.float32), axis=(0, 1))


def project(active, weight, bias_row):
    model_width = active.shape[-1]
    joined = apply_weight(active, weight)
    queries = (joined[..., :model_width] + bias_row[:model_width]).astype(jnp.bfloat16)
    key_part = joined[..., model_width : 2 * model_width].astype(jnp.bfloat16)
    value_part = (joined[..., 2 * model_width :] + bias_row[model_width:]).astype(jnp.bfloat16)
    return (queries, key_part, value_part)


def split_heads(values):
    return values.reshape(values.shape[0], values.shape[1], HEADS, HEAD_DIM)


def join_heads(values):
    return values.reshape(values.shape[0], values.shape[1], HEADS * HEAD_DIM)


def soft_weights(scores):
    top_score = jnp.max(scores, axis=-1, keepdims=True)
    raised = jnp.exp(scores - top_score)
    return raised / jnp.sum(raised, axis=-1, keepdims=True)


def feature_attend(queries, key_part, value_part):
    score_scale = HEAD_DIM ** (-0.5)
    scores = (
        jnp.einsum(
            "sfhd,sghd->shfg",
            split_heads(queries),
            split_heads(key_part),
            preferred_element_type=jnp.float32,
        )
        * score_scale
    )
    probability = soft_weights(scores)
    mixed = jnp.einsum(
        "shfg,sghd->sfhd",
        probability.astype(jnp.bfloat16),
        split_heads(value_part),
        preferred_element_type=jnp.float32,
    )
    return (join_heads(mixed).astype(jnp.bfloat16), probability)


def feature_grads(queries, key_part, value_part, probability, grad_mixed):
    score_scale = HEAD_DIM ** (-0.5)
    grad_heads = split_heads(grad_mixed)
    grad_weights = jnp.einsum(
        "sfhd,sghd->shfg", grad_heads, split_heads(value_part), preferred_element_type=jnp.float32
    )
    inner_sum = jnp.sum(probability * grad_weights, axis=-1, keepdims=True)
    grad_scores = (probability * (grad_weights - inner_sum)).astype(jnp.bfloat16)
    grad_queries = (
        jnp.einsum(
            "shfg,sghd->sfhd",
            grad_scores,
            split_heads(key_part),
            preferred_element_type=jnp.float32,
        )
        * score_scale
    )
    grad_keys = (
        jnp.einsum(
            "shfg,sfhd->sghd", grad_scores, split_heads(queries), preferred_element_type=jnp.float32
        )
        * score_scale
    )
    grad_values = jnp.einsum(
        "shfg,sfhd->sghd",
        probability.astype(jnp.bfloat16),
        grad_heads,
        preferred_element_type=jnp.float32,
    )
    return (join_heads(grad_queries), join_heads(grad_keys), join_heads(grad_values))


def local_large(
    layer_input,
    segment_ids,
    context_flags,
    first_gain,
    first_shift,
    sample_weight,
    sample_bias,
    sample_mixer,
    sample_offset,
    second_gain,
    second_shift,
    feature_weight,
    feature_bias,
    feature_mixer,
    feature_offset,
    third_gain,
    third_shift,
    expand_weight,
    expand_bias,
    reduce_weight,
    reduce_bias,
    cotangent,
):
    sample_rows = layer_input.shape[0]
    feature_rows = layer_input.shape[1]
    model_width = layer_input.shape[2]
    score_scale = HEAD_DIM ** (-0.5)
    shard_count = lax.axis_size("samp")
    context_shards = shard_count // 8
    total_context = context_shards * sample_rows
    residual_zero = layer_input.astype(jnp.float32)
    normed_one, norm_one_back = jax.vjp(layer_norm, residual_zero, first_gain, first_shift)
    active_one = normed_one.astype(jnp.bfloat16)
    queries_one, keys_one, values_one = project(active_one, sample_weight, sample_bias)
    my_index = lax.axis_index("samp")
    shard_flags = context_flags.reshape(shard_count, sample_rows)[:, 0]
    shard_rank = jnp.cumsum(shard_flags) - 1
    shard_ids = jnp.arange(shard_count, dtype=jnp.int32)
    slot_ids = jnp.arange(context_shards, dtype=jnp.int32)
    root_hits = (shard_rank[None, :] == slot_ids[:, None]) & (shard_flags[None, :] == 1)
    roots = jnp.sum(jnp.where(root_hits, shard_ids[None, :], 0), axis=1)
    context_tasks = jnp.take(segment_ids.reshape(shard_count, sample_rows), roots, axis=0).reshape(
        total_context
    )
    local_tasks = lax.dynamic_slice_in_dim(segment_ids, my_index * sample_rows, sample_rows)
    allowed = local_tasks[:, None] == context_tasks[None, :]
    is_context = shard_flags[my_index] == 1
    own_rank = jnp.maximum(shard_rank[my_index], 0)
    own_block = jnp.concatenate([keys_one, values_one], axis=-1)

    def fetch_rows(step, buffer):
        piece = spread_2(own_block, "samp", roots[step])
        return lax.dynamic_update_slice_in_dim(buffer, piece, step * sample_rows, 0)

    empty_rows = jnp.zeros((total_context, feature_rows, 2 * model_width), jnp.bfloat16)
    fetched = lax.fori_loop(0, context_shards, fetch_rows, empty_rows)
    context_keys = fetched[..., :model_width]
    context_values = fetched[..., model_width:]
    query_heads = split_heads(queries_one)
    key_heads = split_heads(context_keys)
    value_heads = split_heads(context_values)
    scores = (
        jnp.einsum("sfhd,cfhd->fhsc", query_heads, key_heads, preferred_element_type=jnp.float32)
        * score_scale
    )
    sample_prob = soft_weights(jnp.where(allowed[None, None], scores, MASKED))
    sample_weights = sample_prob.astype(jnp.bfloat16)
    mixed_one = join_heads(
        jnp.einsum(
            "fhsc,cfhd->sfhd", sample_weights, value_heads, preferred_element_type=jnp.float32
        )
    ).astype(jnp.bfloat16)
    residual_one = residual_zero + apply_weight(mixed_one, sample_mixer) + sample_offset
    normed_two, norm_two_back = jax.vjp(layer_norm, residual_one, second_gain, second_shift)
    active_two = normed_two.astype(jnp.bfloat16)
    queries_two, keys_two, values_two = project(active_two, feature_weight, feature_bias)
    all_keys, all_values = (
        lax.all_gather(keys_two, "feat", axis=1, tiled=True),
        lax.all_gather(values_two, "feat", axis=1, tiled=True),
    )
    mixed_two, feature_prob = feature_attend(queries_two, all_keys, all_values)
    residual_two = residual_one + apply_weight(mixed_two, feature_mixer) + feature_offset
    normed_three, norm_three_back = jax.vjp(layer_norm, residual_two, third_gain, third_shift)
    active_three = normed_three.astype(jnp.bfloat16)
    expanded = apply_weight(active_three, expand_weight) + expand_bias
    activated, gelu_back = jax.vjp(partial(jax.nn.gelu, approximate=False), expanded)
    hidden = activated.astype(jnp.bfloat16)
    layer_output = (residual_two + apply_weight(hidden, reduce_weight) + reduce_bias).astype(
        jnp.bfloat16
    )
    grad_out = cotangent.astype(jnp.float32)
    grad_branch = cotangent
    reduce_bias_grad = column_sum(grad_branch)
    reduce_weight_grad = weight_grad(hidden, grad_branch)
    grad_hidden = input_back(grad_branch, reduce_weight).astype(jnp.bfloat16)
    grad_expanded = gelu_back(grad_hidden.astype(jnp.float32))[0].astype(jnp.bfloat16)
    expand_bias_grad = column_sum(grad_expanded)
    expand_weight_grad = weight_grad(active_three, grad_expanded)
    grad_norm, third_gain_grad, third_shift_grad = norm_three_back(
        input_back(grad_expanded, expand_weight)
    )
    grad_two = grad_out + grad_norm
    grad_branch = grad_two.astype(jnp.bfloat16)
    feature_offset_grad = column_sum(grad_branch)
    feature_mixer_grad = weight_grad(mixed_two, grad_branch)
    grad_mixed = input_back(grad_branch, feature_mixer).astype(jnp.bfloat16)
    grad_queries, grad_keys, grad_values = feature_grads(
        queries_two, all_keys, all_values, feature_prob, grad_mixed
    )
    own_key_grads, own_value_grads = (
        lax.psum_scatter(grad_keys, "feat", scatter_dimension=1, tiled=True),
        lax.psum_scatter(grad_values, "feat", scatter_dimension=1, tiled=True),
    )
    grad_project = jnp.concatenate(
        [
            grad_queries.astype(jnp.bfloat16),
            own_key_grads.astype(jnp.bfloat16),
            own_value_grads.astype(jnp.bfloat16),
        ],
        axis=-1,
    )
    feature_weight_grad = weight_grad(active_two, grad_project)
    feature_bias_grad = jnp.concatenate(
        [
            column_sum(grad_project[..., :model_width]),
            column_sum(grad_project[..., 2 * model_width :]),
        ]
    )
    grad_norm, second_gain_grad, second_shift_grad = norm_two_back(
        input_back(grad_project, feature_weight)
    )
    grad_one = grad_two + grad_norm
    grad_branch = grad_one.astype(jnp.bfloat16)
    sample_offset_grad = column_sum(grad_branch)
    sample_mixer_grad = weight_grad(mixed_one, grad_branch)
    grad_heads = split_heads(input_back(grad_branch, sample_mixer).astype(jnp.bfloat16))
    grad_weights = jnp.einsum(
        "sfhd,cfhd->fhsc", grad_heads, value_heads, preferred_element_type=jnp.float32
    )
    inner_sum = jnp.sum(sample_prob * grad_weights, axis=-1, keepdims=True)
    grad_scores = (sample_prob * (grad_weights - inner_sum)).astype(jnp.bfloat16)
    grad_queries = (
        join_heads(
            jnp.einsum(
                "fhsc,cfhd->sfhd", grad_scores, key_heads, preferred_element_type=jnp.float32
            )
        )
        * score_scale
    ).astype(jnp.bfloat16)
    key_terms = (
        join_heads(
            jnp.einsum(
                "fhsc,sfhd->cfhd", grad_scores, query_heads, preferred_element_type=jnp.float32
            )
        )
        * score_scale
    )
    value_terms = join_heads(
        jnp.einsum(
            "fhsc,sfhd->cfhd", sample_weights, grad_heads, preferred_element_type=jnp.float32
        )
    )
    term_block = jnp.concatenate([key_terms, value_terms], axis=-1)
    summed_terms = lax.psum_scatter(term_block, "samp", scatter_dimension=0, tiled=True)
    summed_rows = lax.all_gather(summed_terms.astype(jnp.bfloat16), "samp", axis=0, tiled=True)
    own_grads = lax.dynamic_slice_in_dim(summed_rows, own_rank * sample_rows, sample_rows, 0)
    own_grads = jnp.where(is_context, own_grads, jnp.zeros_like(own_grads))
    grad_project = jnp.concatenate([grad_queries, own_grads], axis=-1)
    sample_weight_grad = weight_grad(active_one, grad_project)
    sample_bias_grad = jnp.concatenate(
        [column_sum(grad_queries), column_sum(own_grads[..., model_width:])]
    )
    grad_norm, first_gain_grad, first_shift_grad = norm_one_back(
        input_back(grad_project, sample_weight)
    )
    input_grad = (grad_one + grad_norm).astype(jnp.bfloat16)
    summed = lax.psum(
        (
            first_gain_grad,
            first_shift_grad,
            sample_weight_grad,
            sample_bias_grad,
            sample_mixer_grad,
            sample_offset_grad,
            second_gain_grad,
            second_shift_grad,
            feature_weight_grad,
            feature_bias_grad,
            feature_mixer_grad,
            feature_offset_grad,
            third_gain_grad,
            third_shift_grad,
            expand_weight_grad,
            expand_bias_grad,
            reduce_weight_grad,
            reduce_bias_grad,
        ),
        "feat",
    )
    shares = (
        lax.psum_scatter(summed[0], "samp", scatter_dimension=0, tiled=True),
        lax.psum_scatter(summed[1], "samp", scatter_dimension=0, tiled=True),
        lax.psum_scatter(summed[2], "samp", scatter_dimension=0, tiled=True),
        lax.psum_scatter(summed[3], "samp", scatter_dimension=0, tiled=True),
        lax.psum_scatter(summed[4], "samp", scatter_dimension=0, tiled=True),
        lax.psum_scatter(summed[5], "samp", scatter_dimension=0, tiled=True),
        lax.psum_scatter(summed[6], "samp", scatter_dimension=0, tiled=True),
        lax.psum_scatter(summed[7], "samp", scatter_dimension=0, tiled=True),
        lax.psum_scatter(summed[8], "samp", scatter_dimension=0, tiled=True),
        lax.psum_scatter(summed[9], "samp", scatter_dimension=0, tiled=True),
        lax.psum_scatter(summed[10], "samp", scatter_dimension=0, tiled=True),
        lax.psum_scatter(summed[11], "samp", scatter_dimension=0, tiled=True),
        lax.psum_scatter(summed[12], "samp", scatter_dimension=0, tiled=True),
        lax.psum_scatter(summed[13], "samp", scatter_dimension=0, tiled=True),
        lax.psum_scatter(summed[14], "samp", scatter_dimension=0, tiled=True),
        lax.psum_scatter(summed[15], "samp", scatter_dimension=0, tiled=True),
        lax.psum_scatter(summed[16], "samp", scatter_dimension=0, tiled=True),
        lax.psum_scatter(summed[17], "samp", scatter_dimension=0, tiled=True),
    )
    return (
        layer_output,
        input_grad,
        shares[0],
        shares[1],
        shares[2],
        shares[3],
        shares[4],
        shares[5],
        shares[6],
        shares[7],
        shares[8],
        shares[9],
        shares[10],
        shares[11],
        shares[12],
        shares[13],
        shares[14],
        shares[15],
        shares[16],
        shares[17],
    )


def solution(mesh):
    if mesh.shape["samp"] == 8 and mesh.shape["feat"] == 4:
        return solution_small(mesh)
    return jax.shard_map(
        local_large,
        mesh=mesh,
        in_specs=(
            P("samp", "feat", None),
            P(),
            P(),
            P(),
            P(),
            P(),
            P(),
            P(),
            P(),
            P(),
            P(),
            P(),
            P(),
            P(),
            P(),
            P(),
            P(),
            P(),
            P(),
            P(),
            P(),
            P("samp", "feat", None),
        ),
        out_specs=(
            P("samp", "feat", None),
            P("samp", "feat", None),
            P("samp"),
            P("samp"),
            P("samp", None),
            P("samp"),
            P("samp", None),
            P("samp"),
            P("samp"),
            P("samp"),
            P("samp", None),
            P("samp"),
            P("samp", None),
            P("samp"),
            P("samp"),
            P("samp"),
            P("samp", None),
            P("samp"),
            P("samp", None),
            P("samp"),
        ),
        check_vma=False,
    )


def solution_small(mesh):
    mesh = jax.sharding.Mesh(mesh.devices.reshape(2, 4, 4), ("half", "quad", "feat"))
    tokens, copied = P(SAMP, "feat", None), P()
    vector, matrix = P(SAMP), P(SAMP, None)
    return jax.shard_map(
        local_small,
        mesh=mesh,
        in_specs=(tokens,) + (copied,) * 20 + (tokens,),
        out_specs=(
            tokens, tokens, vector, vector, matrix, vector, matrix, vector,
            vector, vector, matrix, vector, matrix, vector,
            vector, vector, matrix, vector, matrix, vector,
        ),
        check_vma=False,
    )
```

```python
from functools import partial

import jax
import jax.numpy as jnp
from jax import lax
from jax.experimental import pallas as pl
from jax.experimental.pallas import tpu as pltpu
from jax.sharding import PartitionSpec as P

HEADS = 8
HEAD_DIM = 64
EPS = 1e-05
MASKED = -1000000000.0
SCALE = HEAD_DIM ** (-0.5)
QUAD = 4 * HEAD_DIM
BF = jnp.bfloat16
F32 = jnp.float32


def mm(a, b, ca=1, cb=0):
    return lax.dot_general(a, b, (((ca,), (cb,)), ((), ())), preferred_element_type=F32)


def norm_parts(values):
    center = jnp.mean(values, axis=-1, keepdims=True)
    spread = values - center
    variance = jnp.mean(spread * spread, axis=-1, keepdims=True)
    inverse = lax.rsqrt(variance + EPS)
    return spread * inverse, inverse


def norm_back(grad, unit, inverse, gain):
    scaled = grad * gain
    first = jnp.mean(scaled, axis=-1, keepdims=True)
    second = jnp.mean(scaled * unit, axis=-1, keepdims=True)
    return (scaled - first - unit * second) * inverse


def lane_ids(rows):
    return lax.broadcasted_iota(jnp.int32, (rows, 128), 1)


def group_reduce(values, op, fill):
    rows = values.shape[0]
    low = lane_ids(rows) < HEAD_DIM
    outs = []
    for t in range(values.shape[1] // 128):
        tile = values[:, t * 128 : (t + 1) * 128]
        left = op(jnp.where(low, tile, fill), axis=1, keepdims=True)
        right = op(jnp.where(low, fill, tile), axis=1, keepdims=True)
        outs.append(jnp.where(low, left, right))
    return jnp.concatenate(outs, axis=1)


def head_masks(dtype):
    lanes = lax.broadcasted_iota(jnp.int32, (1, QUAD), 1) // HEAD_DIM
    return [jnp.where(lanes == h, 1.0, 0.0).astype(dtype) for h in range(4)]


def stack_heads(part, masks):
    return jnp.concatenate([part * m for m in masks], axis=0)


def pick_heads(stacked, masks):
    rows = stacked.shape[0] // 4
    total = stacked[:rows] * masks[0]
    for h in range(1, 4):
        total = total + stacked[h * rows : (h + 1) * rows] * masks[h]
    return total


def attend(q, k, v, masks, allow):
    outs, probs = [], []
    for quad in range(2):
        cols = slice(quad * QUAD, (quad + 1) * QUAD)
        scores = mm(q[:, cols], stack_heads(k[:, cols], masks), 1, 1)
        if allow is not None:
            scores = jnp.where(allow, scores, MASKED)
        raised = jnp.exp(scores - group_reduce(scores, jnp.max, -jnp.inf))
        prob = raised / group_reduce(raised, jnp.sum, 0.0)
        outs.append(mm(prob.astype(BF), stack_heads(v[:, cols], masks)))
        probs.append(prob)
    return jnp.concatenate(outs, axis=1), jnp.concatenate(probs, axis=1)


def attend_back(q, k, v, prob, grad, masks, masks32):
    dqs, dks, dvs = [], [], []
    for quad in range(2):
        cols = slice(quad * QUAD, (quad + 1) * QUAD)
        p, g = prob[:, cols], grad[:, cols]
        back = mm(g, stack_heads(v[:, cols], masks), 1, 1)
        inner = group_reduce(p * back, jnp.sum, 0.0)
        gs = (p * (back - inner)).astype(BF)
        dqs.append(mm(gs, stack_heads(k[:, cols], masks)) * SCALE)
        dks.append(pick_heads(mm(gs, q[:, cols], 0, 0), masks32))
        dvs.append(pick_heads(mm(p.astype(BF), g, 0, 0), masks32))
    join = lambda parts: jnp.concatenate(parts, axis=1).astype(BF)
    return join(dqs), join(dks), join(dvs)


def swap_matrix(rows=16):
    n = rows * 16
    r = lax.broadcasted_iota(jnp.int32, (n, n), 0)
    c = lax.broadcasted_iota(jnp.int32, (n, n), 1)
    return jnp.where((r // rows == c % 16) & (r % rows == c // 16), 1.0, 0.0).astype(BF)


def swap(matrix, values, back=False):
    return mm(matrix, values, 0 if back else 1, 0).astype(BF)


def gelu_parts(u):
    cdf = 0.5 * (1.0 + lax.erf(u * (2.0**-0.5)))
    density = jnp.exp(u * u * -0.5) * 0.3989422804014327
    return cdf, density


def col_sum(values):
    return jnp.sum(values.astype(F32), axis=0, keepdims=True)


def turn_in(x_ref, out_ref):
    matrix = swap_matrix()
    for d in range(4):
        rows = x_ref[d * 256 : (d + 1) * 256]
        out_ref[:, d] = swap(matrix, rows).reshape(16, 16, 512)


def turn_out(got_ref, out_ref):
    matrix = swap_matrix()
    for d in range(4):
        out_ref[d * 256 : (d + 1) * 256] = swap(matrix, got_ref[:, d].reshape(256, 512))


def project_queries(x_ref, gain_ref, shift_ref, w_ref, b_ref, act_ref, q_ref):
    unit, _ = norm_parts(x_ref[:, 0].reshape(256, 512).astype(F32))
    act = (unit * gain_ref[...] + shift_ref[...]).astype(BF)
    act_ref[0] = act
    q = (mm(act, w_ref[:, :512]) + b_ref[:, :512]).astype(BF)
    q_ref[0] = q * jnp.asarray(SCALE, BF)


def forward_one(
    me_ref, q_ref, own_ref, got_ref, x_ref, tasks_ref, context_ref, gain_ref, shift_ref, w_ref,
    b_ref, wm_ref, off_ref,
    r_ref, o_ref, c_ref, cact_ref, k_ref, v_ref, p_ref,
):
    here = me_ref[1] == me_ref[2]
    masks = head_masks(BF)
    allow = tasks_ref[...] == context_ref[...]

    @pl.when(here)
    def _():
        c_ref[...] = own_ref[...]

    @pl.when(jnp.logical_not(here))
    def _():
        c_ref[...] = got_ref[...]

    for e in range(c_ref.shape[0]):
        unit, _ = norm_parts(c_ref[e].astype(F32))
        act = (unit * gain_ref[...] + shift_ref[...]).astype(BF)
        cact_ref[e] = act
        kv = mm(act, w_ref[:, 512:])
        k_ref[e] = kv[:, :512].astype(BF)
        v_ref[e] = (kv[:, 512:] + b_ref[:, 512:]).astype(BF)
    for e in range(c_ref.shape[0]):
        out, prob = attend(q_ref[e], k_ref[e], v_ref[e], masks, allow)
        o_ref[e] = out.astype(BF)
        p_ref[e] = prob
    for e in range(c_ref.shape[0]):
        r1 = x_ref[:, e].reshape(256, 512).astype(F32) + mm(o_ref[e], wm_ref[...]) + off_ref[...]
        r_ref[:, :, e] = r1.astype(BF).reshape(4, 4, 16, 512)


HALF = 512


def middle(me_ref, *refs):
    (
        r1_ref, c0, c1, c2, c3, g2_ref, s2_ref, bf_ref, off2_ref, g3_ref, s3_ref, be_ref, br_ref,
    ) = refs[:13]
    weights_hbm = refs[13:17]
    gb1_ref, vec_ref, bias_ref, out0, out1, out2, out3 = refs[17:24]
    targets = refs[24:28]
    wf_ref, wm2_ref, we_ref, wr_ref = refs[28:32]
    kept = refs[32:40]
    (
        r_scr, g_scr, q_scr, k_scr, v_scr, p_scr, e_scr, gs_scr, go_scr, out_scr, back_scr,
        part_p, part_q, turn, in_sems, out_sems,
    ) = refs[40:]
    me, step = me_ref[0], pl.program_id(0)
    tokens = pl.ds(pl.multiple_of(step * HALF, HALF), HALF)
    a2_ref, dqkv_ref, o2_ref, gb2_ref, a3_ref, gu_ref, hid_ref, gb3_ref = (
        ref.at[tokens] for ref in kept
    )
    loads = [
        pltpu.make_async_copy(source, target, in_sems.at[i])
        for i, (source, target) in enumerate(zip(weights_hbm, refs[28:32]))
    ]

    def first(make):
        pl.when(step == 0)(make)

    matrix = swap_matrix()
    masks, masks32 = head_masks(BF), head_masks(F32)

    @first
    def _():
        loads[0].start()
        loads[1].start()
        for f in range(4):
            r_scr[f] = swap(matrix, r1_ref[:, f].reshape(256, 512))

    now = pl.ds(pl.multiple_of(step * 128, 128), 128)

    def gather(*refs):
        return jnp.concatenate(
            [ref[s * 16 : (s + 1) * 16] for s in range(8) for ref in refs], axis=0
        )

    def scatter(values, *refs):
        for s in range(8):
            for d, ref in enumerate(refs):
                at = (s * 4 + d) * 16
                ref[s * 16 : (s + 1) * 16] = values[at : at + 16]

    def each_sample(body):
        def step(i, carry):
            for j in range(SAMPLE_UNROLL):
                rows = pl.ds(pl.multiple_of((i * SAMPLE_UNROLL + j) * 64, 64), 64)
                for quad in range(2):
                    body(rows, slice(quad * QUAD, (quad + 1) * QUAD))
            return carry

        lax.fori_loop(0, 8 // SAMPLE_UNROLL, step, 0)

    gb3_ref[...] = gather(c0, c1, c2, c3)
    r1 = gather(*(r_scr.at[d ^ me, now] for d in range(4))).astype(F32)
    unit2, inv2 = norm_parts(r1)
    a2_ref[...] = (unit2 * g2_ref[...] + s2_ref[...]).astype(BF)

    @first
    def _():
        loads[0].wait()
        loads[2].start()
        loads[3].start()

    q = (mm(a2_ref[...], wf_ref[:, :512]) + bf_ref[:, :512]).astype(BF)
    q_scr[...] = q * jnp.asarray(SCALE, BF)
    k_scr[...] = mm(a2_ref[...], wf_ref[:, 512:1024]).astype(BF)
    v_scr[...] = (mm(a2_ref[...], wf_ref[:, 1024:]) + bf_ref[:, 512:]).astype(BF)

    def score(rows, cols):
        p_scr[rows, cols] = mm(q_scr[rows, cols], stack_heads(k_scr[rows, cols], masks), 1, 1)

    each_sample(score)
    for i in range(4):
        rows = slice(i * 128, (i + 1) * 128)
        scores = p_scr[rows]
        raised = jnp.exp(scores - group_reduce(scores, jnp.max, -jnp.inf))
        p_scr[rows] = raised / group_reduce(raised, jnp.sum, 0.0)

    def mix(rows, cols):
        o2_ref[rows, cols] = mm(
            p_scr[rows, cols].astype(BF), stack_heads(v_scr[rows, cols], masks)
        ).astype(BF)

    each_sample(mix)
    first(loads[1].wait)
    r2 = r1 + mm(o2_ref[...], wm2_ref[...]) + off2_ref[...]
    unit3, inv3 = norm_parts(r2)
    a3_ref[...] = (unit3 * g3_ref[...] + s3_ref[...]).astype(BF)
    first(loads[2].wait)
    first(loads[3].wait)

    @first
    def _():
        vec_ref[...] = jnp.zeros((8, 512), F32)
        bias_ref[...] = jnp.zeros((1, 2048), F32)

    out_scr[...] = r2 + br_ref[...]
    back_scr[...] = jnp.zeros((HALF, 512), F32)

    def expand(b, carry):
        cols = pl.ds(pl.multiple_of(b * WIDE, WIDE), WIDE)
        u = mm(a3_ref[...], we_ref[:, cols]) + be_ref[:, cols]
        cdf, density = gelu_parts(u)
        hidden = (u * cdf).astype(BF)
        hid_ref[:, cols] = hidden
        gh = mm(gb3_ref[...], wr_ref[cols, :], 1, 1).astype(BF).astype(F32)
        gu = (gh * (cdf + u * density)).astype(BF)
        gu_ref[:, cols] = gu
        bias_ref[:, cols] += col_sum(gu)
        out_scr[...] += mm(hidden, wr_ref[cols, :])
        back_scr[...] += mm(gu, we_ref[:, cols], 1, 1)
        return carry

    lax.fori_loop(0, 2048 // WIDE, expand, 0, unroll=EXPAND_UNROLL)
    scatter(out_scr[...].astype(BF), out0, out1, out2, out3)
    back, cot = back_scr[...], gb3_ref[...]
    vecs = [col_sum(back * unit3), col_sum(back)]
    gr2 = cot.astype(F32) + norm_back(back, unit3, inv3, g3_ref[...])
    gb2_ref[...] = gr2.astype(BF)
    go_scr[...] = mm(gb2_ref[...], wm2_ref[...], 1, 1).astype(BF)

    def weigh(rows, cols):
        e_scr[rows, cols] = mm(go_scr[rows, cols], stack_heads(v_scr[rows, cols], masks), 1, 1)

    each_sample(weigh)
    for i in range(4):
        rows = slice(i * 128, (i + 1) * 128)
        prob, grad = p_scr[rows], e_scr[rows]
        inner = group_reduce(prob * grad, jnp.sum, 0.0)
        gs_scr[rows] = (prob * (grad - inner)).astype(BF)

    def spread(rows, cols):
        gs, at = gs_scr[rows, cols], cols.start
        dq = mm(gs, stack_heads(k_scr[rows, cols], masks)) * SCALE
        dqkv_ref[rows, at : at + QUAD] = dq.astype(BF)
        dk = pick_heads(mm(gs, q_scr[rows, cols], 0, 0), masks32)
        dqkv_ref[rows, 512 + at : 512 + at + QUAD] = dk.astype(BF)
        dv = pick_heads(mm(p_scr[rows, cols].astype(BF), go_scr[rows, cols], 0, 0), masks32)
        dqkv_ref[rows, 1024 + at : 1024 + at + QUAD] = dv.astype(BF)

    each_sample(spread)
    dqkv = dqkv_ref[...]
    back = mm(dqkv, wf_ref[...], 1, 1)
    vecs += [col_sum(back * unit2), col_sum(back)]
    gr1 = gr2 + norm_back(back, unit2, inv2, g2_ref[...])
    scatter(gr1.astype(BF), *(g_scr.at[d ^ me, now] for d in range(4)))
    vecs += [
        col_sum(gb2_ref[...]), col_sum(cot), col_sum(dqkv[:, :512]), col_sum(dqkv[:, 1024:])
    ]
    vec_ref[...] += jnp.concatenate(vecs, axis=0)

    @pl.when(step == 1)
    def _():
        for f in range(4):
            gb1_ref[:, f] = swap(matrix, g_scr[f]).reshape(4, 4, 16, 512)
        grads_middle(me_ref, kept, (part_p, part_q), turn, targets, out_sems)


SAMPLE_UNROLL = 8
EXPAND_UNROLL = True
WIDE = 512


def backward_one(
    me_ref, g_ref, o_ref, act_ref, cact_ref, x_ref, c_ref, q_ref, k_ref, v_ref,
    p_ref, w_ref, wm_ref,
    gb1_ref, a_ref, term_ref, vec_ref, keep_ref, send_ref,
    dq_scr, dkv_scr, g_scr,
):
    masks, masks32 = head_masks(BF), head_masks(F32)

    @pl.when(pl.program_id(0) == 0)
    def _():
        vec_ref[...] = jnp.zeros((8, 512), F32)

    step, per = pl.program_id(0), q_ref.shape[0]
    for e in range(per):
        gb1 = g_ref[:, :, e].reshape(256, 512)
        gb1_ref[e] = gb1
        go = mm(gb1, wm_ref[...], 1, 1).astype(BF)
        dq, dk, dv = attend_back(q_ref[e], k_ref[e], v_ref[e], p_ref[e], go, masks, masks32)
        dkv = jnp.concatenate([dk, dv], axis=1)
        at = step * per + e
        rows = pl.ds(pl.multiple_of(at * 256, 256), 256)
        dq_scr[rows], g_scr[rows] = dq, gb1
        dkv_scr[pl.ds(pl.multiple_of(at * 64, 64), 64)] = dkv
        back = mm(dq, w_ref[:, :512], 1, 1)
        a_ref[e] = back
        term = mm(dkv, w_ref[:, 512:], 1, 1)
        term_ref[e] = term.astype(BF)
        unit, _ = norm_parts(x_ref[:, e].reshape(256, 512).astype(F32))
        unit_c, _ = norm_parts(c_ref[e].astype(F32))
        zero = jnp.zeros((3, 512), F32)
        vec_ref[...] += jnp.concatenate(
            [
                col_sum(back * unit) + col_sum(term * unit_c), col_sum(back) + col_sum(term),
                col_sum(gb1), col_sum(dq), col_sum(dv), zero,
            ],
            axis=0,
        )

    @pl.when(step == pl.num_programs(0) - 1)
    def _():
        whole_rows = lambda ref: ref[...].reshape(-1, 512)
        act_c = whole_rows(cact_ref)
        terms = (
            (whole_rows(act_ref), dq_scr[...]), (act_c, dkv_scr[:, :512]),
            (act_c, dkv_scr[:, 512:]), (whole_rows(o_ref), g_scr[...]),
        )
        for unit, (left, right) in enumerate(terms):
            place_sample(me_ref, mm(left, right, 0, 0).astype(BF), unit, keep_ref, send_ref)


def backward_input(me_ref, gb1_ref, x_ref, a_ref, term_ref, got_ref, gain_ref, grad_ref, a_scr):
    here, quad = me_ref[1] == me_ref[2], me_ref[3]
    unit, inverse = norm_parts(x_ref[:, 0].reshape(256, 512).astype(F32))
    a_scr[...] = a_ref[0].reshape(4, 64, 512)

    @pl.when(here)
    def _():
        a_scr[quad] += term_ref[0].astype(F32) + got_ref[0].astype(F32)

    back = a_scr[...].reshape(256, 512)
    grad = gb1_ref[0].astype(F32) + norm_back(back, unit, inverse, gain_ref[...])
    grad_ref[:, 0] = grad.astype(BF).reshape(4, 64, 512)


VECTORS = (64,) * 6 + (128, 256, 128) + (64,) * 3


def finale(early_ref, last_ref, fw_ref, fm_ref, ew_ref, rw_ref, sw_ref, sm_ref, *vector_refs):
    for unit, feat in enumerate((0, 2, 1, 3)):
        cols = slice(unit * 512, (unit + 1) * 512)
        feature, sample = early_ref[feat, 0:64].astype(F32), last_ref[feat, 0:64].astype(F32)
        if unit < 3:
            fw_ref[:, cols], sw_ref[:, cols] = feature, sample
        else:
            fm_ref[...], sm_ref[...] = feature, sample
        ew_ref[:, cols] = early_ref[feat, 64:128].astype(F32)
        rw_ref[unit * 64 : unit * 64 + 64] = early_ref[feat, 128:192].astype(F32)
    planes = last_ref[:, 64:88].astype(F32)
    total = (planes[0] + planes[1]) + (planes[2] + planes[3])
    total = total[0:8] + total[8:16] + total[16:24]
    start = 0
    for size, ref in zip(VECTORS, vector_refs):
        row, at = start // 512, start % 512
        ref[...] = total[row : row + 1, at : at + size]
        start += size


def split(got_ref, out_ref):
    rest = got_ref[...]
    for i in range(3):
        term = rest.astype(BF)
        out_ref[i * 8 : (i + 1) * 8] = term
        rest = rest - term.astype(F32)


def place(me_ref, b0, b1, b2, b3, out_ref):
    for d, ref in enumerate((b0, b1, b2, b3)):
        out_ref[d ^ me_ref[0]] = ref[...]


def piece_index(me_ref, unit, shard, order):
    core, xx, yy, zz = me_ref[4], me_ref[5], me_ref[6], me_ref[7]
    other_z = (shard >> 1) ^ zz
    bit = {
        "x": (unit & 1) ^ xx, "y": (shard & 1) ^ yy, "z": other_z & 1, "w": other_z >> 1,
    }
    index = sum(bit[name] * weight for name, weight in zip(order, (8, 4, 2, 1)))
    return (unit >> 1) ^ core, index


def grads_middle(me_ref, kept, staged, turn, targets, out_sems):
    act2, dqkv, o2, gb2, act3, gu, hid, gb3 = kept
    stores = []

    def put(part):
        for i in range(2):
            source = staged[part].at[pl.ds(16 * i, 16)]
            place = 2 * part + i
            stores.append(pltpu.make_async_copy(source, targets[place], out_sems.at[place]))
            stores[-1].start()

    def loop(count, body):
        lax.fori_loop(0, count, lambda n, carry: (body(n), carry)[1], 0)

    block = lambda n: pl.ds(pl.multiple_of(n * 512, 512), 512)

    def place_piece(part, value, unit, shard, rows):
        send, index = piece_index(me_ref, unit, shard, ("xyzw", "yxzw")[part])
        staged[part][send * 16 + index, rows] = value

    def place_unit(part, value, unit):
        for shard in range(8):
            place_piece(part, value[shard * 64 : (shard + 1) * 64], unit, shard, slice(0, 64))

    def from_hidden(n):
        piece = mm(hid[:, block(n)], gb3[...], 0, 0).astype(BF)
        for i in range(8):
            rows = piece[i * 64 : (i + 1) * 64]
            place_piece(1, rows, i % 4, 2 * n + i // 4, slice(64, 128))

    loop(4, from_hidden)
    turn[...] = act3[...].T

    def from_expand(n):
        place_unit(1, mm(turn[...], gu[:, block(n)]).astype(BF), n)

    loop(4, from_expand)
    put(1)
    turn[...] = act2[...].T

    def from_feature(n):
        place_unit(0, mm(turn[...], dqkv[:, block(n)]).astype(BF), n)

    loop(3, from_feature)
    place_unit(0, mm(o2[...], gb2[...], 0, 0).astype(BF), 3)
    put(0)
    for store in stores:
        store.wait()


def place_sample(me_ref, value, unit, keep_ref, send_ref):
    for which, order in enumerate(("xyzw", "yxzw")):
        for shard in range(8):
            at = shard * 64 + which * 32
            send, index = piece_index(me_ref, unit, shard, order)

            @pl.when(send == 0)
            def _(at=at, index=index):
                keep_ref[which, index] = value[at : at + 32]

            @pl.when(send == 1)
            def _(at=at, index=index):
                send_ref[which, index] = value[at : at + 32]


def spec(shape, index=None):
    return pl.BlockSpec(shape, index if index is not None else (lambda *a: (0,) * len(shape)))


def sds(shape, dtype=BF):
    return jax.ShapeDtypeStruct(shape, dtype)


def big(shape, dtype=BF):
    return pltpu.HBM(shape, dtype)


def outside(array):
    if array.size * array.dtype.itemsize < 1 << 18:
        return array
    return pltpu.with_memory_space_constraint(array, pltpu.HBM)


def params(limit):
    return pltpu.CompilerParams(vmem_limit_bytes=limit << 20)


def row(vector):
    return vector.reshape(1, -1)


def cost(microseconds):
    return pl.CostEstimate(
        flops=int(microseconds * 1.1e9), transcendentals=0, bytes_accessed=int(microseconds * 2e6)
    )


def whole_block(out):
    shape = out.shape
    return pl.BlockSpec(shape, lambda i: (0,) * len(shape))


def moving_block(shape, axis, per):
    block = tuple(per if i == axis else n for i, n in enumerate(shape))
    return pl.BlockSpec(block, lambda i: tuple(i if j == axis else 0 for j in range(len(shape))))


def by_feature(kernel, name, limit, outs, scratch, *inputs, time=3, per=1):
    arrays, specs = [], []
    for entry in inputs:
        array, axis = entry if isinstance(entry, tuple) else (entry, None)
        if array.ndim == 1:
            arrays.append(array)
            specs.append(pl.BlockSpec(memory_space=pltpu.SMEM))
            continue
        arrays.append(outside(array))
        specs.append(
            whole_block(array) if axis is None else moving_block(array.shape, axis, per)
        )
    return pl.pallas_call(
        kernel,
        grid=(4 // per,),
        out_shape=tuple(out for out, _ in outs),
        in_specs=specs,
        out_specs=[
            whole_block(out) if axis is None else moving_block(out.shape, axis, per)
            for out, axis in outs
        ],
        scratch_shapes=scratch,
        compiler_params=params(limit),
        cost_estimate=cost(time),
        name=name,
    )(*arrays)


def whole(kernel, name, limit, outs, scratch, *inputs, steps=1, time=3):
    arrays, specs = [], []
    for entry in inputs:
        if not isinstance(entry, tuple) and entry.ndim == 1:
            arrays.append(entry)
            specs.append(pl.BlockSpec(memory_space=pltpu.SMEM))
            continue
        array, block, index = entry if isinstance(entry, tuple) else (entry, None, None)
        arrays.append(outside(array))
        block = array.shape if block is None else block
        index = (0,) * array.ndim if index is None else index
        if not callable(index):
            index = lambda i, index=index: index
        specs.append(pl.BlockSpec(block, index))
    return pl.pallas_call(
        kernel,
        grid=(steps,),
        out_shape=outs,
        in_specs=specs,
        out_specs=jax.tree.map(whole_block, outs, is_leaf=lambda o: hasattr(o, "dtype")),
        scratch_shapes=scratch,
        compiler_params=params(limit),
        cost_estimate=cost(time),
        name=name,
    )(*arrays)


def shuffle(value, axis, mask):
    size = lax.axis_size(axis)
    return lax.ppermute(value, axis, [(i, i ^ mask) for i in range(size)])


SAMP = ("half", "quad")
CORE, X, Y, Z, W = ("feat", 1), ("feat", 2), ("quad", 1), ("quad", 2), ("half", 1)


def at(stacked, index, axis=0):
    return lax.dynamic_index_in_dim(stacked, index, axis, keepdims=False)


def fence(tree):
    return lax.optimization_barrier(tree)


def plus(a, b):
    return (a.astype(F32) + b.astype(F32)).astype(BF)


class Chain:
    def __init__(self, keep, sent, dims):
        self.keep, self.sent, self.dims = keep, sent, (CORE,) + dims

    def start(self):
        return shuffle(self.sent, *self.dims[0])

    def take(self, got):
        self.dims = self.dims[1:]
        if self.dims:
            self.keep, self.sent = plus(self.keep[0], got[0]), plus(self.keep[1], got[1])
        else:
            self.keep = plus(self.keep, got)


def together(chains, make=lambda: ()):
    got = [chain.start() for chain in chains]
    got, other = fence((got, make()))
    for chain, value in zip(chains, got):
        chain.take(value)
    return other


def local_small(
    layer_input, segment_ids, context_flags,
    first_gain, first_shift, sample_weight, sample_bias, sample_mixer, sample_offset,
    second_gain, second_shift, feature_weight, feature_bias, feature_mixer, feature_offset,
    third_gain, third_shift, expand_weight, expand_bias, reduce_weight, reduce_bias, cotangent,
):
    half, quad, feat = (lax.axis_index(name) for name in ("half", "quad", "feat"))
    samp = half * 4 + quad
    core, xx = feat % 2, feat // 2
    flags = context_flags.reshape(8, 64)[:, 0]
    root = jnp.sum(jnp.where(flags == 1, jnp.arange(8, dtype=jnp.int32), 0))
    me = [feat, half, root // 4, root % 4, core, xx, samp % 2, samp // 2]
    me = jnp.stack(me).astype(jnp.int32)

    turned = whole(turn_in, "turn_in", 8, big((16, 4, 16, 512)), [], layer_input.reshape(1024, 512))
    turned, cotangent = fence((turned, cotangent))
    x_t = lax.all_to_all(turned.reshape(4, 4, 64, 512), "quad", 0, 0)
    cot4 = cotangent.reshape(4, 256, 512)
    block = lambda value, d: at(value, feat ^ d)
    from_core = shuffle(jnp.stack([block(cot4, 1), block(cot4, 3)]), *CORE)
    cot_far = shuffle(jnp.stack([block(cot4, 2), from_core[1]]), *X)
    x_t, from_core, cot_far = fence((x_t, from_core, cot_far))
    own_context = at(x_t, root % 4)
    got_context = shuffle(own_context, *W)
    full = big((4, 256, 512))
    act1, queries = by_feature(
        project_queries, "project_queries", 12, ((full, 0), (full, 0)), [],
        (x_t, 1), row(first_gain), row(first_shift), sample_weight, row(sample_bias),
    )
    got_context, q1 = fence((got_context, queries))

    tasks = segment_ids.reshape(8, 64)
    context_tasks = jnp.concatenate([at(tasks, root)] * 4).reshape(1, 256)
    sent = big((4, 4, 4, 16, 512))
    four = big((4, 64, 512))
    r1, o1, context, cact, k1, v1, p1 = by_feature(
        forward_one, "forward_one", 20,
        (
            (sent, 2), (full, 0), (four, 0), (four, 0), (four, 0), (four, 0),
            (big((4, 256, 512), F32), 0),
        ),
        [],
        me, (q1, 0), (own_context, 0), (got_context, 0), (x_t, 1),
        at(segment_ids.reshape(2, 256, 1), half), context_tasks,
        row(first_gain), row(first_shift), sample_weight, row(sample_bias), sample_mixer,
        row(sample_offset), time=7, per=4,
    )

    def exchange(value):
        shape = value.shape
        value = value.reshape((16,) + shape[2:])
        return lax.all_to_all(value, ("quad", "feat"), 0, 0).reshape(shape)

    rows_in = [
        row(v)
        for v in (
            second_gain, second_shift, feature_bias, feature_offset, third_gain,
            third_shift, expand_bias, reduce_bias,
        )
    ]
    weights = [feature_weight, feature_mixer, expand_weight, reduce_weight]

    own = spec((None, 128, 512), lambda i, m: (m[0], i, 0))
    part = lambda n: spec((None, 128, 512), lambda i, m: (n, i, 0))
    still = lambda shape: spec(shape, lambda i, m: (0,) * len(shape))
    block = spec((128, 512), lambda i, m: (i, 0))
    far = pl.BlockSpec(memory_space=pl.ANY)
    vmem = lambda shape, dtype=BF: pltpu.VMEM(shape, dtype)
    rows, rows32 = vmem((HALF, 512)), vmem((HALF, 512), F32)
    outs = (sent, sds((8, 512), F32), sds((1, 2048), F32))
    gb1_f, vec2, bias2, out0, out1, out2, out3, *grads = pl.pallas_call(
        middle,
        grid_spec=pltpu.PrefetchScalarGridSpec(
            num_scalar_prefetch=1,
            grid=(2,),
            in_specs=[
                pl.BlockSpec(sent.shape, lambda i, m: (0,) * 5, pipeline_mode=pl.Buffered(1)),
                own, part(0), part(0), part(1),
            ]
            + [still(r.shape) for r in rows_in]
            + [far] * 4,
            out_specs=[still(o.shape) for o in outs] + [block] * 4 + [far] * 4,
            scratch_shapes=[vmem(w.shape) for w in weights]
            + [vmem((1024, n)) for n in (512, 1536, 512, 512, 512, 2048, 2048, 512)]
            + [
                vmem((4, 256, 512)), vmem((4, 256, 512)), rows, rows, rows, rows32, rows32, rows,
                rows, rows32, rows32, vmem((32, 64, 512)), vmem((32, 128, 512)), vmem((512, 1024)),
                pltpu.SemaphoreType.DMA((4,)), pltpu.SemaphoreType.DMA((4,)),
            ],
        ),
        out_shape=outs + (big((256, 512)),) * 4 + (sds((16, 64, 512)),) * 2 + (sds((16, 128, 512)),) * 2,
        compiler_params=params(58),
        cost_estimate=cost(45),
        name="middle",
    )(
        me,
        *(
            outside(array)
            for array in (exchange(r1), cot4, from_core, cot_far, cot_far, *rows_in, *weights)
        ),
    )

    gb_t = exchange(gb1_f)
    outs = [shuffle(out, "feat", d + 1) for d, out in enumerate((out1, out2, out3))]
    pk, ps, qk, qs = (g.reshape(2, 2, 2, 2, -1, 512) for g in grads)
    p_chain, q_chain = Chain(pk, ps, (X, Y)), Chain(qk, qs, (Y, X))
    chains = [p_chain, q_chain]
    for chain in chains:
        chain.take(chain.start())

    half_rows = sds((2, 16, 32, 512))
    for chain in chains:
        chain.take(chain.start())
    gb1, back, term, vec1, keep_ab, send_ab = (
        lambda: by_feature(
            backward_one, "backward_one", 32,
            (
                (full, 0), (big((4, 256, 512), F32), 0), (four, 0), (sds((8, 512), F32), None),
                (half_rows, None), (half_rows, None),
            ),
            [pltpu.VMEM((1024, 512), BF), pltpu.VMEM((256, 1024), BF), pltpu.VMEM((1024, 512), BF)],
            me, (gb_t, 2), o1, act1, cact, (x_t, 1),
            (context, 0), (q1, 0), (k1, 0), (v1, 0), (p1, 0), sample_weight, sample_mixer,
            time=12, per=2,
        )
    )()

    gb1, back, term, vec1, keep_ab, send_ab, outs = fence(
        (gb1, back, term, vec1, keep_ab, send_ab, outs)
    )

    owned = lambda v, n: v.reshape(-1, 8, n).transpose(1, 0, 2).reshape(8, -1)
    vectors = jnp.concatenate(
        [
            owned(vec2[:6], 64), vec2[6:].reshape(8, 128), bias2.reshape(8, 256),
            vec1[3:5].reshape(8, 128), owned(vec1[:3], 64),
        ],
        axis=1,
    )
    got_term = shuffle(term, *W)
    vectors = vectors.reshape(2, 2, 2, 1088)
    got_term, got_ab, v = together(
        chains,
        lambda: (
            got_term, shuffle(send_ab, *CORE), shuffle(at(vectors, 1 - samp % 2, 2), *Y)
        ),
    )
    vectors = at(vectors, samp % 2, 2) + v
    bits = lambda a: a.reshape(2, 2, 2, 2, 2, 32, 512)
    keep_ab, got_ab = bits(keep_ab), bits(got_ab)
    late = []
    for which, dims in enumerate(((X, Y), (Y, X))):
        pair = [plus(keep_ab[which, i], got_ab[which, i]) for i in range(2)]
        late.append(Chain(*pair, ()))
        late[-1].dims = dims
    around_z = lambda value, mask: lax.ppermute(value, SAMP, [(j, j ^ mask) for j in range(8)])

    def to_owner(rows):
        return [around_z(rows[i // 2, i % 2], (0, 4, 2, 6)[i]) for i in (1, 2, 3)]

    def add_up(rows, got):
        total = rows[0, 0].astype(F32)
        for value in got:
            total = total + value.astype(F32)
        return total.astype(BF)

    both = [jnp.concatenate([chain.keep[i] for chain in chains], axis=-2) for i in range(2)]
    both_chain = Chain(*both, ())
    both_chain.dims = (Z, W)
    (grad_t,) = together(
        late + [both_chain],
        lambda: (
            by_feature(
                backward_input, "backward_input", 16, ((big((4, 4, 64, 512)), 1),),
                [pltpu.VMEM((4, 64, 512), F32)],
                me, (gb1, 0), (x_t, 1), (back, 0), (term, 0), (got_term, 0), row(first_gain),
            )
        ),
    )
    both_chain.take(both_chain.start())
    low = samp // 2 % 2
    layer_output = whole(
        place, "place", 16, sds((4, 256, 512)), [], me, out0, *outs
    ).reshape(64, 16, 512)
    early = lax.all_gather(both_chain.keep, "feat")
    got, v, layer_output, early = together(
        late,
        lambda: (
            lax.all_to_all(grad_t, "quad", 0, 0),
            shuffle(at(vectors, 1 - low, 1), *Z),
            layer_output,
            early,
        ),
    )
    vectors = at(vectors, low, 1) + v
    input_grad = whole(
        turn_out, "turn_out", 8, sds((1024, 512)), [], got.reshape(16, 4, 16, 512)
    ).reshape(64, 16, 512)

    rows = jnp.concatenate([chain.keep for chain in late], axis=2)
    from_z, v, input_grad = fence(
        (to_owner(rows), shuffle(at(vectors, 1 - half), *W), input_grad)
    )
    vectors = jnp.pad((at(vectors, half) + v).reshape(-1), (0, 8 * 512 - 1088)).reshape(8, 512)
    vectors = whole(split, "split", 8, sds((24, 512)), [], vectors)
    total = add_up(rows, from_z)
    last = lax.all_gather(jnp.concatenate([total, vectors]), "feat")
    matrices = ((64, 1536), (64, 512), (64, 2048), (256, 512), (64, 1536), (64, 512))
    feature_w, feature_m, expand_w, reduce_w, sample_w, sample_m, *mine = whole(
        finale, "finale", 12,
        tuple(sds(shape, F32) for shape in matrices + tuple((1, n) for n in VECTORS)), [],
        early, last,
    )
    mine = [v.reshape(-1) for v in mine]
    gain3, shift3, gain2, shift2, off2, bias_r, feature_b, expand_b = mine[:8]
    sample_b, gain1, shift1, off1 = mine[8:]
    return (
        layer_output, input_grad,
        gain1, shift1, sample_w, sample_b, sample_m, off1,
        gain2, shift2, feature_w, feature_b, feature_m, off2,
        gain3, shift3, expand_w, expand_b, reduce_w, bias_r,
    )


def spread_2(block, axis, owner):
    block = jnp.where(lax.axis_index(axis) == owner, block, jnp.zeros_like(block))
    return lax.psum(block, axis)


def layer_norm(values, gain_row, shift_row):
    center = jnp.mean(values, axis=-1, keepdims=True)
    spread = values - center
    variance = jnp.mean(spread * spread, axis=-1, keepdims=True)
    return spread * lax.rsqrt(variance + EPS) * gain_row + shift_row


def apply_weight(active, weight):
    return jnp.einsum("sfd,de->sfe", active, weight, preferred_element_type=jnp.float32)


def input_back(grad_out, weight):
    return jnp.einsum("sfe,de->sfd", grad_out, weight, preferred_element_type=jnp.float32)


def weight_grad(active, grad_out):
    return jnp.einsum("sfd,sfe->de", active, grad_out, preferred_element_type=jnp.float32)


def column_sum(values):
    return jnp.sum(values.astype(jnp.float32), axis=(0, 1))


def project(active, weight, bias_row):
    model_width = active.shape[-1]
    joined = apply_weight(active, weight)
    queries = (joined[..., :model_width] + bias_row[:model_width]).astype(jnp.bfloat16)
    key_part = joined[..., model_width : 2 * model_width].astype(jnp.bfloat16)
    value_part = (joined[..., 2 * model_width :] + bias_row[model_width:]).astype(jnp.bfloat16)
    return (queries, key_part, value_part)


def split_heads(values):
    return values.reshape(values.shape[0], values.shape[1], HEADS, HEAD_DIM)


def join_heads(values):
    return values.reshape(values.shape[0], values.shape[1], HEADS * HEAD_DIM)


def soft_weights(scores):
    top_score = jnp.max(scores, axis=-1, keepdims=True)
    raised = jnp.exp(scores - top_score)
    return raised / jnp.sum(raised, axis=-1, keepdims=True)


def feature_attend(queries, key_part, value_part):
    score_scale = HEAD_DIM ** (-0.5)
    scores = (
        jnp.einsum(
            "sfhd,sghd->shfg",
            split_heads(queries),
            split_heads(key_part),
            preferred_element_type=jnp.float32,
        )
        * score_scale
    )
    probability = soft_weights(scores)
    mixed = jnp.einsum(
        "shfg,sghd->sfhd",
        probability.astype(jnp.bfloat16),
        split_heads(value_part),
        preferred_element_type=jnp.float32,
    )
    return (join_heads(mixed).astype(jnp.bfloat16), probability)


def feature_grads(queries, key_part, value_part, probability, grad_mixed):
    score_scale = HEAD_DIM ** (-0.5)
    grad_heads = split_heads(grad_mixed)
    grad_weights = jnp.einsum(
        "sfhd,sghd->shfg", grad_heads, split_heads(value_part), preferred_element_type=jnp.float32
    )
    inner_sum = jnp.sum(probability * grad_weights, axis=-1, keepdims=True)
    grad_scores = (probability * (grad_weights - inner_sum)).astype(jnp.bfloat16)
    grad_queries = (
        jnp.einsum(
            "shfg,sghd->sfhd",
            grad_scores,
            split_heads(key_part),
            preferred_element_type=jnp.float32,
        )
        * score_scale
    )
    grad_keys = (
        jnp.einsum(
            "shfg,sfhd->sghd", grad_scores, split_heads(queries), preferred_element_type=jnp.float32
        )
        * score_scale
    )
    grad_values = jnp.einsum(
        "shfg,sfhd->sghd",
        probability.astype(jnp.bfloat16),
        grad_heads,
        preferred_element_type=jnp.float32,
    )
    return (join_heads(grad_queries), join_heads(grad_keys), join_heads(grad_values))


def local_large(
    layer_input,
    segment_ids,
    context_flags,
    first_gain,
    first_shift,
    sample_weight,
    sample_bias,
    sample_mixer,
    sample_offset,
    second_gain,
    second_shift,
    feature_weight,
    feature_bias,
    feature_mixer,
    feature_offset,
    third_gain,
    third_shift,
    expand_weight,
    expand_bias,
    reduce_weight,
    reduce_bias,
    cotangent,
):
    sample_rows = layer_input.shape[0]
    feature_rows = layer_input.shape[1]
    model_width = layer_input.shape[2]
    score_scale = HEAD_DIM ** (-0.5)
    shard_count = lax.axis_size("samp")
    context_shards = shard_count // 8
    total_context = context_shards * sample_rows
    residual_zero = layer_input.astype(jnp.float32)
    normed_one, norm_one_back = jax.vjp(layer_norm, residual_zero, first_gain, first_shift)
    active_one = normed_one.astype(jnp.bfloat16)
    queries_one, keys_one, values_one = project(active_one, sample_weight, sample_bias)
    my_index = lax.axis_index("samp")
    shard_flags = context_flags.reshape(shard_count, sample_rows)[:, 0]
    shard_rank = jnp.cumsum(shard_flags) - 1
    shard_ids = jnp.arange(shard_count, dtype=jnp.int32)
    slot_ids = jnp.arange(context_shards, dtype=jnp.int32)
    root_hits = (shard_rank[None, :] == slot_ids[:, None]) & (shard_flags[None, :] == 1)
    roots = jnp.sum(jnp.where(root_hits, shard_ids[None, :], 0), axis=1)
    context_tasks = jnp.take(segment_ids.reshape(shard_count, sample_rows), roots, axis=0).reshape(
        total_context
    )
    local_tasks = lax.dynamic_slice_in_dim(segment_ids, my_index * sample_rows, sample_rows)
    allowed = local_tasks[:, None] == context_tasks[None, :]
    is_context = shard_flags[my_index] == 1
    own_rank = jnp.maximum(shard_rank[my_index], 0)
    own_block = jnp.concatenate([keys_one, values_one], axis=-1)

    def fetch_rows(step, buffer):
        piece = spread_2(own_block, "samp", roots[step])
        return lax.dynamic_update_slice_in_dim(buffer, piece, step * sample_rows, 0)

    empty_rows = jnp.zeros((total_context, feature_rows, 2 * model_width), jnp.bfloat16)
    fetched = lax.fori_loop(0, context_shards, fetch_rows, empty_rows)
    context_keys = fetched[..., :model_width]
    context_values = fetched[..., model_width:]
    query_heads = split_heads(queries_one)
    key_heads = split_heads(context_keys)
    value_heads = split_heads(context_values)
    scores = (
        jnp.einsum("sfhd,cfhd->fhsc", query_heads, key_heads, preferred_element_type=jnp.float32)
        * score_scale
    )
    sample_prob = soft_weights(jnp.where(allowed[None, None], scores, MASKED))
    sample_weights = sample_prob.astype(jnp.bfloat16)
    mixed_one = join_heads(
        jnp.einsum(
            "fhsc,cfhd->sfhd", sample_weights, value_heads, preferred_element_type=jnp.float32
        )
    ).astype(jnp.bfloat16)
    residual_one = residual_zero + apply_weight(mixed_one, sample_mixer) + sample_offset
    normed_two, norm_two_back = jax.vjp(layer_norm, residual_one, second_gain, second_shift)
    active_two = normed_two.astype(jnp.bfloat16)
    queries_two, keys_two, values_two = project(active_two, feature_weight, feature_bias)
    all_keys, all_values = (
        lax.all_gather(keys_two, "feat", axis=1, tiled=True),
        lax.all_gather(values_two, "feat", axis=1, tiled=True),
    )
    mixed_two, feature_prob = feature_attend(queries_two, all_keys, all_values)
    residual_two = residual_one + apply_weight(mixed_two, feature_mixer) + feature_offset
    normed_three, norm_three_back = jax.vjp(layer_norm, residual_two, third_gain, third_shift)
    active_three = normed_three.astype(jnp.bfloat16)
    expanded = apply_weight(active_three, expand_weight) + expand_bias
    activated, gelu_back = jax.vjp(partial(jax.nn.gelu, approximate=False), expanded)
    hidden = activated.astype(jnp.bfloat16)
    layer_output = (residual_two + apply_weight(hidden, reduce_weight) + reduce_bias).astype(
        jnp.bfloat16
    )
    grad_out = cotangent.astype(jnp.float32)
    grad_branch = cotangent
    reduce_bias_grad = column_sum(grad_branch)
    reduce_weight_grad = weight_grad(hidden, grad_branch)
    grad_hidden = input_back(grad_branch, reduce_weight).astype(jnp.bfloat16)
    grad_expanded = gelu_back(grad_hidden.astype(jnp.float32))[0].astype(jnp.bfloat16)
    expand_bias_grad = column_sum(grad_expanded)
    expand_weight_grad = weight_grad(active_three, grad_expanded)
    grad_norm, third_gain_grad, third_shift_grad = norm_three_back(
        input_back(grad_expanded, expand_weight)
    )
    grad_two = grad_out + grad_norm
    grad_branch = grad_two.astype(jnp.bfloat16)
    feature_offset_grad = column_sum(grad_branch)
    feature_mixer_grad = weight_grad(mixed_two, grad_branch)
    grad_mixed = input_back(grad_branch, feature_mixer).astype(jnp.bfloat16)
    grad_queries, grad_keys, grad_values = feature_grads(
        queries_two, all_keys, all_values, feature_prob, grad_mixed
    )
    own_key_grads, own_value_grads = (
        lax.psum_scatter(grad_keys, "feat", scatter_dimension=1, tiled=True),
        lax.psum_scatter(grad_values, "feat", scatter_dimension=1, tiled=True),
    )
    grad_project = jnp.concatenate(
        [
            grad_queries.astype(jnp.bfloat16),
            own_key_grads.astype(jnp.bfloat16),
            own_value_grads.astype(jnp.bfloat16),
        ],
        axis=-1,
    )
    feature_weight_grad = weight_grad(active_two, grad_project)
    feature_bias_grad = jnp.concatenate(
        [
            column_sum(grad_project[..., :model_width]),
            column_sum(grad_project[..., 2 * model_width :]),
        ]
    )
    grad_norm, second_gain_grad, second_shift_grad = norm_two_back(
        input_back(grad_project, feature_weight)
    )
    grad_one = grad_two + grad_norm
    grad_branch = grad_one.astype(jnp.bfloat16)
    sample_offset_grad = column_sum(grad_branch)
    sample_mixer_grad = weight_grad(mixed_one, grad_branch)
    grad_heads = split_heads(input_back(grad_branch, sample_mixer).astype(jnp.bfloat16))
    grad_weights = jnp.einsum(
        "sfhd,cfhd->fhsc", grad_heads, value_heads, preferred_element_type=jnp.float32
    )
    inner_sum = jnp.sum(sample_prob * grad_weights, axis=-1, keepdims=True)
    grad_scores = (sample_prob * (grad_weights - inner_sum)).astype(jnp.bfloat16)
    grad_queries = (
        join_heads(
            jnp.einsum(
                "fhsc,cfhd->sfhd", grad_scores, key_heads, preferred_element_type=jnp.float32
            )
        )
        * score_scale
    ).astype(jnp.bfloat16)
    key_terms = (
        join_heads(
            jnp.einsum(
                "fhsc,sfhd->cfhd", grad_scores, query_heads, preferred_element_type=jnp.float32
            )
        )
        * score_scale
    )
    value_terms = join_heads(
        jnp.einsum(
            "fhsc,sfhd->cfhd", sample_weights, grad_heads, preferred_element_type=jnp.float32
        )
    )
    term_block = jnp.concatenate([key_terms, value_terms], axis=-1)
    summed_terms = lax.psum_scatter(term_block, "samp", scatter_dimension=0, tiled=True)
    summed_rows = lax.all_gather(summed_terms.astype(jnp.bfloat16), "samp", axis=0, tiled=True)
    own_grads = lax.dynamic_slice_in_dim(summed_rows, own_rank * sample_rows, sample_rows, 0)
    own_grads = jnp.where(is_context, own_grads, jnp.zeros_like(own_grads))
    grad_project = jnp.concatenate([grad_queries, own_grads], axis=-1)
    sample_weight_grad = weight_grad(active_one, grad_project)
    sample_bias_grad = jnp.concatenate(
        [column_sum(grad_queries), column_sum(own_grads[..., model_width:])]
    )
    grad_norm, first_gain_grad, first_shift_grad = norm_one_back(
        input_back(grad_project, sample_weight)
    )
    input_grad = (grad_one + grad_norm).astype(jnp.bfloat16)
    summed = lax.psum(
        (
            first_gain_grad,
            first_shift_grad,
            sample_weight_grad,
            sample_bias_grad,
            sample_mixer_grad,
            sample_offset_grad,
            second_gain_grad,
            second_shift_grad,
            feature_weight_grad,
            feature_bias_grad,
            feature_mixer_grad,
            feature_offset_grad,
            third_gain_grad,
            third_shift_grad,
            expand_weight_grad,
            expand_bias_grad,
            reduce_weight_grad,
            reduce_bias_grad,
        ),
        "feat",
    )
    shares = (
        lax.psum_scatter(summed[0], "samp", scatter_dimension=0, tiled=True),
        lax.psum_scatter(summed[1], "samp", scatter_dimension=0, tiled=True),
        lax.psum_scatter(summed[2], "samp", scatter_dimension=0, tiled=True),
        lax.psum_scatter(summed[3], "samp", scatter_dimension=0, tiled=True),
        lax.psum_scatter(summed[4], "samp", scatter_dimension=0, tiled=True),
        lax.psum_scatter(summed[5], "samp", scatter_dimension=0, tiled=True),
        lax.psum_scatter(summed[6], "samp", scatter_dimension=0, tiled=True),
        lax.psum_scatter(summed[7], "samp", scatter_dimension=0, tiled=True),
        lax.psum_scatter(summed[8], "samp", scatter_dimension=0, tiled=True),
        lax.psum_scatter(summed[9], "samp", scatter_dimension=0, tiled=True),
        lax.psum_scatter(summed[10], "samp", scatter_dimension=0, tiled=True),
        lax.psum_scatter(summed[11], "samp", scatter_dimension=0, tiled=True),
        lax.psum_scatter(summed[12], "samp", scatter_dimension=0, tiled=True),
        lax.psum_scatter(summed[13], "samp", scatter_dimension=0, tiled=True),
        lax.psum_scatter(summed[14], "samp", scatter_dimension=0, tiled=True),
        lax.psum_scatter(summed[15], "samp", scatter_dimension=0, tiled=True),
        lax.psum_scatter(summed[16], "samp", scatter_dimension=0, tiled=True),
        lax.psum_scatter(summed[17], "samp", scatter_dimension=0, tiled=True),
    )
    return (
        layer_output,
        input_grad,
        shares[0],
        shares[1],
        shares[2],
        shares[3],
        shares[4],
        shares[5],
        shares[6],
        shares[7],
        shares[8],
        shares[9],
        shares[10],
        shares[11],
        shares[12],
        shares[13],
        shares[14],
        shares[15],
        shares[16],
        shares[17],
    )


def solution(mesh):
    if mesh.shape["samp"] == 8 and mesh.shape["feat"] == 4:
        return solution_small(mesh)
    return jax.shard_map(
        local_large,
        mesh=mesh,
        in_specs=(
            P("samp", "feat", None),
            P(),
            P(),
            P(),
            P(),
            P(),
            P(),
            P(),
            P(),
            P(),
            P(),
            P(),
            P(),
            P(),
            P(),
            P(),
            P(),
            P(),
            P(),
            P(),
            P(),
            P("samp", "feat", None),
        ),
        out_specs=(
            P("samp", "feat", None),
            P("samp", "feat", None),
            P("samp"),
            P("samp"),
            P("samp", None),
            P("samp"),
            P("samp", None),
            P("samp"),
            P("samp"),
            P("samp"),
            P("samp", None),
            P("samp"),
            P("samp", None),
            P("samp"),
            P("samp"),
            P("samp"),
            P("samp", None),
            P("samp"),
            P("samp", None),
            P("samp"),
        ),
        check_vma=False,
    )


def solution_small(mesh):
    mesh = jax.sharding.Mesh(mesh.devices.reshape(2, 4, 4), ("half", "quad", "feat"))
    tokens, copied = P(SAMP, "feat", None), P()
    vector, matrix = P(SAMP), P(SAMP, None)
    return jax.shard_map(
        local_small,
        mesh=mesh,
        in_specs=(tokens,) + (copied,) * 20 + (tokens,),
        out_specs=(
            tokens, tokens, vector, vector, matrix, vector, matrix, vector,
            vector, vector, matrix, vector, matrix, vector,
            vector, vector, matrix, vector, matrix, vector,
        ),
        check_vma=False,
    )
```
